32 devices in a mesh: dp: 2 (over core), fsdp: 16 (over z, y, x).
Axes of the slice: x: 2, y: 2, z: 4, core: 2. Of those that a mesh axis runs over, the one named last changes fastest.
Arguments:
- inputs: bfloat16 [32, 512, 1024], P(('dp', 'fsdp')), may hold values from -6 to 6
- cotangent: bfloat16 [32, 512, 1024], P(('dp', 'fsdp')), may hold values from -6 to 6
- seg_lengths: int32 [32, 4], P(('dp', 'fsdp')), may hold values from 1 to 256, 512 in all within a row
- valid_len: int32 [32], P(('dp', 'fsdp')), may hold values from 256 to 512
- w_qkv: bfloat16 [1024, 3072], P(('dp', 'fsdp')), may hold values from -0.1875 to 0.1875
- b_qkv: bfloat16 [3072], P(('dp', 'fsdp')), may hold values from -3 to 3
- w_out: bfloat16 [1024, 1024], P(('dp', 'fsdp')), may hold values from -1.5 to 1.5
- b_out: bfloat16 [1024], P(('dp', 'fsdp')), may hold values from -3 to 3
- gain_one: bfloat16 [1024], P(('dp', 'fsdp')), may hold values from 0.5 to 1.5
- shift_one: bfloat16 [1024], P(('dp', 'fsdp')), may hold values from -2 to 2
- w_up: bfloat16 [1024, 4096], P(('dp', 'fsdp')), may hold values from -0.1875 to 0.1875
- b_up: bfloat16 [4096], P(('dp', 'fsdp')), may hold values from -3 to 3
- w_down: bfloat16 [4096, 1024], P(('dp', 'fsdp')), may hold values from -0.09375 to 0.09375
- b_down: bfloat16 [1024], P(('dp', 'fsdp')), may hold values from -3 to 3
- gain_two: bfloat16 [1024], P(('dp', 'fsdp')), may hold values from 0.5 to 1.5
- shift_two: bfloat16 [1024], P(('dp', 'fsdp')), may hold values from -2 to 2
Outputs:
- result: bfloat16 [32, 512, 1024], P(('dp', 'fsdp'))
- grad_inputs: bfloat16 [32, 512, 1024], P(('dp', 'fsdp'))
- grad_qkv: float32 [1024, 3072], P(('dp', 'fsdp'))
- grad_bqk: float32 [2048], P(('dp', 'fsdp'))
- grad_bv: float32 [1024], P(('dp', 'fsdp'))
- grad_wout: float32 [1024, 1024], P(('dp', 'fsdp'))
- grad_bout: float32 [1024], P(('dp', 'fsdp'))
- grad_gain_one: float32 [1024], P(('dp', 'fsdp'))
- grad_shift_one: float32 [1024], P(('dp', 'fsdp'))
- grad_wup: float32 [1024, 4096], P(('dp', 'fsdp'))
- grad_bup: float32 [4096], P(('dp', 'fsdp'))
- grad_wdown: float32 [4096, 1024], P(('dp', 'fsdp'))
- grad_bdown: float32 [1024], P(('dp', 'fsdp'))
- grad_gain_two: float32 [1024], P(('dp', 'fsdp'))
- grad_shift_two: float32 [1024], P(('dp', 'fsdp'))
The draws below stay inside these ranges and needn't reach their ends.
Inputs may be any that keep to these rules, and one draw needn't show every extreme that they name: `seg_lengths`: each row's 4 image lengths sum to 512.
All inputs are finite; a program needn't handle non-finite values.
Results may differ from the reference program's by a relative error of at most 0.04.
Values may be sent and summed in bfloat16 or wider, within the bound.
No kernel may reach another device: no remote copies, remote signals or barrier semaphores. Data moves between devices by JAX's collectives and lax.ppermute only.
A program may use at most 256 MiB of HBM per device.

```python
import math
import jax
import jax.numpy as jnp
import numpy as np
from jax import lax

D = 1024
HEADS = 16
HDIM = 64
FF = 4096
LEN = 512
NSEG = 4
BATCH = 32


def set_ends(values, own_key, least, top_value):
    place = [jax.random.randint(jax.random.fold_in(own_key, axis), (), 0, length) for axis, length in enumerate(values.shape)]
    longest = values.shape.index(max(values.shape))
    beside = place[:longest] + [(place[longest] + 1) % values.shape[longest]] + place[longest + 1:]
    return values.at[tuple(place)].set(least).at[tuple(beside)].set(top_value)


def spiked(array, stream_key, source, target, blocks, factor):
    def block_of(axis_at):
        return (jnp.arange(array.shape[axis_at]) // (array.shape[axis_at] // blocks)).reshape((-1,) + (1,) * (array.ndim - 1 - axis_at))

    first = jax.random.permutation(stream_key, blocks)[block_of(target)]
    second = (block_of(target) + blocks // 2) % blocks
    return jnp.where((block_of(source) == first) | (block_of(source) == second), factor * array, array)


def levels(stream_key, dims, shards, least, largest):
    gain, own = 1.0, jax.random.fold_in(stream_key, 6)
    for dim, parts in shards:
        steps = jnp.exp(jax.random.uniform(jax.random.fold_in(own, dim), (parts,), jnp.float32, least / len(shards), largest / len(shards)))
        gain = gain * jnp.repeat(steps, dims[dim] // parts).reshape([-1 if axis == dim else 1 for axis in range(len(dims))])
    return gain


def profile(amount, total, reach, lean):
    weights = [(1 << 20) // math.isqrt(standing ** lean) + 1 for standing in range(2, amount + 1)]
    spare, holding = total - reach - (amount - 1), [1] * (amount - 1)
    while spare > 0:
        movable = [i for i in range(amount - 1) if holding[i] < reach]
        whole, budget = sum([weights[i] for i in movable]), spare
        for i in movable:
            extra = min(reach - holding[i], max(1, budget * weights[i] // whole), spare)
            holding[i] = holding[i] + extra
            spare = spare - extra
    return np.array([reach] + holding)


def uneven_parts(own_key, number_of, total, limit, lean):
    if number_of == 2:
        one = jax.random.randint(own_key, (), max(1, total - limit), min(limit, total - 1) + 1)
        return jnp.stack([one, total - one])
    sizes = jnp.asarray(profile(number_of, total, limit, lean), jnp.int32)
    couples = (number_of - 1) // 2
    giver, receiver = sizes[1:1 + 2 * couples:2], sizes[2:2 + 2 * couples:2]
    slack = jnp.minimum(giver - 1, limit - receiver)
    moved = jax.random.randint(jax.random.fold_in(own_key, 1), (couples,), 0, 1 << 20) % (slack + 1)
    sizes = sizes.at[1:1 + 2 * couples:2].set(giver - moved).at[2:2 + 2 * couples:2].set(receiver + moved)
    return sizes[jax.random.permutation(jax.random.fold_in(own_key, 2), number_of)]


def gaussian(own_key, dims, deviation, limit, pieces=(), kind=jnp.bfloat16):
    gain = levels(own_key, dims, pieces, -0.22, 0.18) if pieces else 1.0
    drawn = jax.random.normal(own_key, dims, jnp.float32) * deviation * gain
    return jnp.minimum(jnp.maximum(drawn, -limit), limit).astype(kind)


def bell_draw_with(stream_key, extent, width, reach, cuts, heavy, kind=jnp.bfloat16):
    entries = width * jax.random.normal(stream_key, extent, jnp.float32)
    if cuts:
        entries = entries * levels(stream_key, extent, cuts, -0.22, 0.18)
    return jnp.clip(spiked(entries, jax.random.fold_in(stream_key, 3), *heavy), -reach, reach).astype(kind)


def setup_inputs(seed: int = 0) -> dict:
    key_of = jax.random.split(jax.random.key(seed), 17)
    return {
        "inputs": bell_draw_with(key_of[0], (BATCH, LEN, D), 1.0, 6.0, ((0, 32),), (0, 2, 32, 2.75)),
        "cotangent": gaussian(key_of[1], (BATCH, LEN, D), 1.0, 6.0, ((0, 32),)),
        "seg_lengths": jax.vmap(lambda own: uneven_parts(own, NSEG, LEN, LEN // 2, 0))(jax.random.split(key_of[2], BATCH)).reshape((BATCH, NSEG)).astype(jnp.int32),
        "valid_len": set_ends(jax.random.randint(key_of[3], (BATCH,), LEN // 2, LEN + 1), jax.random.fold_in(key_of[3], 1), LEN // 2, LEN).astype(jnp.int32),
        "w_qkv": gaussian(key_of[4], (D, 3 * D), D ** -0.5, 0.1875, ((0, 32),)),
        "b_qkv": gaussian(key_of[5], (3 * D,), 0.5, 3.0, ((0, 32),)),
        "w_out": gaussian(key_of[6], (D, D), (D // 64) ** -0.5, 1.5, ((0, 32),)),
        "b_out": gaussian(key_of[7], (D,), 0.5, 3.0, ((0, 32),)),
        "gain_one": jnp.clip(1.0 + 0.1 * jax.random.normal(key_of[8], (D,), jnp.float32), 0.5, 1.5).astype(jnp.bfloat16),
        "shift_one": gaussian(key_of[9], (D,), 0.3, 2.0, ((0, 32),)),
        "w_up": gaussian(key_of[10], (D, FF), D ** -0.5, 0.1875, ((0, 32),)),
        "b_up": gaussian(key_of[11], (FF,), 0.5, 3.0, ((0, 32),)),
        "w_down": gaussian(key_of[12], (FF, D), FF ** -0.5, 0.09375, ((0, 32),)),
        "b_down": gaussian(key_of[13], (D,), 0.5, 3.0, ((0, 32),)),
        "gain_two": jnp.clip(1.0 + 0.1 * jax.random.normal(key_of[14], (D,), jnp.float32), 0.5, 1.5).astype(jnp.bfloat16),
        "shift_two": gaussian(key_of[15], (D,), 0.3, 2.0, ((0, 32),)),
    }


@jax.custom_vjp
def low(v):
    return lax.optimization_barrier(v.astype(jnp.bfloat16)).astype(jnp.float32)

@jax.custom_vjp
def low_back(v):
    return v

def low_keep(v):
    return (low(v), None)

def low_pass(kept, grad):
    return (grad,)

def back_keep(v):
    return (v, None)

def back_low(kept, grad):
    return (low(grad),)
low.defvjp(low_keep, low_pass)
low_back.defvjp(back_keep, back_low)
highest = lax.Precision.HIGHEST
norm_eps = 1e-05
denom_eps = 1e-06
gelu_coef = 0.7978845608028654

def product(left_side, right_side):
    return jnp.dot(left_side, right_side, precision=highest, preferred_element_type=jnp.float32)

def layer_norm(values, scale_gain, offset):
    centred = values - lax.optimization_barrier(jnp.mean(values, axis=-1, keepdims=True))
    spread = lax.optimization_barrier(jnp.mean(centred * centred, axis=-1, keepdims=True))
    return centred * lax.rsqrt(spread + norm_eps) * scale_gain + offset

def feature_map(values):
    return jnp.where(values > 0, values + 1.0, jnp.exp(jnp.minimum(values, 0.0)))

def gelu_tanh(values):
    return 0.5 * values * (1.0 + jnp.tanh(gelu_coef * (values + 0.044715 * values * values * values)))

def row_masks(lengths, valid_count, row_length):
    places = jnp.arange(row_length, dtype=jnp.int32)
    bounds = jnp.cumsum(lengths.astype(jnp.int32)).astype(jnp.int32)
    segment = lax.optimization_barrier(jnp.sum((places[:, None] >= bounds[None, :]).astype(jnp.int32), axis=1))
    allowed = (segment[:, None] == segment[None, :]) & (places[None, :] <= places[:, None])
    keeping = (places < valid_count).astype(jnp.float32)
    return (allowed.astype(jnp.float32), keeping)

def row_forward(token_rows, allowed, keeping, params):
    w_qkv, b_qkv, w_out, b_out, gain_one, shift_one, w_up, b_up, w_down, b_down, gain_two, shift_two = params
    normed = low(layer_norm(token_rows, gain_one, shift_one))
    projected = low_back(product(normed, w_qkv) + b_qkv)
    queries = low(feature_map(projected[:, :D])).reshape(LEN, HEADS, HDIM)
    keys_feat = low(feature_map(projected[:, D:2 * D])).reshape(LEN, HEADS, HDIM)
    values = low(projected[:, 2 * D:]).reshape(LEN, HEADS, HDIM)
    scores = low_back(jnp.einsum('qhe,khe->hqk', queries, keys_feat, precision=highest) * allowed[None])
    denominator = lax.optimization_barrier(jnp.sum(scores, axis=2)) + denom_eps
    numerator = low_back(jnp.einsum('hqk,khe->hqe', low(scores), values, precision=highest))
    attended = keeping[None, :, None] * numerator / denominator[:, :, None]
    attended = low(jnp.transpose(attended, (1, 0, 2)).reshape(LEN, D))
    mixed_out = low_back(product(attended, w_out) + b_out)
    middle = token_rows + mixed_out
    normed_two = low(layer_norm(middle, gain_two, shift_two))
    hidden = low_back(product(normed_two, w_up) + b_up)
    activated = low(gelu_tanh(hidden))
    branch = low_back(product(activated, w_down) + b_down)
    return middle + branch

def reference(inputs, cotangent, seg_lengths, valid_len, w_qkv, b_qkv, w_out, b_out, gain_one, shift_one, w_up, b_up, w_down, b_down, gain_two, shift_two):
    params = tuple((weight.astype(jnp.float32) for weight in (w_qkv, b_qkv, w_out, b_out, gain_one, shift_one, w_up, b_up, w_down, b_down, gain_two, shift_two)))
    token_rows = inputs.astype(jnp.float32)

    def forward(all_rows, weights):

        def one_row(row_item):
            single, lengths, valid_count = row_item
            allowed, keeping = row_masks(lengths, valid_count, LEN)
            return row_forward(single, allowed, keeping, weights)
        return lax.map(jax.checkpoint(one_row), (all_rows, seg_lengths, valid_len))
    result, pullback = jax.vjp(forward, token_rows, params)
    grad_rows, grad_params = pullback(cotangent.astype(jnp.float32))
    bias_grad = grad_params[1]
    return (result.astype(jnp.bfloat16), grad_rows.astype(jnp.bfloat16), grad_params[0], bias_grad[:2 * D], bias_grad[2 * D:], grad_params[2], grad_params[3], grad_params[4], grad_params[5], grad_params[6], grad_params[7], grad_params[8], grad_params[9], grad_params[10], grad_params[11])
```

```python
from functools import partial

import jax
import jax.numpy as jnp
from jax import lax
from jax.experimental import pallas as pl
from jax.experimental.pallas import tpu as pltpu
from jax.sharding import PartitionSpec as P

HEADS = 16


norm_eps = 1e-05
denom_eps = 1e-06
gelu_coef = 0.7978845608028654


def layer_norm(values, scale_gain, offset):
    centred = values - jnp.mean(values, axis=-1, keepdims=True)
    spread = jnp.mean(centred * centred, axis=-1, keepdims=True)
    return centred * lax.rsqrt(spread + norm_eps) * scale_gain + offset


def feature_map(values):
    return jnp.where(values > 0, values + 1.0, jnp.exp(jnp.minimum(values, 0.0)))


def gelu_tanh(values):
    return (
        0.5 * values * (1.0 + jnp.tanh(gelu_coef * (values + 0.044715 * values * values * values)))
    )


def contract_rows(left_side, right_side):
    return lax.dot_general(
        left_side, right_side, (((0,), (0,)), ((), ())), preferred_element_type=jnp.float32
    )


def contract_cols(left_side, right_side):
    return lax.dot_general(
        left_side, right_side, (((1,), (1,)), ((), ())), preferred_element_type=jnp.float32
    )


def row_masks(lengths, valid_count, row_length):
    places = jnp.arange(row_length, dtype=jnp.int32)
    bounds = jnp.stack([jnp.sum(lengths[: end + 1]) for end in range(lengths.shape[0])])
    segment = jnp.sum((places[:, None] >= bounds[None, :]).astype(jnp.int32), axis=1)
    allowed = (segment[:, None] == segment[None, :]) & (places[None, :] <= places[:, None])
    keeping = (places < valid_count).astype(jnp.float32)
    return (allowed.astype(jnp.float32), keeping)


def split_heads(matrix):
    return jnp.transpose(matrix.reshape(matrix.shape[0], HEADS, -1), (1, 0, 2))


def join_heads(stacked):
    return jnp.transpose(stacked, (1, 0, 2)).reshape(stacked.shape[1], -1)


def pull_group(first, second, third, fourth, fifth, sixth):
    return (
        lax.all_gather(first, ("dp", "fsdp"), axis=0, tiled=True),
        lax.all_gather(second, ("dp", "fsdp"), axis=0, tiled=True),
        lax.all_gather(third, ("dp", "fsdp"), axis=0, tiled=True),
        lax.all_gather(fourth, ("dp", "fsdp"), axis=0, tiled=True),
        lax.all_gather(fifth, ("dp", "fsdp"), axis=0, tiled=True),
        lax.all_gather(sixth, ("dp", "fsdp"), axis=0, tiled=True),
    )


def push_group(first, second, third, stacked):
    return (
        lax.psum_scatter(first, ("dp", "fsdp"), scatter_dimension=0, tiled=True),
        lax.psum_scatter(second, ("dp", "fsdp"), scatter_dimension=0, tiled=True),
        lax.psum_scatter(third, ("dp", "fsdp"), scatter_dimension=0, tiled=True),
        lax.psum_scatter(stacked, ("dp", "fsdp"), scatter_dimension=1, tiled=True),
    )


def head_forward(allowed, head_item):
    query_head, key_head, value_head = head_item
    scores = contract_cols(query_head, key_head) * allowed
    denominator = jnp.sum(scores, axis=1) + denom_eps
    numerator = jnp.dot(scores.astype(jnp.bfloat16), value_head, preferred_element_type=jnp.float32)
    return (numerator, denominator)


def head_backward(allowed, head_item):
    query_head, key_head, value_head, grad_numer, grad_denom = head_item
    scores = contract_cols(query_head, key_head) * allowed
    grad_prob = contract_cols(grad_numer, value_head)
    grad_value = contract_rows(scores.astype(jnp.bfloat16), grad_numer)
    grad_scores = ((grad_prob + grad_denom[:, None]) * allowed).astype(jnp.bfloat16)
    grad_query = jnp.dot(grad_scores, key_head, preferred_element_type=jnp.float32)
    grad_key = contract_rows(grad_scores, query_head)
    return (grad_query, grad_key, grad_value)


def plain_body(
    inputs,
    cotangent,
    seg_lengths,
    valid_len,
    w_qkv,
    b_qkv,
    w_out,
    b_out,
    gain_one,
    shift_one,
    w_up,
    b_up,
    w_down,
    b_down,
    gain_two,
    shift_two,
):
    token_rows = inputs[0].astype(jnp.float32)
    row_length = token_rows.shape[0]
    model_width = token_rows.shape[1]
    allowed, keeping = row_masks(seg_lengths[0], valid_len[0], row_length)
    full_qkv, full_bqkv, full_out, full_bout, full_gain, full_shift = pull_group(
        w_qkv, b_qkv, w_out, b_out, gain_one, shift_one
    )
    normed, norm_back = jax.vjp(
        layer_norm, token_rows, full_gain.astype(jnp.float32), full_shift.astype(jnp.float32)
    )
    normed_low = normed.astype(jnp.bfloat16)
    projected = jnp.dot(
        normed_low, full_qkv, preferred_element_type=jnp.float32
    ) + full_bqkv.astype(jnp.float32)
    query_feat, query_back = jax.vjp(feature_map, projected[:, :model_width])
    key_feat, key_back = jax.vjp(feature_map, projected[:, model_width : 2 * model_width])
    query_heads = split_heads(query_feat.astype(jnp.bfloat16))
    key_heads = split_heads(key_feat.astype(jnp.bfloat16))
    value_heads = split_heads(projected[:, 2 * model_width :].astype(jnp.bfloat16))
    numerator, denominator = lax.map(
        partial(head_forward, allowed), (query_heads, key_heads, value_heads)
    )
    attended = keeping[None, :, None] * numerator / denominator[:, :, None]
    attended_low = join_heads(attended).astype(jnp.bfloat16)
    middle = (
        token_rows
        + jnp.dot(attended_low, full_out, preferred_element_type=jnp.float32)
        + full_bout.astype(jnp.float32)
    )
    full_up, full_bup, full_down, full_bdown, full_gain_two, full_shift_two = pull_group(
        w_up, b_up, w_down, b_down, gain_two, shift_two
    )
    normed_two, norm_two_back = jax.vjp(
        layer_norm, middle, full_gain_two.astype(jnp.float32), full_shift_two.astype(jnp.float32)
    )
    normed_two_low = normed_two.astype(jnp.bfloat16)
    hidden = jnp.dot(normed_two_low, full_up, preferred_element_type=jnp.float32) + full_bup.astype(
        jnp.float32
    )
    activated, gelu_back = jax.vjp(gelu_tanh, hidden)
    activated_low = activated.astype(jnp.bfloat16)
    result = (
        middle
        + jnp.dot(activated_low, full_down, preferred_element_type=jnp.float32)
        + full_bdown.astype(jnp.float32)
    )
    again_up, again_bup, again_down, again_bdown, again_gain_two, again_shift_two = pull_group(
        w_up, b_up, w_down, b_down, gain_two, shift_two
    )
    grad_top = cotangent[0]
    grad_top_full = grad_top.astype(jnp.float32)
    grad_down = contract_rows(activated_low, grad_top)
    grad_bdown = jnp.sum(grad_top_full, axis=0)
    grad_hidden = gelu_back(contract_cols(grad_top, again_down))[0]
    grad_hidden_low = grad_hidden.astype(jnp.bfloat16)
    grad_bup = jnp.sum(grad_hidden_low.astype(jnp.float32), axis=0)
    grad_up = contract_rows(normed_two_low, grad_hidden_low)
    grad_normed_two = contract_cols(grad_hidden_low, again_up)
    grad_middle_norm, grad_gain_two, grad_shift_two = norm_two_back(grad_normed_two)
    grad_middle = grad_top_full + grad_middle_norm
    shard_up, shard_bup, shard_down, shard_small_two = push_group(
        grad_up, grad_bup, grad_down, jnp.stack([grad_bdown, grad_gain_two, grad_shift_two])
    )
    again_qkv, again_bqkv, again_out, again_bout, again_gain, again_shift = pull_group(
        w_qkv, b_qkv, w_out, b_out, gain_one, shift_one
    )
    grad_mixed = grad_middle.astype(jnp.bfloat16)
    grad_bout = jnp.sum(grad_mixed.astype(jnp.float32), axis=0)
    grad_wout = contract_rows(attended_low, grad_mixed)
    grad_attended = split_heads(contract_cols(grad_mixed, again_out))
    grad_numer = (keeping[None, :, None] * grad_attended / denominator[:, :, None]).astype(
        jnp.bfloat16
    )
    grad_denom = -jnp.sum(grad_attended * attended, axis=2) / denominator
    grad_query_heads, grad_key_heads, grad_value_heads = lax.map(
        partial(head_backward, allowed),
        (query_heads, key_heads, value_heads, grad_numer, grad_denom),
    )
    grad_query = query_back(join_heads(grad_query_heads))[0]
    grad_key = key_back(join_heads(grad_key_heads))[0]
    grad_projected = jnp.concatenate(
        [grad_query, grad_key, join_heads(grad_value_heads)], axis=1
    ).astype(jnp.bfloat16)
    grad_bias_all = jnp.sum(grad_projected.astype(jnp.float32), axis=0)
    grad_bias_qk = grad_bias_all[: 2 * model_width]
    grad_bias_v = grad_bias_all[2 * model_width :]
    grad_qkv = contract_rows(normed_low, grad_projected)
    grad_normed = contract_cols(grad_projected, again_qkv)
    grad_rows_norm, grad_gain_one, grad_shift_one = norm_back(grad_normed)
    grad_inputs = (grad_middle + grad_rows_norm).astype(jnp.bfloat16)
    shard_qkv, shard_bias_qk, shard_wout, shard_small_one = push_group(
        grad_qkv,
        grad_bias_qk,
        grad_wout,
        jnp.stack([grad_bout, grad_bias_v, grad_gain_one, grad_shift_one]),
    )
    return (
        result.astype(jnp.bfloat16)[None],
        grad_inputs[None],
        shard_qkv,
        shard_bias_qk,
        shard_small_one[1],
        shard_wout,
        shard_small_one[0],
        shard_small_one[2],
        shard_small_one[3],
        shard_up,
        shard_bup,
        shard_down,
        shard_small_two[0],
        shard_small_two[1],
        shard_small_two[2],
    )


HALF_LANES = 64
TILE = 512
Z_HIGH, Z_LOW, Y_BIT, X_BIT = 8, 4, 2, 1
ORDERS = ((Z_HIGH, X_BIT, Z_LOW, Y_BIT), (Z_HIGH, Y_BIT, Z_LOW, X_BIT))
ANY = pl.BlockSpec(memory_space=pl.ANY)
SMEM = pl.BlockSpec(memory_space=pltpu.SMEM)
VMEM = pl.BlockSpec(memory_space=pltpu.VMEM)
MIB = 1 << 20


def swap_chips(block, bit):
    return lax.ppermute(block, "fsdp", [(place, place ^ bit) for place in range(16)])


def swap_cores(block):
    return lax.ppermute(block, "dp", [(0, 1), (1, 0)])


def relative_place(order, slot, last):
    return (
        order[0] * (slot & 1)
        + order[1] * ((slot >> 1) & 1)
        + order[2] * ((slot >> 2) & 1)
        + order[3] * last
    )


def gather_half(shard, order):
    held = shard[None]
    for bit in order[:-1]:
        held = jnp.concatenate([held, swap_chips(held, bit)], axis=0)
    across = swap_chips(held, order[-1])
    return [held, across, swap_cores(held), swap_cores(across)]


def gather_shards(shard):
    half = shard.shape[1] // 2
    return gather_half(shard[:, :half], ORDERS[0]) + gather_half(shard[:, half:], ORDERS[1])


def reduce_half(kept, sent, order):
    for step, bit in enumerate(reversed(order)):
        arrived = swap_chips(sent, bit)
        total = kept.astype(jnp.float32) + arrived.astype(jnp.float32)
        if step == len(order) - 1:
            return total[0]
        total = total.astype(jnp.bfloat16)
        middle = total.shape[0] // 2
        kept, sent = total[:middle], total[middle:]


def reduce_shards(parts):
    return jnp.concatenate(
        [reduce_half(parts[0], parts[1], ORDERS[0]), reduce_half(parts[2], parts[3], ORDERS[1])],
        axis=1,
    )


def sum_everywhere(block):
    for bit in (X_BIT, Y_BIT, Z_LOW, Z_HIGH):
        block = block + swap_chips(block, bit)
    return block + swap_cores(block)


def call(kernel, outs, scratch, mib, grid=None, in_specs=None, out_specs=None, flops=0, moved=0):
    extra = {} if grid is None else {"grid": grid}
    return pl.pallas_call(
        kernel,
        out_shape=outs,
        in_specs=in_specs,
        out_specs=out_specs,
        scratch_shapes=scratch,
        compiler_params=pltpu.CompilerParams(vmem_limit_bytes=mib * MIB),
        cost_estimate=pl.CostEstimate(flops=flops, bytes_accessed=moved, transcendentals=0),
        **extra,
    )


def shaped(shape, dtype):
    return jax.ShapeDtypeStruct(shape, dtype)


def dot_nn(left, right):
    return lax.dot_general(left, right, (((1,), (0,)), ((), ())), preferred_element_type=jnp.float32)


def dot_nt(left, right):
    return lax.dot_general(left, right, (((1,), (1,)), ((), ())), preferred_element_type=jnp.float32)


def fetch(place, pieces, whole, sems):
    rows, half = pieces[0].shape[1], pieces[0].shape[2]
    copies = []
    for side, order in enumerate(ORDERS):
        for core in range(2):
            for last in range(2):
                piece = pieces[side * 4 + core * 2 + last]
                for slot in range(8):
                    owner = (place[1] ^ core) * 16 + (place[0] ^ relative_place(order, slot, last))
                    start = pl.multiple_of(owner * rows, rows)
                    copies.append(
                        pltpu.make_async_copy(
                            piece.at[slot],
                            whole.at[pl.ds(start, rows), pl.ds(side * half, half)],
                            sems.at[len(copies)],
                        )
                    )
    for copy in copies:
        copy.start()
    return copies


def wait_all(copies):
    for copy in copies:
        copy.wait()


def standardize(block):
    centred = block - jnp.mean(block, axis=1, keepdims=True)
    scale = lax.rsqrt(jnp.mean(centred * centred, axis=1, keepdims=True) + norm_eps)
    return centred * scale, scale


def norm_pull(grad, standard, scale, gain):
    scaled = grad * gain
    return scale * (
        scaled
        - jnp.mean(scaled, axis=1, keepdims=True)
        - standard * jnp.mean(scaled * standard, axis=1, keepdims=True)
    )


def qkv_kernel(place, rows_in, gain, shift, bias, *rest):
    pieces, (normed, query, key, value, whole, sems) = rest[:8], rest[8:]
    copies = fetch(place, pieces, whole, sems)
    for part in range(4):
        at = pl.ds(part * 128, 128)
        standard, _ = standardize(rows_in[at, :].astype(jnp.float32))
        normed[at, :] = (standard * gain[...] + shift[...]).astype(jnp.bfloat16)
    wait_all(copies)
    for tile in range(6):
        cols = pl.ds(tile * TILE, TILE)
        projected = dot_nn(normed[...], whole[:, cols]) + bias[:, cols]
        goal = (query, key, value)[tile // 2]
        if tile < 4:
            projected = feature_map(projected)
        goal[:, pl.ds((tile % 2) * TILE, TILE)] = projected.astype(jnp.bfloat16)


def run_qkv(place, rows_in, gain, shift, bias, pieces):
    length, width = rows_in.shape
    narrow = shaped((length, width), jnp.bfloat16)
    return call(
        qkv_kernel,
        (narrow,) * 4,
        [pltpu.VMEM((width, 3 * width), jnp.bfloat16), pltpu.SemaphoreType.DMA((64,))],
        28,
        in_specs=[SMEM] + [VMEM] * 4 + [ANY] * 8,
        out_specs=(VMEM,) * 4,
        flops=6 * length * width * width,
        moved=11 * MIB,
    )(place, rows_in, gain, shift, bias, *pieces)


def image_of(place, positions):
    image = jnp.zeros(positions.shape, jnp.int32)
    for end in range(2, 5):
        image = image + jnp.where(positions >= place[end], 1, 0)
    return image


def allowed_block(place, length, flipped):
    first = lax.broadcasted_iota(jnp.int32, (length, 1), 0)
    second = lax.broadcasted_iota(jnp.int32, (1, length), 1)
    same = image_of(place, first) == image_of(place, second)
    ordered = (first <= second) if flipped else (second <= first)
    return jnp.where(same & ordered, 1.0, 0.0).astype(jnp.float32)


def head_lanes():
    lane = lax.broadcasted_iota(jnp.int32, (1, 2 * HALF_LANES), 1)
    low = jnp.where(lane < HALF_LANES, 1.0, 0.0)
    return (low.astype(jnp.bfloat16), (1.0 - low).astype(jnp.bfloat16))


def keeping_rows(place, start, amount):
    position = lax.broadcasted_iota(jnp.int32, (amount, 1), 0) + start
    return jnp.where(position < place[5], 1.0, 0.0)


def with_ones(block, lanes):
    return jnp.concatenate([block * lanes, jnp.broadcast_to(lanes, block.shape)], axis=1)


def attend_kernel(place, query, key, value, attended, exact, inverse, allowed):
    length = query.shape[0]
    step = length // 2

    @pl.when(pl.program_id(0) == 0)
    def _():
        allowed[...] = allowed_block(place, length, False)

    for part in range(2):
        rows, seen = pl.ds(part * step, step), (part + 1) * step
        total = None
        for lanes in head_lanes():
            scores = dot_nt(query[rows, :], key[:seen, :] * lanes) * allowed[rows, :seen]
            mixed = dot_nn(scores.astype(jnp.bfloat16), with_ones(value[:seen, :], lanes))
            total = mixed if total is None else total + mixed
        width = 2 * HALF_LANES
        over = 1.0 / (total[:, width:] + denom_eps)
        inverse[rows, :] = over
        mixed = keeping_rows(place, part * step, step) * total[:, :width] * over
        exact[rows, :] = mixed
        attended[rows, :] = mixed.astype(jnp.bfloat16)


def run_attend(place, query, key, value):
    length, width = query.shape
    pair = pl.BlockSpec((length, 2 * HALF_LANES), lambda p: (0, p))
    return call(
        attend_kernel,
        (
            shaped((length, width), jnp.bfloat16),
            shaped((length, width), jnp.float32),
            shaped((length, width), jnp.float32),
        ),
        [pltpu.VMEM((length, length), jnp.float32)],
        16,
        grid=(width // (2 * HALF_LANES),),
        in_specs=[SMEM] + [pair] * 3,
        out_specs=(pair,) * 3,
        flops=8 * length * length * width,
        moved=6 * MIB,
    )(place, query, key, value)


def attend_back_kernel(
    place, query, key, value, grad_att, exact, inverse, *rest
):
    outs, sums, (allowed, flipped, left) = rest[:3], rest[3:6], rest[6:]
    length = query.shape[0]
    step = length // 2
    width = 2 * HALF_LANES

    @pl.when(pl.program_id(0) == 0)
    def _():
        allowed[...] = allowed_block(place, length, False)
        flipped[...] = allowed_block(place, length, True)

    over = grad_att[...] * inverse[...]
    left[:, :width] = (keeping_rows(place, 0, length) * over).astype(jnp.bfloat16)
    lane = lax.broadcasted_iota(jnp.int32, (1, width), 1)
    terms, low = over * exact[...], lane < HALF_LANES
    first = jnp.sum(jnp.where(low, terms, 0.0), axis=1, keepdims=True)
    second = jnp.sum(jnp.where(low, 0.0, terms), axis=1, keepdims=True)
    spread = -jnp.where(low, first, second)
    high = spread.astype(jnp.bfloat16).astype(jnp.float32)
    within = lane & (HALF_LANES - 1)
    spread = jnp.where(within == 0, high, jnp.where(within == 1, spread - high, 0.0))
    left[:, width:] = spread.astype(jnp.bfloat16)
    for part in range(2):
        rows, seen = pl.ds(part * step, step), (part + 1) * step
        later, grad_query, grad_key, grad_value = pl.ds(part * step, length - part * step), 0.0, 0.0, 0.0
        for lanes in head_lanes():
            grad_scores = dot_nt(left[rows, :], with_ones(value[:seen, :], lanes))
            grad_scores = (grad_scores * allowed[rows, :seen]).astype(jnp.bfloat16)
            grad_query += dot_nn(grad_scores, key[:seen, :] * lanes)
            scores = dot_nt(key[rows, :] * lanes, query[later, :])
            scores = (scores * flipped[rows, later]).astype(jnp.bfloat16)
            grad_value += dot_nn(scores, left[later, :width] * lanes)
            grad_scores = dot_nt(with_ones(value[rows, :], lanes), left[later, :])
            grad_scores = (grad_scores * flipped[rows, later]).astype(jnp.bfloat16)
            grad_key += dot_nn(grad_scores, query[later, :] * lanes)
        grads = (
            grad_query * jnp.minimum(query[rows, :].astype(jnp.float32), 1.0),
            grad_key * jnp.minimum(key[rows, :].astype(jnp.float32), 1.0),
            grad_value,
        )
        for goal, amount, grad in zip(outs, sums, grads):
            low = grad.astype(jnp.bfloat16)
            goal[rows, :] = low
            added = jnp.sum(low.astype(jnp.float32), axis=0, keepdims=True)
            amount[...] = added if part == 0 else amount[...] + added


def run_attend_back(place, query, key, value, grad_att, exact, inverse):
    length, width = query.shape
    pair = pl.BlockSpec((length, 2 * HALF_LANES), lambda p: (0, p))
    line = pl.BlockSpec((1, 2 * HALF_LANES), lambda p: (0, p))
    return call(
        attend_back_kernel,
        (shaped((length, width), jnp.bfloat16),) * 3 + (shaped((1, width), jnp.float32),) * 3,
        [
            pltpu.VMEM((length, length), jnp.float32),
            pltpu.VMEM((length, length), jnp.float32),
            pltpu.VMEM((length, 4 * HALF_LANES), jnp.bfloat16),
        ],
        20,
        grid=(width // (2 * HALF_LANES),),
        in_specs=[SMEM] + [pair] * 6,
        out_specs=(pair,) * 3 + (line,) * 3,
        flops=24 * length * length * width,
        moved=11 * MIB,
    )(place, query, key, value, grad_att, exact, inverse)


def out_kernel(place, rows_in, attended, bias, gain, shift, *rest):
    pieces, (middle, normed, whole, sems) = rest[:8], rest[8:]
    wait_all(fetch(place, pieces, whole, sems))
    for part in range(2):
        at = pl.ds(part * 256, 256)
        total = rows_in[at, :].astype(jnp.float32) + dot_nn(attended[at, :], whole[...]) + bias[...]
        middle[at, :] = total
        standard, _ = standardize(total)
        normed[at, :] = (standard * gain[...] + shift[...]).astype(jnp.bfloat16)


def run_out(place, rows_in, attended, bias, gain, shift, pieces):
    length, width = rows_in.shape
    return call(
        out_kernel,
        (shaped((length, width), jnp.float32), shaped((length, width), jnp.bfloat16)),
        [pltpu.VMEM((width, width), jnp.bfloat16), pltpu.SemaphoreType.DMA((64,))],
        24,
        in_specs=[SMEM] + [VMEM] * 5 + [ANY] * 8,
        out_specs=(VMEM,) * 2,
        flops=2 * length * width * width,
        moved=7 * MIB,
    )(place, rows_in, attended, bias, gain, shift, *pieces)


def up_kernel(place, normed, bias, *rest):
    pieces, (activated, slope, whole, sems) = rest[:8], rest[8:]
    wait_all(fetch(place, pieces, whole, sems))

    @pl.loop(0, whole.shape[1] // TILE)
    def _(tile):
        cols = pl.ds(pl.multiple_of(tile * TILE, TILE), TILE)
        hidden = dot_nn(normed[...], whole[:, cols]) + bias[:, cols]
        square = hidden * hidden
        bend = jnp.tanh(gelu_coef * (hidden + 0.044715 * square * hidden))
        activated[:, cols] = (0.5 * hidden * (1.0 + bend)).astype(jnp.bfloat16)
        rate = gelu_coef * (1.0 + 3.0 * 0.044715 * square)
        slope[:, cols] = (
            0.5 * (1.0 + bend) + 0.5 * hidden * (1.0 - bend * bend) * rate
        ).astype(jnp.bfloat16)


def run_up(place, normed, bias, pieces):
    length, width = normed.shape
    wide = bias.shape[1]
    return call(
        up_kernel,
        (shaped((length, wide), jnp.bfloat16),) * 2,
        [pltpu.VMEM((width, wide), jnp.bfloat16), pltpu.SemaphoreType.DMA((64,))],
        30,
        in_specs=[SMEM] + [VMEM] * 2 + [ANY] * 8,
        out_specs=(VMEM,) * 2,
        flops=2 * length * width * wide,
        moved=17 * MIB,
    )(place, normed, bias, *pieces)


def down_kernel(place, activated, slope, grad_top, middle, bias, *rest):
    pieces, (result, grad_hidden, sum_up, sum_down, whole, total, sems) = rest[:8], rest[8:]
    wait_all(fetch(place, pieces, whole, sems))
    total[...] = middle[...] + bias[...]

    @pl.loop(0, whole.shape[0] // TILE)
    def _(tile):
        cols = pl.ds(pl.multiple_of(tile * TILE, TILE), TILE)
        block = whole[cols, :]
        total[...] += dot_nn(activated[:, cols], block)
        grad = dot_nt(grad_top[...], block) * slope[:, cols].astype(jnp.float32)
        low = grad.astype(jnp.bfloat16)
        grad_hidden[:, cols] = low
        sum_up[:, cols] = jnp.sum(low.astype(jnp.float32), axis=0, keepdims=True)

    result[...] = total[...].astype(jnp.bfloat16)
    sum_down[...] = jnp.sum(grad_top[...].astype(jnp.float32), axis=0, keepdims=True)


def run_down(place, activated, slope, grad_top, middle, bias, pieces):
    length, width = middle.shape
    wide = activated.shape[1]
    return call(
        down_kernel,
        (
            shaped((length, width), jnp.bfloat16),
            shaped((length, wide), jnp.bfloat16),
            shaped((1, wide), jnp.float32),
            shaped((1, width), jnp.float32),
        ),
        [
            pltpu.VMEM((wide, width), jnp.bfloat16),
            pltpu.VMEM((length, width), jnp.float32),
            pltpu.SemaphoreType.DMA((64,)),
        ],
        40,
        in_specs=[SMEM] + [VMEM] * 5 + [ANY] * 8,
        out_specs=(VMEM,) * 4,
        flops=4 * length * width * wide,
        moved=24 * MIB,
    )(place, activated, slope, grad_top, middle, bias, *pieces)


def middle_back_kernel(place, grad_hidden, middle, grad_top, gain, *rest):
    pieces_up, pieces_out, rest = rest[:8], rest[8:16], rest[16:]
    grad_middle, mixed, grad_att, sum_gain, sum_shift, sum_out, whole, outer, total, sems, more = rest
    first = fetch(place, pieces_up, whole, sems)
    second = fetch(place, pieces_out, outer, more)
    total[...] = jnp.zeros_like(total)
    wait_all(first)

    @pl.loop(0, whole.shape[1] // TILE)
    def _(tile):
        cols = pl.ds(pl.multiple_of(tile * TILE, TILE), TILE)
        total[...] += dot_nt(grad_hidden[:, cols], whole[:, cols])

    wait_all(second)
    for part in range(4):
        at = pl.ds(part * 128, 128)
        grad = total[at, :]
        standard, scale = standardize(middle[at, :])
        back = grad_top[at, :].astype(jnp.float32) + norm_pull(grad, standard, scale, gain[...])
        grad_middle[at, :] = back
        low = back.astype(jnp.bfloat16)
        mixed[at, :] = low
        for goal, added in (
            (sum_gain, grad * standard),
            (sum_shift, grad),
            (sum_out, low.astype(jnp.float32)),
        ):
            added = jnp.sum(added, axis=0, keepdims=True)
            goal[...] = added if part == 0 else goal[...] + added
    for part in range(2):
        at = pl.ds(part * 256, 256)
        grad_att[at, :] = dot_nt(mixed[at, :], outer[...])


def run_middle_back(place, grad_hidden, middle, grad_top, gain, pieces_up, pieces_out):
    length, width = middle.shape
    wide = grad_hidden.shape[1]
    full, line = shaped((length, width), jnp.float32), shaped((1, width), jnp.float32)
    return call(
        middle_back_kernel,
        (full, shaped((length, width), jnp.bfloat16), full, line, line, line),
        [
            pltpu.VMEM((width, wide), jnp.bfloat16),
            pltpu.VMEM((width, width), jnp.bfloat16),
            pltpu.VMEM((length, width), jnp.float32),
            pltpu.SemaphoreType.DMA((64,)),
            pltpu.SemaphoreType.DMA((64,)),
        ],
        40,
        in_specs=[SMEM] + [VMEM] * 4 + [ANY] * 16,
        out_specs=(VMEM,) * 6,
        flops=2 * length * width * (wide + width),
        moved=22 * MIB,
    )(place, grad_hidden, middle, grad_top, gain, *pieces_up, *pieces_out)


def inputs_back_kernel(place, grad_q, grad_k, grad_v, rows_in, gain, grad_middle, *rest):
    pieces, (grad_rows, sum_gain, sum_shift, whole, sems) = rest[:8], rest[8:]
    wait_all(fetch(place, pieces, whole, sems))
    width = rows_in.shape[1]
    for part in range(4):
        at = pl.ds(part * 128, 128)
        grad = 0.0
        for index, source in enumerate((grad_q, grad_k, grad_v)):
            grad += dot_nt(source[at, :], whole[:, pl.ds(index * width, width)])
        standard, scale = standardize(rows_in[at, :].astype(jnp.float32))
        back = grad_middle[at, :] + norm_pull(grad, standard, scale, gain[...])
        grad_rows[at, :] = back.astype(jnp.bfloat16)
        for goal, added in ((sum_gain, grad * standard), (sum_shift, grad)):
            added = jnp.sum(added, axis=0, keepdims=True)
            goal[...] = added if part == 0 else goal[...] + added


def run_inputs_back(place, grad_q, grad_k, grad_v, rows_in, gain, grad_middle, pieces):
    length, width = rows_in.shape
    line = shaped((1, width), jnp.float32)
    return call(
        inputs_back_kernel,
        (shaped((length, width), jnp.bfloat16), line, line),
        [pltpu.VMEM((width, 3 * width), jnp.bfloat16), pltpu.SemaphoreType.DMA((64,))],
        30,
        in_specs=[SMEM] + [VMEM] * 6 + [ANY] * 8,
        out_specs=(VMEM,) * 3,
        flops=6 * length * width * width,
        moved=13 * MIB,
    )(place, grad_q, grad_k, grad_v, rows_in, gain, grad_middle, *pieces)


def weight_kernel(count, place, left_own, left_other, *rest):
    owns, others, outs = rest[:count], rest[count : 2 * count], rest[2 * count : 2 * count + 4]
    whole, turned, sems = rest[2 * count + 4 :]
    length, height = left_other.shape
    each = owns[0].shape[1]
    start = pl.multiple_of(place[1] * height, height)

    @pl.loop(0, height // 256)
    def _(tile):
        low = pl.multiple_of(tile * 256, 256)
        turned[:, :length] = left_own[:, pl.ds(start + low, 256)].T
        turned[:, length:] = left_other[:, pl.ds(low, 256)].T
        for index in range(count):
            for cut in range(each // TILE):
                cols = pl.ds(cut * TILE, TILE)
                block = dot_nn(turned[:, :length], owns[index][:, cols])
                block += dot_nn(turned[:, length:], others[index][:, cols])
                whole[pl.ds(low, 256), pl.ds(index * each + cut * TILE, TILE)] = block.astype(
                    jnp.bfloat16
                )

    rows, half = outs[0].shape[1], outs[0].shape[2]
    copies = []
    for side, order in enumerate(ORDERS):
        for last in range(2):
            for slot in range(8):
                owner = place[0] ^ relative_place(order, slot, last)
                at = pl.multiple_of(owner * rows, rows)
                copies.append(
                    pltpu.make_async_copy(
                        whole.at[pl.ds(at, rows), pl.ds(side * half, half)],
                        outs[side * 2 + last].at[slot],
                        sems.at[len(copies)],
                    )
                )
                copies[-1].start()
    wait_all(copies)


def run_weight(place, left_own, left_other, owns, others):
    length, height = left_other.shape
    total = owns[0].shape[1] * len(owns)
    part = shaped((8, height // 16, total // 2), jnp.bfloat16)
    return call(
        partial(weight_kernel, len(owns)),
        (part,) * 4,
        [
            pltpu.VMEM((height, total), jnp.bfloat16),
            pltpu.VMEM((256, 2 * length), jnp.bfloat16),
            pltpu.SemaphoreType.DMA((32,)),
        ],
        32,
        in_specs=[SMEM] + [VMEM] * (2 + 2 * len(owns)),
        out_specs=(ANY,) * 4,
        flops=4 * length * height * total,
        moved=18 * MIB,
    )(place, left_own, left_other, *owns, *others)


def other_half(block, core):
    half = block.shape[1] // 2
    return swap_cores(lax.dynamic_slice_in_dim(block, (1 - core) * half, half, axis=1))


def paired_body(
    inputs,
    cotangent,
    seg_lengths,
    valid_len,
    w_qkv,
    b_qkv,
    w_out,
    b_out,
    gain_one,
    shift_one,
    w_up,
    b_up,
    w_down,
    b_down,
    gain_two,
    shift_two,
):
    core, chip = lax.axis_index("dp"), lax.axis_index("fsdp")
    device = core * 16 + chip
    lengths = seg_lengths[0]
    ends = [jnp.sum(lengths[: end + 1]) for end in range(3)]
    place = jnp.stack([chip, core, *ends, valid_len[0]]).astype(jnp.int32)
    rows_in, grad_top = inputs[0], cotangent[0]

    vectors = (b_qkv, b_out, gain_one, shift_one, b_up, b_down, gain_two, shift_two)
    spread = jnp.zeros((32, 512), jnp.bfloat16)
    line = jnp.concatenate(vectors)
    line = jnp.pad(line, (0, 512 - line.shape[0]))
    spread = sum_everywhere(lax.dynamic_update_slice(spread, line[None], (device, 0)))
    full, at = [], 0
    for vector in vectors:
        size = vector.shape[0]
        full.append(spread[:, at : at + size].reshape(1, -1).astype(jnp.float32))
        at += size
    full_bqkv, full_bout, full_gain, full_shift, full_bup, full_bdown, full_gain_two, full_shift_two = full

    pieces_qkv = gather_shards(w_qkv)
    pieces_out = gather_shards(w_out)
    pieces_up = gather_shards(w_up)
    pieces_down = gather_shards(w_down)

    normed, query, key, value = run_qkv(place, rows_in, full_gain, full_shift, full_bqkv, pieces_qkv)
    attended, exact, inverse = run_attend(place, query, key, value)
    middle, normed_two = run_out(
        place, rows_in, attended, full_bout, full_gain_two, full_shift_two, pieces_out
    )
    activated, slope = run_up(place, normed_two, full_bup, pieces_up)

    top_other = swap_cores(grad_top)
    parts_down = run_weight(place, activated, other_half(activated, core), (grad_top,), (top_other,))
    shard_down = reduce_shards(parts_down)

    result, grad_hidden, sum_up, sum_down = run_down(
        place, activated, slope, grad_top, middle, full_bdown, pieces_down
    )
    hidden_other = swap_cores(grad_hidden)
    parts_up = run_weight(place, normed_two, other_half(normed_two, core), (grad_hidden,), (hidden_other,))
    shard_up = reduce_shards(parts_up)

    grad_middle, mixed, grad_att, sum_gain_two, sum_shift_two, sum_out = run_middle_back(
        place, grad_hidden, middle, grad_top, full_gain_two, pieces_up, pieces_out
    )
    parts_out = run_weight(place, attended, other_half(attended, core), (mixed,), (swap_cores(mixed),))
    shard_out = reduce_shards(parts_out)

    grad_q, grad_k, grad_v, sum_q, sum_k, sum_v = run_attend_back(
        place, query, key, value, grad_att, exact, inverse
    )
    grads = (grad_q, grad_k, grad_v)
    parts_qkv = run_weight(
        place, normed, other_half(normed, core), grads, tuple(swap_cores(grad) for grad in grads)
    )
    shard_qkv = reduce_shards(parts_qkv)
    grad_rows, sum_gain, sum_shift = run_inputs_back(
        place, *grads, rows_in, full_gain, grad_middle, pieces_qkv
    )

    def packed(*lines):
        return jnp.concatenate([line.reshape(32, -1) for line in lines], axis=1)

    def own(block):
        return lax.dynamic_slice_in_dim(sum_everywhere(block), device, 1, axis=0)[0]

    early = own(packed(sum_up, sum_down, sum_gain_two, sum_shift_two, sum_out))
    late = own(packed(jnp.concatenate([sum_q, sum_k], axis=1), sum_v, sum_gain, sum_shift))
    wide = b_up.shape[0]
    narrow = b_out.shape[0]
    return (
        result[None],
        grad_rows[None],
        shard_qkv,
        late[: 2 * narrow],
        late[2 * narrow : 3 * narrow],
        shard_out,
        early[wide + 3 * narrow :],
        late[3 * narrow : 4 * narrow],
        late[4 * narrow :],
        shard_up,
        early[:wide],
        shard_down,
        early[wide : wide + narrow],
        early[wide + narrow : wide + 2 * narrow],
        early[wide + 2 * narrow : wide + 3 * narrow],
    )


def solution(mesh):
    placed = (
        P(("dp", "fsdp"), None, None),
        P(("dp", "fsdp"), None, None),
        P(("dp", "fsdp"), None),
        P(("dp", "fsdp")),
        P(("dp", "fsdp"), None),
        P(("dp", "fsdp")),
        P(("dp", "fsdp"), None),
        P(("dp", "fsdp")),
        P(("dp", "fsdp")),
        P(("dp", "fsdp")),
        P(("dp", "fsdp"), None),
        P(("dp", "fsdp")),
        P(("dp", "fsdp"), None),
        P(("dp", "fsdp")),
        P(("dp", "fsdp")),
        P(("dp", "fsdp")),
    )
    paired = dict(mesh.shape) == {"dp": 2, "fsdp": 16}
    return jax.shard_map(
        paired_body if paired else plain_body,
        mesh=mesh,
        in_specs=placed,
        out_specs=(
            P(("dp", "fsdp"), None, None),
            P(("dp", "fsdp"), None, None),
            P(("dp", "fsdp"), None),
            P(("dp", "fsdp")),
            P(("dp", "fsdp")),
            P(("dp", "fsdp"), None),
            P(("dp", "fsdp")),
            P(("dp", "fsdp")),
            P(("dp", "fsdp")),
            P(("dp", "fsdp"), None),
            P(("dp", "fsdp")),
            P(("dp", "fsdp"), None),
            P(("dp", "fsdp")),
            P(("dp", "fsdp")),
            P(("dp", "fsdp")),
        ),
        check_vma=False,
    )
```

```python
from functools import partial

import jax
import jax.numpy as jnp
from jax import lax
from jax.experimental import pallas as pl
from jax.experimental.pallas import tpu as pltpu
from jax.sharding import PartitionSpec as P

HEADS = 16


norm_eps = 1e-05
denom_eps = 1e-06
gelu_coef = 0.7978845608028654


def layer_norm(values, scale_gain, offset):
    centred = values - jnp.mean(values, axis=-1, keepdims=True)
    spread = jnp.mean(centred * centred, axis=-1, keepdims=True)
    return centred * lax.rsqrt(spread + norm_eps) * scale_gain + offset


def feature_map(values):
    return jnp.where(values > 0, values + 1.0, jnp.exp(jnp.minimum(values, 0.0)))


def gelu_tanh(values):
    return (
        0.5 * values * (1.0 + jnp.tanh(gelu_coef * (values + 0.044715 * values * values * values)))
    )


def contract_rows(left_side, right_side):
    return lax.dot_general(
        left_side, right_side, (((0,), (0,)), ((), ())), preferred_element_type=jnp.float32
    )


def contract_cols(left_side, right_side):
    return lax.dot_general(
        left_side, right_side, (((1,), (1,)), ((), ())), preferred_element_type=jnp.float32
    )


def row_masks(lengths, valid_count, row_length):
    places = jnp.arange(row_length, dtype=jnp.int32)
    bounds = jnp.stack([jnp.sum(lengths[: end + 1]) for end in range(lengths.shape[0])])
    segment = jnp.sum((places[:, None] >= bounds[None, :]).astype(jnp.int32), axis=1)
    allowed = (segment[:, None] == segment[None, :]) & (places[None, :] <= places[:, None])
    keeping = (places < valid_count).astype(jnp.float32)
    return (allowed.astype(jnp.float32), keeping)


def split_heads(matrix):
    return jnp.transpose(matrix.reshape(matrix.shape[0], HEADS, -1), (1, 0, 2))


def join_heads(stacked):
    return jnp.transpose(stacked, (1, 0, 2)).reshape(stacked.shape[1], -1)


def pull_group(first, second, third, fourth, fifth, sixth):
    return (
        lax.all_gather(first, ("dp", "fsdp"), axis=0, tiled=True),
        lax.all_gather(second, ("dp", "fsdp"), axis=0, tiled=True),
        lax.all_gather(third, ("dp", "fsdp"), axis=0, tiled=True),
        lax.all_gather(fourth, ("dp", "fsdp"), axis=0, tiled=True),
        lax.all_gather(fifth, ("dp", "fsdp"), axis=0, tiled=True),
        lax.all_gather(sixth, ("dp", "fsdp"), axis=0, tiled=True),
    )


def push_group(first, second, third, stacked):
    return (
        lax.psum_scatter(first, ("dp", "fsdp"), scatter_dimension=0, tiled=True),
        lax.psum_scatter(second, ("dp", "fsdp"), scatter_dimension=0, tiled=True),
        lax.psum_scatter(third, ("dp", "fsdp"), scatter_dimension=0, tiled=True),
        lax.psum_scatter(stacked, ("dp", "fsdp"), scatter_dimension=1, tiled=True),
    )


def head_forward(allowed, head_item):
    query_head, key_head, value_head = head_item
    scores = contract_cols(query_head, key_head) * allowed
    denominator = jnp.sum(scores, axis=1) + denom_eps
    numerator = jnp.dot(scores.astype(jnp.bfloat16), value_head, preferred_element_type=jnp.float32)
    return (numerator, denominator)


def head_backward(allowed, head_item):
    query_head, key_head, value_head, grad_numer, grad_denom = head_item
    scores = contract_cols(query_head, key_head) * allowed
    grad_prob = contract_cols(grad_numer, value_head)
    grad_value = contract_rows(scores.astype(jnp.bfloat16), grad_numer)
    grad_scores = ((grad_prob + grad_denom[:, None]) * allowed).astype(jnp.bfloat16)
    grad_query = jnp.dot(grad_scores, key_head, preferred_element_type=jnp.float32)
    grad_key = contract_rows(grad_scores, query_head)
    return (grad_query, grad_key, grad_value)


def plain_body(
    inputs,
    cotangent,
    seg_lengths,
    valid_len,
    w_qkv,
    b_qkv,
    w_out,
    b_out,
    gain_one,
    shift_one,
    w_up,
    b_up,
    w_down,
    b_down,
    gain_two,
    shift_two,
):
    token_rows = inputs[0].astype(jnp.float32)
    row_length = token_rows.shape[0]
    model_width = token_rows.shape[1]
    allowed, keeping = row_masks(seg_lengths[0], valid_len[0], row_length)
    full_qkv, full_bqkv, full_out, full_bout, full_gain, full_shift = pull_group(
        w_qkv, b_qkv, w_out, b_out, gain_one, shift_one
    )
    normed, norm_back = jax.vjp(
        layer_norm, token_rows, full_gain.astype(jnp.float32), full_shift.astype(jnp.float32)
    )
    normed_low = normed.astype(jnp.bfloat16)
    projected = jnp.dot(
        normed_low, full_qkv, preferred_element_type=jnp.float32
    ) + full_bqkv.astype(jnp.float32)
    query_feat, query_back = jax.vjp(feature_map, projected[:, :model_width])
    key_feat, key_back = jax.vjp(feature_map, projected[:, model_width : 2 * model_width])
    query_heads = split_heads(query_feat.astype(jnp.bfloat16))
    key_heads = split_heads(key_feat.astype(jnp.bfloat16))
    value_heads = split_heads(projected[:, 2 * model_width :].astype(jnp.bfloat16))
    numerator, denominator = lax.map(
        partial(head_forward, allowed), (query_heads, key_heads, value_heads)
    )
    attended = keeping[None, :, None] * numerator / denominator[:, :, None]
    attended_low = join_heads(attended).astype(jnp.bfloat16)
    middle = (
        token_rows
        + jnp.dot(attended_low, full_out, preferred_element_type=jnp.float32)
        + full_bout.astype(jnp.float32)
    )
    full_up, full_bup, full_down, full_bdown, full_gain_two, full_shift_two = pull_group(
        w_up, b_up, w_down, b_down, gain_two, shift_two
    )
    normed_two, norm_two_back = jax.vjp(
        layer_norm, middle, full_gain_two.astype(jnp.float32), full_shift_two.astype(jnp.float32)
    )
    normed_two_low = normed_two.astype(jnp.bfloat16)
    hidden = jnp.dot(normed_two_low, full_up, preferred_element_type=jnp.float32) + full_bup.astype(
        jnp.float32
    )
    activated, gelu_back = jax.vjp(gelu_tanh, hidden)
    activated_low = activated.astype(jnp.bfloat16)
    result = (
        middle
        + jnp.dot(activated_low, full_down, preferred_element_type=jnp.float32)
        + full_bdown.astype(jnp.float32)
    )
    again_up, again_bup, again_down, again_bdown, again_gain_two, again_shift_two = pull_group(
        w_up, b_up, w_down, b_down, gain_two, shift_two
    )
    grad_top = cotangent[0]
    grad_top_full = grad_top.astype(jnp.float32)
    grad_down = contract_rows(activated_low, grad_top)
    grad_bdown = jnp.sum(grad_top_full, axis=0)
    grad_hidden = gelu_back(contract_cols(grad_top, again_down))[0]
    grad_hidden_low = grad_hidden.astype(jnp.bfloat16)
    grad_bup = jnp.sum(grad_hidden_low.astype(jnp.float32), axis=0)
    grad_up = contract_rows(normed_two_low, grad_hidden_low)
    grad_normed_two = contract_cols(grad_hidden_low, again_up)
    grad_middle_norm, grad_gain_two, grad_shift_two = norm_two_back(grad_normed_two)
    grad_middle = grad_top_full + grad_middle_norm
    shard_up, shard_bup, shard_down, shard_small_two = push_group(
        grad_up, grad_bup, grad_down, jnp.stack([grad_bdown, grad_gain_two, grad_shift_two])
    )
    again_qkv, again_bqkv, again_out, again_bout, again_gain, again_shift = pull_group(
        w_qkv, b_qkv, w_out, b_out, gain_one, shift_one
    )
    grad_mixed = grad_middle.astype(jnp.bfloat16)
    grad_bout = jnp.sum(grad_mixed.astype(jnp.float32), axis=0)
    grad_wout = contract_rows(attended_low, grad_mixed)
    grad_attended = split_heads(contract_cols(grad_mixed, again_out))
    grad_numer = (keeping[None, :, None] * grad_attended / denominator[:, :, None]).astype(
        jnp.bfloat16
    )
    grad_denom = -jnp.sum(grad_attended * attended, axis=2) / denominator
    grad_query_heads, grad_key_heads, grad_value_heads = lax.map(
        partial(head_backward, allowed),
        (query_heads, key_heads, value_heads, grad_numer, grad_denom),
    )
    grad_query = query_back(join_heads(grad_query_heads))[0]
    grad_key = key_back(join_heads(grad_key_heads))[0]
    grad_projected = jnp.concatenate(
        [grad_query, grad_key, join_heads(grad_value_heads)], axis=1
    ).astype(jnp.bfloat16)
    grad_bias_all = jnp.sum(grad_projected.astype(jnp.float32), axis=0)
    grad_bias_qk = grad_bias_all[: 2 * model_width]
    grad_bias_v = grad_bias_all[2 * model_width :]
    grad_qkv = contract_rows(normed_low, grad_projected)
    grad_normed = contract_cols(grad_projected, again_qkv)
    grad_rows_norm, grad_gain_one, grad_shift_one = norm_back(grad_normed)
    grad_inputs = (grad_middle + grad_rows_norm).astype(jnp.bfloat16)
    shard_qkv, shard_bias_qk, shard_wout, shard_small_one = push_group(
        grad_qkv,
        grad_bias_qk,
        grad_wout,
        jnp.stack([grad_bout, grad_bias_v, grad_gain_one, grad_shift_one]),
    )
    return (
        result.astype(jnp.bfloat16)[None],
        grad_inputs[None],
        shard_qkv,
        shard_bias_qk,
        shard_small_one[1],
        shard_wout,
        shard_small_one[0],
        shard_small_one[2],
        shard_small_one[3],
        shard_up,
        shard_bup,
        shard_down,
        shard_small_two[0],
        shard_small_two[1],
        shard_small_two[2],
    )


HALF_LANES = 64
TILE = 512
Z_HIGH, Z_LOW, Y_BIT, X_BIT = 8, 4, 2, 1
MIXED = ((Z_HIGH, X_BIT, Z_LOW, Y_BIT), (Z_HIGH, Y_BIT, Z_LOW, X_BIT))
LINED = ((Z_HIGH, Z_LOW, X_BIT, Y_BIT), (Z_HIGH, Z_LOW, Y_BIT, X_BIT))
SMALL = 128
GROUP = 16
ANY = pl.BlockSpec(memory_space=pl.ANY)
SMEM = pl.BlockSpec(memory_space=pltpu.SMEM)
VMEM = pl.BlockSpec(memory_space=pltpu.VMEM)
MIB = 1 << 20


def swap_chips(block, bit):
    return lax.ppermute(block, "fsdp", [(place, place ^ bit) for place in range(16)])


def swap_cores(block):
    return lax.ppermute(block, "dp", [(0, 1), (1, 0)])


def relative_place(order, slot, last):
    return (
        order[0] * (slot & 1)
        + order[1] * ((slot >> 1) & 1)
        + order[2] * ((slot >> 2) & 1)
        + order[3] * last
    )


def tie(*blocks):
    return lax.optimization_barrier(blocks)


def by_side(shard):
    rows, width = shard.shape
    return jnp.stack([shard[:, : width // 2], shard[:, width // 2 :]])[:, None]


def grown(held, arrived):
    return jnp.concatenate([held, arrived], axis=1)


def gather_start(held):
    return swap_chips(held, Z_HIGH)


def gather_plane(held):
    return swap_chips(held[0], X_BIT), swap_chips(held[1], Y_BIT)


def gather_line(held):
    return swap_chips(held, Z_LOW)


def gather_across(held):
    return swap_chips(held[0], Y_BIT), swap_chips(held[1], X_BIT)


def gather_cores(held, across):
    return (held, *across, swap_cores(held), swap_cores(across[0]), swap_cores(across[1]))


def added(parts, start, stop):
    return sum(part[:, start:stop].astype(jnp.float32) for part in parts)


def sent_slots(parts, amount):
    return added(parts, amount, 2 * amount).astype(jnp.bfloat16)


def reduce_across(first, second):
    return swap_chips(first, Y_BIT), swap_chips(second, X_BIT)


def reduce_line(parts, amount):
    return swap_chips(sent_slots(parts, amount), Z_LOW)


def reduce_plane(parts, amount):
    sent = sent_slots(parts, amount)
    return swap_chips(sent[0], X_BIT), swap_chips(sent[1], Y_BIT)


def reduce_end(parts):
    parts = parts + [swap_chips(sent_slots(parts, 1), Z_HIGH)]
    return added(parts, 0, 1)[:, 0]


def side_by_side(total, start, stop):
    return jnp.concatenate([total[0, :, start:stop], total[1, :, start:stop]], axis=1)


def sum_everywhere(block):
    block = block + swap_cores(block)
    for bit in (Z_LOW, Z_HIGH, X_BIT, Y_BIT):
        block = block + swap_chips(block, bit)
    return block


def call(kernel, outs, scratch, mib, args, in_specs, out_specs, grid=None, flops=0, gates=()):
    inputs, ignored = len(in_specs), len(gates)

    def gated(*refs):
        kernel(*refs[:inputs], *refs[inputs + ignored :])

    extra = {} if grid is None else {"grid": grid}
    return pl.pallas_call(
        gated,
        out_shape=outs,
        in_specs=list(in_specs) + [ANY] * ignored,
        out_specs=out_specs,
        scratch_shapes=scratch,
        compiler_params=pltpu.CompilerParams(vmem_limit_bytes=mib * MIB),
        cost_estimate=pl.CostEstimate(flops=flops, bytes_accessed=0, transcendentals=0),
        **extra,
    )(*args, *gates)


def shaped(shape, dtype):
    return jax.ShapeDtypeStruct(shape, dtype)


def dot_nn(left, right):
    return lax.dot_general(left, right, (((1,), (0,)), ((), ())), preferred_element_type=jnp.float32)


def dot_nt(left, right):
    return lax.dot_general(left, right, (((1,), (1,)), ((), ())), preferred_element_type=jnp.float32)


def fetch(place, orders, pieces, whole, sems, skip=0):
    rows, half = pieces[0].shape[2], whole.shape[1] // 2
    copies = []
    for side, order in enumerate(orders):
        for core in range(2):
            for last in range(2):
                mine = pieces[core * 3 : core * 3 + 3]
                piece = mine[1 + side] if last else mine[0].at[side]
                for slot in range(8):
                    owner = (place[1] ^ core) * 16 + (place[0] ^ relative_place(order, slot, last))
                    start = pl.multiple_of(owner * rows, rows)
                    copies.append(
                        pltpu.make_async_copy(
                            piece.at[slot, :, pl.ds(skip, half)],
                            whole.at[pl.ds(start, rows), pl.ds(side * half, half)],
                            sems.at[len(copies)],
                        )
                    )
    for copy in copies:
        copy.start()
    return copies


def wait_all(copies):
    for copy in copies:
        copy.wait()


def standardize(block):
    centred = block - jnp.mean(block, axis=1, keepdims=True)
    scale = lax.rsqrt(jnp.mean(centred * centred, axis=1, keepdims=True) + norm_eps)
    return centred * scale, scale


def norm_pull(grad, standard, scale, gain):
    scaled = grad * gain
    return scale * (
        scaled
        - jnp.mean(scaled, axis=1, keepdims=True)
        - standard * jnp.mean(scaled * standard, axis=1, keepdims=True)
    )


def fetch_small(place, pieces, small, skip, sems):
    copies = []
    for core in range(2):
        for last in range(2):
            piece = pieces[core * 3 + 1] if last else pieces[core * 3].at[0]
            for slot in range(8):
                far = relative_place(MIXED[0], slot, last)
                owner = (place[1] ^ core) * 16 + (place[0] ^ far)
                start = pl.multiple_of(owner * GROUP, GROUP)
                copies.append(
                    pltpu.make_async_copy(
                        piece.at[slot, pl.ds(0, GROUP), pl.ds(skip, SMALL)],
                        small.at[pl.ds(start, GROUP), :],
                        sems.at[len(copies)],
                    )
                )
                copies[-1].start()
    return copies


def unfold(small, each, rows):
    total = 32 * each
    column = lax.broadcasted_iota(jnp.int32, (1, total), 1).astype(jnp.float32)
    turn = jnp.floor((column + 0.5) / each)
    lane = lax.broadcasted_iota(jnp.int32, (SMALL, 1), 0).astype(jnp.float32)
    spread = jnp.where(column - turn * each == lane, 1.0, 0.0).astype(jnp.bfloat16)
    owner = lax.broadcasted_iota(jnp.int32, (32, 1), 0).astype(jnp.float32)
    lines = []
    for row in rows:
        parts = small[pl.ds(row, 32, stride=GROUP), :].astype(jnp.bfloat16)
        parts = jnp.where(owner == turn, dot_nn(parts, spread), 0.0)
        lines.append(jnp.sum(parts, axis=0, keepdims=True))
    return lines


def qkv_kernel(place, rows_in, *rest):
    pieces, (normed, query, key, value), lines, rest = rest[:6], rest[6:10], rest[10:16], rest[16:]
    whole, small, smalls, bias, sems, more = rest
    few = fetch_small(place, pieces, small, 4 * whole.shape[1] // 6, more)
    copies = fetch(place, MIXED, pieces, whole, sems)
    wait_all(few)
    smalls[...] = small[...].astype(jnp.float32)
    width = rows_in.shape[1]
    (bias[...],) = unfold(smalls, 3 * width // 32, (0,))
    (lines[5][...],) = unfold(smalls, 4 * width // 32, (4,))
    bias_out, gain, shift, bias_down, gain_two, shift_two = unfold(
        smalls, width // 32, (1, 2, 3, 5, 6, 7)
    )
    for goal, line in zip(lines, (gain, bias_out, gain_two, shift_two, bias_down)):
        goal[...] = line
    for part in range(4):
        at = pl.ds(part * 128, 128)
        standard, _ = standardize(rows_in[at, :].astype(jnp.float32))
        normed[at, :] = (standard * gain + shift).astype(jnp.bfloat16)
    wait_all(copies)
    for tile in range(6):
        cols = pl.ds(tile * TILE, TILE)
        projected = dot_nn(normed[...], whole[:, cols]) + bias[:, cols]
        goal = (query, key, value)[tile // 2]
        if tile < 4:
            projected = feature_map(projected)
        goal[:, pl.ds((tile % 2) * TILE, TILE)] = projected.astype(jnp.bfloat16)


def run_qkv(place, rows_in, pieces, gates=()):
    length, width = rows_in.shape
    narrow = shaped((length, width), jnp.bfloat16)
    line = shaped((1, width), jnp.float32)
    return call(
        qkv_kernel,
        (narrow,) * 4 + (line,) * 5 + (shaped((1, 4 * width), jnp.float32),),
        [
            pltpu.VMEM((width, 3 * width), jnp.bfloat16),
            pltpu.VMEM((32 * GROUP, SMALL), jnp.bfloat16),
            pltpu.VMEM((32 * GROUP, SMALL), jnp.float32),
            pltpu.VMEM((1, 3 * width), jnp.float32),
            pltpu.SemaphoreType.DMA((64,)),
            pltpu.SemaphoreType.DMA((32,)),
        ],
        28,
        (place, rows_in, *pieces),
        in_specs=[SMEM, VMEM] + [ANY] * 6,
        out_specs=(VMEM,) * 10,
        gates=gates,
    )


def image_of(place, positions):
    image = jnp.zeros(positions.shape, jnp.int32)
    for end in range(2, 5):
        image = image + jnp.where(positions >= place[end], 1, 0)
    return image


def allowed_block(place, length, flipped):
    first = lax.broadcasted_iota(jnp.int32, (length, 1), 0)
    second = lax.broadcasted_iota(jnp.int32, (1, length), 1)
    same = image_of(place, first) == image_of(place, second)
    ordered = (first <= second) if flipped else (second <= first)
    return jnp.where(same & ordered, 1.0, 0.0).astype(jnp.float32)


def head_lanes():
    lane = lax.broadcasted_iota(jnp.int32, (1, 2 * HALF_LANES), 1)
    low = jnp.where(lane < HALF_LANES, 1.0, 0.0)
    return (low.astype(jnp.bfloat16), (1.0 - low).astype(jnp.bfloat16))


def keeping_rows(place, start, amount):
    position = lax.broadcasted_iota(jnp.int32, (amount, 1), 0) + start
    return jnp.where(position < place[5], 1.0, 0.0)


def with_ones(block, lanes):
    return jnp.concatenate([block * lanes, jnp.broadcast_to(lanes, block.shape)], axis=1)


def attend_kernel(place, query, key, value, attended, exact, inverse, allowed):
    length = query.shape[0]
    step = length // 2

    @pl.when(pl.program_id(0) == 0)
    def _():
        allowed[...] = allowed_block(place, length, False)

    for part in range(2):
        rows, seen = pl.ds(part * step, step), (part + 1) * step
        total = None
        for lanes in head_lanes():
            scores = dot_nt(query[rows, :], key[:seen, :] * lanes) * allowed[rows, :seen]
            mixed = dot_nn(scores.astype(jnp.bfloat16), with_ones(value[:seen, :], lanes))
            total = mixed if total is None else total + mixed
        width = 2 * HALF_LANES
        over = 1.0 / (total[:, width:] + denom_eps)
        inverse[rows, :] = over
        mixed = keeping_rows(place, part * step, step) * total[:, :width] * over
        exact[rows, :] = mixed
        attended[rows, :] = mixed.astype(jnp.bfloat16)


def run_attend(place, query, key, value, gates=()):
    length, width = query.shape
    pair = pl.BlockSpec((length, 2 * HALF_LANES), lambda p: (0, p))
    return call(
        attend_kernel,
        (
            shaped((length, width), jnp.bfloat16),
            shaped((length, width), jnp.float32),
            shaped((length, width), jnp.float32),
        ),
        [pltpu.VMEM((length, length), jnp.float32)],
        16,
        (place, query, key, value),
        grid=(width // (2 * HALF_LANES),),
        in_specs=[SMEM] + [pair] * 3,
        out_specs=(pair,) * 3,
        gates=gates,
    )


def attend_back_kernel(
    place, query, key, value, grad_att, exact, inverse, *rest
):
    stacked, sums, (allowed, flipped, left) = rest[0], rest[1], rest[2:]
    length = query.shape[0]
    step = length // 2
    width = 2 * HALF_LANES

    @pl.when(pl.program_id(0) == 0)
    def _():
        allowed[...] = allowed_block(place, length, False)
        flipped[...] = allowed_block(place, length, True)

    over = grad_att[...] * inverse[...]
    left[:, :width] = (keeping_rows(place, 0, length) * over).astype(jnp.bfloat16)
    lane = lax.broadcasted_iota(jnp.int32, (1, width), 1)
    terms, low = over * exact[...], lane < HALF_LANES
    first = jnp.sum(jnp.where(low, terms, 0.0), axis=1, keepdims=True)
    second = jnp.sum(jnp.where(low, 0.0, terms), axis=1, keepdims=True)
    spread = -jnp.where(low, first, second)
    high = spread.astype(jnp.bfloat16).astype(jnp.float32)
    within = lane & (HALF_LANES - 1)
    spread = jnp.where(within == 0, high, jnp.where(within == 1, spread - high, 0.0))
    left[:, width:] = spread.astype(jnp.bfloat16)
    for part in range(2):
        rows, seen = pl.ds(part * step, step), (part + 1) * step
        later, grad_query, grad_key, grad_value = pl.ds(part * step, length - part * step), 0.0, 0.0, 0.0
        for lanes in head_lanes():
            grad_scores = dot_nt(left[rows, :], with_ones(value[:seen, :], lanes))
            grad_scores = (grad_scores * allowed[rows, :seen]).astype(jnp.bfloat16)
            grad_query += dot_nn(grad_scores, key[:seen, :] * lanes)
            scores = dot_nt(key[rows, :] * lanes, query[later, :])
            scores = (scores * flipped[rows, later]).astype(jnp.bfloat16)
            grad_value += dot_nn(scores, left[later, :width] * lanes)
            grad_scores = dot_nt(with_ones(value[rows, :], lanes), left[later, :])
            grad_scores = (grad_scores * flipped[rows, later]).astype(jnp.bfloat16)
            grad_key += dot_nn(grad_scores, query[later, :] * lanes)
        grads = (
            grad_query * jnp.minimum(query[rows, :].astype(jnp.float32), 1.0),
            grad_key * jnp.minimum(key[rows, :].astype(jnp.float32), 1.0),
            grad_value,
        )
        for index, grad in enumerate(grads):
            low, line = grad.astype(jnp.bfloat16), pl.ds(index, 1)
            stacked[index, rows, :] = low
            added = jnp.sum(low.astype(jnp.float32), axis=0, keepdims=True)
            sums[line, :] = added if part == 0 else sums[line, :] + added


def run_attend_back(place, query, key, value, grad_att, exact, inverse, gates=()):
    length, width = query.shape
    pair = pl.BlockSpec((length, 2 * HALF_LANES), lambda p: (0, p))
    stack = pl.BlockSpec((3, length, 2 * HALF_LANES), lambda p: (0, 0, p))
    lines = pl.BlockSpec((3, 2 * HALF_LANES), lambda p: (0, p))
    return call(
        attend_back_kernel,
        (shaped((3, length, width), jnp.bfloat16), shaped((3, width), jnp.float32)),
        [
            pltpu.VMEM((length, length), jnp.float32),
            pltpu.VMEM((length, length), jnp.float32),
            pltpu.VMEM((length, 4 * HALF_LANES), jnp.bfloat16),
        ],
        20,
        (place, query, key, value, grad_att, exact, inverse),
        grid=(width // (2 * HALF_LANES),),
        in_specs=[SMEM] + [pair] * 6,
        out_specs=(stack, lines),
        gates=gates,
    )


def hand_over(place, sources, goal, sems):
    copies, at = [], 0
    for source in sources:
        half = source.shape[1] // 2
        start = pl.multiple_of((1 - place[1]) * half, half)
        copies.append(
            pltpu.make_async_copy(
                source.at[:, pl.ds(start, half)], goal.at[:, pl.ds(at, half)], sems.at[len(copies)]
            )
        )
        copies[-1].start()
        at += half
    return copies


def out_kernel(place, rows_in, early, attended, bias, gain, shift, *rest):
    pieces, (middle, normed, handed, whole, sems, more) = rest[:6], rest[6:]
    copies = fetch(place, MIXED, pieces, whole, sems, 3 * whole.shape[1] // 2)
    handing = hand_over(place, (early, attended), handed, more)
    wait_all(copies)
    for part in range(2):
        at = pl.ds(part * 256, 256)
        total = rows_in[at, :].astype(jnp.float32) + dot_nn(attended[at, :], whole[...]) + bias[...]
        middle[at, :] = total
        standard, _ = standardize(total)
        normed[at, :] = (standard * gain[...] + shift[...]).astype(jnp.bfloat16)
    wait_all(handing)


def run_out(place, rows_in, early, attended, bias, gain, shift, pieces, gates=()):
    length, width = rows_in.shape
    narrow = shaped((length, width), jnp.bfloat16)
    return call(
        out_kernel,
        (shaped((length, width), jnp.float32), narrow, narrow),
        [
            pltpu.VMEM((width, width), jnp.bfloat16),
            pltpu.SemaphoreType.DMA((64,)),
            pltpu.SemaphoreType.DMA((2,)),
        ],
        24,
        (place, rows_in, early, attended, bias, gain, shift, *pieces),
        in_specs=[SMEM] + [VMEM] * 6 + [ANY] * 6,
        out_specs=(VMEM, VMEM, ANY),
        gates=gates,
    )


def up_kernel(place, normed, bias, *rest):
    pieces, (activated, slope, handed, whole, sems, more) = rest[:6], rest[6:]
    wait_all(fetch(place, MIXED, pieces, whole, sems))

    @pl.loop(0, whole.shape[1] // TILE)
    def _(tile):
        cols = pl.ds(pl.multiple_of(tile * TILE, TILE), TILE)
        hidden = dot_nn(normed[...], whole[:, cols]) + bias[:, cols]
        square = hidden * hidden
        bend = jnp.tanh(gelu_coef * (hidden + 0.044715 * square * hidden))
        activated[:, cols] = (0.5 * hidden * (1.0 + bend)).astype(jnp.bfloat16)
        rate = gelu_coef * (1.0 + 3.0 * 0.044715 * square)
        slope[:, cols] = (
            0.5 * (1.0 + bend) + 0.5 * hidden * (1.0 - bend * bend) * rate
        ).astype(jnp.bfloat16)

    wait_all(hand_over(place, (normed, activated), handed, more))


def run_up(place, normed, bias, pieces, gates=()):
    length, width = normed.shape
    wide = bias.shape[1]
    return call(
        up_kernel,
        (shaped((length, wide), jnp.bfloat16),) * 2
        + (shaped((length, (width + wide) // 2), jnp.bfloat16),),
        [
            pltpu.VMEM((width, wide), jnp.bfloat16),
            pltpu.SemaphoreType.DMA((64,)),
            pltpu.SemaphoreType.DMA((2,)),
        ],
        30,
        (place, normed, bias, *pieces),
        in_specs=[SMEM] + [VMEM] * 2 + [ANY] * 6,
        out_specs=(VMEM, VMEM, ANY),
        gates=gates,
    )


def down_kernel(place, activated, slope, grad_top, middle, bias, *rest):
    pieces, (result, grad_hidden, sum_up, sum_down, whole, total, sems) = rest[:6], rest[6:]
    wait_all(fetch(place, LINED, pieces, whole, sems))
    total[...] = middle[...] + bias[...]

    @pl.loop(0, whole.shape[0] // TILE)
    def _(tile):
        cols = pl.ds(pl.multiple_of(tile * TILE, TILE), TILE)
        block = whole[cols, :]
        total[...] += dot_nn(activated[:, cols], block)
        grad = dot_nt(grad_top[...], block) * slope[:, cols].astype(jnp.float32)
        low = grad.astype(jnp.bfloat16)
        grad_hidden[:, cols] = low
        sum_up[:, cols] = jnp.sum(low.astype(jnp.float32), axis=0, keepdims=True)

    result[...] = total[...].astype(jnp.bfloat16)
    sum_down[...] = jnp.sum(grad_top[...].astype(jnp.float32), axis=0, keepdims=True)


def run_down(place, activated, slope, grad_top, middle, bias, pieces, gates=()):
    length, width = middle.shape
    wide = activated.shape[1]
    return call(
        down_kernel,
        (
            shaped((length, width), jnp.bfloat16),
            shaped((length, wide), jnp.bfloat16),
            shaped((1, wide), jnp.float32),
            shaped((1, width), jnp.float32),
        ),
        [
            pltpu.VMEM((wide, width), jnp.bfloat16),
            pltpu.VMEM((length, width), jnp.float32),
            pltpu.SemaphoreType.DMA((64,)),
        ],
        40,
        (place, activated, slope, grad_top, middle, bias, *pieces),
        in_specs=[SMEM] + [VMEM] * 5 + [ANY] * 6,
        out_specs=(VMEM,) * 4,
        flops=64 * length * width * wide,
        gates=gates,
    )


def middle_back_kernel(place, grad_hidden, middle, grad_top, gain, *rest):
    pieces_up, pieces_in, rest = rest[:6], rest[6:12], rest[12:]
    grad_middle, mixed, grad_att, sum_gain, sum_shift, sum_out, whole, outer, total, sems, more = rest
    copies = fetch(place, MIXED, pieces_up, whole, sems)
    second = fetch(place, MIXED, pieces_in, outer, more, 3 * outer.shape[1] // 2)
    total[...] = jnp.zeros_like(total)
    wait_all(copies)

    @pl.loop(0, whole.shape[1] // TILE)
    def _(tile):
        cols = pl.ds(pl.multiple_of(tile * TILE, TILE), TILE)
        total[...] += dot_nt(grad_hidden[:, cols], whole[:, cols])

    for part in range(4):
        at = pl.ds(part * 128, 128)
        grad = total[at, :]
        standard, scale = standardize(middle[at, :])
        back = grad_top[at, :].astype(jnp.float32) + norm_pull(grad, standard, scale, gain[...])
        grad_middle[at, :] = back
        low = back.astype(jnp.bfloat16)
        mixed[at, :] = low
        for goal, added in (
            (sum_gain, grad * standard),
            (sum_shift, grad),
            (sum_out, low.astype(jnp.float32)),
        ):
            added = jnp.sum(added, axis=0, keepdims=True)
            goal[...] = added if part == 0 else goal[...] + added
    wait_all(second)
    for part in range(2):
        at = pl.ds(part * 256, 256)
        grad_att[at, :] = dot_nt(mixed[at, :], outer[...])


def run_middle_back(place, grad_hidden, middle, grad_top, gain, pieces_up, pieces_in, gates=()):
    length, width = middle.shape
    wide = grad_hidden.shape[1]
    full, line = shaped((length, width), jnp.float32), shaped((1, width), jnp.float32)
    return call(
        middle_back_kernel,
        (full, shaped((length, width), jnp.bfloat16), full, line, line, line),
        [
            pltpu.VMEM((width, wide), jnp.bfloat16),
            pltpu.VMEM((width, width), jnp.bfloat16),
            pltpu.VMEM((length, width), jnp.float32),
            pltpu.SemaphoreType.DMA((64,)),
            pltpu.SemaphoreType.DMA((64,)),
        ],
        40,
        (place, grad_hidden, middle, grad_top, gain, *pieces_up, *pieces_in),
        in_specs=[SMEM] + [VMEM] * 4 + [ANY] * 12,
        out_specs=(VMEM,) * 6,
        gates=gates,
    )


def inputs_back_kernel(place, grads, rows_in, gain, grad_middle, *rest):
    pieces, (grad_rows, sum_gain, sum_shift, whole, sems) = rest[:6], rest[6:]
    wait_all(fetch(place, MIXED, pieces, whole, sems))
    width = rows_in.shape[1]
    for part in range(4):
        at = pl.ds(part * 128, 128)
        grad = 0.0
        for index in range(3):
            grad += dot_nt(grads[index, at, :], whole[:, pl.ds(index * width, width)])
        standard, scale = standardize(rows_in[at, :].astype(jnp.float32))
        back = grad_middle[at, :] + norm_pull(grad, standard, scale, gain[...])
        grad_rows[at, :] = back.astype(jnp.bfloat16)
        for goal, added in ((sum_gain, grad * standard), (sum_shift, grad)):
            added = jnp.sum(added, axis=0, keepdims=True)
            goal[...] = added if part == 0 else goal[...] + added


def run_inputs_back(place, grads, rows_in, gain, grad_middle, pieces, gates=()):
    length, width = rows_in.shape
    line = shaped((1, width), jnp.float32)
    return call(
        inputs_back_kernel,
        (shaped((length, width), jnp.bfloat16), line, line),
        [pltpu.VMEM((width, 3 * width), jnp.bfloat16), pltpu.SemaphoreType.DMA((64,))],
        30,
        (place, grads, rows_in, gain, grad_middle, *pieces),
        in_specs=[SMEM] + [VMEM] * 4 + [ANY] * 6,
        out_specs=(VMEM,) * 3,
        gates=gates,
    )


def weight_kernel(orders, skips, place, *rest):
    groups = len(skips)
    inputs, (kept, *sent), rest = rest[: 4 * groups], rest[4 * groups : 4 * groups + 3], rest[4 * groups + 3 :]
    wholes, (turned, sems) = rest[:groups], rest[groups:]
    length = inputs[0].shape[0]
    for group, (skip, whole) in enumerate(zip(skips, wholes)):
        left_own, left_other, own, other = inputs[4 * group : 4 * group + 4]
        height, count, each = whole.shape[0], own.shape[0], own.shape[2]
        start = pl.multiple_of(place[1] * height, height)

        @pl.loop(0, height // 256)
        def _(tile):
            low = pl.multiple_of(tile * 256, 256)
            turned[:, :length] = left_own[:, pl.ds(start + low, 256)].T
            turned[:, length:] = left_other[:, pl.ds(skip + low, 256)].T
            for index in range(count):
                for step in range(each // TILE):
                    cols = pl.ds(step * TILE, TILE)
                    block = dot_nn(turned[:, :length], own[index, :, cols])
                    block += dot_nn(turned[:, length:], other[index, :, cols])
                    goal = pl.ds(index * each + step * TILE, TILE)
                    whole[pl.ds(low, 256), goal] = block.astype(jnp.bfloat16)

    rows, at, copies = kept.shape[2], 0, []
    for whole in wholes:
        half = whole.shape[1] // 2
        for side, order in enumerate(orders):
            for last in range(2):
                for slot in range(8):
                    owner = place[0] ^ relative_place(order, slot, last)
                    start = pl.multiple_of(owner * rows, rows)
                    goal = sent[side].at[slot] if last else kept.at[side, slot]
                    copies.append(
                        pltpu.make_async_copy(
                            whole.at[pl.ds(start, rows), pl.ds(side * half, half)],
                            goal.at[:, pl.ds(at, half)],
                            sems.at[len(copies)],
                        )
                    )
                    copies[-1].start()
        at += half
    wait_all(copies)


def run_weight(place, orders, height, groups, gates=()):
    length = groups[0][0].shape[0]
    totals = [own.shape[0] * own.shape[2] for _, _, _, own, _ in groups]
    kept = (2, 8, height // 16, sum(totals) // 2)
    return call(
        partial(weight_kernel, orders, tuple(group[2] for group in groups)),
        (shaped(kept, jnp.bfloat16),) + (shaped(kept[1:], jnp.bfloat16),) * 2,
        [pltpu.VMEM((height, total), jnp.bfloat16) for total in totals]
        + [
            pltpu.VMEM((256, 2 * length), jnp.bfloat16),
            pltpu.SemaphoreType.DMA((32 * len(groups),)),
        ],
        36,
        (place, *(array for group in groups for array in group[:2] + group[3:])),
        in_specs=[SMEM] + [VMEM] * (4 * len(groups)),
        out_specs=(ANY,) * 3,
        gates=gates,
    )


def paired_body(
    inputs,
    cotangent,
    seg_lengths,
    valid_len,
    w_qkv,
    b_qkv,
    w_out,
    b_out,
    gain_one,
    shift_one,
    w_up,
    b_up,
    w_down,
    b_down,
    gain_two,
    shift_two,
):
    core, chip = lax.axis_index("dp"), lax.axis_index("fsdp")
    device = core * 16 + chip
    lengths = seg_lengths[0]
    ends = [jnp.sum(lengths[: end + 1]) for end in range(3)]
    place = jnp.stack([chip, core, *ends, valid_len[0]]).astype(jnp.int32)
    rows_in, grad_top = inputs[0], cotangent[0]

    vectors = (b_qkv, b_out, gain_one, shift_one, b_up, b_down, gain_two, shift_two)
    small = jnp.stack([jnp.pad(vector, (0, SMALL - vector.shape[0])) for vector in vectors])
    small = jnp.pad(small, ((0, w_out.shape[0] - small.shape[0]), (0, 0)))
    cut = w_qkv.shape[1] // 2
    edge = w_out.shape[1] // 2
    inner = jnp.stack(
        [
            jnp.concatenate([w_qkv[:, :cut], w_out[:, :edge], small], axis=1),
            jnp.concatenate([w_qkv[:, cut:], w_out[:, edge:], jnp.zeros_like(small)], axis=1),
        ]
    )[:, None]
    outer = by_side(w_up)
    lower = by_side(w_down)
    held_in = grown(inner, gather_start(inner))
    outer, held_in = tie(outer, held_in)
    held_up = grown(outer, gather_start(outer))
    held_in = grown(held_in, jnp.stack(gather_plane(held_in)))
    held_in, held_up = tie(held_in, held_up)
    held_in = grown(held_in, gather_line(held_in))
    held_up = grown(held_up, jnp.stack(gather_plane(held_up)))
    held_in, held_up = tie(held_in, held_up)
    across_in = gather_across(held_in)
    held_up = grown(held_up, gather_line(held_up))
    lower, held_up = tie(lower, held_up)
    pieces_in = gather_cores(held_in, across_in)
    across_up = gather_across(held_up)
    down_start = gather_start(lower)
    core_up = swap_cores(held_up)

    normed, query, key, value, *lines = run_qkv(place, rows_in, pieces_in, (held_up,))
    full_gain, full_bout, full_gain_two, full_shift_two, full_bdown, full_bup = lines
    down_start, normed = tie(down_start, normed)
    held_down = grown(lower, down_start)
    down_line = gather_line(held_down)
    attended, exact, inverse = run_attend(place, query, key, value, (held_down, core_up))
    across_up, down_line, attended = tie(across_up, down_line, attended)
    pieces_up = (held_up, *across_up, core_up, swap_cores(across_up[0]), swap_cores(across_up[1]))
    held_down = grown(held_down, down_line)
    plane_down = gather_plane(held_down)
    middle, normed_two, inner_half = run_out(
        place,
        rows_in,
        normed,
        attended,
        full_bout,
        full_gain_two,
        full_shift_two,
        pieces_in,
        (held_down, *across_up),
    )
    inner_other = swap_cores(inner_half)
    plane_down, normed_two = tie(plane_down, normed_two)
    held_down = grown(held_down, jnp.stack(plane_down))
    across_down = gather_across(held_down)
    core_down = swap_cores(held_down)
    activated, slope, outer_half = run_up(place, normed_two, full_bup, pieces_up, (held_down,))
    grad_top = grad_top[None]
    across_down, activated, grad_top = tie(across_down, activated, grad_top)
    outer_other = swap_cores(outer_half)
    top_other = swap_cores(grad_top)
    thin = normed_two.shape[1] // 2
    pieces_down = (
        held_down,
        *across_down,
        core_down,
        swap_cores(across_down[0]),
        swap_cores(across_down[1]),
    )
    result, grad_hidden, sum_up, sum_down = run_down(
        place, activated, slope, grad_top[0], middle, full_bdown, pieces_down, (inner_other,)
    )

    grad_hidden = grad_hidden[None]
    outer_other, top_other, grad_hidden = tie(outer_other, top_other, grad_hidden)
    hidden_other = swap_cores(grad_hidden)
    kept_down, *sent_down = run_weight(
        place, MIXED, activated.shape[1] // 2, [(activated, outer_other, thin, grad_top, top_other)]
    )
    hidden_other, kept_down = tie(hidden_other, kept_down)
    down_one = reduce_across(*sent_down)
    kept_up, *sent_up = run_weight(
        place, MIXED, thin, [(normed_two, outer_other, 0, grad_hidden, hidden_other)]
    )
    up_one = reduce_across(*sent_up)
    grad_middle, mixed, grad_att, sum_gain_two, sum_shift_two, sum_out = run_middle_back(
        place, grad_hidden[0], middle, grad_top[0], full_gain_two, pieces_up, pieces_in, (kept_up,)
    )
    mixed = mixed[None]
    down_one, mixed = tie(down_one, mixed)
    mixed_other = swap_cores(mixed)
    down_parts = [kept_down, jnp.stack(down_one)]
    down_two = reduce_line(down_parts, 4)
    grads, sums = run_attend_back(
        place, query, key, value, grad_att, exact, inverse, (down_parts[1],)
    )
    down_two, up_one, grads = tie(down_two, up_one, grads)
    grads_other = swap_cores(grads)
    down_parts.append(down_two)
    up_parts = [kept_up, jnp.stack(up_one)]
    down_three = reduce_plane(down_parts, 2)
    up_two = reduce_line(up_parts, 4)
    grad_rows, sum_gain, sum_shift = run_inputs_back(
        place, grads, rows_in, full_gain, grad_middle, pieces_in, (down_two, up_parts[1])
    )
    down_three, grads_other, grad_rows, mixed_other = tie(
        down_three, grads_other, grad_rows, mixed_other
    )
    down_parts.append(jnp.stack(down_three))
    kept_in, *sent_in = run_weight(
        place,
        MIXED,
        thin,
        [
            (normed, inner_other, 0, grads, grads_other),
            (attended, inner_other, thin, mixed, mixed_other),
        ],
        (down_parts[2],),
    )
    up_two, kept_in = tie(up_two, kept_in)
    in_one = reduce_across(*sent_in)
    in_one, sums = tie(in_one, sums)
    in_parts = [kept_in, jnp.stack(in_one)]
    up_parts.append(up_two)
    up_parts.append(jnp.stack(reduce_plane(up_parts, 2)))
    in_parts.append(reduce_line(in_parts, 4))
    in_parts.append(jnp.stack(reduce_plane(in_parts, 2)))
    shard_down = side_by_side(reduce_end(down_parts), 0, edge)
    shard_up = side_by_side(reduce_end(up_parts), 0, w_up.shape[1] // 2)
    shards = reduce_end(in_parts)
    shard_qkv = side_by_side(shards, 0, cut)
    shard_out = side_by_side(shards, cut, cut + edge)

    def packed(*lines):
        return jnp.concatenate([line.reshape(32, -1) for line in lines], axis=1)

    def own(block):
        block = sum_everywhere(block)
        return lax.dynamic_slice_in_dim(block, device, 1, axis=0)[0]

    own = own(
        packed(
            sums[:2],
            sums[2:],
            sum_out,
            sum_gain,
            sum_shift,
            sum_up,
            sum_down,
            sum_gain_two,
            sum_shift_two,
        )
    )
    at, smalls = 0, []
    narrow = b_out.shape[0]
    for size in (2 * narrow, narrow, narrow, narrow, narrow, b_up.shape[0], narrow, narrow, narrow):
        smalls.append(own[at : at + size])
        at += size
    grad_bqk, grad_bv, grad_bout, grad_gain, grad_shift, grad_bup, grad_bdown, grad_gain_two, grad_shift_two = smalls
    return (
        result[None],
        grad_rows[None],
        shard_qkv,
        grad_bqk,
        grad_bv,
        shard_out,
        grad_bout,
        grad_gain,
        grad_shift,
        shard_up,
        grad_bup,
        shard_down,
        grad_bdown,
        grad_gain_two,
        grad_shift_two,
    )


def solution(mesh):
    placed = (
        P(("dp", "fsdp"), None, None),
        P(("dp", "fsdp"), None, None),
        P(("dp", "fsdp"), None),
        P(("dp", "fsdp")),
        P(("dp", "fsdp"), None),
        P(("dp", "fsdp")),
        P(("dp", "fsdp"), None),
        P(("dp", "fsdp")),
        P(("dp", "fsdp")),
        P(("dp", "fsdp")),
        P(("dp", "fsdp"), None),
        P(("dp", "fsdp")),
        P(("dp", "fsdp"), None),
        P(("dp", "fsdp")),
        P(("dp", "fsdp")),
        P(("dp", "fsdp")),
    )
    paired = dict(mesh.shape) == {"dp": 2, "fsdp": 16}
    return jax.shard_map(
        paired_body if paired else plain_body,
        mesh=mesh,
        in_specs=placed,
        out_specs=(
            P(("dp", "fsdp"), None, None),
            P(("dp", "fsdp"), None, None),
            P(("dp", "fsdp"), None),
            P(("dp", "fsdp")),
            P(("dp", "fsdp")),
            P(("dp", "fsdp"), None),
            P(("dp", "fsdp")),
            P(("dp", "fsdp")),
            P(("dp", "fsdp")),
            P(("dp", "fsdp"), None),
            P(("dp", "fsdp")),
            P(("dp", "fsdp"), None),
            P(("dp", "fsdp")),
            P(("dp", "fsdp")),
            P(("dp", "fsdp")),
        ),
        check_vma=False,
    )
```

```python
from functools import partial

import jax
import jax.numpy as jnp
from jax import lax
from jax.experimental import pallas as pl
from jax.experimental.pallas import tpu as pltpu
from jax.sharding import PartitionSpec as P

HEADS = 16


norm_eps = 1e-05
denom_eps = 1e-06
gelu_coef = 0.7978845608028654


def layer_norm(values, scale_gain, offset):
    centred = values - jnp.mean(values, axis=-1, keepdims=True)
    spread = jnp.mean(centred * centred, axis=-1, keepdims=True)
    return centred * lax.rsqrt(spread + norm_eps) * scale_gain + offset


def feature_map(values):
    return jnp.where(values > 0, values + 1.0, jnp.exp(jnp.minimum(values, 0.0)))


def gelu_tanh(values):
    return (
        0.5 * values * (1.0 + jnp.tanh(gelu_coef * (values + 0.044715 * values * values * values)))
    )


def contract_rows(left_side, right_side):
    return lax.dot_general(
        left_side, right_side, (((0,), (0,)), ((), ())), preferred_element_type=jnp.float32
    )


def contract_cols(left_side, right_side):
    return lax.dot_general(
        left_side, right_side, (((1,), (1,)), ((), ())), preferred_element_type=jnp.float32
    )


def row_masks(lengths, valid_count, row_length):
    places = jnp.arange(row_length, dtype=jnp.int32)
    bounds = jnp.stack([jnp.sum(lengths[: end + 1]) for end in range(lengths.shape[0])])
    segment = jnp.sum((places[:, None] >= bounds[None, :]).astype(jnp.int32), axis=1)
    allowed = (segment[:, None] == segment[None, :]) & (places[None, :] <= places[:, None])
    keeping = (places < valid_count).astype(jnp.float32)
    return (allowed.astype(jnp.float32), keeping)


def split_heads(matrix):
    return jnp.transpose(matrix.reshape(matrix.shape[0], HEADS, -1), (1, 0, 2))


def join_heads(stacked):
    return jnp.transpose(stacked, (1, 0, 2)).reshape(stacked.shape[1], -1)


def pull_group(first, second, third, fourth, fifth, sixth):
    return (
        lax.all_gather(first, ("dp", "fsdp"), axis=0, tiled=True),
        lax.all_gather(second, ("dp", "fsdp"), axis=0, tiled=True),
        lax.all_gather(third, ("dp", "fsdp"), axis=0, tiled=True),
        lax.all_gather(fourth, ("dp", "fsdp"), axis=0, tiled=True),
        lax.all_gather(fifth, ("dp", "fsdp"), axis=0, tiled=True),
        lax.all_gather(sixth, ("dp", "fsdp"), axis=0, tiled=True),
    )


def push_group(first, second, third, stacked):
    return (
        lax.psum_scatter(first, ("dp", "fsdp"), scatter_dimension=0, tiled=True),
        lax.psum_scatter(second, ("dp", "fsdp"), scatter_dimension=0, tiled=True),
        lax.psum_scatter(third, ("dp", "fsdp"), scatter_dimension=0, tiled=True),
        lax.psum_scatter(stacked, ("dp", "fsdp"), scatter_dimension=1, tiled=True),
    )


def head_forward(allowed, head_item):
    query_head, key_head, value_head = head_item
    scores = contract_cols(query_head, key_head) * allowed
    denominator = jnp.sum(scores, axis=1) + denom_eps
    numerator = jnp.dot(scores.astype(jnp.bfloat16), value_head, preferred_element_type=jnp.float32)
    return (numerator, denominator)


def head_backward(allowed, head_item):
    query_head, key_head, value_head, grad_numer, grad_denom = head_item
    scores = contract_cols(query_head, key_head) * allowed
    grad_prob = contract_cols(grad_numer, value_head)
    grad_value = contract_rows(scores.astype(jnp.bfloat16), grad_numer)
    grad_scores = ((grad_prob + grad_denom[:, None]) * allowed).astype(jnp.bfloat16)
    grad_query = jnp.dot(grad_scores, key_head, preferred_element_type=jnp.float32)
    grad_key = contract_rows(grad_scores, query_head)
    return (grad_query, grad_key, grad_value)


def plain_body(
    inputs,
    cotangent,
    seg_lengths,
    valid_len,
    w_qkv,
    b_qkv,
    w_out,
    b_out,
    gain_one,
    shift_one,
    w_up,
    b_up,
    w_down,
    b_down,
    gain_two,
    shift_two,
):
    token_rows = inputs[0].astype(jnp.float32)
    row_length = token_rows.shape[0]
    model_width = token_rows.shape[1]
    allowed, keeping = row_masks(seg_lengths[0], valid_len[0], row_length)
    full_qkv, full_bqkv, full_out, full_bout, full_gain, full_shift = pull_group(
        w_qkv, b_qkv, w_out, b_out, gain_one, shift_one
    )
    normed, norm_back = jax.vjp(
        layer_norm, token_rows, full_gain.astype(jnp.float32), full_shift.astype(jnp.float32)
    )
    normed_low = normed.astype(jnp.bfloat16)
    projected = jnp.dot(
        normed_low, full_qkv, preferred_element_type=jnp.float32
    ) + full_bqkv.astype(jnp.float32)
    query_feat, query_back = jax.vjp(feature_map, projected[:, :model_width])
    key_feat, key_back = jax.vjp(feature_map, projected[:, model_width : 2 * model_width])
    query_heads = split_heads(query_feat.astype(jnp.bfloat16))
    key_heads = split_heads(key_feat.astype(jnp.bfloat16))
    value_heads = split_heads(projected[:, 2 * model_width :].astype(jnp.bfloat16))
    numerator, denominator = lax.map(
        partial(head_forward, allowed), (query_heads, key_heads, value_heads)
    )
    attended = keeping[None, :, None] * numerator / denominator[:, :, None]
    attended_low = join_heads(attended).astype(jnp.bfloat16)
    middle = (
        token_rows
        + jnp.dot(attended_low, full_out, preferred_element_type=jnp.float32)
        + full_bout.astype(jnp.float32)
    )
    full_up, full_bup, full_down, full_bdown, full_gain_two, full_shift_two = pull_group(
        w_up, b_up, w_down, b_down, gain_two, shift_two
    )
    normed_two, norm_two_back = jax.vjp(
        layer_norm, middle, full_gain_two.astype(jnp.float32), full_shift_two.astype(jnp.float32)
    )
    normed_two_low = normed_two.astype(jnp.bfloat16)
    hidden = jnp.dot(normed_two_low, full_up, preferred_element_type=jnp.float32) + full_bup.astype(
        jnp.float32
    )
    activated, gelu_back = jax.vjp(gelu_tanh, hidden)
    activated_low = activated.astype(jnp.bfloat16)
    result = (
        middle
        + jnp.dot(activated_low, full_down, preferred_element_type=jnp.float32)
        + full_bdown.astype(jnp.float32)
    )
    again_up, again_bup, again_down, again_bdown, again_gain_two, again_shift_two = pull_group(
        w_up, b_up, w_down, b_down, gain_two, shift_two
    )
    grad_top = cotangent[0]
    grad_top_full = grad_top.astype(jnp.float32)
    grad_down = contract_rows(activated_low, grad_top)
    grad_bdown = jnp.sum(grad_top_full, axis=0)
    grad_hidden = gelu_back(contract_cols(grad_top, again_down))[0]
    grad_hidden_low = grad_hidden.astype(jnp.bfloat16)
    grad_bup = jnp.sum(grad_hidden_low.astype(jnp.float32), axis=0)
    grad_up = contract_rows(normed_two_low, grad_hidden_low)
    grad_normed_two = contract_cols(grad_hidden_low, again_up)
    grad_middle_norm, grad_gain_two, grad_shift_two = norm_two_back(grad_normed_two)
    grad_middle = grad_top_full + grad_middle_norm
    shard_up, shard_bup, shard_down, shard_small_two = push_group(
        grad_up, grad_bup, grad_down, jnp.stack([grad_bdown, grad_gain_two, grad_shift_two])
    )
    again_qkv, again_bqkv, again_out, again_bout, again_gain, again_shift = pull_group(
        w_qkv, b_qkv, w_out, b_out, gain_one, shift_one
    )
    grad_mixed = grad_middle.astype(jnp.bfloat16)
    grad_bout = jnp.sum(grad_mixed.astype(jnp.float32), axis=0)
    grad_wout = contract_rows(attended_low, grad_mixed)
    grad_attended = split_heads(contract_cols(grad_mixed, again_out))
    grad_numer = (keeping[None, :, None] * grad_attended / denominator[:, :, None]).astype(
        jnp.bfloat16
    )
    grad_denom = -jnp.sum(grad_attended * attended, axis=2) / denominator
    grad_query_heads, grad_key_heads, grad_value_heads = lax.map(
        partial(head_backward, allowed),
        (query_heads, key_heads, value_heads, grad_numer, grad_denom),
    )
    grad_query = query_back(join_heads(grad_query_heads))[0]
    grad_key = key_back(join_heads(grad_key_heads))[0]
    grad_projected = jnp.concatenate(
        [grad_query, grad_key, join_heads(grad_value_heads)], axis=1
    ).astype(jnp.bfloat16)
    grad_bias_all = jnp.sum(grad_projected.astype(jnp.float32), axis=0)
    grad_bias_qk = grad_bias_all[: 2 * model_width]
    grad_bias_v = grad_bias_all[2 * model_width :]
    grad_qkv = contract_rows(normed_low, grad_projected)
    grad_normed = contract_cols(grad_projected, again_qkv)
    grad_rows_norm, grad_gain_one, grad_shift_one = norm_back(grad_normed)
    grad_inputs = (grad_middle + grad_rows_norm).astype(jnp.bfloat16)
    shard_qkv, shard_bias_qk, shard_wout, shard_small_one = push_group(
        grad_qkv,
        grad_bias_qk,
        grad_wout,
        jnp.stack([grad_bout, grad_bias_v, grad_gain_one, grad_shift_one]),
    )
    return (
        result.astype(jnp.bfloat16)[None],
        grad_inputs[None],
        shard_qkv,
        shard_bias_qk,
        shard_small_one[1],
        shard_wout,
        shard_small_one[0],
        shard_small_one[2],
        shard_small_one[3],
        shard_up,
        shard_bup,
        shard_down,
        shard_small_two[0],
        shard_small_two[1],
        shard_small_two[2],
    )


HALF_LANES = 64
TILE = 512
Z_HIGH, Z_LOW, Y_BIT, X_BIT = 8, 4, 2, 1
MIXED = ((Z_HIGH, X_BIT, Z_LOW, Y_BIT), (Z_HIGH, Y_BIT, Z_LOW, X_BIT))
LINED = ((Z_HIGH, Z_LOW, X_BIT, Y_BIT), (Z_HIGH, Z_LOW, Y_BIT, X_BIT))
SMALL = 128
GROUP = 16
ANY = pl.BlockSpec(memory_space=pl.ANY)
SMEM = pl.BlockSpec(memory_space=pltpu.SMEM)
VMEM = pl.BlockSpec(memory_space=pltpu.VMEM)
MIB = 1 << 20


def swap_chips(block, bit):
    return lax.ppermute(block, "fsdp", [(place, place ^ bit) for place in range(16)])


def swap_cores(block):
    return lax.ppermute(block, "dp", [(0, 1), (1, 0)])


def relative_place(order, slot, last):
    return (
        order[0] * (slot & 1)
        + order[1] * ((slot >> 1) & 1)
        + order[2] * ((slot >> 2) & 1)
        + order[3] * last
    )


def tie(*blocks):
    return lax.optimization_barrier(blocks)


def by_side(shard):
    half = shard.shape[1] // 2
    return shard[None, :, :half], shard[None, :, half:]


def swap_sides(sides, orders, step):
    first, second = orders[0][step], orders[1][step]
    if first == second:
        return (swap_chips(jnp.stack(sides), first),)
    return swap_chips(sides[0], first), swap_chips(sides[1], second)


def sides_of(arrived):
    return (arrived[0][0], arrived[0][1]) if len(arrived) == 1 else arrived


def grown(sides, arrived):
    return tuple(jnp.concatenate([held, more]) for held, more in zip(sides, sides_of(arrived)))


def swap_both(sides):
    return swap_cores(sides[0]), swap_cores(sides[1])


def pieces_of(held, across, core_held, core_across):
    return tuple(
        block for side in range(2) for block in (held[side], across[side], core_held[side], core_across[side])
    )


def added(parts, start, stop):
    return sum(part[start:stop].astype(jnp.float32) for part in parts)


def reduce_step(sides, orders, step, amount):
    sent = [added(parts, amount, 2 * amount).astype(jnp.bfloat16) for parts in sides]
    return swap_sides(sent, orders, step)


def with_arrived(sides, arrived):
    return [parts + [more] for parts, more in zip(sides, sides_of(arrived))]


def reduce_end(sides, orders):
    sides = with_arrived(sides, reduce_step(sides, orders, 0, 1))
    return [added(parts, 0, 1)[0] for parts in sides]


def side_by_side(sides, start, stop):
    return jnp.concatenate([side[:, start:stop] for side in sides], axis=1)


def sum_everywhere(block):
    block = block + swap_cores(block)
    for bit in (Z_LOW, Z_HIGH, X_BIT, Y_BIT):
        block = block + swap_chips(block, bit)
    return block


def far(array):
    return pltpu.with_memory_space_constraint(array, pltpu.HBM)


def call(kernel, outs, scratch, mib, args, in_specs, out_specs, grid=None, flops=0, gates=()):
    inputs, ignored = len(in_specs), len(gates)

    def gated(*refs):
        kernel(*refs[:inputs], *refs[inputs + ignored :])

    extra = {} if grid is None else {"grid": grid}
    args = [far(arg) if spec is ANY else arg for arg, spec in zip(args, in_specs)]
    gates = [far(gate) for gate in gates]
    if isinstance(outs, tuple):
        outs = tuple(
            pltpu.HBM(out.shape, out.dtype) if spec is ANY else out
            for out, spec in zip(outs, out_specs)
        )
    return pl.pallas_call(
        gated,
        out_shape=outs,
        in_specs=list(in_specs) + [ANY] * ignored,
        out_specs=out_specs,
        scratch_shapes=scratch,
        compiler_params=pltpu.CompilerParams(vmem_limit_bytes=mib * MIB),
        cost_estimate=pl.CostEstimate(flops=flops, bytes_accessed=0, transcendentals=0),
        **extra,
    )(*args, *gates)


def shaped(shape, dtype):
    return jax.ShapeDtypeStruct(shape, dtype)


def dot_nn(left, right):
    return lax.dot_general(left, right, (((1,), (0,)), ((), ())), preferred_element_type=jnp.float32)


def dot_nt(left, right):
    return lax.dot_general(left, right, (((1,), (1,)), ((), ())), preferred_element_type=jnp.float32)


def fetch(place, pieces, whole, sems, skip=0):
    rows, half = pieces[0].shape[1], whole.shape[1] // 2
    copies = []
    for side, order in enumerate(LINED):
        for core in range(2):
            for last in range(2):
                piece = pieces[side * 4 + core * 2 + last]
                for slot in range(8):
                    owner = (place[1] ^ core) * 16 + (place[0] ^ relative_place(order, slot, last))
                    start = pl.multiple_of(owner * rows, rows)
                    copies.append(
                        pltpu.make_async_copy(
                            piece.at[slot, :, pl.ds(skip, half)],
                            whole.at[pl.ds(start, rows), pl.ds(side * half, half)],
                            sems.at[len(copies)],
                        )
                    )
    for copy in copies:
        copy.start()
    return copies


def wait_side(copies, side):
    half = len(copies) // 2
    wait_all(copies[side * half : (side + 1) * half])


def wait_all(copies):
    for copy in copies:
        copy.wait()


def standardize(block):
    centred = block - jnp.mean(block, axis=1, keepdims=True)
    scale = lax.rsqrt(jnp.mean(centred * centred, axis=1, keepdims=True) + norm_eps)
    return centred * scale, scale


def norm_pull(grad, standard, scale, gain):
    scaled = grad * gain
    return scale * (
        scaled
        - jnp.mean(scaled, axis=1, keepdims=True)
        - standard * jnp.mean(scaled * standard, axis=1, keepdims=True)
    )


def fetch_small(place, pieces, small, skip, sems):
    copies = []
    for core in range(2):
        for last in range(2):
            piece = pieces[core * 2 + last]
            for slot in range(8):
                far = relative_place(LINED[0], slot, last)
                owner = (place[1] ^ core) * 16 + (place[0] ^ far)
                start = pl.multiple_of(owner * GROUP, GROUP)
                copies.append(
                    pltpu.make_async_copy(
                        piece.at[slot, pl.ds(0, GROUP), pl.ds(skip, SMALL)],
                        small.at[pl.ds(start, GROUP), :],
                        sems.at[len(copies)],
                    )
                )
                copies[-1].start()
    return copies


def tables(each):
    total = 32 * each
    column = lax.broadcasted_iota(jnp.int32, (1, total), 1).astype(jnp.float32)
    turn = jnp.floor((column + 0.5) / each)
    lane = lax.broadcasted_iota(jnp.int32, (SMALL, 1), 0).astype(jnp.float32)
    spread = jnp.where(column - turn * each == lane, 1.0, 0.0).astype(jnp.bfloat16)
    owner = lax.broadcasted_iota(jnp.int32, (32, 1), 0).astype(jnp.float32)
    return owner == turn, spread


def unfold(small, each, rows):
    mine, spread = tables(each)
    lines = []
    for row in rows:
        parts = small[pl.ds(row, 32, stride=GROUP), :].astype(jnp.bfloat16)
        parts = jnp.where(mine, dot_nn(parts, spread), 0.0)
        lines.append(jnp.sum(parts, axis=0, keepdims=True))
    return lines


def fold(small, each, vectors):
    mine, spread = tables(each)
    for row, vector in vectors:
        parts = jnp.where(mine, vector, 0.0).astype(jnp.bfloat16)
        small[pl.ds(row, 32, stride=32), :] = dot_nt(parts, spread)


def qkv_kernel(place, rows_in, *rest):
    pieces, (normed, query, key, value), lines, rest = rest[:8], rest[8:12], rest[12:18], rest[18:]
    whole, small, smalls, bias, sems, more = rest
    few = fetch_small(place, pieces, small, 4 * whole.shape[1] // 6, more)
    copies = fetch(place, pieces, whole, sems)
    wait_all(few)
    smalls[...] = small[...].astype(jnp.float32)
    width = rows_in.shape[1]
    (bias[...],) = unfold(smalls, 3 * width // 32, (0,))
    (lines[5][...],) = unfold(smalls, 4 * width // 32, (4,))
    bias_out, gain, shift, bias_down, gain_two, shift_two = unfold(
        smalls, width // 32, (1, 2, 3, 5, 6, 7)
    )
    for goal, line in zip(lines, (gain, bias_out, gain_two, shift_two, bias_down)):
        goal[...] = line
    for part in range(4):
        at = pl.ds(part * 128, 128)
        standard, _ = standardize(rows_in[at, :].astype(jnp.float32))
        normed[at, :] = (standard * gain + shift).astype(jnp.bfloat16)
    for tile in range(6):
        if tile % 3 == 0:
            wait_side(copies, tile // 3)
        cols = pl.ds(tile * TILE, TILE)
        projected = dot_nn(normed[...], whole[:, cols]) + bias[:, cols]
        goal = (query, key, value)[tile // 2]
        if tile < 4:
            projected = feature_map(projected)
        goal[:, pl.ds((tile % 2) * TILE, TILE)] = projected.astype(jnp.bfloat16)


def run_qkv(place, rows_in, pieces, gates=()):
    length, width = rows_in.shape
    narrow = shaped((length, width), jnp.bfloat16)
    line = shaped((1, width), jnp.float32)
    return call(
        qkv_kernel,
        (narrow,) * 4 + (line,) * 5 + (shaped((1, 4 * width), jnp.float32),),
        [
            pltpu.VMEM((width, 3 * width), jnp.bfloat16),
            pltpu.VMEM((32 * GROUP, SMALL), jnp.bfloat16),
            pltpu.VMEM((32 * GROUP, SMALL), jnp.float32),
            pltpu.VMEM((1, 3 * width), jnp.float32),
            pltpu.SemaphoreType.DMA((64,)),
            pltpu.SemaphoreType.DMA((32,)),
        ],
        28,
        (place, rows_in, *pieces),
        in_specs=[SMEM, VMEM] + [ANY] * 8,
        out_specs=(VMEM,) * 10,
        gates=gates,
    )


def image_of(place, positions):
    image = jnp.zeros(positions.shape, jnp.int32)
    for end in range(2, 5):
        image = image + jnp.where(positions >= place[end], 1, 0)
    return image


def allowed_block(place, length, flipped):
    first = lax.broadcasted_iota(jnp.int32, (length, 1), 0)
    second = lax.broadcasted_iota(jnp.int32, (1, length), 1)
    same = image_of(place, first) == image_of(place, second)
    ordered = (first <= second) if flipped else (second <= first)
    return jnp.where(same & ordered, 1.0, 0.0).astype(jnp.float32)


def low_lanes():
    return lax.broadcasted_iota(jnp.int32, (1, 2 * HALF_LANES), 1) < HALF_LANES


def two_heads(block):
    low = jnp.where(low_lanes(), 1.0, 0.0)
    high = (1.0 - low).astype(jnp.bfloat16)
    return jnp.concatenate([block * low.astype(jnp.bfloat16), block * high], axis=0)


def one_pair(stacked):
    half = stacked.shape[0] // 2
    return jnp.where(low_lanes(), stacked[:half], stacked[half:])


def masked(stacked, allowed):
    half = stacked.shape[0] // 2
    return jnp.concatenate(
        [(stacked[:half] * allowed).astype(jnp.bfloat16), (stacked[half:] * allowed).astype(jnp.bfloat16)],
        axis=0,
    )


def keeping_rows(place, start, amount):
    position = lax.broadcasted_iota(jnp.int32, (amount, 1), 0) + start
    return jnp.where(position < place[5], 1.0, 0.0)


def attend_kernel(place, query, key, value, attended, exact, inverse, allowed, wide):
    length, width = query.shape
    step = length // 2

    @pl.when(pl.program_id(0) == 0)
    def _():
        allowed[...] = allowed_block(place, length, False)
        wide[:, width:] = jnp.ones((length, width), jnp.bfloat16)

    wide[:, :width] = value[...]
    for part in range(2):
        rows, seen = pl.ds(part * step, step), (part + 1) * step
        scores = dot_nt(two_heads(query[rows, :]), key[:seen, :])
        total = dot_nn(masked(scores, allowed[rows, :seen]), wide[:seen, :])
        over = 1.0 / (one_pair(total[:, width:]) + denom_eps)
        inverse[rows, :] = over
        mixed = keeping_rows(place, part * step, step) * one_pair(total[:, :width]) * over
        exact[rows, :] = mixed
        attended[rows, :] = mixed.astype(jnp.bfloat16)


def run_attend(place, query, key, value, gates=()):
    length, width = query.shape
    pair = pl.BlockSpec((length, 2 * HALF_LANES), lambda p: (0, p))
    return call(
        attend_kernel,
        (
            shaped((length, width), jnp.bfloat16),
            shaped((length, width), jnp.float32),
            shaped((length, width), jnp.float32),
        ),
        [
            pltpu.VMEM((length, length), jnp.float32),
            pltpu.VMEM((length, 4 * HALF_LANES), jnp.bfloat16),
        ],
        16,
        (place, query, key, value),
        grid=(width // (2 * HALF_LANES),),
        in_specs=[SMEM] + [pair] * 3,
        out_specs=(pair,) * 3,
        gates=gates,
    )


def attend_back_kernel(
    place, query, key, value, grad_att, exact, inverse, *rest
):
    stacked, sums, (allowed, flipped, left, wide) = rest[0], rest[1], rest[2:]
    length, width = query.shape
    step = length // 2

    @pl.when(pl.program_id(0) == 0)
    def _():
        allowed[...] = allowed_block(place, length, False)
        flipped[...] = allowed_block(place, length, True)
        wide[:, width:] = jnp.ones((length, width), jnp.bfloat16)

    wide[:, :width] = value[...]
    over = grad_att[...] * inverse[...]
    lane = lax.broadcasted_iota(jnp.int32, (1, width), 1)
    terms, low = over * exact[...], lane < HALF_LANES
    first = jnp.sum(jnp.where(low, terms, 0.0), axis=1, keepdims=True)
    second = jnp.sum(jnp.where(low, 0.0, terms), axis=1, keepdims=True)
    spread = -jnp.where(low, first, second)
    high = spread.astype(jnp.bfloat16).astype(jnp.float32)
    within = lane & (HALF_LANES - 1)
    spread = jnp.where(within == 0, high, jnp.where(within == 1, spread - high, 0.0))
    numer = (keeping_rows(place, 0, length) * over).astype(jnp.bfloat16)
    for head in range(2):
        here = jnp.where(low, 1.0 - head, 1.0 * head)
        at = pl.ds(head * length, length)
        left[at, :width] = numer * here.astype(jnp.bfloat16)
        left[at, width:] = (spread * here).astype(jnp.bfloat16)
    for part in range(2):
        rows, seen = pl.ds(part * step, step), (part + 1) * step
        start = part * step
        later = pl.ds(start, length - start)
        both = jnp.concatenate([left[rows, :], left[pl.ds(length + start, step), :]], axis=0)
        grad_scores = masked(dot_nt(both, wide[:seen, :]), allowed[rows, :seen])
        grad_query = one_pair(dot_nn(grad_scores, key[:seen, :]))
        full = left[later, :] + left[pl.ds(length + start, length - start), :]
        scores = masked(dot_nt(two_heads(key[rows, :]), query[later, :]), flipped[rows, later])
        grad_value = one_pair(dot_nn(scores, full[:, :width]))
        ones = jnp.concatenate([two_heads(value[rows, :]), two_heads(wide[rows, width:])], axis=1)
        grad_scores = masked(dot_nt(ones, full), flipped[rows, later])
        grad_key = one_pair(dot_nn(grad_scores, query[later, :]))
        grads = (
            grad_query * jnp.minimum(query[rows, :].astype(jnp.float32), 1.0),
            grad_key * jnp.minimum(key[rows, :].astype(jnp.float32), 1.0),
            grad_value,
        )
        for index, grad in enumerate(grads):
            low_grad, line = grad.astype(jnp.bfloat16), pl.ds(index, 1)
            stacked[index, rows, :] = low_grad
            extra = jnp.sum(low_grad.astype(jnp.float32), axis=0, keepdims=True)
            sums[line, :] = extra if part == 0 else sums[line, :] + extra


def run_attend_back(place, first, query, key, value, grad_att, exact, inverse, gates=()):
    length, width = query.shape
    half = width // 2
    start = first * half // (2 * HALF_LANES)
    pair = pl.BlockSpec((length, 2 * HALF_LANES), lambda p: (0, p + start))
    stack = pl.BlockSpec((3, length, 2 * HALF_LANES), lambda p: (0, 0, p))
    lines = pl.BlockSpec((3, 2 * HALF_LANES), lambda p: (0, p))
    return call(
        attend_back_kernel,
        (shaped((3, length, half), jnp.bfloat16), shaped((3, half), jnp.float32)),
        [
            pltpu.VMEM((length, length), jnp.float32),
            pltpu.VMEM((length, length), jnp.float32),
            pltpu.VMEM((2 * length, 4 * HALF_LANES), jnp.bfloat16),
            pltpu.VMEM((length, 4 * HALF_LANES), jnp.bfloat16),
        ],
        20,
        (place, query, key, value, grad_att, exact, inverse),
        grid=(half // (2 * HALF_LANES),),
        in_specs=[SMEM] + [pair] * 6,
        out_specs=(stack, lines),
        gates=gates,
    )


def hand_over(place, sources, goal, sems):
    copies, at = [], 0
    for source in sources:
        half = source.shape[1] // 2
        start = pl.multiple_of((1 - place[1]) * half, half)
        copies.append(
            pltpu.make_async_copy(
                source.at[:, pl.ds(start, half)], goal.at[:, pl.ds(at, half)], sems.at[len(copies)]
            )
        )
        copies[-1].start()
        at += half
    return copies


def out_kernel(place, rows_in, early, attended, bias, gain, shift, *rest):
    pieces, (middle, normed, handed, whole, sems, more) = rest[:8], rest[8:]
    copies = fetch(place, pieces, whole, sems, 3 * whole.shape[1] // 2)
    handing = hand_over(place, (early, attended), handed, more)
    for side in range(2):
        wait_side(copies, side)
        cols = pl.ds(side * TILE, TILE)
        middle[:, cols] = (
            rows_in[:, cols].astype(jnp.float32) + dot_nn(attended[...], whole[:, cols]) + bias[:, cols]
        )
    for part in range(4):
        at = pl.ds(part * 128, 128)
        standard, _ = standardize(middle[at, :])
        normed[at, :] = (standard * gain[...] + shift[...]).astype(jnp.bfloat16)
    wait_all(handing)


def run_out(place, rows_in, early, attended, bias, gain, shift, pieces, gates=()):
    length, width = rows_in.shape
    narrow = shaped((length, width), jnp.bfloat16)
    return call(
        out_kernel,
        (shaped((length, width), jnp.float32), narrow, narrow),
        [
            pltpu.VMEM((width, width), jnp.bfloat16),
            pltpu.SemaphoreType.DMA((64,)),
            pltpu.SemaphoreType.DMA((2,)),
        ],
        24,
        (place, rows_in, early, attended, bias, gain, shift, *pieces),
        in_specs=[SMEM] + [VMEM] * 6 + [ANY] * 8,
        out_specs=(VMEM, VMEM, ANY),
        gates=gates,
    )


def bend_tile(hidden, activated, slope):
    square = hidden * hidden
    rate = gelu_coef + (gelu_coef * 0.044715) * square
    bend = jnp.tanh(hidden * rate)
    share = 0.5 + 0.5 * bend
    activated[...] = (hidden * share).astype(jnp.bfloat16)
    rate = gelu_coef + (3.0 * gelu_coef * 0.044715) * square
    slope[...] = (share + (0.5 * hidden) * (1.0 - bend * bend) * rate).astype(jnp.bfloat16)


def up_kernel(place, normed, bias, *rest):
    pieces, (activated, slope, handed, whole, hidden, sems, more) = rest[:8], rest[8:]
    copies = fetch(place, pieces, whole, sems)
    tiles = whole.shape[1] // TILE

    def columns(tile):
        return pl.ds(tile * TILE, TILE)

    for tile in range(tiles + 1):
        if tile % (tiles // 2) == 0 and tile < tiles:
            wait_side(copies, tile // (tiles // 2))
        if tile < tiles:
            cols = columns(tile)
            hidden[tile % 2] = dot_nn(normed[...], whole[:, cols]) + bias[:, cols]
        if tile > 0:
            cols = columns(tile - 1)
            bend_tile(hidden[(tile - 1) % 2], activated.at[:, cols], slope.at[:, cols])

    wait_all(hand_over(place, (normed, activated), handed, more))


def run_up(place, normed, bias, pieces, gates=()):
    length, width = normed.shape
    wide = bias.shape[1]
    return call(
        up_kernel,
        (shaped((length, wide), jnp.bfloat16),) * 2
        + (shaped((length, (width + wide) // 2), jnp.bfloat16),),
        [
            pltpu.VMEM((width, wide), jnp.bfloat16),
            pltpu.VMEM((2, length, TILE), jnp.float32),
            pltpu.SemaphoreType.DMA((64,)),
            pltpu.SemaphoreType.DMA((2,)),
        ],
        34,
        (place, normed, bias, *pieces),
        in_specs=[SMEM] + [VMEM] * 2 + [ANY] * 8,
        out_specs=(VMEM, VMEM, ANY),
        gates=gates,
    )


def sum_kernel(block, total):
    total[...] = jnp.sum(block[...].astype(jnp.float32), axis=0, keepdims=True)


def run_sum(block, cover, gates=()):
    return call(
        sum_kernel,
        shaped((1, block.shape[1]), jnp.float32),
        [],
        8,
        (block,),
        in_specs=[VMEM],
        out_specs=VMEM,
        flops=cover,
        gates=gates,
    )


def down_kernel(place, activated, slope, grad_top, middle, bias, *rest):
    pieces, (result, grad_hidden, sum_up, whole, total, sems) = rest[:8], rest[8:]
    copies = fetch(place, pieces, whole, sems)
    wait_all(copies)
    total[...] = middle[...] + bias[...]
    step = 2 * TILE

    @pl.loop(0, whole.shape[0] // step)
    def _(tile):
        cols = pl.ds(pl.multiple_of(tile * step, step), step)
        total[...] += dot_nn(activated[:, cols], whole[cols, :])
        grad = dot_nt(grad_top[...], whole[cols, :]) * slope[:, cols].astype(jnp.float32)
        low = grad.astype(jnp.bfloat16)
        grad_hidden[:, cols] = low
        sum_up[:, cols] = jnp.sum(low.astype(jnp.float32), axis=0, keepdims=True)

    result[...] = total[...].astype(jnp.bfloat16)


def run_down(place, activated, slope, grad_top, middle, bias, pieces, gates=()):
    length, width = middle.shape
    wide = activated.shape[1]
    return call(
        down_kernel,
        (
            shaped((length, width), jnp.bfloat16),
            shaped((length, wide), jnp.bfloat16),
            shaped((1, wide), jnp.float32),
        ),
        [
            pltpu.VMEM((wide, width), jnp.bfloat16),
            pltpu.VMEM((length, width), jnp.float32),
            pltpu.SemaphoreType.DMA((64,)),
        ],
        40,
        (place, activated, slope, grad_top, middle, bias, *pieces),
        in_specs=[SMEM] + [VMEM] * 5 + [ANY] * 8,
        out_specs=(VMEM,) * 3,
        flops=64 * length * width * wide,
        gates=gates,
    )


def middle_back_kernel(place, grad_hidden, middle, grad_top, gain, *rest):
    pieces_up, pieces_in, rest = rest[:8], rest[8:16], rest[16:]
    grad_middle, mixed, grad_att, sum_gain, sum_shift, whole, outer, total, sems, more = rest
    copies = fetch(place, pieces_up, whole, sems)
    second = fetch(place, pieces_in, outer, more, 3 * outer.shape[1] // 2)
    step = 2 * TILE
    for tile in range(whole.shape[1] // step):
        if tile % 2 == 0:
            wait_side(copies, tile // 2)
        cols = pl.ds(tile * step, step)
        block = dot_nt(grad_hidden[:, cols], whole[:, cols])
        total[...] = block if tile == 0 else total[...] + block

    for part in range(4):
        at = pl.ds(part * 128, 128)
        grad = total[at, :]
        standard, scale = standardize(middle[at, :])
        back = grad_top[at, :].astype(jnp.float32) + norm_pull(grad, standard, scale, gain[...])
        grad_middle[at, :] = back
        low = back.astype(jnp.bfloat16)
        mixed[at, :] = low
        for goal, added in ((sum_gain, grad * standard), (sum_shift, grad)):
            added = jnp.sum(added, axis=0, keepdims=True)
            goal[...] = added if part == 0 else goal[...] + added
    wait_all(second)
    for part in range(2):
        cols = pl.ds(part * TILE, TILE)
        grad_att[:, cols] = dot_nt(mixed[...], outer[cols, :])


def run_middle_back(place, grad_hidden, middle, grad_top, gain, pieces_up, pieces_in, gates=()):
    length, width = middle.shape
    wide = grad_hidden.shape[1]
    full, line = shaped((length, width), jnp.float32), shaped((1, width), jnp.float32)
    return call(
        middle_back_kernel,
        (full, shaped((length, width), jnp.bfloat16), full, line, line),
        [
            pltpu.VMEM((width, wide), jnp.bfloat16),
            pltpu.VMEM((width, width), jnp.bfloat16),
            pltpu.VMEM((length, width), jnp.float32),
            pltpu.SemaphoreType.DMA((64,)),
            pltpu.SemaphoreType.DMA((64,)),
        ],
        40,
        (place, grad_hidden, middle, grad_top, gain, *pieces_up, *pieces_in),
        in_specs=[SMEM] + [VMEM] * 4 + [ANY] * 16,
        out_specs=(VMEM,) * 5,
        gates=gates,
    )


def inputs_back_kernel(place, early, late, rows_in, gain, grad_middle, *rest):
    pieces, (grad_rows, sum_gain, sum_shift, whole, total, sems) = rest[:8], rest[8:]
    copies = fetch(place, pieces, whole, sems)
    width = rows_in.shape[1]
    for tile in range(6):
        if tile % 3 == 0:
            wait_side(copies, tile // 3)
        grads = (early, late)[tile % 2]
        block = dot_nt(grads[tile // 2], whole[:, pl.ds(tile * TILE, TILE)])
        total[...] = block if tile == 0 else total[...] + block
    for part in range(4):
        at = pl.ds(part * 128, 128)
        grad = total[at, :]
        standard, scale = standardize(rows_in[at, :].astype(jnp.float32))
        back = grad_middle[at, :] + norm_pull(grad, standard, scale, gain[...])
        grad_rows[at, :] = back.astype(jnp.bfloat16)
        for goal, extra in ((sum_gain, grad * standard), (sum_shift, grad)):
            extra = jnp.sum(extra, axis=0, keepdims=True)
            goal[...] = extra if part == 0 else goal[...] + extra


def run_inputs_back(place, early, late, rows_in, gain, grad_middle, pieces, gates=()):
    length, width = rows_in.shape
    line = shaped((1, width), jnp.float32)
    return call(
        inputs_back_kernel,
        (shaped((length, width), jnp.bfloat16), line, line),
        [
            pltpu.VMEM((width, 3 * width), jnp.bfloat16),
            pltpu.VMEM((length, width), jnp.float32),
            pltpu.SemaphoreType.DMA((64,)),
        ],
        30,
        (place, early, late, rows_in, gain, grad_middle, *pieces),
        in_specs=[SMEM] + [VMEM] * 5 + [ANY] * 8,
        out_specs=(VMEM,) * 3,
        gates=gates,
    )


def weight_kernel(orders, skips, sizes, place, *rest):
    groups = len(skips)
    if sizes:
        mine, other_lines, rest = rest[4 * groups], rest[4 * groups + 1], rest[: 4 * groups] + rest[4 * groups + 2 :]
    inputs, outs, rest = rest[: 4 * groups], rest[4 * groups : 4 * groups + 4], rest[4 * groups + 4 :]
    wholes, (turned, sems), rest = rest[:groups], rest[groups : groups + 2], rest[groups + 2 :]
    length = inputs[0].shape[0]
    for group, (skip, whole) in enumerate(zip(skips, wholes)):
        left_own, left_other, own, other = inputs[4 * group : 4 * group + 4]
        height, count, each = whole.shape[0], own.shape[0], own.shape[2]
        start = pl.multiple_of(place[1] * height, height)

        @pl.loop(0, height // 256)
        def _(tile):
            low = pl.multiple_of(tile * 256, 256)
            turned[:, :length] = left_own[:, pl.ds(start + low, 256)].T
            turned[:, length:] = left_other[:, pl.ds(skip + low, 256)].T
            for index in range(count):
                for step in range(each // TILE):
                    cols = pl.ds(step * TILE, TILE)
                    block = dot_nn(turned[:, :length], own[index, :, cols])
                    block += dot_nn(turned[:, length:], other[index, :, cols])
                    goal = pl.ds(index * each + step * TILE, TILE)
                    whole[pl.ds(low, 256), goal] = block.astype(jnp.bfloat16)

    rows, at, copies = outs[0].shape[1], 0, []
    for whole in wholes:
        half = whole.shape[1] // 2
        for side, order in enumerate(orders):
            for last in range(2):
                for slot in range(8):
                    owner = place[0] ^ relative_place(order, slot, last)
                    start = pl.multiple_of(owner * rows, rows)
                    goal = outs[last * 2 + side].at[slot]
                    copies.append(
                        pltpu.make_async_copy(
                            whole.at[pl.ds(start, rows), pl.ds(side * half, half)],
                            goal.at[:, pl.ds(at, half)],
                            sems.at[len(copies)],
                        )
                    )
                    copies[-1].start()
        at += half
    if sizes:
        wide_small, small, more = rest
        wide_small[...] = jnp.zeros_like(wide_small)
        start, by_size = 0, {}
        for row, size in enumerate(sizes):
            line = mine[:, start : start + size] + other_lines[:, start : start + size]
            by_size.setdefault(size, []).append((row, line))
            start += size
        for size, vectors in by_size.items():
            fold(wide_small, size // 32, vectors)
        small[...] = wide_small[...].astype(jnp.bfloat16)
        for last in range(2):
            for slot in range(8):
                chip = place[0] ^ relative_place(orders[0], slot, last)
                start = pl.multiple_of((place[1] * 16 + chip) * 32, 32)
                copies.append(
                    pltpu.make_async_copy(
                        small.at[pl.ds(start, 32), :],
                        outs[last * 2].at[slot, :, pl.ds(at, SMALL)],
                        more.at[last * 8 + slot],
                    )
                )
                copies[-1].start()
    wait_all(copies)


def run_weight(place, orders, height, groups, gates=(), sizes=(), lines=()):
    length = groups[0][0].shape[0]
    totals = [own.shape[0] * own.shape[2] for _, _, _, own, _ in groups]
    half = sum(totals) // 2
    part = shaped((8, height // 16, half), jnp.bfloat16)
    first = shaped((8, height // 16, half + (SMALL if sizes else 0)), jnp.bfloat16)
    extra = [
        pltpu.VMEM((32 * 32, SMALL), jnp.float32),
        pltpu.VMEM((32 * 32, SMALL), jnp.bfloat16),
        pltpu.SemaphoreType.DMA((16,)),
    ]
    return call(
        partial(weight_kernel, orders, tuple(group[2] for group in groups), sizes),
        (first,) * 4,
        [pltpu.VMEM((height, total), jnp.bfloat16) for total in totals]
        + [
            pltpu.VMEM((256, 2 * length), jnp.bfloat16),
            pltpu.SemaphoreType.DMA((32 * len(groups),)),
        ]
        + (extra if sizes else []),
        36,
        (place, *(array for group in groups for array in group[:2] + group[3:]), *lines),
        in_specs=[SMEM] + [VMEM] * (4 * len(groups) + len(lines)),
        out_specs=(ANY,) * 4,
        gates=gates,
    )


def paired_body(
    inputs,
    cotangent,
    seg_lengths,
    valid_len,
    w_qkv,
    b_qkv,
    w_out,
    b_out,
    gain_one,
    shift_one,
    w_up,
    b_up,
    w_down,
    b_down,
    gain_two,
    shift_two,
):
    core, chip = lax.axis_index("dp"), lax.axis_index("fsdp")
    device = core * 16 + chip
    lengths = seg_lengths[0]
    ends = [jnp.sum(lengths[: end + 1]) for end in range(3)]
    place = jnp.stack([chip, core, *ends, valid_len[0]]).astype(jnp.int32)
    rows_in, grad_top = inputs[0], cotangent[0]

    vectors = (b_qkv, b_out, gain_one, shift_one, b_up, b_down, gain_two, shift_two)
    small = jnp.stack([jnp.pad(vector, (0, SMALL - vector.shape[0])) for vector in vectors])
    small = jnp.pad(small, ((0, w_out.shape[0] - small.shape[0]), (0, 0)))
    cut = w_qkv.shape[1] // 2
    edge = w_out.shape[1] // 2
    held_in = (
        jnp.concatenate([w_qkv[:, :cut], w_out[:, :edge], small], axis=1)[None],
        jnp.concatenate([w_qkv[:, cut:], w_out[:, edge:], jnp.zeros_like(small)], axis=1)[None],
    )
    held_up, held_down = by_side(w_up), by_side(w_down)
    top = grad_top[None]
    held_in = grown(held_in, swap_sides(held_in, LINED, 0))
    held_in = grown(held_in, swap_sides(held_in, LINED, 1))
    held_in, held_up = tie(held_in, held_up)
    start_up = swap_sides(held_up, LINED, 0)
    held_in = grown(held_in, swap_sides(held_in, LINED, 2))
    across_in = swap_sides(held_in, LINED, 3)
    core_in = swap_both(held_in)
    held_up = grown(held_up, start_up)
    held_up = grown(held_up, swap_sides(held_up, LINED, 1))
    held_up, held_down = tie(held_up, held_down)
    start_down = swap_sides(held_down, LINED, 0)
    across_in, start_down = tie(across_in, start_down)
    pieces_in = pieces_of(held_in, across_in, core_in, swap_both(across_in))
    plane_up = swap_sides(held_up, LINED, 2)
    held_down = grown(held_down, start_down)
    line_down = swap_sides(held_down, LINED, 1)
    top_other = swap_cores(top)

    normed, query, key, value, *lines = run_qkv(
        place, rows_in, pieces_in, (*held_up, *held_down, top_other)
    )
    full_gain, full_bout, full_gain_two, full_shift_two, full_bdown, full_bup = lines
    plane_up, line_down, normed = tie(plane_up, line_down, normed)
    held_up = grown(held_up, plane_up)
    across_up = swap_sides(held_up, LINED, 3)
    core_up = swap_both(held_up)
    held_down = grown(held_down, line_down)
    attended, exact, inverse = run_attend(place, query, key, value, (*held_up, *held_down))
    core_up, held_down, attended = tie(core_up, held_down, attended)
    plane_down = swap_sides(held_down, LINED, 2)
    middle, normed_two, inner_half = run_out(
        place,
        rows_in,
        normed,
        attended,
        full_bout,
        full_gain_two,
        full_shift_two,
        pieces_in,
    )
    inner_other = swap_cores(inner_half)
    across_up, plane_down, normed_two = tie(across_up, plane_down, normed_two)
    pieces_up = pieces_of(held_up, across_up, core_up, swap_both(across_up))
    held_down = grown(held_down, plane_down)
    across_down = swap_sides(held_down, LINED, 3)
    core_down = swap_both(held_down)
    activated, slope, outer_half = run_up(
        place, normed_two, full_bup, pieces_up, (*held_down, inner_other)
    )
    outer_other = swap_cores(outer_half)
    sum_down = run_sum(grad_top, 1 << 40, (outer_half,))
    thin = normed_two.shape[1] // 2
    parts = run_weight(
        place,
        MIXED,
        activated.shape[1] // 2,
        [(activated, outer_other, thin, top, top_other)],
        (*core_down, sum_down),
    )
    across_down, parts = tie(across_down, parts)
    down_one = swap_sides(parts[2:], MIXED, 3)
    pieces_down = pieces_of(held_down, across_down, core_down, swap_both(across_down))
    result, grad_hidden, sum_up = run_down(
        place, activated, slope, grad_top, middle, full_bdown, pieces_down, parts[2:]
    )
    down_one, grad_hidden = tie(down_one, grad_hidden)
    hidden_other = swap_cores(grad_hidden[None])
    down_sides = with_arrived([[parts[0]], [parts[1]]], down_one)
    down_two = reduce_step(down_sides, MIXED, 2, 4)
    grad_middle, mixed, grad_att, sum_gain_two, sum_shift_two = run_middle_back(
        place, grad_hidden, middle, grad_top, full_gain_two, pieces_up, pieces_in, down_one
    )
    mixed = mixed[None]
    hidden_other, mixed = tie(hidden_other, mixed)
    mixed_other = swap_cores(mixed)
    parts = run_weight(
        place, LINED, thin, [(normed_two, outer_other, 0, grad_hidden[None], hidden_other)]
    )
    up_one = swap_sides(parts[2:], LINED, 3)
    grads, sums = run_attend_back(
        place, 0, query, key, value, grad_att, exact, inverse, parts[2:]
    )
    down_two, mixed_other, grads = tie(down_two, mixed_other, grads)
    grads_other = swap_cores(grads)
    down_sides = with_arrived(down_sides, down_two)
    down_three = reduce_step(down_sides, MIXED, 1, 2)
    late, late_sums = run_attend_back(
        place, 1, query, key, value, grad_att, exact, inverse, (grads, *down_two)
    )
    up_one, late = tie(up_one, late)
    up_sides = with_arrived([[parts[0]], [parts[1]]], up_one)
    late_other = swap_cores(late)
    sum_out = run_sum(mixed[0], 1 << 40, (late, *up_one))
    grads_other, sum_out = tie(grads_other, sum_out)
    up_two = reduce_step(up_sides, LINED, 2, 4)
    parts = run_weight(
        place,
        LINED,
        thin,
        [
            (normed, inner_other, 0, grads, grads_other),
            (attended, inner_other, thin, mixed, mixed_other),
        ],
    )
    in_sides = [[parts[0]], [parts[1]]]
    down_three, parts = tie(down_three, parts)
    down_sides = with_arrived(down_sides, down_three)
    in_one = swap_sides(parts[2:], LINED, 3)
    grad_rows, sum_gain, sum_shift = run_inputs_back(
        place, grads, late, rows_in, full_gain, grad_middle, pieces_in, (*parts[:1], *down_three)
    )
    late_other, sum_gain = tie(late_other, sum_gain)
    wide = [jnp.concatenate([sums[row : row + 1], late_sums[row : row + 1]], axis=1) for row in range(3)]
    lines = (
        *wide,
        sum_out,
        sum_gain,
        sum_shift,
        sum_up,
        sum_down,
        sum_gain_two,
        sum_shift_two,
    )
    sizes = (2 * sum_out.shape[1],) + tuple(line.shape[1] for line in lines[2:])
    lines = jnp.concatenate(lines, axis=1)
    lines_other = swap_cores(lines)
    parts = run_weight(
        place,
        LINED,
        thin,
        [(normed, inner_other, 0, late, late_other)],
        (),
        sizes,
        (lines, lines_other),
    )
    up_two, parts = tie(up_two, parts)
    up_sides = with_arrived(up_sides, up_two)
    late_sides = [[parts[0]], [parts[1]]]
    late_one = swap_sides(parts[2:], LINED, 3)
    in_sides = with_arrived(in_sides, in_one)
    late_sides = with_arrived(late_sides, late_one)
    up_sides = with_arrived(up_sides, reduce_step(up_sides, LINED, 1, 2))
    in_sides = with_arrived(in_sides, reduce_step(in_sides, LINED, 2, 4))
    late_sides = with_arrived(late_sides, reduce_step(late_sides, LINED, 2, 4))
    in_sides = with_arrived(in_sides, reduce_step(in_sides, LINED, 1, 2))
    late_sides = with_arrived(late_sides, reduce_step(late_sides, LINED, 1, 2))
    shard_down = side_by_side(reduce_end(down_sides, MIXED), 0, edge)
    shard_up = side_by_side(reduce_end(up_sides, LINED), 0, w_up.shape[1] // 2)
    shards = reduce_end(in_sides, LINED)
    cut = cut // 2
    first = side_by_side(shards, 0, cut)
    shard_out = side_by_side(shards, cut, cut + edge)
    shards = reduce_end(late_sides, LINED)
    second = side_by_side(shards, 0, cut)
    third = edge
    shard_qkv = jnp.concatenate(
        [
            half[:, part * third : (part + 1) * third]
            for part in range(3)
            for half in (first, second)
        ],
        axis=1,
    )
    smalls = [shards[0][row, cut : cut + size // 32] for row, size in enumerate(sizes)]
    grad_bqk, grad_bv, grad_bout, grad_gain, grad_shift, grad_bup, grad_bdown, grad_gain_two, grad_shift_two = smalls
    return (
        result[None],
        grad_rows[None],
        shard_qkv,
        grad_bqk,
        grad_bv,
        shard_out,
        grad_bout,
        grad_gain,
        grad_shift,
        shard_up,
        grad_bup,
        shard_down,
        grad_bdown,
        grad_gain_two,
        grad_shift_two,
    )


def solution(mesh):
    placed = (
        P(("dp", "fsdp"), None, None),
        P(("dp", "fsdp"), None, None),
        P(("dp", "fsdp"), None),
        P(("dp", "fsdp")),
        P(("dp", "fsdp"), None),
        P(("dp", "fsdp")),
        P(("dp", "fsdp"), None),
        P(("dp", "fsdp")),
        P(("dp", "fsdp")),
        P(("dp", "fsdp")),
        P(("dp", "fsdp"), None),
        P(("dp", "fsdp")),
        P(("dp", "fsdp"), None),
        P(("dp", "fsdp")),
        P(("dp", "fsdp")),
        P(("dp", "fsdp")),
    )
    paired = dict(mesh.shape) == {"dp": 2, "fsdp": 16}
    return jax.shard_map(
        paired_body if paired else plain_body,
        mesh=mesh,
        in_specs=placed,
        out_specs=(
            P(("dp", "fsdp"), None, None),
            P(("dp", "fsdp"), None, None),
            P(("dp", "fsdp"), None),
            P(("dp", "fsdp")),
            P(("dp", "fsdp")),
            P(("dp", "fsdp"), None),
            P(("dp", "fsdp")),
            P(("dp", "fsdp")),
            P(("dp", "fsdp")),
            P(("dp", "fsdp"), None),
            P(("dp", "fsdp")),
            P(("dp", "fsdp"), None),
            P(("dp", "fsdp")),
            P(("dp", "fsdp")),
            P(("dp", "fsdp")),
        ),
        check_vma=False,
    )
```

```python
from functools import partial

import jax
import jax.numpy as jnp
from jax import lax
from jax.experimental import pallas as pl
from jax.experimental.pallas import tpu as pltpu
from jax.sharding import PartitionSpec as P

HEADS = 16


norm_eps = 1e-05
denom_eps = 1e-06
gelu_coef = 0.7978845608028654


def layer_norm(values, scale_gain, offset):
    centred = values - jnp.mean(values, axis=-1, keepdims=True)
    spread = jnp.mean(centred * centred, axis=-1, keepdims=True)
    return centred * lax.rsqrt(spread + norm_eps) * scale_gain + offset


def feature_map(values):
    return jnp.where(values > 0, values + 1.0, jnp.exp(jnp.minimum(values, 0.0)))


def gelu_tanh(values):
    return (
        0.5 * values * (1.0 + jnp.tanh(gelu_coef * (values + 0.044715 * values * values * values)))
    )


def contract_rows(left_side, right_side):
    return lax.dot_general(
        left_side, right_side, (((0,), (0,)), ((), ())), preferred_element_type=jnp.float32
    )


def contract_cols(left_side, right_side):
    return lax.dot_general(
        left_side, right_side, (((1,), (1,)), ((), ())), preferred_element_type=jnp.float32
    )


def row_masks(lengths, valid_count, row_length):
    places = jnp.arange(row_length, dtype=jnp.int32)
    bounds = jnp.stack([jnp.sum(lengths[: end + 1]) for end in range(lengths.shape[0])])
    segment = jnp.sum((places[:, None] >= bounds[None, :]).astype(jnp.int32), axis=1)
    allowed = (segment[:, None] == segment[None, :]) & (places[None, :] <= places[:, None])
    keeping = (places < valid_count).astype(jnp.float32)
    return (allowed.astype(jnp.float32), keeping)


def split_heads(matrix):
    return jnp.transpose(matrix.reshape(matrix.shape[0], HEADS, -1), (1, 0, 2))


def join_heads(stacked):
    return jnp.transpose(stacked, (1, 0, 2)).reshape(stacked.shape[1], -1)


def pull_group(first, second, third, fourth, fifth, sixth):
    return (
        lax.all_gather(first, ("dp", "fsdp"), axis=0, tiled=True),
        lax.all_gather(second, ("dp", "fsdp"), axis=0, tiled=True),
        lax.all_gather(third, ("dp", "fsdp"), axis=0, tiled=True),
        lax.all_gather(fourth, ("dp", "fsdp"), axis=0, tiled=True),
        lax.all_gather(fifth, ("dp", "fsdp"), axis=0, tiled=True),
        lax.all_gather(sixth, ("dp", "fsdp"), axis=0, tiled=True),
    )


def push_group(first, second, third, stacked):
    return (
        lax.psum_scatter(first, ("dp", "fsdp"), scatter_dimension=0, tiled=True),
        lax.psum_scatter(second, ("dp", "fsdp"), scatter_dimension=0, tiled=True),
        lax.psum_scatter(third, ("dp", "fsdp"), scatter_dimension=0, tiled=True),
        lax.psum_scatter(stacked, ("dp", "fsdp"), scatter_dimension=1, tiled=True),
    )


def head_forward(allowed, head_item):
    query_head, key_head, value_head = head_item
    scores = contract_cols(query_head, key_head) * allowed
    denominator = jnp.sum(scores, axis=1) + denom_eps
    numerator = jnp.dot(scores.astype(jnp.bfloat16), value_head, preferred_element_type=jnp.float32)
    return (numerator, denominator)


def head_backward(allowed, head_item):
    query_head, key_head, value_head, grad_numer, grad_denom = head_item
    scores = contract_cols(query_head, key_head) * allowed
    grad_prob = contract_cols(grad_numer, value_head)
    grad_value = contract_rows(scores.astype(jnp.bfloat16), grad_numer)
    grad_scores = ((grad_prob + grad_denom[:, None]) * allowed).astype(jnp.bfloat16)
    grad_query = jnp.dot(grad_scores, key_head, preferred_element_type=jnp.float32)
    grad_key = contract_rows(grad_scores, query_head)
    return (grad_query, grad_key, grad_value)


def plain_body(
    inputs,
    cotangent,
    seg_lengths,
    valid_len,
    w_qkv,
    b_qkv,
    w_out,
    b_out,
    gain_one,
    shift_one,
    w_up,
    b_up,
    w_down,
    b_down,
    gain_two,
    shift_two,
):
    token_rows = inputs[0].astype(jnp.float32)
    row_length = token_rows.shape[0]
    model_width = token_rows.shape[1]
    allowed, keeping = row_masks(seg_lengths[0], valid_len[0], row_length)
    full_qkv, full_bqkv, full_out, full_bout, full_gain, full_shift = pull_group(
        w_qkv, b_qkv, w_out, b_out, gain_one, shift_one
    )
    normed, norm_back = jax.vjp(
        layer_norm, token_rows, full_gain.astype(jnp.float32), full_shift.astype(jnp.float32)
    )
    normed_low = normed.astype(jnp.bfloat16)
    projected = jnp.dot(
        normed_low, full_qkv, preferred_element_type=jnp.float32
    ) + full_bqkv.astype(jnp.float32)
    query_feat, query_back = jax.vjp(feature_map, projected[:, :model_width])
    key_feat, key_back = jax.vjp(feature_map, projected[:, model_width : 2 * model_width])
    query_heads = split_heads(query_feat.astype(jnp.bfloat16))
    key_heads = split_heads(key_feat.astype(jnp.bfloat16))
    value_heads = split_heads(projected[:, 2 * model_width :].astype(jnp.bfloat16))
    numerator, denominator = lax.map(
        partial(head_forward, allowed), (query_heads, key_heads, value_heads)
    )
    attended = keeping[None, :, None] * numerator / denominator[:, :, None]
    attended_low = join_heads(attended).astype(jnp.bfloat16)
    middle = (
        token_rows
        + jnp.dot(attended_low, full_out, preferred_element_type=jnp.float32)
        + full_bout.astype(jnp.float32)
    )
    full_up, full_bup, full_down, full_bdown, full_gain_two, full_shift_two = pull_group(
        w_up, b_up, w_down, b_down, gain_two, shift_two
    )
    normed_two, norm_two_back = jax.vjp(
        layer_norm, middle, full_gain_two.astype(jnp.float32), full_shift_two.astype(jnp.float32)
    )
    normed_two_low = normed_two.astype(jnp.bfloat16)
    hidden = jnp.dot(normed_two_low, full_up, preferred_element_type=jnp.float32) + full_bup.astype(
        jnp.float32
    )
    activated, gelu_back = jax.vjp(gelu_tanh, hidden)
    activated_low = activated.astype(jnp.bfloat16)
    result = (
        middle
        + jnp.dot(activated_low, full_down, preferred_element_type=jnp.float32)
        + full_bdown.astype(jnp.float32)
    )
    again_up, again_bup, again_down, again_bdown, again_gain_two, again_shift_two = pull_group(
        w_up, b_up, w_down, b_down, gain_two, shift_two
    )
    grad_top = cotangent[0]
    grad_top_full = grad_top.astype(jnp.float32)
    grad_down = contract_rows(activated_low, grad_top)
    grad_bdown = jnp.sum(grad_top_full, axis=0)
    grad_hidden = gelu_back(contract_cols(grad_top, again_down))[0]
    grad_hidden_low = grad_hidden.astype(jnp.bfloat16)
    grad_bup = jnp.sum(grad_hidden_low.astype(jnp.float32), axis=0)
    grad_up = contract_rows(normed_two_low, grad_hidden_low)
    grad_normed_two = contract_cols(grad_hidden_low, again_up)
    grad_middle_norm, grad_gain_two, grad_shift_two = norm_two_back(grad_normed_two)
    grad_middle = grad_top_full + grad_middle_norm
    shard_up, shard_bup, shard_down, shard_small_two = push_group(
        grad_up, grad_bup, grad_down, jnp.stack([grad_bdown, grad_gain_two, grad_shift_two])
    )
    again_qkv, again_bqkv, again_out, again_bout, again_gain, again_shift = pull_group(
        w_qkv, b_qkv, w_out, b_out, gain_one, shift_one
    )
    grad_mixed = grad_middle.astype(jnp.bfloat16)
    grad_bout = jnp.sum(grad_mixed.astype(jnp.float32), axis=0)
    grad_wout = contract_rows(attended_low, grad_mixed)
    grad_attended = split_heads(contract_cols(grad_mixed, again_out))
    grad_numer = (keeping[None, :, None] * grad_attended / denominator[:, :, None]).astype(
        jnp.bfloat16
    )
    grad_denom = -jnp.sum(grad_attended * attended, axis=2) / denominator
    grad_query_heads, grad_key_heads, grad_value_heads = lax.map(
        partial(head_backward, allowed),
        (query_heads, key_heads, value_heads, grad_numer, grad_denom),
    )
    grad_query = query_back(join_heads(grad_query_heads))[0]
    grad_key = key_back(join_heads(grad_key_heads))[0]
    grad_projected = jnp.concatenate(
        [grad_query, grad_key, join_heads(grad_value_heads)], axis=1
    ).astype(jnp.bfloat16)
    grad_bias_all = jnp.sum(grad_projected.astype(jnp.float32), axis=0)
    grad_bias_qk = grad_bias_all[: 2 * model_width]
    grad_bias_v = grad_bias_all[2 * model_width :]
    grad_qkv = contract_rows(normed_low, grad_projected)
    grad_normed = contract_cols(grad_projected, again_qkv)
    grad_rows_norm, grad_gain_one, grad_shift_one = norm_back(grad_normed)
    grad_inputs = (grad_middle + grad_rows_norm).astype(jnp.bfloat16)
    shard_qkv, shard_bias_qk, shard_wout, shard_small_one = push_group(
        grad_qkv,
        grad_bias_qk,
        grad_wout,
        jnp.stack([grad_bout, grad_bias_v, grad_gain_one, grad_shift_one]),
    )
    return (
        result.astype(jnp.bfloat16)[None],
        grad_inputs[None],
        shard_qkv,
        shard_bias_qk,
        shard_small_one[1],
        shard_wout,
        shard_small_one[0],
        shard_small_one[2],
        shard_small_one[3],
        shard_up,
        shard_bup,
        shard_down,
        shard_small_two[0],
        shard_small_two[1],
        shard_small_two[2],
    )


HALF_LANES = 64
TILE = 512
Z_HIGH, Z_LOW, Y_BIT, X_BIT = 8, 4, 2, 1
MIXED = ((Z_HIGH, X_BIT, Z_LOW, Y_BIT), (Z_HIGH, Y_BIT, Z_LOW, X_BIT))
LINED = ((Z_HIGH, Z_LOW, X_BIT, Y_BIT), (Z_HIGH, Z_LOW, Y_BIT, X_BIT))
SMALL = 128
GROUP = 16
ANY = pl.BlockSpec(memory_space=pl.ANY)
SMEM = pl.BlockSpec(memory_space=pltpu.SMEM)
VMEM = pl.BlockSpec(memory_space=pltpu.VMEM)
MIB = 1 << 20


def swap_chips(block, bit):
    return lax.ppermute(block, "fsdp", [(place, place ^ bit) for place in range(16)])


def swap_cores(block):
    return lax.ppermute(block, "dp", [(0, 1), (1, 0)])


def relative_place(order, slot, last):
    return (
        order[0] * (slot & 1)
        + order[1] * ((slot >> 1) & 1)
        + order[2] * ((slot >> 2) & 1)
        + order[3] * last
    )


def tie(*blocks):
    return lax.optimization_barrier(blocks)


def by_side(shard):
    half = shard.shape[1] // 2
    return shard[None, :, :half], shard[None, :, half:]


def swap_sides(sides, orders, step):
    first, second = orders[0][step], orders[1][step]
    if first == second:
        return (swap_chips(jnp.stack(sides), first),)
    return swap_chips(sides[0], first), swap_chips(sides[1], second)


def sides_of(arrived):
    return (arrived[0][0], arrived[0][1]) if len(arrived) == 1 else arrived


def grown(sides, arrived):
    return tuple(jnp.concatenate([held, more]) for held, more in zip(sides, sides_of(arrived)))


def swap_both(sides):
    return swap_cores(sides[0]), swap_cores(sides[1])


def pieces_of(held, plane, across, core_held, core_across):
    plane = sides_of(plane)
    return tuple(
        block
        for side in range(2)
        for block in (held[side], plane[side], across[side], core_held[side], core_across[side])
    )


def added(parts, start, stop):
    return sum(part[start:stop].astype(jnp.float32) for part in parts)


def reduce_step(sides, orders, step, amount):
    sent = [added(parts, amount, 2 * amount).astype(jnp.bfloat16) for parts in sides]
    return swap_sides(sent, orders, step)


def with_arrived(sides, arrived):
    return [parts + [more] for parts, more in zip(sides, sides_of(arrived))]


def reduce_end(sides, orders):
    sides = with_arrived(sides, reduce_step(sides, orders, 0, 1))
    return [added(parts, 0, 1)[0] for parts in sides]


def side_by_side(sides, start, stop):
    return jnp.concatenate([side[:, start:stop] for side in sides], axis=1)


def far(array):
    return pltpu.with_memory_space_constraint(array, pltpu.HBM)


def call(kernel, outs, scratch, mib, args, in_specs, out_specs, grid=None, flops=0, gates=()):
    inputs, ignored = len(in_specs), len(gates)

    def gated(*refs):
        kernel(*refs[:inputs], *refs[inputs + ignored :])

    extra = {} if grid is None else {"grid": grid}
    near = (SMEM,) if grid else (SMEM, VMEM)
    args = [arg if spec in near else far(arg) for arg, spec in zip(args, in_specs)]
    gates = [far(gate) for gate in gates]
    if isinstance(outs, tuple):
        outs = tuple(
            out if spec in near else pltpu.HBM(out.shape, out.dtype)
            for out, spec in zip(outs, out_specs)
        )
    return pl.pallas_call(
        gated,
        out_shape=outs,
        in_specs=list(in_specs) + [ANY] * ignored,
        out_specs=out_specs,
        scratch_shapes=scratch,
        compiler_params=pltpu.CompilerParams(vmem_limit_bytes=mib * MIB),
        cost_estimate=pl.CostEstimate(flops=flops, bytes_accessed=0, transcendentals=0),
        **extra,
    )(*args, *gates)


def shaped(shape, dtype):
    return jax.ShapeDtypeStruct(shape, dtype)


def dot_nn(left, right):
    return lax.dot_general(left, right, (((1,), (0,)), ((), ())), preferred_element_type=jnp.float32)


def dot_nt(left, right):
    return lax.dot_general(left, right, (((1,), (1,)), ((), ())), preferred_element_type=jnp.float32)


def piece_at(pieces, side, core, last, slot):
    mine = pieces[5 * side : 5 * side + 5]
    if core or last:
        return mine[1 + core * 2 + last], slot
    return mine[slot // 4], slot % 4


def fetch(place, pieces, whole, sems, skip=0):
    rows, half = pieces[0].shape[1], whole.shape[1] // 2
    copies = []
    for side, order in enumerate(LINED):
        for core in range(2):
            for last in range(2):
                for slot in range(8):
                    piece, index = piece_at(pieces, side, core, last, slot)
                    owner = (place[1] ^ core) * 16 + (place[0] ^ relative_place(order, slot, last))
                    start = pl.multiple_of(owner * rows, rows)
                    copies.append(
                        pltpu.make_async_copy(
                            piece.at[index, :, pl.ds(skip, half)],
                            whole.at[pl.ds(start, rows), pl.ds(side * half, half)],
                            sems.at[len(copies)],
                        )
                    )
    for copy in copies:
        copy.start()
    return copies


def wait_side(copies, side):
    half = len(copies) // 2
    wait_all(copies[side * half : (side + 1) * half])


def wait_all(copies):
    for copy in copies:
        copy.wait()


def standardize(block):
    centred = block - jnp.mean(block, axis=1, keepdims=True)
    scale = lax.rsqrt(jnp.mean(centred * centred, axis=1, keepdims=True) + norm_eps)
    return centred * scale, scale


def norm_pull(grad, standard, scale, gain):
    scaled = grad * gain
    return scale * (
        scaled
        - jnp.mean(scaled, axis=1, keepdims=True)
        - standard * jnp.mean(scaled * standard, axis=1, keepdims=True)
    )


def place_kernel(where, lengths, valid, place):
    place[0] = where[0] & 15
    place[1] = where[0] >> 4
    end = lengths[0, 0]
    place[2] = end
    for image in range(1, 3):
        end = end + lengths[0, image]
        place[2 + image] = end
    place[5] = valid[0]


def run_place(where, lengths, valid):
    return call(
        place_kernel,
        shaped((6,), jnp.int32),
        [],
        8,
        (where, lengths, valid),
        in_specs=[SMEM] * 3,
        out_specs=SMEM,
    )


def fetch_small(place, pieces, small, skip, sems):
    copies = []
    for core in range(2):
        for last in range(2):
            for slot in range(8):
                piece, index = piece_at(pieces, 0, core, last, slot)
                far = relative_place(LINED[0], slot, last)
                owner = (place[1] ^ core) * 16 + (place[0] ^ far)
                start = pl.multiple_of(owner * GROUP, GROUP)
                copies.append(
                    pltpu.make_async_copy(
                        piece.at[index, pl.ds(0, GROUP), pl.ds(skip, SMALL)],
                        small.at[pl.ds(start, GROUP), :],
                        sems.at[len(copies)],
                    )
                )
                copies[-1].start()
    return copies


def tables(each):
    total = 32 * each
    column = lax.broadcasted_iota(jnp.int32, (1, total), 1).astype(jnp.float32)
    turn = jnp.floor((column + 0.5) / each)
    lane = lax.broadcasted_iota(jnp.int32, (SMALL, 1), 0).astype(jnp.float32)
    spread = jnp.where(column - turn * each == lane, 1.0, 0.0).astype(jnp.bfloat16)
    owner = lax.broadcasted_iota(jnp.int32, (32, 1), 0).astype(jnp.float32)
    return owner == turn, spread


def unfold(small, each, rows):
    mine, spread = tables(each)
    lines = []
    for row in rows:
        parts = small[pl.ds(row, 32, stride=GROUP), :].astype(jnp.bfloat16)
        parts = jnp.where(mine, dot_nn(parts, spread), 0.0)
        lines.append(jnp.sum(parts, axis=0, keepdims=True))
    return lines


def fold(small, each, vectors):
    mine, spread = tables(each)
    for row, vector in vectors:
        parts = jnp.where(mine, vector, 0.0).astype(jnp.bfloat16)
        small[pl.ds(row, 32, stride=32), :] = dot_nt(parts, spread)


def qkv_kernel(place, rows_in, *rest):
    pieces, (normed, query, key, value), lines, rest = rest[:10], rest[10:14], rest[14:20], rest[20:]
    whole, small, smalls, bias, sems, more = rest
    few = fetch_small(place, pieces, small, 4 * whole.shape[1] // 6, more)
    copies = fetch(place, pieces, whole, sems)
    wait_all(few)
    smalls[...] = small[...].astype(jnp.float32)
    width = rows_in.shape[1]
    (bias[...],) = unfold(smalls, 3 * width // 32, (0,))
    (lines[5][...],) = unfold(smalls, 4 * width // 32, (4,))
    bias_out, gain, shift, bias_down, gain_two, shift_two = unfold(
        smalls, width // 32, (1, 2, 3, 5, 6, 7)
    )
    for goal, line in zip(lines, (gain, bias_out, gain_two, shift_two, bias_down)):
        goal[...] = line
    for part in range(4):
        at = pl.ds(part * 128, 128)
        standard, _ = standardize(rows_in[at, :].astype(jnp.float32))
        normed[at, :] = (standard * gain + shift).astype(jnp.bfloat16)
    for tile in range(6):
        if tile % 3 == 0:
            wait_side(copies, tile // 3)
        cols = pl.ds(tile * TILE, TILE)
        projected = dot_nn(normed[...], whole[:, cols]) + bias[:, cols]
        goal = (query, key, value)[tile // 2]
        if tile < 4:
            projected = feature_map(projected)
        goal[:, pl.ds((tile % 2) * TILE, TILE)] = projected.astype(jnp.bfloat16)


def run_qkv(place, rows_in, pieces, gates=()):
    length, width = rows_in.shape
    narrow = shaped((length, width), jnp.bfloat16)
    line = shaped((1, width), jnp.float32)
    return call(
        qkv_kernel,
        (narrow,) * 4 + (line,) * 5 + (shaped((1, 4 * width), jnp.float32),),
        [
            pltpu.VMEM((width, 3 * width), jnp.bfloat16),
            pltpu.VMEM((32 * GROUP, SMALL), jnp.bfloat16),
            pltpu.VMEM((32 * GROUP, SMALL), jnp.float32),
            pltpu.VMEM((1, 3 * width), jnp.float32),
            pltpu.SemaphoreType.DMA((64,)),
            pltpu.SemaphoreType.DMA((32,)),
        ],
        22,
        (place, rows_in, *pieces),
        in_specs=[SMEM, VMEM] + [ANY] * 10,
        out_specs=(VMEM,) * 10,
        gates=gates,
    )


def image_of(place, positions):
    image = jnp.zeros(positions.shape, jnp.int32)
    for end in range(2, 5):
        image = image + jnp.where(positions >= place[end], 1, 0)
    return image


def allowed_block(place, length, flipped):
    first = lax.broadcasted_iota(jnp.int32, (length, 1), 0)
    second = lax.broadcasted_iota(jnp.int32, (1, length), 1)
    same = image_of(place, first) == image_of(place, second)
    ordered = (first <= second) if flipped else (second <= first)
    return jnp.where(same & ordered, 1.0, 0.0).astype(jnp.float32)


def low_lanes():
    return lax.broadcasted_iota(jnp.int32, (1, 2 * HALF_LANES), 1) < HALF_LANES


def two_heads(block):
    low = jnp.where(low_lanes(), 1.0, 0.0)
    high = (1.0 - low).astype(jnp.bfloat16)
    return jnp.concatenate([block * low.astype(jnp.bfloat16), block * high], axis=0)


def one_pair(stacked):
    half = stacked.shape[0] // 2
    return jnp.where(low_lanes(), stacked[:half], stacked[half:])


def masked(stacked, allowed):
    half = stacked.shape[0] // 2
    return jnp.concatenate(
        [(stacked[:half] * allowed).astype(jnp.bfloat16), (stacked[half:] * allowed).astype(jnp.bfloat16)],
        axis=0,
    )


def keeping_rows(place, start, amount):
    position = lax.broadcasted_iota(jnp.int32, (amount, 1), 0) + start
    return jnp.where(position < place[5], 1.0, 0.0)


def attend_kernel(place, query, key, value, attended, exact, inverse, allowed, wide):
    length, width = query.shape
    step = length // 2

    @pl.when(pl.program_id(0) == 0)
    def _():
        allowed[...] = allowed_block(place, length, False)
        wide[:, width:] = jnp.ones((length, width), jnp.bfloat16)

    wide[:, :width] = value[...]
    for part in range(2):
        rows, seen = pl.ds(part * step, step), (part + 1) * step
        scores = dot_nt(two_heads(query[rows, :]), key[:seen, :])
        total = dot_nn(masked(scores, allowed[rows, :seen]), wide[:seen, :])
        over = 1.0 / (one_pair(total[:, width:]) + denom_eps)
        inverse[rows, :] = over
        mixed = keeping_rows(place, part * step, step) * one_pair(total[:, :width]) * over
        exact[rows, :] = mixed
        attended[rows, :] = mixed.astype(jnp.bfloat16)


def run_attend(place, query, key, value, gates=()):
    length, width = query.shape
    pair = pl.BlockSpec((length, 2 * HALF_LANES), lambda p: (0, p))
    return call(
        attend_kernel,
        (
            shaped((length, width), jnp.bfloat16),
            shaped((length, width), jnp.float32),
            shaped((length, width), jnp.float32),
        ),
        [
            pltpu.VMEM((length, length), jnp.float32),
            pltpu.VMEM((length, 4 * HALF_LANES), jnp.bfloat16),
        ],
        16,
        (place, query, key, value),
        grid=(width // (2 * HALF_LANES),),
        in_specs=[SMEM] + [pair] * 3,
        out_specs=(pair,) * 3,
        gates=gates,
    )


def attend_back_kernel(
    place, query, key, value, grad_att, exact, inverse, *rest
):
    stacked, sums, (allowed, flipped, left, wide) = rest[0], rest[1], rest[2:]
    length, width = query.shape
    step = length // 2

    @pl.when(pl.program_id(0) == 0)
    def _():
        allowed[...] = allowed_block(place, length, False)
        flipped[...] = allowed_block(place, length, True)
        wide[:, width:] = jnp.ones((length, width), jnp.bfloat16)

    wide[:, :width] = value[...]
    over = grad_att[...] * inverse[...]
    lane = lax.broadcasted_iota(jnp.int32, (1, width), 1)
    terms, low = over * exact[...], lane < HALF_LANES
    first = jnp.sum(jnp.where(low, terms, 0.0), axis=1, keepdims=True)
    second = jnp.sum(jnp.where(low, 0.0, terms), axis=1, keepdims=True)
    spread = -jnp.where(low, first, second)
    high = spread.astype(jnp.bfloat16).astype(jnp.float32)
    within = lane & (HALF_LANES - 1)
    spread = jnp.where(within == 0, high, jnp.where(within == 1, spread - high, 0.0))
    numer = (keeping_rows(place, 0, length) * over).astype(jnp.bfloat16)
    for head in range(2):
        here = jnp.where(low, 1.0 - head, 1.0 * head)
        at = pl.ds(head * length, length)
        left[at, :width] = numer * here.astype(jnp.bfloat16)
        left[at, width:] = (spread * here).astype(jnp.bfloat16)
    for part in range(2):
        rows, seen = pl.ds(part * step, step), (part + 1) * step
        start = part * step
        later = pl.ds(start, length - start)
        both = jnp.concatenate([left[rows, :], left[pl.ds(length + start, step), :]], axis=0)
        grad_scores = masked(dot_nt(both, wide[:seen, :]), allowed[rows, :seen])
        grad_query = one_pair(dot_nn(grad_scores, key[:seen, :]))
        full = left[later, :] + left[pl.ds(length + start, length - start), :]
        scores = masked(dot_nt(two_heads(key[rows, :]), query[later, :]), flipped[rows, later])
        grad_value = one_pair(dot_nn(scores, full[:, :width]))
        ones = jnp.concatenate([two_heads(value[rows, :]), two_heads(wide[rows, width:])], axis=1)
        grad_scores = masked(dot_nt(ones, full), flipped[rows, later])
        grad_key = one_pair(dot_nn(grad_scores, query[later, :]))
        grads = (
            grad_query * jnp.minimum(query[rows, :].astype(jnp.float32), 1.0),
            grad_key * jnp.minimum(key[rows, :].astype(jnp.float32), 1.0),
            grad_value,
        )
        for index, grad in enumerate(grads):
            low_grad, line = grad.astype(jnp.bfloat16), pl.ds(index, 1)
            stacked[index, rows, :] = low_grad
            extra = jnp.sum(low_grad.astype(jnp.float32), axis=0, keepdims=True)
            sums[line, :] = extra if part == 0 else sums[line, :] + extra


def run_attend_back(place, first, query, key, value, grad_att, exact, inverse, gates=()):
    length, width = query.shape
    half = width // 2
    start = first * half // (2 * HALF_LANES)
    pair = pl.BlockSpec((length, 2 * HALF_LANES), lambda p: (0, p + start))
    stack = pl.BlockSpec((3, length, 2 * HALF_LANES), lambda p: (0, 0, p))
    lines = pl.BlockSpec((3, 2 * HALF_LANES), lambda p: (0, p))
    return call(
        attend_back_kernel,
        (shaped((3, length, half), jnp.bfloat16), shaped((3, half), jnp.float32)),
        [
            pltpu.VMEM((length, length), jnp.float32),
            pltpu.VMEM((length, length), jnp.float32),
            pltpu.VMEM((2 * length, 4 * HALF_LANES), jnp.bfloat16),
            pltpu.VMEM((length, 4 * HALF_LANES), jnp.bfloat16),
        ],
        20,
        (place, query, key, value, grad_att, exact, inverse),
        grid=(half // (2 * HALF_LANES),),
        in_specs=[SMEM] + [pair] * 6,
        out_specs=(stack, lines),
        gates=gates,
    )


def hand_over(place, sources, goal, sems):
    copies, at = [], 0
    for source in sources:
        half = source.shape[1] // 2
        start = pl.multiple_of((1 - place[1]) * half, half)
        copies.append(
            pltpu.make_async_copy(
                source.at[:, pl.ds(start, half)], goal.at[:, pl.ds(at, half)], sems.at[len(copies)]
            )
        )
        copies[-1].start()
        at += half
    return copies


def out_kernel(place, rows_in, early, attended, bias, gain, shift, *rest):
    pieces, (middle, normed, handed, whole, sems, more) = rest[:10], rest[10:]
    copies = fetch(place, pieces, whole, sems, 3 * whole.shape[1] // 2)
    handing = hand_over(place, (early, attended), handed, more)
    for side in range(2):
        wait_side(copies, side)
        cols = pl.ds(side * TILE, TILE)
        middle[:, cols] = (
            rows_in[:, cols].astype(jnp.float32) + dot_nn(attended[...], whole[:, cols]) + bias[:, cols]
        )
    for part in range(4):
        at = pl.ds(part * 128, 128)
        standard, _ = standardize(middle[at, :])
        normed[at, :] = (standard * gain[...] + shift[...]).astype(jnp.bfloat16)
    wait_all(handing)


def run_out(place, rows_in, early, attended, bias, gain, shift, pieces, gates=()):
    length, width = rows_in.shape
    narrow = shaped((length, width), jnp.bfloat16)
    return call(
        out_kernel,
        (shaped((length, width), jnp.float32), narrow, narrow),
        [
            pltpu.VMEM((width, width), jnp.bfloat16),
            pltpu.SemaphoreType.DMA((64,)),
            pltpu.SemaphoreType.DMA((2,)),
        ],
        24,
        (place, rows_in, early, attended, bias, gain, shift, *pieces),
        in_specs=[SMEM] + [VMEM] * 6 + [ANY] * 10,
        out_specs=(VMEM, VMEM, ANY),
        gates=gates,
    )


def bend_tile(hidden, activated, slope):
    square = hidden * hidden
    rate = gelu_coef + (gelu_coef * 0.044715) * square
    bend = jnp.tanh(hidden * rate)
    share = 0.5 + 0.5 * bend
    activated[...] = (hidden * share).astype(jnp.bfloat16)
    rate = gelu_coef + (3.0 * gelu_coef * 0.044715) * square
    slope[...] = (share + (0.5 * hidden) * (1.0 - bend * bend) * rate).astype(jnp.bfloat16)


def up_kernel(place, normed, bias, *rest):
    pieces, (activated, slope, handed, whole, hidden, sems, more) = rest[:10], rest[10:]
    copies = fetch(place, pieces, whole, sems)
    tiles = whole.shape[1] // TILE

    def columns(tile):
        return pl.ds(tile * TILE, TILE)

    for tile in range(tiles + 1):
        if tile % (tiles // 2) == 0 and tile < tiles:
            wait_side(copies, tile // (tiles // 2))
        if tile < tiles:
            cols = columns(tile)
            hidden[tile % 2] = dot_nn(normed[...], whole[:, cols]) + bias[:, cols]
        if tile > 0:
            cols = columns(tile - 1)
            bend_tile(hidden[(tile - 1) % 2], activated.at[:, cols], slope.at[:, cols])

    wait_all(hand_over(place, (normed, activated), handed, more))


def run_up(place, normed, bias, pieces, gates=()):
    length, width = normed.shape
    wide = bias.shape[1]
    return call(
        up_kernel,
        (shaped((length, wide), jnp.bfloat16),) * 2
        + (shaped((length, (width + wide) // 2), jnp.bfloat16),),
        [
            pltpu.VMEM((width, wide), jnp.bfloat16),
            pltpu.VMEM((2, length, TILE), jnp.float32),
            pltpu.SemaphoreType.DMA((64,)),
            pltpu.SemaphoreType.DMA((2,)),
        ],
        34,
        (place, normed, bias, *pieces),
        in_specs=[SMEM] + [VMEM] * 2 + [ANY] * 10,
        out_specs=(VMEM, VMEM, ANY),
        gates=gates,
    )


def sum_kernel(block, total):
    total[...] = jnp.sum(block[...].astype(jnp.float32), axis=0, keepdims=True)


def run_sum(block, cover, gates=()):
    return call(
        sum_kernel,
        shaped((1, block.shape[1]), jnp.float32),
        [],
        8,
        (block,),
        in_specs=[VMEM],
        out_specs=VMEM,
        flops=cover,
        gates=gates,
    )


def down_kernel(place, activated, slope, grad_top, middle, bias, *rest):
    pieces, (result, grad_hidden, sum_up, whole, sems) = rest[:10], rest[10:]
    copies = fetch(place, pieces, whole, sems)
    wait_all(copies)
    for tile in range(4):
        cols = pl.ds(tile * 256, 256)
        result[:, cols] = (
            middle[:, cols] + bias[:, cols] + dot_nn(activated[...], whole[:, cols])
        ).astype(jnp.bfloat16)
        for half in range(2):
            cols = pl.ds((2 * tile + half) * TILE, TILE)
            grad = dot_nt(grad_top[...], whole[cols, :]) * slope[:, cols].astype(jnp.float32)
            low = grad.astype(jnp.bfloat16)
            grad_hidden[:, cols] = low
            sum_up[:, cols] = jnp.sum(low.astype(jnp.float32), axis=0, keepdims=True)


def run_down(place, activated, slope, grad_top, middle, bias, pieces, gates=()):
    length, width = middle.shape
    wide = activated.shape[1]
    return call(
        down_kernel,
        (
            shaped((length, width), jnp.bfloat16),
            shaped((length, wide), jnp.bfloat16),
            shaped((1, wide), jnp.float32),
        ),
        [
            pltpu.VMEM((wide, width), jnp.bfloat16),
            pltpu.SemaphoreType.DMA((64,)),
        ],
        40,
        (place, activated, slope, grad_top, middle, bias, *pieces),
        in_specs=[SMEM] + [VMEM] * 5 + [ANY] * 10,
        out_specs=(VMEM,) * 3,
        flops=64 * length * width * wide,
        gates=gates,
    )


def middle_back_kernel(place, grad_hidden, middle, grad_top, gain, *rest):
    pieces_up, pieces_in, rest = rest[:10], rest[10:20], rest[20:]
    grad_middle, mixed, grad_att, sum_gain, sum_shift, whole, outer, total, sems, more = rest
    copies = fetch(place, pieces_up, whole, sems)
    second = fetch(place, pieces_in, outer, more, 3 * outer.shape[1] // 2)
    step = 2 * TILE
    for tile in range(whole.shape[1] // step):
        if tile % 2 == 0:
            wait_side(copies, tile // 2)
        cols = pl.ds(tile * step, step)
        block = dot_nt(grad_hidden[:, cols], whole[:, cols])
        total[...] = block if tile == 0 else total[...] + block

    for part in range(4):
        at = pl.ds(part * 128, 128)
        grad = total[at, :]
        standard, scale = standardize(middle[at, :])
        back = grad_top[at, :].astype(jnp.float32) + norm_pull(grad, standard, scale, gain[...])
        grad_middle[at, :] = back
        low = back.astype(jnp.bfloat16)
        mixed[at, :] = low
        for goal, added in ((sum_gain, grad * standard), (sum_shift, grad)):
            added = jnp.sum(added, axis=0, keepdims=True)
            goal[...] = added if part == 0 else goal[...] + added
    wait_all(second)
    for part in range(2):
        cols = pl.ds(part * TILE, TILE)
        grad_att[:, cols] = dot_nt(mixed[...], outer[cols, :])


def run_middle_back(place, grad_hidden, middle, grad_top, gain, pieces_up, pieces_in, gates=()):
    length, width = middle.shape
    wide = grad_hidden.shape[1]
    full, line = shaped((length, width), jnp.float32), shaped((1, width), jnp.float32)
    return call(
        middle_back_kernel,
        (full, shaped((length, width), jnp.bfloat16), full, line, line),
        [
            pltpu.VMEM((width, wide), jnp.bfloat16),
            pltpu.VMEM((width, width), jnp.bfloat16),
            pltpu.VMEM((length, width), jnp.float32),
            pltpu.SemaphoreType.DMA((64,)),
            pltpu.SemaphoreType.DMA((64,)),
        ],
        40,
        (place, grad_hidden, middle, grad_top, gain, *pieces_up, *pieces_in),
        in_specs=[SMEM] + [VMEM] * 4 + [ANY] * 20,
        out_specs=(VMEM,) * 5,
        gates=gates,
    )


def inputs_back_kernel(place, early, late, rows_in, gain, grad_middle, mixed, *rest):
    (sums, late_sums, *ready), pieces, rest = rest[:6], rest[6:16], rest[16:]
    grad_rows, lines, whole, total, sems = rest
    copies = fetch(place, pieces, whole, sems)
    width = rows_in.shape[1]
    for tile in range(6):
        if tile % 3 == 0:
            wait_side(copies, tile // 3)
        grads = (early, late)[tile % 2]
        block = dot_nt(grads[tile // 2], whole[:, pl.ds(tile * TILE, TILE)])
        total[...] = block if tile == 0 else total[...] + block
    for part in range(4):
        at = pl.ds(part * 128, 128)
        grad = total[at, :]
        standard, scale = standardize(rows_in[at, :].astype(jnp.float32))
        back = grad_middle[at, :] + norm_pull(grad, standard, scale, gain[...])
        grad_rows[at, :] = back.astype(jnp.bfloat16)
        extras = (mixed[at, :].astype(jnp.float32), grad * standard, grad)
        for index, extra in enumerate(extras):
            goal = lines.at[:, pl.ds((3 + index) * width, width)]
            extra = jnp.sum(extra, axis=0, keepdims=True)
            goal[...] = extra if part == 0 else goal[...] + extra
    half = width // 2
    for row in range(3):
        for index, source in enumerate((sums, late_sums)):
            lines[:, pl.ds(row * width + index * half, half)] = source[pl.ds(row, 1), :]
    at = 6 * width
    for source in ready:
        lines[:, pl.ds(at, source.shape[1])] = source[...]
        at += source.shape[1]


def run_inputs_back(
    place, early, late, rows_in, gain, grad_middle, mixed, ready, pieces, gates=()
):
    length, width = rows_in.shape
    total = 6 * width + sum(line.shape[1] for line in ready[2:])
    return call(
        inputs_back_kernel,
        (shaped((length, width), jnp.bfloat16), shaped((1, total), jnp.float32)),
        [
            pltpu.VMEM((width, 3 * width), jnp.bfloat16),
            pltpu.VMEM((length, width), jnp.float32),
            pltpu.SemaphoreType.DMA((64,)),
        ],
        24,
        (place, early, late, rows_in, gain, grad_middle, mixed, *ready, *pieces),
        in_specs=[SMEM] + [VMEM] * 12 + [ANY] * 10,
        out_specs=(VMEM,) * 2,
        flops=1 << 40,
        gates=gates,
    )


def weight_kernel(orders, skips, sizes, place, *rest):
    groups = len(skips)
    if sizes:
        mine, other_lines, rest = rest[4 * groups], rest[4 * groups + 1], rest[: 4 * groups] + rest[4 * groups + 2 :]
    inputs, outs, rest = rest[: 4 * groups], rest[4 * groups : 4 * groups + 4], rest[4 * groups + 4 :]
    wholes, (turned, sems), rest = rest[:groups], rest[groups : groups + 2], rest[groups + 2 :]
    length = inputs[0].shape[0]
    for group, (skip, whole) in enumerate(zip(skips, wholes)):
        left_own, left_other, own, other = inputs[4 * group : 4 * group + 4]
        height, count, each = whole.shape[0], own.shape[0], own.shape[2]
        start = pl.multiple_of(place[1] * height, height)

        @pl.loop(0, height // 256)
        def _(tile):
            low = pl.multiple_of(tile * 256, 256)
            turned[:, :length] = left_own[:, pl.ds(start + low, 256)].T
            turned[:, length:] = left_other[:, pl.ds(skip + low, 256)].T
            for index in range(count):
                for step in range(each // TILE):
                    cols = pl.ds(step * TILE, TILE)
                    block = dot_nn(turned[:, :length], own[index, :, cols])
                    block += dot_nn(turned[:, length:], other[index, :, cols])
                    goal = pl.ds(index * each + step * TILE, TILE)
                    whole[pl.ds(low, 256), goal] = block.astype(jnp.bfloat16)

    rows, at, copies = outs[0].shape[1], 0, []
    for whole in wholes:
        half = whole.shape[1] // 2
        for side, order in enumerate(orders):
            for last in range(2):
                for slot in range(8):
                    owner = place[0] ^ relative_place(order, slot, last)
                    start = pl.multiple_of(owner * rows, rows)
                    goal = outs[last * 2 + side].at[slot]
                    copies.append(
                        pltpu.make_async_copy(
                            whole.at[pl.ds(start, rows), pl.ds(side * half, half)],
                            goal.at[:, pl.ds(at, half)],
                            sems.at[len(copies)],
                        )
                    )
                    copies[-1].start()
        at += half
    if sizes:
        wide_small, small, more = rest
        wide_small[...] = jnp.zeros_like(wide_small)
        start, by_size = 0, {}
        for row, size in enumerate(sizes):
            line = mine[:, start : start + size] + other_lines[:, start : start + size]
            by_size.setdefault(size, []).append((row, line))
            start += size
        for size, vectors in by_size.items():
            fold(wide_small, size // 32, vectors)
        small[...] = wide_small[...].astype(jnp.bfloat16)
        for last in range(2):
            for slot in range(8):
                chip = place[0] ^ relative_place(orders[0], slot, last)
                start = pl.multiple_of((place[1] * 16 + chip) * 32, 32)
                copies.append(
                    pltpu.make_async_copy(
                        small.at[pl.ds(start, 32), :],
                        outs[last * 2].at[slot, :, pl.ds(at, SMALL)],
                        more.at[last * 8 + slot],
                    )
                )
                copies[-1].start()
    wait_all(copies)


def run_weight(place, orders, height, groups, gates=(), sizes=(), lines=()):
    length = groups[0][0].shape[0]
    totals = [own.shape[0] * own.shape[2] for _, _, _, own, _ in groups]
    half = sum(totals) // 2
    part = shaped((8, height // 16, half), jnp.bfloat16)
    first = shaped((8, height // 16, half + (SMALL if sizes else 0)), jnp.bfloat16)
    extra = [
        pltpu.VMEM((32 * 32, SMALL), jnp.float32),
        pltpu.VMEM((32 * 32, SMALL), jnp.bfloat16),
        pltpu.SemaphoreType.DMA((16,)),
    ]
    return call(
        partial(weight_kernel, orders, tuple(group[2] for group in groups), sizes),
        (first,) * 4,
        [pltpu.VMEM((height, total), jnp.bfloat16) for total in totals]
        + [
            pltpu.VMEM((256, 2 * length), jnp.bfloat16),
            pltpu.SemaphoreType.DMA((32 * len(groups),)),
        ]
        + (extra if sizes else []),
        36,
        (place, *(array for group in groups for array in group[:2] + group[3:]), *lines),
        in_specs=[SMEM] + [VMEM] * (4 * len(groups) + len(lines)),
        out_specs=(ANY,) * 4,
        gates=gates,
    )


def paired_body(
    inputs,
    cotangent,
    seg_lengths,
    valid_len,
    w_qkv,
    b_qkv,
    w_out,
    b_out,
    gain_one,
    shift_one,
    w_up,
    b_up,
    w_down,
    b_down,
    gain_two,
    shift_two,
):
    where = (lax.axis_index("dp") * 16 + lax.axis_index("fsdp")).astype(jnp.int32)[None]
    rows_in, grad_top = inputs[0], cotangent[0]
    vectors = (b_qkv, b_out, gain_one, shift_one, b_up, b_down, gain_two, shift_two)
    cut = w_qkv.shape[1] // 2
    edge = w_out.shape[1] // 2
    held_in = (
        jnp.concatenate([w_qkv[:, :cut], w_out[:, :edge]], axis=1)[None],
        jnp.concatenate([w_qkv[:, cut:], w_out[:, edge:]], axis=1)[None],
    )
    small = jnp.stack([jnp.pad(vector, (0, SMALL - vector.shape[0])) for vector in vectors])
    small = jnp.pad(small, ((0, w_out.shape[0] - small.shape[0]), (0, 0)))[None]
    small_far = swap_chips(small, Z_HIGH)
    place = run_place(where, seg_lengths, valid_len)
    place, small_far = tie(place, small_far)
    small = jnp.concatenate([small, small_far])
    held_up, held_down = by_side(w_up), by_side(w_down)
    top = grad_top[None]
    held_in = grown(held_in, swap_sides(held_in, LINED, 0))
    held_in = (
        jnp.concatenate([held_in[0], small], axis=2),
        jnp.concatenate([held_in[1], jnp.zeros_like(small)], axis=2),
    )
    held_in = grown(held_in, swap_sides(held_in, LINED, 1))
    held_in, held_up = tie(held_in, held_up)
    held_up = grown(held_up, swap_sides(held_up, LINED, 0))
    held_up, held_down = tie(held_up, held_down)
    plane_in = swap_sides(held_in, LINED, 2)
    full_in = grown(held_in, plane_in)
    across_in = swap_sides(full_in, LINED, 3)
    core_in = swap_both(full_in)
    held_up = grown(held_up, swap_sides(held_up, LINED, 1))
    start_down = swap_sides(held_down, LINED, 0)
    across_in, start_down = tie(across_in, start_down)
    pieces_in = pieces_of(held_in, plane_in, across_in, core_in, swap_both(across_in))
    plane_up = swap_sides(held_up, LINED, 2)
    held_down = grown(held_down, start_down)
    line_down = swap_sides(held_down, LINED, 1)
    top_other = swap_cores(top)

    normed, query, key, value, *lines = run_qkv(
        place, rows_in, pieces_in, (*held_up, *held_down, top_other)
    )
    full_gain, full_bout, full_gain_two, full_shift_two, full_bdown, full_bup = lines
    plane_up, line_down, normed = tie(plane_up, line_down, normed)
    full_up = grown(held_up, plane_up)
    across_up = swap_sides(full_up, LINED, 3)
    core_up = swap_both(full_up)
    held_down = grown(held_down, line_down)
    attended, exact, inverse = run_attend(place, query, key, value, (*plane_up, *held_down))
    core_up, held_down, attended = tie(core_up, held_down, attended)
    plane_down = swap_sides(held_down, LINED, 2)
    middle, normed_two, inner_half = run_out(
        place,
        rows_in,
        normed,
        attended,
        full_bout,
        full_gain_two,
        full_shift_two,
        pieces_in,
    )
    inner_other = swap_cores(inner_half)
    across_up, plane_down, normed_two = tie(across_up, plane_down, normed_two)
    pieces_up = pieces_of(held_up, plane_up, across_up, core_up, swap_both(across_up))
    full_down = grown(held_down, plane_down)
    across_down = swap_sides(full_down, LINED, 3)
    core_down = swap_both(full_down)
    activated, slope, outer_half = run_up(
        place, normed_two, full_bup, pieces_up, (*plane_down, inner_other)
    )
    outer_other = swap_cores(outer_half)
    sum_down = run_sum(grad_top, 1 << 40, (outer_half,))
    thin = normed_two.shape[1] // 2
    parts = run_weight(
        place,
        LINED,
        activated.shape[1] // 2,
        [(activated, outer_other, thin, top, top_other)],
        (*core_down, sum_down),
    )
    across_down, parts = tie(across_down, parts)
    down_one = swap_sides(parts[2:], LINED, 3)
    pieces_down = pieces_of(held_down, plane_down, across_down, core_down, swap_both(across_down))
    result, grad_hidden, sum_up = run_down(
        place, activated, slope, grad_top, middle, full_bdown, pieces_down, parts[2:]
    )
    down_one, grad_hidden = tie(down_one, grad_hidden)
    hidden_other = swap_cores(grad_hidden[None])
    down_sides = with_arrived([[parts[0]], [parts[1]]], down_one)
    down_two = reduce_step(down_sides, LINED, 2, 4)
    grad_middle, mixed, grad_att, sum_gain_two, sum_shift_two = run_middle_back(
        place, grad_hidden, middle, grad_top, full_gain_two, pieces_up, pieces_in, down_one
    )
    mixed = mixed[None]
    down_two, mixed = tie(down_two, mixed)
    hidden_other, mixed = tie(hidden_other, mixed)
    mixed_other = swap_cores(mixed)
    down_sides = with_arrived(down_sides, down_two)
    down_three = reduce_step(down_sides, LINED, 1, 2)
    parts = run_weight(
        place, LINED, thin, [(normed_two, outer_other, 0, grad_hidden[None], hidden_other)], down_two
    )
    mixed_other, parts = tie(mixed_other, parts)
    up_one = swap_sides(parts[2:], LINED, 3)
    grads, sums = run_attend_back(
        place, 0, query, key, value, grad_att, exact, inverse, parts[2:]
    )
    down_three, grads = tie(down_three, grads)
    down_sides = with_arrived(down_sides, down_three)
    down_four = reduce_step(down_sides, LINED, 0, 1)
    grads_other = swap_cores(grads)
    late, late_sums = run_attend_back(
        place, 1, query, key, value, grad_att, exact, inverse, (grads,)
    )
    up_one, down_four, late = tie(up_one, down_four, late)
    down_sides = with_arrived(down_sides, down_four)
    up_sides = with_arrived([[parts[0]], [parts[1]]], up_one)
    late_other = swap_cores(late)
    up_two = reduce_step(up_sides, LINED, 2, 4)
    grad_rows, lines = run_inputs_back(
        place,
        grads,
        late,
        rows_in,
        full_gain,
        grad_middle,
        mixed[0],
        (sums, late_sums, sum_up, sum_down, sum_gain_two, sum_shift_two),
        pieces_in,
        up_one,
    )
    up_two, grads_other, late_other, lines = tie(up_two, grads_other, late_other, lines)
    up_sides = with_arrived(up_sides, up_two)
    up_three = reduce_step(up_sides, LINED, 1, 2)
    lines_other = swap_cores(lines)
    parts = run_weight(
        place,
        MIXED,
        thin,
        [
            (normed, inner_other, 0, grads, grads_other),
            (attended, inner_other, thin, mixed, mixed_other),
        ],
    )
    lines_other, parts = tie(lines_other, parts)
    in_sides = [[parts[0]], [parts[1]]]
    in_one = swap_sides(parts[2:], MIXED, 3)
    narrow, wide = mixed.shape[2], sum_up.shape[1]
    sizes = (2 * narrow, narrow, narrow, narrow, narrow, wide, narrow, narrow, narrow)
    parts = run_weight(
        place,
        LINED,
        thin,
        [(normed, inner_other, 0, late, late_other)],
        parts[:1],
        sizes,
        (lines, lines_other),
    )
    up_three, parts = tie(up_three, parts)
    up_sides = with_arrived(up_sides, up_three)
    up_four = reduce_step(up_sides, LINED, 0, 1)
    late_sides = [[parts[0]], [parts[1]]]
    late_one = swap_sides(parts[2:], LINED, 3)
    in_sides = with_arrived(in_sides, in_one)
    late_sides = with_arrived(late_sides, late_one)
    in_sides = with_arrived(in_sides, reduce_step(in_sides, MIXED, 2, 4))
    late_sides = with_arrived(late_sides, reduce_step(late_sides, LINED, 2, 4))
    up_sides = with_arrived(up_sides, up_four)
    in_sides = with_arrived(in_sides, reduce_step(in_sides, MIXED, 1, 2))
    late_sides = with_arrived(late_sides, reduce_step(late_sides, LINED, 1, 2))
    shard_down = side_by_side([added(parts, 0, 1)[0] for parts in down_sides], 0, edge)
    shard_up = side_by_side([added(parts, 0, 1)[0] for parts in up_sides], 0, w_up.shape[1] // 2)
    shards = reduce_end(in_sides, MIXED)
    cut = cut // 2
    first = side_by_side(shards, 0, cut)
    shard_out = side_by_side(shards, cut, cut + edge)
    shards = reduce_end(late_sides, LINED)
    second = side_by_side(shards, 0, cut)
    third = edge
    shard_qkv = jnp.concatenate(
        [
            half[:, part * third : (part + 1) * third]
            for part in range(3)
            for half in (first, second)
        ],
        axis=1,
    )
    smalls = [shards[0][row, cut : cut + size // 32] for row, size in enumerate(sizes)]
    grad_bqk, grad_bv, grad_bout, grad_gain, grad_shift, grad_bup, grad_bdown, grad_gain_two, grad_shift_two = smalls
    return (
        result[None],
        grad_rows[None],
        shard_qkv,
        grad_bqk,
        grad_bv,
        shard_out,
        grad_bout,
        grad_gain,
        grad_shift,
        shard_up,
        grad_bup,
        shard_down,
        grad_bdown,
        grad_gain_two,
        grad_shift_two,
    )


def solution(mesh):
    placed = (
        P(("dp", "fsdp"), None, None),
        P(("dp", "fsdp"), None, None),
        P(("dp", "fsdp"), None),
        P(("dp", "fsdp")),
        P(("dp", "fsdp"), None),
        P(("dp", "fsdp")),
        P(("dp", "fsdp"), None),
        P(("dp", "fsdp")),
        P(("dp", "fsdp")),
        P(("dp", "fsdp")),
        P(("dp", "fsdp"), None),
        P(("dp", "fsdp")),
        P(("dp", "fsdp"), None),
        P(("dp", "fsdp")),
        P(("dp", "fsdp")),
        P(("dp", "fsdp")),
    )
    paired = dict(mesh.shape) == {"dp": 2, "fsdp": 16}
    return jax.shard_map(
        paired_body if paired else plain_body,
        mesh=mesh,
        in_specs=placed,
        out_specs=(
            P(("dp", "fsdp"), None, None),
            P(("dp", "fsdp"), None, None),
            P(("dp", "fsdp"), None),
            P(("dp", "fsdp")),
            P(("dp", "fsdp")),
            P(("dp", "fsdp"), None),
            P(("dp", "fsdp")),
            P(("dp", "fsdp")),
            P(("dp", "fsdp")),
            P(("dp", "fsdp"), None),
            P(("dp", "fsdp")),
            P(("dp", "fsdp"), None),
            P(("dp", "fsdp")),
            P(("dp", "fsdp")),
            P(("dp", "fsdp")),
        ),
        check_vma=False,
    )
```

```python
from functools import partial

import jax
import jax.numpy as jnp
from jax import lax
from jax.experimental import pallas as pl
from jax.experimental.pallas import tpu as pltpu
from jax.sharding import PartitionSpec as P

HEADS = 16


norm_eps = 1e-05
denom_eps = 1e-06
gelu_coef = 0.7978845608028654


def layer_norm(values, scale_gain, offset):
    centred = values - jnp.mean(values, axis=-1, keepdims=True)
    spread = jnp.mean(centred * centred, axis=-1, keepdims=True)
    return centred * lax.rsqrt(spread + norm_eps) * scale_gain + offset


def feature_map(values):
    return jnp.where(values > 0, values + 1.0, jnp.exp(jnp.minimum(values, 0.0)))


def gelu_tanh(values):
    return (
        0.5 * values * (1.0 + jnp.tanh(gelu_coef * (values + 0.044715 * values * values * values)))
    )


def contract_rows(left_side, right_side):
    return lax.dot_general(
        left_side, right_side, (((0,), (0,)), ((), ())), preferred_element_type=jnp.float32
    )


def contract_cols(left_side, right_side):
    return lax.dot_general(
        left_side, right_side, (((1,), (1,)), ((), ())), preferred_element_type=jnp.float32
    )


def row_masks(lengths, valid_count, row_length):
    places = jnp.arange(row_length, dtype=jnp.int32)
    bounds = jnp.stack([jnp.sum(lengths[: end + 1]) for end in range(lengths.shape[0])])
    segment = jnp.sum((places[:, None] >= bounds[None, :]).astype(jnp.int32), axis=1)
    allowed = (segment[:, None] == segment[None, :]) & (places[None, :] <= places[:, None])
    keeping = (places < valid_count).astype(jnp.float32)
    return (allowed.astype(jnp.float32), keeping)


def split_heads(matrix):
    return jnp.transpose(matrix.reshape(matrix.shape[0], HEADS, -1), (1, 0, 2))


def join_heads(stacked):
    return jnp.transpose(stacked, (1, 0, 2)).reshape(stacked.shape[1], -1)


def pull_group(first, second, third, fourth, fifth, sixth):
    return (
        lax.all_gather(first, ("dp", "fsdp"), axis=0, tiled=True),
        lax.all_gather(second, ("dp", "fsdp"), axis=0, tiled=True),
        lax.all_gather(third, ("dp", "fsdp"), axis=0, tiled=True),
        lax.all_gather(fourth, ("dp", "fsdp"), axis=0, tiled=True),
        lax.all_gather(fifth, ("dp", "fsdp"), axis=0, tiled=True),
        lax.all_gather(sixth, ("dp", "fsdp"), axis=0, tiled=True),
    )


def push_group(first, second, third, stacked):
    return (
        lax.psum_scatter(first, ("dp", "fsdp"), scatter_dimension=0, tiled=True),
        lax.psum_scatter(second, ("dp", "fsdp"), scatter_dimension=0, tiled=True),
        lax.psum_scatter(third, ("dp", "fsdp"), scatter_dimension=0, tiled=True),
        lax.psum_scatter(stacked, ("dp", "fsdp"), scatter_dimension=1, tiled=True),
    )


def head_forward(allowed, head_item):
    query_head, key_head, value_head = head_item
    scores = contract_cols(query_head, key_head) * allowed
    denominator = jnp.sum(scores, axis=1) + denom_eps
    numerator = jnp.dot(scores.astype(jnp.bfloat16), value_head, preferred_element_type=jnp.float32)
    return (numerator, denominator)


def head_backward(allowed, head_item):
    query_head, key_head, value_head, grad_numer, grad_denom = head_item
    scores = contract_cols(query_head, key_head) * allowed
    grad_prob = contract_cols(grad_numer, value_head)
    grad_value = contract_rows(scores.astype(jnp.bfloat16), grad_numer)
    grad_scores = ((grad_prob + grad_denom[:, None]) * allowed).astype(jnp.bfloat16)
    grad_query = jnp.dot(grad_scores, key_head, preferred_element_type=jnp.float32)
    grad_key = contract_rows(grad_scores, query_head)
    return (grad_query, grad_key, grad_value)


def plain_body(
    inputs,
    cotangent,
    seg_lengths,
    valid_len,
    w_qkv,
    b_qkv,
    w_out,
    b_out,
    gain_one,
    shift_one,
    w_up,
    b_up,
    w_down,
    b_down,
    gain_two,
    shift_two,
):
    token_rows = inputs[0].astype(jnp.float32)
    row_length = token_rows.shape[0]
    model_width = token_rows.shape[1]
    allowed, keeping = row_masks(seg_lengths[0], valid_len[0], row_length)
    full_qkv, full_bqkv, full_out, full_bout, full_gain, full_shift = pull_group(
        w_qkv, b_qkv, w_out, b_out, gain_one, shift_one
    )
    normed, norm_back = jax.vjp(
        layer_norm, token_rows, full_gain.astype(jnp.float32), full_shift.astype(jnp.float32)
    )
    normed_low = normed.astype(jnp.bfloat16)
    projected = jnp.dot(
        normed_low, full_qkv, preferred_element_type=jnp.float32
    ) + full_bqkv.astype(jnp.float32)
    query_feat, query_back = jax.vjp(feature_map, projected[:, :model_width])
    key_feat, key_back = jax.vjp(feature_map, projected[:, model_width : 2 * model_width])
    query_heads = split_heads(query_feat.astype(jnp.bfloat16))
    key_heads = split_heads(key_feat.astype(jnp.bfloat16))
    value_heads = split_heads(projected[:, 2 * model_width :].astype(jnp.bfloat16))
    numerator, denominator = lax.map(
        partial(head_forward, allowed), (query_heads, key_heads, value_heads)
    )
    attended = keeping[None, :, None] * numerator / denominator[:, :, None]
    attended_low = join_heads(attended).astype(jnp.bfloat16)
    middle = (
        token_rows
        + jnp.dot(attended_low, full_out, preferred_element_type=jnp.float32)
        + full_bout.astype(jnp.float32)
    )
    full_up, full_bup, full_down, full_bdown, full_gain_two, full_shift_two = pull_group(
        w_up, b_up, w_down, b_down, gain_two, shift_two
    )
    normed_two, norm_two_back = jax.vjp(
        layer_norm, middle, full_gain_two.astype(jnp.float32), full_shift_two.astype(jnp.float32)
    )
    normed_two_low = normed_two.astype(jnp.bfloat16)
    hidden = jnp.dot(normed_two_low, full_up, preferred_element_type=jnp.float32) + full_bup.astype(
        jnp.float32
    )
    activated, gelu_back = jax.vjp(gelu_tanh, hidden)
    activated_low = activated.astype(jnp.bfloat16)
    result = (
        middle
        + jnp.dot(activated_low, full_down, preferred_element_type=jnp.float32)
        + full_bdown.astype(jnp.float32)
    )
    again_up, again_bup, again_down, again_bdown, again_gain_two, again_shift_two = pull_group(
        w_up, b_up, w_down, b_down, gain_two, shift_two
    )
    grad_top = cotangent[0]
    grad_top_full = grad_top.astype(jnp.float32)
    grad_down = contract_rows(activated_low, grad_top)
    grad_bdown = jnp.sum(grad_top_full, axis=0)
    grad_hidden = gelu_back(contract_cols(grad_top, again_down))[0]
    grad_hidden_low = grad_hidden.astype(jnp.bfloat16)
    grad_bup = jnp.sum(grad_hidden_low.astype(jnp.float32), axis=0)
    grad_up = contract_rows(normed_two_low, grad_hidden_low)
    grad_normed_two = contract_cols(grad_hidden_low, again_up)
    grad_middle_norm, grad_gain_two, grad_shift_two = norm_two_back(grad_normed_two)
    grad_middle = grad_top_full + grad_middle_norm
    shard_up, shard_bup, shard_down, shard_small_two = push_group(
        grad_up, grad_bup, grad_down, jnp.stack([grad_bdown, grad_gain_two, grad_shift_two])
    )
    again_qkv, again_bqkv, again_out, again_bout, again_gain, again_shift = pull_group(
        w_qkv, b_qkv, w_out, b_out, gain_one, shift_one
    )
    grad_mixed = grad_middle.astype(jnp.bfloat16)
    grad_bout = jnp.sum(grad_mixed.astype(jnp.float32), axis=0)
    grad_wout = contract_rows(attended_low, grad_mixed)
    grad_attended = split_heads(contract_cols(grad_mixed, again_out))
    grad_numer = (keeping[None, :, None] * grad_attended / denominator[:, :, None]).astype(
        jnp.bfloat16
    )
    grad_denom = -jnp.sum(grad_attended * attended, axis=2) / denominator
    grad_query_heads, grad_key_heads, grad_value_heads = lax.map(
        partial(head_backward, allowed),
        (query_heads, key_heads, value_heads, grad_numer, grad_denom),
    )
    grad_query = query_back(join_heads(grad_query_heads))[0]
    grad_key = key_back(join_heads(grad_key_heads))[0]
    grad_projected = jnp.concatenate(
        [grad_query, grad_key, join_heads(grad_value_heads)], axis=1
    ).astype(jnp.bfloat16)
    grad_bias_all = jnp.sum(grad_projected.astype(jnp.float32), axis=0)
    grad_bias_qk = grad_bias_all[: 2 * model_width]
    grad_bias_v = grad_bias_all[2 * model_width :]
    grad_qkv = contract_rows(normed_low, grad_projected)
    grad_normed = contract_cols(grad_projected, again_qkv)
    grad_rows_norm, grad_gain_one, grad_shift_one = norm_back(grad_normed)
    grad_inputs = (grad_middle + grad_rows_norm).astype(jnp.bfloat16)
    shard_qkv, shard_bias_qk, shard_wout, shard_small_one = push_group(
        grad_qkv,
        grad_bias_qk,
        grad_wout,
        jnp.stack([grad_bout, grad_bias_v, grad_gain_one, grad_shift_one]),
    )
    return (
        result.astype(jnp.bfloat16)[None],
        grad_inputs[None],
        shard_qkv,
        shard_bias_qk,
        shard_small_one[1],
        shard_wout,
        shard_small_one[0],
        shard_small_one[2],
        shard_small_one[3],
        shard_up,
        shard_bup,
        shard_down,
        shard_small_two[0],
        shard_small_two[1],
        shard_small_two[2],
    )


HALF_LANES = 64
TILE = 512
Z_HIGH, Z_LOW, Y_BIT, X_BIT = 8, 4, 2, 1
MIXED = ((Z_HIGH, X_BIT, Z_LOW, Y_BIT), (Z_HIGH, Y_BIT, Z_LOW, X_BIT))
LINED = ((Z_HIGH, Z_LOW, X_BIT, Y_BIT), (Z_HIGH, Z_LOW, Y_BIT, X_BIT))
SMALL = 128
GROUP = 16
ANY = pl.BlockSpec(memory_space=pl.ANY)
SMEM = pl.BlockSpec(memory_space=pltpu.SMEM)
VMEM = pl.BlockSpec(memory_space=pltpu.VMEM)
MIB = 1 << 20


def swap_chips(block, bit):
    return lax.ppermute(block, "fsdp", [(place, place ^ bit) for place in range(16)])


def swap_cores(block):
    return lax.ppermute(block, "dp", [(0, 1), (1, 0)])


def relative_place(order, slot, last):
    return (
        order[0] * (slot & 1)
        + order[1] * ((slot >> 1) & 1)
        + order[2] * ((slot >> 2) & 1)
        + order[3] * last
    )


def tie(*blocks):
    return lax.optimization_barrier(blocks)


def by_side(shard):
    half = shard.shape[1] // 2
    return shard[None, :, :half], shard[None, :, half:]


def swap_sides(sides, orders, step):
    first, second = orders[0][step], orders[1][step]
    if first == second:
        return (swap_chips(jnp.stack(sides), first),)
    return swap_chips(sides[0], first), swap_chips(sides[1], second)


def sides_of(arrived):
    return (arrived[0][0], arrived[0][1]) if len(arrived) == 1 else arrived


def grown(sides, arrived):
    return tuple(jnp.concatenate([held, more]) for held, more in zip(sides, sides_of(arrived)))


def swap_both(sides):
    return swap_cores(sides[0]), swap_cores(sides[1])


def pieces_of(held, plane, across, core_held, core_across):
    plane = sides_of(plane)
    return tuple(
        block
        for side in range(2)
        for block in (held[side], plane[side], across[side], core_held[side], core_across[side])
    )


def added(parts, start, stop):
    return sum(part[start:stop].astype(jnp.float32) for part in parts)


def reduce_step(sides, orders, step, amount):
    sent = [added(parts, amount, 2 * amount).astype(jnp.bfloat16) for parts in sides]
    return swap_sides(sent, orders, step)


def with_arrived(sides, arrived):
    return [parts + [more] for parts, more in zip(sides, sides_of(arrived))]


def reduce_end(sides, orders):
    sides = with_arrived(sides, reduce_step(sides, orders, 0, 1))
    return [added(parts, 0, 1)[0] for parts in sides]


def side_by_side(sides, start, stop):
    return jnp.concatenate([side[:, start:stop] for side in sides], axis=1)


def far(array):
    return pltpu.with_memory_space_constraint(array, pltpu.HBM)


def call(kernel, outs, scratch, mib, args, in_specs, out_specs, grid=None, flops=0, gates=()):
    inputs, ignored = len(in_specs), len(gates)

    def gated(*refs):
        kernel(*refs[:inputs], *refs[inputs + ignored :])

    extra = {} if grid is None else {"grid": grid}
    near = (SMEM,) if grid else (SMEM, VMEM)
    args = [arg if spec in near else far(arg) for arg, spec in zip(args, in_specs)]
    gates = [far(gate) for gate in gates]
    if isinstance(outs, tuple):
        outs = tuple(
            out if spec in near else pltpu.HBM(out.shape, out.dtype)
            for out, spec in zip(outs, out_specs)
        )
    return pl.pallas_call(
        gated,
        out_shape=outs,
        in_specs=list(in_specs) + [ANY] * ignored,
        out_specs=out_specs,
        scratch_shapes=scratch,
        compiler_params=pltpu.CompilerParams(vmem_limit_bytes=mib * MIB),
        cost_estimate=pl.CostEstimate(flops=flops, bytes_accessed=0, transcendentals=0),
        **extra,
    )(*args, *gates)


def shaped(shape, dtype):
    return jax.ShapeDtypeStruct(shape, dtype)


def dot_nn(left, right):
    return lax.dot_general(left, right, (((1,), (0,)), ((), ())), preferred_element_type=jnp.float32)


def dot_nt(left, right):
    return lax.dot_general(left, right, (((1,), (1,)), ((), ())), preferred_element_type=jnp.float32)


def piece_at(pieces, side, core, last, slot):
    mine = pieces[5 * side : 5 * side + 5]
    if core or last:
        return mine[1 + core * 2 + last], slot
    return mine[slot // 4], slot % 4


def fetch(place, pieces, whole, sems, skip=0):
    rows, half = pieces[0].shape[1], whole.shape[1] // 2
    copies = []
    for side, order in enumerate(LINED):
        for core in range(2):
            for last in range(2):
                for slot in range(8):
                    piece, index = piece_at(pieces, side, core, last, slot)
                    owner = (place[1] ^ core) * 16 + (place[0] ^ relative_place(order, slot, last))
                    start = pl.multiple_of(owner * rows, rows)
                    copies.append(
                        pltpu.make_async_copy(
                            piece.at[index, :, pl.ds(skip, half)],
                            whole.at[pl.ds(start, rows), pl.ds(side * half, half)],
                            sems.at[len(copies)],
                        )
                    )
    for copy in copies:
        copy.start()
    return copies


def wait_side(copies, side):
    half = len(copies) // 2
    wait_all(copies[side * half : (side + 1) * half])


def wait_all(copies):
    for copy in copies:
        copy.wait()


def standardize(block):
    centred = block - jnp.mean(block, axis=1, keepdims=True)
    scale = lax.rsqrt(jnp.mean(centred * centred, axis=1, keepdims=True) + norm_eps)
    return centred * scale, scale


def norm_pull(grad, standard, scale, gain):
    scaled = grad * gain
    return scale * (
        scaled
        - jnp.mean(scaled, axis=1, keepdims=True)
        - standard * jnp.mean(scaled * standard, axis=1, keepdims=True)
    )


def place_kernel(where, lengths, valid, place):
    place[0] = where[0] & 15
    place[1] = where[0] >> 4
    end = lengths[0, 0]
    place[2] = end
    for image in range(1, 3):
        end = end + lengths[0, image]
        place[2 + image] = end
    place[5] = valid[0]


def run_place(where, lengths, valid):
    return call(
        place_kernel,
        shaped((6,), jnp.int32),
        [],
        8,
        (where, lengths, valid),
        in_specs=[SMEM] * 3,
        out_specs=SMEM,
    )


def fetch_small(place, pieces, small, skip, sems):
    copies = []
    for core in range(2):
        for last in range(2):
            for slot in range(8):
                piece, index = piece_at(pieces, 0, core, last, slot)
                far = relative_place(LINED[0], slot, last)
                owner = (place[1] ^ core) * 16 + (place[0] ^ far)
                start = pl.multiple_of(owner * GROUP, GROUP)
                copies.append(
                    pltpu.make_async_copy(
                        piece.at[index, pl.ds(0, GROUP), pl.ds(skip, SMALL)],
                        small.at[pl.ds(start, GROUP), :],
                        sems.at[len(copies)],
                    )
                )
                copies[-1].start()
    return copies


def tables(each):
    total = 32 * each
    column = lax.broadcasted_iota(jnp.int32, (1, total), 1).astype(jnp.float32)
    turn = jnp.floor((column + 0.5) / each)
    lane = lax.broadcasted_iota(jnp.int32, (SMALL, 1), 0).astype(jnp.float32)
    spread = jnp.where(column - turn * each == lane, 1.0, 0.0).astype(jnp.bfloat16)
    owner = lax.broadcasted_iota(jnp.int32, (32, 1), 0).astype(jnp.float32)
    return owner == turn, spread


def unfold(small, each, rows):
    mine, spread = tables(each)
    lines = []
    for row in rows:
        parts = small[pl.ds(row, 32, stride=GROUP), :].astype(jnp.bfloat16)
        parts = jnp.where(mine, dot_nn(parts, spread), 0.0)
        lines.append(jnp.sum(parts, axis=0, keepdims=True))
    return lines


def fold(small, each, vectors):
    mine, spread = tables(each)
    for row, vector in vectors:
        parts = jnp.where(mine, vector, 0.0).astype(jnp.bfloat16)
        small[pl.ds(row, 32, stride=32), :] = dot_nt(parts, spread)


def qkv_kernel(place, rows_in, *rest):
    pieces, (normed, query, key, value), lines, rest = rest[:10], rest[10:14], rest[14:20], rest[20:]
    whole, small, smalls, bias, sems, more = rest
    few = fetch_small(place, pieces, small, 4 * whole.shape[1] // 6, more)
    copies = fetch(place, pieces, whole, sems)
    wait_all(few)
    smalls[...] = small[...].astype(jnp.float32)
    width = rows_in.shape[1]
    (bias[...],) = unfold(smalls, 3 * width // 32, (0,))
    (lines[5][...],) = unfold(smalls, 4 * width // 32, (4,))
    bias_out, gain, shift, bias_down, gain_two, shift_two = unfold(
        smalls, width // 32, (1, 2, 3, 5, 6, 7)
    )
    for goal, line in zip(lines, (gain, bias_out, gain_two, shift_two, bias_down)):
        goal[...] = line
    for part in range(4):
        at = pl.ds(part * 128, 128)
        standard, _ = standardize(rows_in[at, :].astype(jnp.float32))
        normed[at, :] = (standard * gain + shift).astype(jnp.bfloat16)
    for tile in range(6):
        if tile % 3 == 0:
            wait_side(copies, tile // 3)
        cols = pl.ds(tile * TILE, TILE)
        projected = dot_nn(normed[...], whole[:, cols]) + bias[:, cols]
        goal = (query, key, value)[tile // 2]
        if tile < 4:
            projected = feature_map(projected)
        goal[:, pl.ds((tile % 2) * TILE, TILE)] = projected.astype(jnp.bfloat16)


def run_qkv(place, rows_in, pieces, gates=()):
    length, width = rows_in.shape
    narrow = shaped((length, width), jnp.bfloat16)
    line = shaped((1, width), jnp.float32)
    return call(
        qkv_kernel,
        (narrow,) * 4 + (line,) * 5 + (shaped((1, 4 * width), jnp.float32),),
        [
            pltpu.VMEM((width, 3 * width), jnp.bfloat16),
            pltpu.VMEM((32 * GROUP, SMALL), jnp.bfloat16),
            pltpu.VMEM((32 * GROUP, SMALL), jnp.float32),
            pltpu.VMEM((1, 3 * width), jnp.float32),
            pltpu.SemaphoreType.DMA((64,)),
            pltpu.SemaphoreType.DMA((32,)),
        ],
        18,
        (place, rows_in, *pieces),
        in_specs=[SMEM, VMEM] + [ANY] * 10,
        out_specs=(VMEM,) * 10,
        gates=gates,
    )


def image_of(place, positions):
    image = jnp.zeros(positions.shape, jnp.int32)
    for end in range(2, 5):
        image = image + jnp.where(positions >= place[end], 1, 0)
    return image


def allowed_block(place, length, flipped):
    first = lax.broadcasted_iota(jnp.int32, (length, 1), 0)
    second = lax.broadcasted_iota(jnp.int32, (1, length), 1)
    same = image_of(place, first) == image_of(place, second)
    ordered = (first <= second) if flipped else (second <= first)
    return jnp.where(same & ordered, 1.0, 0.0).astype(jnp.float32)


def low_lanes():
    return lax.broadcasted_iota(jnp.int32, (1, 2 * HALF_LANES), 1) < HALF_LANES


def two_heads(block):
    low = jnp.where(low_lanes(), 1.0, 0.0)
    high = (1.0 - low).astype(jnp.bfloat16)
    return jnp.concatenate([block * low.astype(jnp.bfloat16), block * high], axis=0)


def one_pair(stacked):
    half = stacked.shape[0] // 2
    return jnp.where(low_lanes(), stacked[:half], stacked[half:])


def masked(stacked, allowed):
    half = stacked.shape[0] // 2
    return jnp.concatenate(
        [(stacked[:half] * allowed).astype(jnp.bfloat16), (stacked[half:] * allowed).astype(jnp.bfloat16)],
        axis=0,
    )


def keeping_rows(place, start, amount):
    position = lax.broadcasted_iota(jnp.int32, (amount, 1), 0) + start
    return jnp.where(position < place[5], 1.0, 0.0)


def attend_kernel(place, query, key, value, attended, exact, inverse, allowed, wide):
    length, width = query.shape
    step = length // 2

    @pl.when(pl.program_id(0) == 0)
    def _():
        allowed[...] = allowed_block(place, length, False)
        wide[:, width:] = jnp.ones((length, width), jnp.bfloat16)

    wide[:, :width] = value[...]
    for part in range(2):
        rows, seen = pl.ds(part * step, step), (part + 1) * step
        scores = dot_nt(two_heads(query[rows, :]), key[:seen, :])
        total = dot_nn(masked(scores, allowed[rows, :seen]), wide[:seen, :])
        over = 1.0 / (one_pair(total[:, width:]) + denom_eps)
        inverse[rows, :] = over
        mixed = keeping_rows(place, part * step, step) * one_pair(total[:, :width]) * over
        exact[rows, :] = mixed
        attended[rows, :] = mixed.astype(jnp.bfloat16)


def run_attend(place, query, key, value, gates=()):
    length, width = query.shape
    pair = pl.BlockSpec((length, 2 * HALF_LANES), lambda p: (0, p))
    return call(
        attend_kernel,
        (
            shaped((length, width), jnp.bfloat16),
            shaped((length, width), jnp.float32),
            shaped((length, width), jnp.float32),
        ),
        [
            pltpu.VMEM((length, length), jnp.float32),
            pltpu.VMEM((length, 4 * HALF_LANES), jnp.bfloat16),
        ],
        10,
        (place, query, key, value),
        grid=(width // (2 * HALF_LANES),),
        in_specs=[SMEM] + [pair] * 3,
        out_specs=(pair,) * 3,
        gates=gates,
    )


def attend_back_pair(
    place, query, key, value, grad_att, exact, inverse, stacked, sums, allowed, flipped, left, wide
):
    length, width = query.shape
    step = length // 2
    wide[:, :width] = value[...]
    over = grad_att[...] * inverse[...]
    lane = lax.broadcasted_iota(jnp.int32, (1, width), 1)
    terms, low = over * exact[...], lane < HALF_LANES
    first = jnp.sum(jnp.where(low, terms, 0.0), axis=1, keepdims=True)
    second = jnp.sum(jnp.where(low, 0.0, terms), axis=1, keepdims=True)
    spread = -jnp.where(low, first, second)
    high = spread.astype(jnp.bfloat16).astype(jnp.float32)
    within = lane & (HALF_LANES - 1)
    spread = jnp.where(within == 0, high, jnp.where(within == 1, spread - high, 0.0))
    numer = (keeping_rows(place, 0, length) * over).astype(jnp.bfloat16)
    for head in range(2):
        here = jnp.where(low, 1.0 - head, 1.0 * head)
        at = pl.ds(head * length, length)
        left[at, :width] = numer * here.astype(jnp.bfloat16)
        left[at, width:] = (spread * here).astype(jnp.bfloat16)
    for part in range(2):
        rows, seen = pl.ds(part * step, step), (part + 1) * step
        start = part * step
        later = pl.ds(start, length - start)
        both = jnp.concatenate([left[rows, :], left[pl.ds(length + start, step), :]], axis=0)
        grad_scores = masked(dot_nt(both, wide[:seen, :]), allowed[rows, :seen])
        grad_query = one_pair(dot_nn(grad_scores, key[:seen, :]))
        full = left[later, :] + left[pl.ds(length + start, length - start), :]
        scores = masked(dot_nt(two_heads(key[rows, :]), query[later, :]), flipped[rows, later])
        grad_value = one_pair(dot_nn(scores, full[:, :width]))
        ones = jnp.concatenate([two_heads(value[rows, :]), two_heads(wide[rows, width:])], axis=1)
        grad_scores = masked(dot_nt(ones, full), flipped[rows, later])
        grad_key = one_pair(dot_nn(grad_scores, query[later, :]))
        grads = (
            grad_query * jnp.minimum(query[rows, :].astype(jnp.float32), 1.0),
            grad_key * jnp.minimum(key[rows, :].astype(jnp.float32), 1.0),
            grad_value,
        )
        for index, grad in enumerate(grads):
            low_grad, line = grad.astype(jnp.bfloat16), pl.ds(index, 1)
            stacked[index, rows, :] = low_grad
            extra = jnp.sum(low_grad.astype(jnp.float32), axis=0, keepdims=True)
            sums[line, :] = extra if part == 0 else sums[line, :] + extra


def attend_back_kernel(
    place, query, key, value, grad_att, exact, inverse, stacked, sums, allowed, flipped, left, wide
):
    length, width = query.shape[0], 2 * HALF_LANES
    pairs = query.shape[1] // width

    @pl.when(pl.program_id(0) == 0)
    def _():
        allowed[...] = allowed_block(place, length, False)
        flipped[...] = allowed_block(place, length, True)
        for pair in range(pairs):
            wide[pair, :, width:] = jnp.ones((length, width), jnp.bfloat16)

    for pair in range(pairs):
        cols = pl.ds(pair * width, width)
        attend_back_pair(
            place,
            *(ref.at[:, cols] for ref in (query, key, value, grad_att, exact, inverse)),
            stacked.at[:, :, cols],
            sums.at[:, cols],
            allowed,
            flipped,
            left.at[pair],
            wide.at[pair],
        )


def run_attend_back(place, first, query, key, value, grad_att, exact, inverse, gates=()):
    length, width = query.shape
    half = width // 2
    start = first * half // (4 * HALF_LANES)
    pair = pl.BlockSpec((length, 4 * HALF_LANES), lambda p: (0, p + start))
    stack = pl.BlockSpec((3, length, 4 * HALF_LANES), lambda p: (0, 0, p))
    lines = pl.BlockSpec((3, 4 * HALF_LANES), lambda p: (0, p))
    return call(
        attend_back_kernel,
        (shaped((3, length, half), jnp.bfloat16), shaped((3, half), jnp.float32)),
        [
            pltpu.VMEM((length, length), jnp.float32),
            pltpu.VMEM((length, length), jnp.float32),
            pltpu.VMEM((2, 2 * length, 4 * HALF_LANES), jnp.bfloat16),
            pltpu.VMEM((2, length, 4 * HALF_LANES), jnp.bfloat16),
        ],
        20,
        (place, query, key, value, grad_att, exact, inverse),
        grid=(half // (4 * HALF_LANES),),
        in_specs=[SMEM] + [pair] * 6,
        out_specs=(stack, lines),
        gates=gates,
    )


def hand_over(place, sources, goal, sems):
    copies, at = [], 0
    for source in sources:
        half = source.shape[1] // 2
        start = pl.multiple_of((1 - place[1]) * half, half)
        copies.append(
            pltpu.make_async_copy(
                source.at[:, pl.ds(start, half)], goal.at[:, pl.ds(at, half)], sems.at[len(copies)]
            )
        )
        copies[-1].start()
        at += half
    return copies


def out_kernel(place, rows_in, early, attended, bias, gain, shift, *rest):
    pieces, (middle, normed, handed, whole, sems, more) = rest[:10], rest[10:]
    copies = fetch(place, pieces, whole, sems, 3 * whole.shape[1] // 2)
    handing = hand_over(place, (early, attended), handed, more)
    for side in range(2):
        wait_side(copies, side)
        cols = pl.ds(side * TILE, TILE)
        middle[:, cols] = (
            rows_in[:, cols].astype(jnp.float32) + dot_nn(attended[...], whole[:, cols]) + bias[:, cols]
        )
    for part in range(4):
        at = pl.ds(part * 128, 128)
        standard, _ = standardize(middle[at, :])
        normed[at, :] = (standard * gain[...] + shift[...]).astype(jnp.bfloat16)
    wait_all(handing)


def run_out(place, rows_in, early, attended, bias, gain, shift, pieces, gates=()):
    length, width = rows_in.shape
    narrow = shaped((length, width), jnp.bfloat16)
    return call(
        out_kernel,
        (shaped((length, width), jnp.float32), narrow, narrow),
        [
            pltpu.VMEM((width, width), jnp.bfloat16),
            pltpu.SemaphoreType.DMA((64,)),
            pltpu.SemaphoreType.DMA((2,)),
        ],
        16,
        (place, rows_in, early, attended, bias, gain, shift, *pieces),
        in_specs=[SMEM] + [VMEM] * 6 + [ANY] * 10,
        out_specs=(VMEM, VMEM, ANY),
        gates=gates,
    )


def bend_tile(hidden, activated, slope):
    square = hidden * hidden
    rate = gelu_coef + (gelu_coef * 0.044715) * square
    bend = jnp.tanh(hidden * rate)
    share = 0.5 + 0.5 * bend
    activated[...] = (hidden * share).astype(jnp.bfloat16)
    rate = gelu_coef + (3.0 * gelu_coef * 0.044715) * square
    slope[...] = (share + (0.5 * hidden) * (1.0 - bend * bend) * rate).astype(jnp.bfloat16)


def up_kernel(place, normed, bias, *rest):
    pieces, (activated, slope, handed, whole, hidden, sems, more) = rest[:10], rest[10:]
    copies = fetch(place, pieces, whole, sems)
    tiles = whole.shape[1] // TILE

    def columns(tile):
        return pl.ds(tile * TILE, TILE)

    for tile in range(tiles + 1):
        if tile % (tiles // 2) == 0 and tile < tiles:
            wait_side(copies, tile // (tiles // 2))
        if tile < tiles:
            cols = columns(tile)
            hidden[tile % 2] = dot_nn(normed[...], whole[:, cols]) + bias[:, cols]
        if tile > 0:
            cols = columns(tile - 1)
            bend_tile(hidden[(tile - 1) % 2], activated.at[:, cols], slope.at[:, cols])

    wait_all(hand_over(place, (normed, activated), handed, more))


def run_up(place, normed, bias, pieces, gates=()):
    length, width = normed.shape
    wide = bias.shape[1]
    return call(
        up_kernel,
        (shaped((length, wide), jnp.bfloat16),) * 2
        + (shaped((length, (width + wide) // 2), jnp.bfloat16),),
        [
            pltpu.VMEM((width, wide), jnp.bfloat16),
            pltpu.VMEM((2, length, TILE), jnp.float32),
            pltpu.SemaphoreType.DMA((64,)),
            pltpu.SemaphoreType.DMA((2,)),
        ],
        26,
        (place, normed, bias, *pieces),
        in_specs=[SMEM] + [VMEM] * 2 + [ANY] * 10,
        out_specs=(VMEM, VMEM, ANY),
        gates=gates,
    )


def sum_kernel(block, total):
    total[...] = jnp.sum(block[...].astype(jnp.float32), axis=0, keepdims=True)


def run_sum(block, cover, gates=()):
    return call(
        sum_kernel,
        shaped((1, block.shape[1]), jnp.float32),
        [],
        8,
        (block,),
        in_specs=[VMEM],
        out_specs=VMEM,
        flops=cover,
        gates=gates,
    )


def down_kernel(place, activated, slope, grad_top, middle, bias, *rest):
    pieces, (result, grad_hidden, sum_up, whole, sems) = rest[:10], rest[10:]
    copies = fetch(place, pieces, whole, sems)
    wait_all(copies)
    for tile in range(4):
        cols = pl.ds(tile * 256, 256)
        result[:, cols] = (
            middle[:, cols] + bias[:, cols] + dot_nn(activated[...], whole[:, cols])
        ).astype(jnp.bfloat16)
        for half in range(2):
            cols = pl.ds((2 * tile + half) * TILE, TILE)
            grad = dot_nt(grad_top[...], whole[cols, :]) * slope[:, cols].astype(jnp.float32)
            low = grad.astype(jnp.bfloat16)
            grad_hidden[:, cols] = low
            sum_up[:, cols] = jnp.sum(low.astype(jnp.float32), axis=0, keepdims=True)


def run_down(place, activated, slope, grad_top, middle, bias, pieces, gates=()):
    length, width = middle.shape
    wide = activated.shape[1]
    return call(
        down_kernel,
        (
            shaped((length, width), jnp.bfloat16),
            shaped((length, wide), jnp.bfloat16),
            shaped((1, wide), jnp.float32),
        ),
        [
            pltpu.VMEM((wide, width), jnp.bfloat16),
            pltpu.SemaphoreType.DMA((64,)),
        ],
        30,
        (place, activated, slope, grad_top, middle, bias, *pieces),
        in_specs=[SMEM] + [VMEM] * 5 + [ANY] * 10,
        out_specs=(VMEM,) * 3,
        flops=64 * length * width * wide,
        gates=gates,
    )


def middle_back_kernel(place, grad_hidden, middle, grad_top, gain, *rest):
    pieces_up, pieces_in, rest = rest[:10], rest[10:20], rest[20:]
    grad_middle, mixed, grad_att, sum_gain, sum_shift, whole, outer, total, sems, more = rest
    copies = fetch(place, pieces_up, whole, sems)
    second = fetch(place, pieces_in, outer, more, 3 * outer.shape[1] // 2)
    step = 2 * TILE
    for tile in range(whole.shape[1] // step):
        if tile % 2 == 0:
            wait_side(copies, tile // 2)
        cols = pl.ds(tile * step, step)
        block = dot_nt(grad_hidden[:, cols], whole[:, cols])
        total[...] = block if tile == 0 else total[...] + block

    for part in range(4):
        at = pl.ds(part * 128, 128)
        grad = total[at, :]
        standard, scale = standardize(middle[at, :])
        back = grad_top[at, :].astype(jnp.float32) + norm_pull(grad, standard, scale, gain[...])
        grad_middle[at, :] = back
        low = back.astype(jnp.bfloat16)
        mixed[at, :] = low
        for goal, added in ((sum_gain, grad * standard), (sum_shift, grad)):
            added = jnp.sum(added, axis=0, keepdims=True)
            goal[...] = added if part == 0 else goal[...] + added
    wait_all(second)
    for part in range(2):
        cols = pl.ds(part * TILE, TILE)
        grad_att[:, cols] = dot_nt(mixed[...], outer[cols, :])


def run_middle_back(place, grad_hidden, middle, grad_top, gain, pieces_up, pieces_in, gates=()):
    length, width = middle.shape
    wide = grad_hidden.shape[1]
    full, line = shaped((length, width), jnp.float32), shaped((1, width), jnp.float32)
    return call(
        middle_back_kernel,
        (full, shaped((length, width), jnp.bfloat16), full, line, line),
        [
            pltpu.VMEM((width, wide), jnp.bfloat16),
            pltpu.VMEM((width, width), jnp.bfloat16),
            pltpu.VMEM((length, width), jnp.float32),
            pltpu.SemaphoreType.DMA((64,)),
            pltpu.SemaphoreType.DMA((64,)),
        ],
        30,
        (place, grad_hidden, middle, grad_top, gain, *pieces_up, *pieces_in),
        in_specs=[SMEM] + [VMEM] * 4 + [ANY] * 20,
        out_specs=(VMEM,) * 5,
        gates=gates,
    )


def inputs_back_kernel(place, early, late, rows_in, gain, grad_middle, mixed, *rest):
    (sums, late_sums, *ready), pieces, rest = rest[:6], rest[6:16], rest[16:]
    grad_rows, lines, whole, total, sems = rest
    copies = fetch(place, pieces, whole, sems)
    width = rows_in.shape[1]
    for tile in range(6):
        if tile % 3 == 0:
            wait_side(copies, tile // 3)
        grads = (early, late)[tile % 2]
        block = dot_nt(grads[tile // 2], whole[:, pl.ds(tile * TILE, TILE)])
        total[...] = block if tile == 0 else total[...] + block
    for part in range(4):
        at = pl.ds(part * 128, 128)
        grad = total[at, :]
        standard, scale = standardize(rows_in[at, :].astype(jnp.float32))
        back = grad_middle[at, :] + norm_pull(grad, standard, scale, gain[...])
        grad_rows[at, :] = back.astype(jnp.bfloat16)
        extras = (mixed[at, :].astype(jnp.float32), grad * standard, grad)
        for index, extra in enumerate(extras):
            goal = lines.at[:, pl.ds((3 + index) * width, width)]
            extra = jnp.sum(extra, axis=0, keepdims=True)
            goal[...] = extra if part == 0 else goal[...] + extra
    half = width // 2
    for row in range(3):
        for index, source in enumerate((sums, late_sums)):
            lines[:, pl.ds(row * width + index * half, half)] = source[pl.ds(row, 1), :]
    at = 6 * width
    for source in ready:
        lines[:, pl.ds(at, source.shape[1])] = source[...]
        at += source.shape[1]


def run_inputs_back(
    place, early, late, rows_in, gain, grad_middle, mixed, ready, pieces, gates=()
):
    length, width = rows_in.shape
    total = 6 * width + sum(line.shape[1] for line in ready[2:])
    return call(
        inputs_back_kernel,
        (shaped((length, width), jnp.bfloat16), shaped((1, total), jnp.float32)),
        [
            pltpu.VMEM((width, 3 * width), jnp.bfloat16),
            pltpu.VMEM((length, width), jnp.float32),
            pltpu.SemaphoreType.DMA((64,)),
        ],
        20,
        (place, early, late, rows_in, gain, grad_middle, mixed, *ready, *pieces),
        in_specs=[SMEM] + [VMEM] * 12 + [ANY] * 10,
        out_specs=(VMEM,) * 2,
        flops=1 << 40,
        gates=gates,
    )


def weight_kernel(orders, skips, sizes, place, *rest):
    groups = len(skips)
    if sizes:
        mine, other_lines, rest = rest[4 * groups], rest[4 * groups + 1], rest[: 4 * groups] + rest[4 * groups + 2 :]
    inputs, outs, rest = rest[: 4 * groups], rest[4 * groups : 4 * groups + 4], rest[4 * groups + 4 :]
    wholes, (turned, sems), rest = rest[:groups], rest[groups : groups + 2], rest[groups + 2 :]
    length, rows = inputs[0].shape[0], outs[0].shape[1]
    owners = 256 // rows
    at, copies = 0, []
    for group, (skip, whole) in enumerate(zip(skips, wholes)):
        left_own, left_other, own, other = inputs[4 * group : 4 * group + 4]
        count, each = own.shape[0], own.shape[2]
        tiles, half = whole.shape[0], whole.shape[2] // 2
        for tile in range(tiles):
            low = pl.multiple_of(((place[0] // owners) ^ tile) * 256, 256)
            start = pl.multiple_of(place[1] * (256 * tiles) + low, 256)
            left = turned.at[tile % 2]
            left[:, :length] = left_own[:, pl.ds(start, 256)].T
            left[:, length:] = left_other[:, pl.ds(skip + low, 256)].T
            for index in range(count):
                for step in range(each // TILE):
                    cols = pl.ds(step * TILE, TILE)
                    block = dot_nn(left[:, :length], own[index, :, cols])
                    block += dot_nn(left[:, length:], other[index, :, cols])
                    goal = pl.ds(index * each + step * TILE, TILE)
                    whole[tile, :, goal] = block.astype(jnp.bfloat16)
            for side, order in enumerate(orders):
                for last in range(2):
                    for slot in range(8):
                        far_place = relative_place(order, slot, last)
                        if far_place // owners != tile:
                            continue
                        start = pl.multiple_of(((place[0] ^ far_place) % owners) * rows, rows)
                        copies.append(
                            pltpu.make_async_copy(
                                whole.at[tile, pl.ds(start, rows), pl.ds(side * half, half)],
                                outs[last * 2 + side].at[slot, :, pl.ds(at, half)],
                                sems.at[len(copies)],
                            )
                        )
                        copies[-1].start()
        at += half
    if sizes:
        wide_small, small, more = rest
        wide_small[...] = jnp.zeros_like(wide_small)
        start, by_size = 0, {}
        for row, size in enumerate(sizes):
            line = mine[:, start : start + size] + other_lines[:, start : start + size]
            by_size.setdefault(size, []).append((row, line))
            start += size
        for size, vectors in by_size.items():
            fold(wide_small, size // 32, vectors)
        small[...] = wide_small[...].astype(jnp.bfloat16)
        for last in range(2):
            for slot in range(8):
                chip = place[0] ^ relative_place(orders[0], slot, last)
                start = pl.multiple_of((place[1] * 16 + chip) * 32, 32)
                copies.append(
                    pltpu.make_async_copy(
                        small.at[pl.ds(start, 32), :],
                        outs[last * 2].at[slot, :, pl.ds(at, SMALL)],
                        more.at[last * 8 + slot],
                    )
                )
                copies[-1].start()
    wait_all(copies)


def run_weight(place, orders, height, groups, gates=(), sizes=(), lines=()):
    length = groups[0][0].shape[0]
    totals = [own.shape[0] * own.shape[2] for _, _, _, own, _ in groups]
    half = sum(totals) // 2
    part = shaped((8, height // 16, half), jnp.bfloat16)
    first = shaped((8, height // 16, half + (SMALL if sizes else 0)), jnp.bfloat16)
    extra = [
        pltpu.VMEM((32 * 32, SMALL), jnp.float32),
        pltpu.VMEM((32 * 32, SMALL), jnp.bfloat16),
        pltpu.SemaphoreType.DMA((16,)),
    ]
    return call(
        partial(weight_kernel, orders, tuple(group[2] for group in groups), sizes),
        (first,) * 4,
        [pltpu.VMEM((height // 256, 256, total), jnp.bfloat16) for total in totals]
        + [
            pltpu.VMEM((2, 256, 2 * length), jnp.bfloat16),
            pltpu.SemaphoreType.DMA((32 * len(groups),)),
        ]
        + (extra if sizes else []),
        22,
        (place, *(array for group in groups for array in group[:2] + group[3:]), *lines),
        in_specs=[SMEM] + [VMEM] * (4 * len(groups) + len(lines)),
        out_specs=(ANY,) * 4,
        gates=gates,
    )


def paired_body(
    inputs,
    cotangent,
    seg_lengths,
    valid_len,
    w_qkv,
    b_qkv,
    w_out,
    b_out,
    gain_one,
    shift_one,
    w_up,
    b_up,
    w_down,
    b_down,
    gain_two,
    shift_two,
):
    where = (lax.axis_index("dp") * 16 + lax.axis_index("fsdp")).astype(jnp.int32)[None]
    rows_in, grad_top = inputs[0], cotangent[0]
    vectors = (b_qkv, b_out, gain_one, shift_one, b_up, b_down, gain_two, shift_two)
    cut = w_qkv.shape[1] // 2
    edge = w_out.shape[1] // 2
    held_in = (
        jnp.concatenate([w_qkv[:, :cut], w_out[:, :edge]], axis=1)[None],
        jnp.concatenate([w_qkv[:, cut:], w_out[:, edge:]], axis=1)[None],
    )
    small = jnp.stack([jnp.pad(vector, (0, SMALL - vector.shape[0])) for vector in vectors])
    small = jnp.pad(small, ((0, w_out.shape[0] - small.shape[0]), (0, 0)))[None]
    small_far = swap_chips(small, Z_HIGH)
    place = run_place(where, seg_lengths, valid_len)
    place, small_far = tie(place, small_far)
    small = jnp.concatenate([small, small_far])
    held_up, held_down = by_side(w_up), by_side(w_down)
    top = grad_top[None]
    held_in = grown(held_in, swap_sides(held_in, LINED, 0))
    held_in = (
        jnp.concatenate([held_in[0], small], axis=2),
        jnp.concatenate([held_in[1], jnp.zeros_like(small)], axis=2),
    )
    held_in = grown(held_in, swap_sides(held_in, LINED, 1))
    held_in, held_up = tie(held_in, held_up)
    start_up = swap_sides(held_up, LINED, 0)
    plane_in = swap_sides(held_in, LINED, 2)
    start_up, plane_in = tie(start_up, plane_in)
    held_up = grown(held_up, start_up)
    held_up, held_down = tie(held_up, held_down)
    full_in = grown(held_in, plane_in)
    across_in = swap_sides(full_in, LINED, 3)
    core_in = swap_both(full_in)
    held_up = grown(held_up, swap_sides(held_up, LINED, 1))
    start_down = swap_sides(held_down, LINED, 0)
    across_in, start_down = tie(across_in, start_down)
    pieces_in = pieces_of(held_in, plane_in, across_in, core_in, swap_both(across_in))
    plane_up = swap_sides(held_up, LINED, 2)
    held_down = grown(held_down, start_down)
    line_down = swap_sides(held_down, LINED, 1)
    top_other = swap_cores(top)

    normed, query, key, value, *lines = run_qkv(
        place, rows_in, pieces_in, (*held_up, *held_down, top_other)
    )
    full_gain, full_bout, full_gain_two, full_shift_two, full_bdown, full_bup = lines
    plane_up, line_down, normed = tie(plane_up, line_down, normed)
    full_up = grown(held_up, plane_up)
    across_up = swap_sides(full_up, LINED, 3)
    core_up = swap_both(full_up)
    held_down = grown(held_down, line_down)
    attended, exact, inverse = run_attend(place, query, key, value, (*plane_up, *held_down))
    core_up, held_down, attended = tie(core_up, held_down, attended)
    plane_down = swap_sides(held_down, LINED, 2)
    middle, normed_two, inner_half = run_out(
        place,
        rows_in,
        normed,
        attended,
        full_bout,
        full_gain_two,
        full_shift_two,
        pieces_in,
    )
    inner_other = swap_cores(inner_half)
    across_up, plane_down, normed_two = tie(across_up, plane_down, normed_two)
    pieces_up = pieces_of(held_up, plane_up, across_up, core_up, swap_both(across_up))
    full_down = grown(held_down, plane_down)
    across_down = swap_sides(full_down, LINED, 3)
    core_down = swap_both(full_down)
    activated, slope, outer_half = run_up(
        place, normed_two, full_bup, pieces_up, (*plane_down, inner_other)
    )
    outer_other = swap_cores(outer_half)
    sum_down = run_sum(grad_top, 1 << 40, (outer_half,))
    thin = normed_two.shape[1] // 2
    parts = run_weight(
        place,
        LINED,
        activated.shape[1] // 2,
        [(activated, outer_other, thin, top, top_other)],
        (*core_down, sum_down),
    )
    across_down, parts = tie(across_down, parts)
    down_one = swap_sides(parts[2:], LINED, 3)
    pieces_down = pieces_of(held_down, plane_down, across_down, core_down, swap_both(across_down))
    result, grad_hidden, sum_up = run_down(
        place, activated, slope, grad_top, middle, full_bdown, pieces_down, parts[2:]
    )
    down_one, grad_hidden = tie(down_one, grad_hidden)
    hidden_other = swap_cores(grad_hidden[None])
    down_sides = with_arrived([[parts[0]], [parts[1]]], down_one)
    down_two = reduce_step(down_sides, LINED, 2, 4)
    grad_middle, mixed, grad_att, sum_gain_two, sum_shift_two = run_middle_back(
        place, grad_hidden, middle, grad_top, full_gain_two, pieces_up, pieces_in, down_one
    )
    mixed = mixed[None]
    down_two, mixed = tie(down_two, mixed)
    hidden_other, mixed = tie(hidden_other, mixed)
    mixed_other = swap_cores(mixed)
    down_sides = with_arrived(down_sides, down_two)
    down_three = reduce_step(down_sides, LINED, 1, 2)
    parts = run_weight(
        place, LINED, thin, [(normed_two, outer_other, 0, grad_hidden[None], hidden_other)], down_two
    )
    mixed_other, parts = tie(mixed_other, parts)
    up_one = swap_sides(parts[2:], LINED, 3)
    grads, sums = run_attend_back(
        place, 0, query, key, value, grad_att, exact, inverse, parts[2:]
    )
    down_three, grads = tie(down_three, grads)
    down_sides = with_arrived(down_sides, down_three)
    down_four = reduce_step(down_sides, LINED, 0, 1)
    grads_other = swap_cores(grads)
    late, late_sums = run_attend_back(
        place, 1, query, key, value, grad_att, exact, inverse, (grads,)
    )
    up_one, down_four, late = tie(up_one, down_four, late)
    down_sides = with_arrived(down_sides, down_four)
    up_sides = with_arrived([[parts[0]], [parts[1]]], up_one)
    late_other = swap_cores(late)
    up_two = reduce_step(up_sides, LINED, 2, 4)
    grad_rows, lines = run_inputs_back(
        place,
        grads,
        late,
        rows_in,
        full_gain,
        grad_middle,
        mixed[0],
        (sums, late_sums, sum_up, sum_down, sum_gain_two, sum_shift_two),
        pieces_in,
        up_one,
    )
    up_two, grads_other, late_other, lines = tie(up_two, grads_other, late_other, lines)
    up_sides = with_arrived(up_sides, up_two)
    up_three = reduce_step(up_sides, LINED, 1, 2)
    lines_other = swap_cores(lines)
    parts = run_weight(
        place,
        MIXED,
        thin,
        [
            (normed, inner_other, 0, grads, grads_other),
            (attended, inner_other, thin, mixed, mixed_other),
        ],
    )
    lines_other, parts = tie(lines_other, parts)
    in_sides = [[parts[0]], [parts[1]]]
    in_one = swap_sides(parts[2:], MIXED, 3)
    narrow, wide = mixed.shape[2], sum_up.shape[1]
    sizes = (2 * narrow, narrow, narrow, narrow, narrow, wide, narrow, narrow, narrow)
    parts = run_weight(
        place,
        LINED,
        thin,
        [(normed, inner_other, 0, late, late_other)],
        parts[:1],
        sizes,
        (lines, lines_other),
    )
    up_three, parts = tie(up_three, parts)
    up_sides = with_arrived(up_sides, up_three)
    up_four = reduce_step(up_sides, LINED, 0, 1)
    late_sides = [[parts[0]], [parts[1]]]
    late_one = swap_sides(parts[2:], LINED, 3)
    in_sides = with_arrived(in_sides, in_one)
    late_one, down_sides = tie(late_one, down_sides)
    late_sides = with_arrived(late_sides, late_one)
    in_sides = with_arrived(in_sides, reduce_step(in_sides, MIXED, 2, 4))
    late_sides = with_arrived(late_sides, reduce_step(late_sides, LINED, 2, 4))
    up_sides = with_arrived(up_sides, up_four)
    in_sides = with_arrived(in_sides, reduce_step(in_sides, MIXED, 1, 2))
    late_sides = with_arrived(late_sides, reduce_step(late_sides, LINED, 1, 2))
    shard_down = side_by_side([added(parts, 0, 1)[0] for parts in down_sides], 0, edge)
    shard_up = side_by_side([added(parts, 0, 1)[0] for parts in up_sides], 0, w_up.shape[1] // 2)
    shards = reduce_end(in_sides, MIXED)
    cut = cut // 2
    first = side_by_side(shards, 0, cut)
    shard_out = side_by_side(shards, cut, cut + edge)
    shards = reduce_end(late_sides, LINED)
    second = side_by_side(shards, 0, cut)
    third = edge
    shard_qkv = jnp.concatenate(
        [
            half[:, part * third : (part + 1) * third]
            for part in range(3)
            for half in (first, second)
        ],
        axis=1,
    )
    smalls = [shards[0][row, cut : cut + size // 32] for row, size in enumerate(sizes)]
    grad_bqk, grad_bv, grad_bout, grad_gain, grad_shift, grad_bup, grad_bdown, grad_gain_two, grad_shift_two = smalls
    return (
        result[None],
        grad_rows[None],
        shard_qkv,
        grad_bqk,
        grad_bv,
        shard_out,
        grad_bout,
        grad_gain,
        grad_shift,
        shard_up,
        grad_bup,
        shard_down,
        grad_bdown,
        grad_gain_two,
        grad_shift_two,
    )


def solution(mesh):
    placed = (
        P(("dp", "fsdp"), None, None),
        P(("dp", "fsdp"), None, None),
        P(("dp", "fsdp"), None),
        P(("dp", "fsdp")),
        P(("dp", "fsdp"), None),
        P(("dp", "fsdp")),
        P(("dp", "fsdp"), None),
        P(("dp", "fsdp")),
        P(("dp", "fsdp")),
        P(("dp", "fsdp")),
        P(("dp", "fsdp"), None),
        P(("dp", "fsdp")),
        P(("dp", "fsdp"), None),
        P(("dp", "fsdp")),
        P(("dp", "fsdp")),
        P(("dp", "fsdp")),
    )
    paired = dict(mesh.shape) == {"dp": 2, "fsdp": 16}
    return jax.shard_map(
        paired_body if paired else plain_body,
        mesh=mesh,
        in_specs=placed,
        out_specs=(
            P(("dp", "fsdp"), None, None),
            P(("dp", "fsdp"), None, None),
            P(("dp", "fsdp"), None),
            P(("dp", "fsdp")),
            P(("dp", "fsdp")),
            P(("dp", "fsdp"), None),
            P(("dp", "fsdp")),
            P(("dp", "fsdp")),
            P(("dp", "fsdp")),
            P(("dp", "fsdp"), None),
            P(("dp", "fsdp")),
            P(("dp", "fsdp"), None),
            P(("dp", "fsdp")),
            P(("dp", "fsdp")),
            P(("dp", "fsdp")),
        ),
        check_vma=False,
    )
```

```python
from functools import partial

import jax
import jax.numpy as jnp
from jax import lax
from jax.experimental import pallas as pl
from jax.experimental.pallas import tpu as pltpu
from jax.sharding import PartitionSpec as P

HEADS = 16


norm_eps = 1e-05
denom_eps = 1e-06
gelu_coef = 0.7978845608028654


def layer_norm(values, scale_gain, offset):
    centred = values - jnp.mean(values, axis=-1, keepdims=True)
    spread = jnp.mean(centred * centred, axis=-1, keepdims=True)
    return centred * lax.rsqrt(spread + norm_eps) * scale_gain + offset


def feature_map(values):
    return jnp.where(values > 0, values + 1.0, jnp.exp(jnp.minimum(values, 0.0)))


def gelu_tanh(values):
    return (
        0.5 * values * (1.0 + jnp.tanh(gelu_coef * (values + 0.044715 * values * values * values)))
    )


def contract_rows(left_side, right_side):
    return lax.dot_general(
        left_side, right_side, (((0,), (0,)), ((), ())), preferred_element_type=jnp.float32
    )


def contract_cols(left_side, right_side):
    return lax.dot_general(
        left_side, right_side, (((1,), (1,)), ((), ())), preferred_element_type=jnp.float32
    )


def row_masks(lengths, valid_count, row_length):
    places = jnp.arange(row_length, dtype=jnp.int32)
    bounds = jnp.stack([jnp.sum(lengths[: end + 1]) for end in range(lengths.shape[0])])
    segment = jnp.sum((places[:, None] >= bounds[None, :]).astype(jnp.int32), axis=1)
    allowed = (segment[:, None] == segment[None, :]) & (places[None, :] <= places[:, None])
    keeping = (places < valid_count).astype(jnp.float32)
    return (allowed.astype(jnp.float32), keeping)


def split_heads(matrix):
    return jnp.transpose(matrix.reshape(matrix.shape[0], HEADS, -1), (1, 0, 2))


def join_heads(stacked):
    return jnp.transpose(stacked, (1, 0, 2)).reshape(stacked.shape[1], -1)


def pull_group(first, second, third, fourth, fifth, sixth):
    return (
        lax.all_gather(first, ("dp", "fsdp"), axis=0, tiled=True),
        lax.all_gather(second, ("dp", "fsdp"), axis=0, tiled=True),
        lax.all_gather(third, ("dp", "fsdp"), axis=0, tiled=True),
        lax.all_gather(fourth, ("dp", "fsdp"), axis=0, tiled=True),
        lax.all_gather(fifth, ("dp", "fsdp"), axis=0, tiled=True),
        lax.all_gather(sixth, ("dp", "fsdp"), axis=0, tiled=True),
    )


def push_group(first, second, third, stacked):
    return (
        lax.psum_scatter(first, ("dp", "fsdp"), scatter_dimension=0, tiled=True),
        lax.psum_scatter(second, ("dp", "fsdp"), scatter_dimension=0, tiled=True),
        lax.psum_scatter(third, ("dp", "fsdp"), scatter_dimension=0, tiled=True),
        lax.psum_scatter(stacked, ("dp", "fsdp"), scatter_dimension=1, tiled=True),
    )


def head_forward(allowed, head_item):
    query_head, key_head, value_head = head_item
    scores = contract_cols(query_head, key_head) * allowed
    denominator = jnp.sum(scores, axis=1) + denom_eps
    numerator = jnp.dot(scores.astype(jnp.bfloat16), value_head, preferred_element_type=jnp.float32)
    return (numerator, denominator)


def head_backward(allowed, head_item):
    query_head, key_head, value_head, grad_numer, grad_denom = head_item
    scores = contract_cols(query_head, key_head) * allowed
    grad_prob = contract_cols(grad_numer, value_head)
    grad_value = contract_rows(scores.astype(jnp.bfloat16), grad_numer)
    grad_scores = ((grad_prob + grad_denom[:, None]) * allowed).astype(jnp.bfloat16)
    grad_query = jnp.dot(grad_scores, key_head, preferred_element_type=jnp.float32)
    grad_key = contract_rows(grad_scores, query_head)
    return (grad_query, grad_key, grad_value)


def plain_body(
    inputs,
    cotangent,
    seg_lengths,
    valid_len,
    w_qkv,
    b_qkv,
    w_out,
    b_out,
    gain_one,
    shift_one,
    w_up,
    b_up,
    w_down,
    b_down,
    gain_two,
    shift_two,
):
    token_rows = inputs[0].astype(jnp.float32)
    row_length = token_rows.shape[0]
    model_width = token_rows.shape[1]
    allowed, keeping = row_masks(seg_lengths[0], valid_len[0], row_length)
    full_qkv, full_bqkv, full_out, full_bout, full_gain, full_shift = pull_group(
        w_qkv, b_qkv, w_out, b_out, gain_one, shift_one
    )
    normed, norm_back = jax.vjp(
        layer_norm, token_rows, full_gain.astype(jnp.float32), full_shift.astype(jnp.float32)
    )
    normed_low = normed.astype(jnp.bfloat16)
    projected = jnp.dot(
        normed_low, full_qkv, preferred_element_type=jnp.float32
    ) + full_bqkv.astype(jnp.float32)
    query_feat, query_back = jax.vjp(feature_map, projected[:, :model_width])
    key_feat, key_back = jax.vjp(feature_map, projected[:, model_width : 2 * model_width])
    query_heads = split_heads(query_feat.astype(jnp.bfloat16))
    key_heads = split_heads(key_feat.astype(jnp.bfloat16))
    value_heads = split_heads(projected[:, 2 * model_width :].astype(jnp.bfloat16))
    numerator, denominator = lax.map(
        partial(head_forward, allowed), (query_heads, key_heads, value_heads)
    )
    attended = keeping[None, :, None] * numerator / denominator[:, :, None]
    attended_low = join_heads(attended).astype(jnp.bfloat16)
    middle = (
        token_rows
        + jnp.dot(attended_low, full_out, preferred_element_type=jnp.float32)
        + full_bout.astype(jnp.float32)
    )
    full_up, full_bup, full_down, full_bdown, full_gain_two, full_shift_two = pull_group(
        w_up, b_up, w_down, b_down, gain_two, shift_two
    )
    normed_two, norm_two_back = jax.vjp(
        layer_norm, middle, full_gain_two.astype(jnp.float32), full_shift_two.astype(jnp.float32)
    )
    normed_two_low = normed_two.astype(jnp.bfloat16)
    hidden = jnp.dot(normed_two_low, full_up, preferred_element_type=jnp.float32) + full_bup.astype(
        jnp.float32
    )
    activated, gelu_back = jax.vjp(gelu_tanh, hidden)
    activated_low = activated.astype(jnp.bfloat16)
    result = (
        middle
        + jnp.dot(activated_low, full_down, preferred_element_type=jnp.float32)
        + full_bdown.astype(jnp.float32)
    )
    again_up, again_bup, again_down, again_bdown, again_gain_two, again_shift_two = pull_group(
        w_up, b_up, w_down, b_down, gain_two, shift_two
    )
    grad_top = cotangent[0]
    grad_top_full = grad_top.astype(jnp.float32)
    grad_down = contract_rows(activated_low, grad_top)
    grad_bdown = jnp.sum(grad_top_full, axis=0)
    grad_hidden = gelu_back(contract_cols(grad_top, again_down))[0]
    grad_hidden_low = grad_hidden.astype(jnp.bfloat16)
    grad_bup = jnp.sum(grad_hidden_low.astype(jnp.float32), axis=0)
    grad_up = contract_rows(normed_two_low, grad_hidden_low)
    grad_normed_two = contract_cols(grad_hidden_low, again_up)
    grad_middle_norm, grad_gain_two, grad_shift_two = norm_two_back(grad_normed_two)
    grad_middle = grad_top_full + grad_middle_norm
    shard_up, shard_bup, shard_down, shard_small_two = push_group(
        grad_up, grad_bup, grad_down, jnp.stack([grad_bdown, grad_gain_two, grad_shift_two])
    )
    again_qkv, again_bqkv, again_out, again_bout, again_gain, again_shift = pull_group(
        w_qkv, b_qkv, w_out, b_out, gain_one, shift_one
    )
    grad_mixed = grad_middle.astype(jnp.bfloat16)
    grad_bout = jnp.sum(grad_mixed.astype(jnp.float32), axis=0)
    grad_wout = contract_rows(attended_low, grad_mixed)
    grad_attended = split_heads(contract_cols(grad_mixed, again_out))
    grad_numer = (keeping[None, :, None] * grad_attended / denominator[:, :, None]).astype(
        jnp.bfloat16
    )
    grad_denom = -jnp.sum(grad_attended * attended, axis=2) / denominator
    grad_query_heads, grad_key_heads, grad_value_heads = lax.map(
        partial(head_backward, allowed),
        (query_heads, key_heads, value_heads, grad_numer, grad_denom),
    )
    grad_query = query_back(join_heads(grad_query_heads))[0]
    grad_key = key_back(join_heads(grad_key_heads))[0]
    grad_projected = jnp.concatenate(
        [grad_query, grad_key, join_heads(grad_value_heads)], axis=1
    ).astype(jnp.bfloat16)
    grad_bias_all = jnp.sum(grad_projected.astype(jnp.float32), axis=0)
    grad_bias_qk = grad_bias_all[: 2 * model_width]
    grad_bias_v = grad_bias_all[2 * model_width :]
    grad_qkv = contract_rows(normed_low, grad_projected)
    grad_normed = contract_cols(grad_projected, again_qkv)
    grad_rows_norm, grad_gain_one, grad_shift_one = norm_back(grad_normed)
    grad_inputs = (grad_middle + grad_rows_norm).astype(jnp.bfloat16)
    shard_qkv, shard_bias_qk, shard_wout, shard_small_one = push_group(
        grad_qkv,
        grad_bias_qk,
        grad_wout,
        jnp.stack([grad_bout, grad_bias_v, grad_gain_one, grad_shift_one]),
    )
    return (
        result.astype(jnp.bfloat16)[None],
        grad_inputs[None],
        shard_qkv,
        shard_bias_qk,
        shard_small_one[1],
        shard_wout,
        shard_small_one[0],
        shard_small_one[2],
        shard_small_one[3],
        shard_up,
        shard_bup,
        shard_down,
        shard_small_two[0],
        shard_small_two[1],
        shard_small_two[2],
    )


HALF_LANES = 64
TILE = 512
Z_HIGH, Z_LOW, Y_BIT, X_BIT = 8, 4, 2, 1
MIXED = ((Z_HIGH, X_BIT, Z_LOW, Y_BIT), (Z_HIGH, Y_BIT, Z_LOW, X_BIT))
LINED = ((Z_HIGH, Z_LOW, X_BIT, Y_BIT), (Z_HIGH, Z_LOW, Y_BIT, X_BIT))
SMALL = 128
GROUP = 16
ANY = pl.BlockSpec(memory_space=pl.ANY)
SMEM = pl.BlockSpec(memory_space=pltpu.SMEM)
VMEM = pl.BlockSpec(memory_space=pltpu.VMEM)
MIB = 1 << 20


def swap_chips(block, bit):
    return lax.ppermute(block, "fsdp", [(place, place ^ bit) for place in range(16)])


def swap_cores(block):
    return lax.ppermute(block, "dp", [(0, 1), (1, 0)])


def relative_place(order, slot, last):
    return (
        order[0] * (slot & 1)
        + order[1] * ((slot >> 1) & 1)
        + order[2] * ((slot >> 2) & 1)
        + order[3] * last
    )


def tie(*blocks):
    return lax.optimization_barrier(blocks)


def by_side(shard):
    half = shard.shape[1] // 2
    return shard[None, :, :half], shard[None, :, half:]


def swap_sides(sides, orders, step):
    first, second = orders[0][step], orders[1][step]
    if first == second:
        return (swap_chips(jnp.stack(sides), first),)
    return swap_chips(sides[0], first), swap_chips(sides[1], second)


def sides_of(arrived):
    return (arrived[0][0], arrived[0][1]) if len(arrived) == 1 else arrived


def grown(sides, arrived):
    return tuple(jnp.concatenate([held, more]) for held, more in zip(sides, sides_of(arrived)))


def swap_both(sides):
    return swap_cores(sides[0]), swap_cores(sides[1])


def pieces_of(held, plane, across, core_held, core_across):
    plane = sides_of(plane)
    return tuple(
        block
        for side in range(2)
        for block in (held[side], plane[side], across[side], core_held[side], core_across[side])
    )


def added(parts, start, stop):
    return sum(part[start:stop].astype(jnp.float32) for part in parts)


def reduce_step(sides, orders, step, amount):
    sent = [added(parts, amount, 2 * amount).astype(jnp.bfloat16) for parts in sides]
    return swap_sides(sent, orders, step)


def with_arrived(sides, arrived):
    return [parts + [more] for parts, more in zip(sides, sides_of(arrived))]


def reduce_end(sides, orders):
    sides = with_arrived(sides, reduce_step(sides, orders, 0, 1))
    return [added(parts, 0, 1)[0] for parts in sides]


def side_by_side(sides, start, stop):
    return jnp.concatenate([side[:, start:stop] for side in sides], axis=1)


def far(array):
    return pltpu.with_memory_space_constraint(array, pltpu.HBM)


def call(kernel, outs, scratch, mib, args, in_specs, out_specs, grid=None, flops=0, gates=()):
    inputs, ignored = len(in_specs), len(gates)

    def gated(*refs):
        kernel(*refs[:inputs], *refs[inputs + ignored :])

    extra = {} if grid is None else {"grid": grid}
    near = (SMEM,) if grid else (SMEM, VMEM)
    args = [arg if spec in near else far(arg) for arg, spec in zip(args, in_specs)]
    gates = [far(gate) for gate in gates]
    if isinstance(outs, tuple):
        outs = tuple(
            out if spec in near else pltpu.HBM(out.shape, out.dtype)
            for out, spec in zip(outs, out_specs)
        )
    return pl.pallas_call(
        gated,
        out_shape=outs,
        in_specs=list(in_specs) + [ANY] * ignored,
        out_specs=out_specs,
        scratch_shapes=scratch,
        compiler_params=pltpu.CompilerParams(vmem_limit_bytes=mib * MIB),
        cost_estimate=pl.CostEstimate(flops=flops, bytes_accessed=0, transcendentals=0),
        **extra,
    )(*args, *gates)


def shaped(shape, dtype):
    return jax.ShapeDtypeStruct(shape, dtype)


def dot_nn(left, right):
    return lax.dot_general(left, right, (((1,), (0,)), ((), ())), preferred_element_type=jnp.float32)


def dot_nt(left, right):
    return lax.dot_general(left, right, (((1,), (1,)), ((), ())), preferred_element_type=jnp.float32)


def piece_at(pieces, side, core, last, slot):
    mine = pieces[5 * side : 5 * side + 5]
    if core or last:
        return mine[1 + core * 2 + last], slot
    return mine[slot // 4], slot % 4


def fetch(place, pieces, whole, sems, skip=0, orders=LINED):
    rows, half = pieces[0].shape[1], whole.shape[1] // 2
    copies = []
    for side, order in enumerate(orders):
        for core in range(2):
            for last in range(2):
                for slot in range(8):
                    piece, index = piece_at(pieces, side, core, last, slot)
                    owner = (place[1] ^ core) * 16 + (place[0] ^ relative_place(order, slot, last))
                    start = pl.multiple_of(owner * rows, rows)
                    copies.append(
                        pltpu.make_async_copy(
                            piece.at[index, :, pl.ds(skip, half)],
                            whole.at[pl.ds(start, rows), pl.ds(side * half, half)],
                            sems.at[len(copies)],
                        )
                    )
    for copy in copies:
        copy.start()
    return copies


def wait_side(copies, side):
    half = len(copies) // 2
    wait_all(copies[side * half : (side + 1) * half])


def wait_all(copies):
    for copy in copies:
        copy.wait()


def standardize(block):
    centred = block - jnp.mean(block, axis=1, keepdims=True)
    scale = lax.rsqrt(jnp.mean(centred * centred, axis=1, keepdims=True) + norm_eps)
    return centred * scale, scale


def norm_pull(grad, standard, scale, gain):
    scaled = grad * gain
    return scale * (
        scaled
        - jnp.mean(scaled, axis=1, keepdims=True)
        - standard * jnp.mean(scaled * standard, axis=1, keepdims=True)
    )


def place_kernel(where, lengths, valid, place):
    place[0] = where[0] & 15
    place[1] = where[0] >> 4
    end = lengths[0, 0]
    place[2] = end
    for image in range(1, 3):
        end = end + lengths[0, image]
        place[2 + image] = end
    place[5] = valid[0]


def run_place(where, lengths, valid):
    return call(
        place_kernel,
        shaped((6,), jnp.int32),
        [],
        8,
        (where, lengths, valid),
        in_specs=[SMEM] * 3,
        out_specs=SMEM,
    )


def fetch_small(place, pieces, small, skip, sems):
    copies = []
    for core in range(2):
        for last in range(2):
            for slot in range(8):
                piece, index = piece_at(pieces, 0, core, last, slot)
                far = relative_place(LINED[0], slot, last)
                owner = (place[1] ^ core) * 16 + (place[0] ^ far)
                start = pl.multiple_of(owner * GROUP, GROUP)
                copies.append(
                    pltpu.make_async_copy(
                        piece.at[index, pl.ds(0, GROUP), pl.ds(skip, SMALL)],
                        small.at[pl.ds(start, GROUP), :],
                        sems.at[len(copies)],
                    )
                )
                copies[-1].start()
    return copies


def tables(each):
    total = 32 * each
    column = lax.broadcasted_iota(jnp.int32, (1, total), 1).astype(jnp.float32)
    turn = jnp.floor((column + 0.5) / each)
    lane = lax.broadcasted_iota(jnp.int32, (SMALL, 1), 0).astype(jnp.float32)
    spread = jnp.where(column - turn * each == lane, 1.0, 0.0).astype(jnp.bfloat16)
    owner = lax.broadcasted_iota(jnp.int32, (32, 1), 0).astype(jnp.float32)
    return owner == turn, spread


def unfold(small, each, rows):
    mine, spread = tables(each)
    lines = []
    for row in rows:
        parts = small[pl.ds(row, 32, stride=GROUP), :].astype(jnp.bfloat16)
        parts = jnp.where(mine, dot_nn(parts, spread), 0.0)
        lines.append(jnp.sum(parts, axis=0, keepdims=True))
    return lines


def fold(small, each, vectors):
    mine, spread = tables(each)
    for row, vector in vectors:
        parts = jnp.where(mine, vector, 0.0).astype(jnp.bfloat16)
        small[pl.ds(row, 32, stride=32), :] = dot_nt(parts, spread)


def qkv_kernel(place, rows_in, *rest):
    pieces, (normed, query, key, value), lines, rest = rest[:10], rest[10:14], rest[14:20], rest[20:]
    whole, small, smalls, bias, sems, more = rest
    few = fetch_small(place, pieces, small, 4 * whole.shape[1] // 6, more)
    copies = fetch(place, pieces, whole, sems)
    wait_all(few)
    smalls[...] = small[...].astype(jnp.float32)
    width = rows_in.shape[1]
    (bias[...],) = unfold(smalls, 3 * width // 32, (0,))
    (lines[5][...],) = unfold(smalls, 4 * width // 32, (4,))
    bias_out, gain, shift, bias_down, gain_two, shift_two = unfold(
        smalls, width // 32, (1, 2, 3, 5, 6, 7)
    )
    for goal, line in zip(lines, (gain, bias_out, gain_two, shift_two, bias_down)):
        goal[...] = line
    for part in range(4):
        at = pl.ds(part * 128, 128)
        standard, _ = standardize(rows_in[at, :].astype(jnp.float32))
        normed[at, :] = (standard * gain + shift).astype(jnp.bfloat16)
    for tile in range(6):
        if tile % 3 == 0:
            wait_side(copies, tile // 3)
        cols = pl.ds(tile * TILE, TILE)
        projected = dot_nn(normed[...], whole[:, cols]) + bias[:, cols]
        goal = (query, key, value)[tile // 2]
        if tile < 4:
            projected = feature_map(projected)
        goal[:, pl.ds((tile % 2) * TILE, TILE)] = projected.astype(jnp.bfloat16)


def run_qkv(place, rows_in, pieces, gates=()):
    length, width = rows_in.shape
    narrow = shaped((length, width), jnp.bfloat16)
    line = shaped((1, width), jnp.float32)
    return call(
        qkv_kernel,
        (narrow,) * 4 + (line,) * 5 + (shaped((1, 4 * width), jnp.float32),),
        [
            pltpu.VMEM((width, 3 * width), jnp.bfloat16),
            pltpu.VMEM((32 * GROUP, SMALL), jnp.bfloat16),
            pltpu.VMEM((32 * GROUP, SMALL), jnp.float32),
            pltpu.VMEM((1, 3 * width), jnp.float32),
            pltpu.SemaphoreType.DMA((64,)),
            pltpu.SemaphoreType.DMA((32,)),
        ],
        18,
        (place, rows_in, *pieces),
        in_specs=[SMEM, VMEM] + [ANY] * 10,
        out_specs=(VMEM,) * 10,
        gates=gates,
    )


def image_of(place, positions):
    image = jnp.zeros(positions.shape, jnp.int32)
    for end in range(2, 5):
        image = image + jnp.where(positions >= place[end], 1, 0)
    return image


def allowed_block(place, length, flipped):
    first = lax.broadcasted_iota(jnp.int32, (length, 1), 0)
    second = lax.broadcasted_iota(jnp.int32, (1, length), 1)
    same = image_of(place, first) == image_of(place, second)
    ordered = (first <= second) if flipped else (second <= first)
    return jnp.where(same & ordered, 1.0, 0.0).astype(jnp.float32)


def low_lanes():
    return lax.broadcasted_iota(jnp.int32, (1, 2 * HALF_LANES), 1) < HALF_LANES


def two_heads(block):
    low = jnp.where(low_lanes(), 1.0, 0.0)
    high = (1.0 - low).astype(jnp.bfloat16)
    return jnp.concatenate([block * low.astype(jnp.bfloat16), block * high], axis=0)


def one_pair(stacked):
    half = stacked.shape[0] // 2
    return jnp.where(low_lanes(), stacked[:half], stacked[half:])


def masked(stacked, allowed):
    half = stacked.shape[0] // 2
    return jnp.concatenate(
        [(stacked[:half] * allowed).astype(jnp.bfloat16), (stacked[half:] * allowed).astype(jnp.bfloat16)],
        axis=0,
    )


def keeping_rows(place, start, amount):
    position = lax.broadcasted_iota(jnp.int32, (amount, 1), 0) + start
    return jnp.where(position < place[5], 1.0, 0.0)


def attend_kernel(place, query, key, value, attended, exact, inverse, allowed, wide):
    length, width = query.shape
    step = length // 2

    @pl.when(pl.program_id(0) == 0)
    def _():
        allowed[...] = allowed_block(place, length, False)
        wide[:, width:] = jnp.ones((length, width), jnp.bfloat16)

    wide[:, :width] = value[...]
    for part in range(2):
        rows, seen = pl.ds(part * step, step), (part + 1) * step
        scores = dot_nt(two_heads(query[rows, :]), key[:seen, :])
        total = dot_nn(masked(scores, allowed[rows, :seen]), wide[:seen, :])
        over = 1.0 / (one_pair(total[:, width:]) + denom_eps)
        inverse[rows, :] = over
        mixed = keeping_rows(place, part * step, step) * one_pair(total[:, :width]) * over
        exact[rows, :] = mixed
        attended[rows, :] = mixed.astype(jnp.bfloat16)


def run_attend(place, query, key, value, gates=()):
    length, width = query.shape
    pair = pl.BlockSpec((length, 2 * HALF_LANES), lambda p: (0, p))
    return call(
        attend_kernel,
        (
            shaped((length, width), jnp.bfloat16),
            shaped((length, width), jnp.float32),
            shaped((length, width), jnp.float32),
        ),
        [
            pltpu.VMEM((length, length), jnp.float32),
            pltpu.VMEM((length, 4 * HALF_LANES), jnp.bfloat16),
        ],
        10,
        (place, query, key, value),
        grid=(width // (2 * HALF_LANES),),
        in_specs=[SMEM] + [pair] * 3,
        out_specs=(pair,) * 3,
        gates=gates,
    )


def attend_back_pair(
    place, query, key, value, grad_att, exact, inverse, stacked, sums, allowed, flipped, left, wide
):
    length, width = query.shape
    step = length // 2
    wide[:, :width] = value[...]
    over = grad_att[...] * inverse[...]
    lane = lax.broadcasted_iota(jnp.int32, (1, width), 1)
    terms, low = over * exact[...], lane < HALF_LANES
    first = jnp.sum(jnp.where(low, terms, 0.0), axis=1, keepdims=True)
    second = jnp.sum(jnp.where(low, 0.0, terms), axis=1, keepdims=True)
    spread = -jnp.where(low, first, second)
    high = spread.astype(jnp.bfloat16).astype(jnp.float32)
    within = lane & (HALF_LANES - 1)
    spread = jnp.where(within == 0, high, jnp.where(within == 1, spread - high, 0.0))
    numer = (keeping_rows(place, 0, length) * over).astype(jnp.bfloat16)
    for head in range(2):
        here = jnp.where(low, 1.0 - head, 1.0 * head)
        at = pl.ds(head * length, length)
        left[at, :width] = numer * here.astype(jnp.bfloat16)
        left[at, width:] = (spread * here).astype(jnp.bfloat16)
    for part in range(2):
        rows, seen = pl.ds(part * step, step), (part + 1) * step
        start = part * step
        later = pl.ds(start, length - start)
        both = jnp.concatenate([left[rows, :], left[pl.ds(length + start, step), :]], axis=0)
        grad_scores = masked(dot_nt(both, wide[:seen, :]), allowed[rows, :seen])
        grad_query = one_pair(dot_nn(grad_scores, key[:seen, :]))
        full = left[later, :] + left[pl.ds(length + start, length - start), :]
        scores = masked(dot_nt(two_heads(key[rows, :]), query[later, :]), flipped[rows, later])
        grad_value = one_pair(dot_nn(scores, full[:, :width]))
        ones = jnp.concatenate([two_heads(value[rows, :]), two_heads(wide[rows, width:])], axis=1)
        grad_scores = masked(dot_nt(ones, full), flipped[rows, later])
        grad_key = one_pair(dot_nn(grad_scores, query[later, :]))
        grads = (
            grad_query * jnp.minimum(query[rows, :].astype(jnp.float32), 1.0),
            grad_key * jnp.minimum(key[rows, :].astype(jnp.float32), 1.0),
            grad_value,
        )
        for index, grad in enumerate(grads):
            low_grad, line = grad.astype(jnp.bfloat16), pl.ds(index, 1)
            stacked[index, rows, :] = low_grad
            extra = jnp.sum(low_grad.astype(jnp.float32), axis=0, keepdims=True)
            sums[line, :] = extra if part == 0 else sums[line, :] + extra


def attend_back_kernel(
    place, query, key, value, grad_att, exact, inverse, stacked, sums, allowed, flipped, left, wide
):
    length, width = query.shape[0], 2 * HALF_LANES
    pairs = query.shape[1] // width

    @pl.when(pl.program_id(0) == 0)
    def _():
        allowed[...] = allowed_block(place, length, False)
        flipped[...] = allowed_block(place, length, True)
        for pair in range(pairs):
            wide[pair, :, width:] = jnp.ones((length, width), jnp.bfloat16)

    for pair in range(pairs):
        cols = pl.ds(pair * width, width)
        attend_back_pair(
            place,
            *(ref.at[:, cols] for ref in (query, key, value, grad_att, exact, inverse)),
            stacked.at[:, :, cols],
            sums.at[:, cols],
            allowed,
            flipped,
            left.at[pair],
            wide.at[pair],
        )


def run_attend_back(place, first, query, key, value, grad_att, exact, inverse, gates=()):
    length, width = query.shape
    half = width // 2
    start = first * half // (4 * HALF_LANES)
    pair = pl.BlockSpec((length, 4 * HALF_LANES), lambda p: (0, p + start))
    stack = pl.BlockSpec((3, length, 4 * HALF_LANES), lambda p: (0, 0, p))
    lines = pl.BlockSpec((3, 4 * HALF_LANES), lambda p: (0, p))
    return call(
        attend_back_kernel,
        (shaped((3, length, half), jnp.bfloat16), shaped((3, half), jnp.float32)),
        [
            pltpu.VMEM((length, length), jnp.float32),
            pltpu.VMEM((length, length), jnp.float32),
            pltpu.VMEM((2, 2 * length, 4 * HALF_LANES), jnp.bfloat16),
            pltpu.VMEM((2, length, 4 * HALF_LANES), jnp.bfloat16),
        ],
        20,
        (place, query, key, value, grad_att, exact, inverse),
        grid=(half // (4 * HALF_LANES),),
        in_specs=[SMEM] + [pair] * 6,
        out_specs=(stack, lines),
        gates=gates,
    )


def hand_over(place, sources, goal, sems):
    copies, at = [], 0
    for source in sources:
        half = source.shape[1] // 2
        start = pl.multiple_of((1 - place[1]) * half, half)
        copies.append(
            pltpu.make_async_copy(
                source.at[:, pl.ds(start, half)], goal.at[:, pl.ds(at, half)], sems.at[len(copies)]
            )
        )
        copies[-1].start()
        at += half
    return copies


def out_kernel(place, rows_in, early, attended, bias, gain, shift, *rest):
    pieces, (middle, normed, handed, whole, sems, more) = rest[:10], rest[10:]
    copies = fetch(place, pieces, whole, sems, 3 * whole.shape[1] // 2)
    handing = hand_over(place, (early, attended), handed, more)
    for side in range(2):
        wait_side(copies, side)
        cols = pl.ds(side * TILE, TILE)
        middle[:, cols] = (
            rows_in[:, cols].astype(jnp.float32) + dot_nn(attended[...], whole[:, cols]) + bias[:, cols]
        )
    for part in range(4):
        at = pl.ds(part * 128, 128)
        standard, _ = standardize(middle[at, :])
        normed[at, :] = (standard * gain[...] + shift[...]).astype(jnp.bfloat16)
    wait_all(handing)


def run_out(place, rows_in, early, attended, bias, gain, shift, pieces, gates=()):
    length, width = rows_in.shape
    narrow = shaped((length, width), jnp.bfloat16)
    return call(
        out_kernel,
        (shaped((length, width), jnp.float32), narrow, narrow),
        [
            pltpu.VMEM((width, width), jnp.bfloat16),
            pltpu.SemaphoreType.DMA((64,)),
            pltpu.SemaphoreType.DMA((2,)),
        ],
        16,
        (place, rows_in, early, attended, bias, gain, shift, *pieces),
        in_specs=[SMEM] + [VMEM] * 6 + [ANY] * 10,
        out_specs=(VMEM, VMEM, ANY),
        gates=gates,
    )


def bend_tile(hidden, activated, slope):
    square = hidden * hidden
    rate = gelu_coef + (gelu_coef * 0.044715) * square
    bend = jnp.tanh(hidden * rate)
    share = 0.5 + 0.5 * bend
    activated[...] = (hidden * share).astype(jnp.bfloat16)
    rate = gelu_coef + (3.0 * gelu_coef * 0.044715) * square
    slope[...] = (share + (0.5 * hidden) * (1.0 - bend * bend) * rate).astype(jnp.bfloat16)


def up_kernel(place, normed, bias, *rest):
    pieces, (activated, slope, handed, whole, hidden, sems, more) = rest[:10], rest[10:]
    copies = fetch(place, pieces, whole, sems)
    tiles = whole.shape[1] // TILE

    def columns(tile):
        return pl.ds(tile * TILE, TILE)

    for tile in range(tiles + 1):
        if tile % (tiles // 2) == 0 and tile < tiles:
            wait_side(copies, tile // (tiles // 2))
        if tile < tiles:
            cols = columns(tile)
            hidden[tile % 2] = dot_nn(normed[...], whole[:, cols]) + bias[:, cols]
        if tile > 0:
            cols = columns(tile - 1)
            bend_tile(hidden[(tile - 1) % 2], activated.at[:, cols], slope.at[:, cols])

    wait_all(hand_over(place, (normed, activated), handed, more))


def run_up(place, normed, bias, pieces, gates=()):
    length, width = normed.shape
    wide = bias.shape[1]
    return call(
        up_kernel,
        (shaped((length, wide), jnp.bfloat16),) * 2
        + (shaped((length, (width + wide) // 2), jnp.bfloat16),),
        [
            pltpu.VMEM((width, wide), jnp.bfloat16),
            pltpu.VMEM((2, length, TILE), jnp.float32),
            pltpu.SemaphoreType.DMA((64,)),
            pltpu.SemaphoreType.DMA((2,)),
        ],
        26,
        (place, normed, bias, *pieces),
        in_specs=[SMEM] + [VMEM] * 2 + [ANY] * 10,
        out_specs=(VMEM, VMEM, ANY),
        gates=gates,
    )


def sum_kernel(block, total):
    total[...] = jnp.sum(block[...].astype(jnp.float32), axis=0, keepdims=True)


def run_sum(block, cover, gates=()):
    return call(
        sum_kernel,
        shaped((1, block.shape[1]), jnp.float32),
        [],
        8,
        (block,),
        in_specs=[VMEM],
        out_specs=VMEM,
        flops=cover,
        gates=gates,
    )


def down_kernel(place, activated, slope, grad_top, middle, bias, *rest):
    pieces, (result, grad_hidden, sum_up, whole, sems) = rest[:10], rest[10:]
    copies = fetch(place, pieces, whole, sems, orders=MIXED)
    wait_all(copies)
    for tile in range(4):
        cols = pl.ds(tile * 256, 256)
        result[:, cols] = (
            middle[:, cols] + bias[:, cols] + dot_nn(activated[...], whole[:, cols])
        ).astype(jnp.bfloat16)
        for half in range(2):
            cols = pl.ds((2 * tile + half) * TILE, TILE)
            grad = dot_nt(grad_top[...], whole[cols, :]) * slope[:, cols].astype(jnp.float32)
            low = grad.astype(jnp.bfloat16)
            grad_hidden[:, cols] = low
            sum_up[:, cols] = jnp.sum(low.astype(jnp.float32), axis=0, keepdims=True)


def run_down(place, activated, slope, grad_top, middle, bias, pieces, gates=()):
    length, width = middle.shape
    wide = activated.shape[1]
    return call(
        down_kernel,
        (
            shaped((length, width), jnp.bfloat16),
            shaped((length, wide), jnp.bfloat16),
            shaped((1, wide), jnp.float32),
        ),
        [
            pltpu.VMEM((wide, width), jnp.bfloat16),
            pltpu.SemaphoreType.DMA((64,)),
        ],
        30,
        (place, activated, slope, grad_top, middle, bias, *pieces),
        in_specs=[SMEM] + [VMEM] * 5 + [ANY] * 10,
        out_specs=(VMEM,) * 3,
        flops=64 * length * width * wide,
        gates=gates,
    )


def middle_back_kernel(place, grad_hidden, middle, grad_top, gain, *rest):
    pieces_up, pieces_in, rest = rest[:10], rest[10:20], rest[20:]
    grad_middle, mixed, grad_att, sum_gain, sum_shift, whole, outer, total, sems, more = rest
    copies = fetch(place, pieces_up, whole, sems)
    second = fetch(place, pieces_in, outer, more, 3 * outer.shape[1] // 2)
    step = 2 * TILE
    for tile in range(whole.shape[1] // step):
        if tile % 2 == 0:
            wait_side(copies, tile // 2)
        cols = pl.ds(tile * step, step)
        block = dot_nt(grad_hidden[:, cols], whole[:, cols])
        total[...] = block if tile == 0 else total[...] + block

    for part in range(4):
        at = pl.ds(part * 128, 128)
        grad = total[at, :]
        standard, scale = standardize(middle[at, :])
        back = grad_top[at, :].astype(jnp.float32) + norm_pull(grad, standard, scale, gain[...])
        grad_middle[at, :] = back
        low = back.astype(jnp.bfloat16)
        mixed[at, :] = low
        for goal, added in ((sum_gain, grad * standard), (sum_shift, grad)):
            added = jnp.sum(added, axis=0, keepdims=True)
            goal[...] = added if part == 0 else goal[...] + added
    wait_all(second)
    for part in range(2):
        cols = pl.ds(part * TILE, TILE)
        grad_att[:, cols] = dot_nt(mixed[...], outer[cols, :])


def run_middle_back(place, grad_hidden, middle, grad_top, gain, pieces_up, pieces_in, gates=()):
    length, width = middle.shape
    wide = grad_hidden.shape[1]
    full, line = shaped((length, width), jnp.float32), shaped((1, width), jnp.float32)
    return call(
        middle_back_kernel,
        (full, shaped((length, width), jnp.bfloat16), full, line, line),
        [
            pltpu.VMEM((width, wide), jnp.bfloat16),
            pltpu.VMEM((width, width), jnp.bfloat16),
            pltpu.VMEM((length, width), jnp.float32),
            pltpu.SemaphoreType.DMA((64,)),
            pltpu.SemaphoreType.DMA((64,)),
        ],
        30,
        (place, grad_hidden, middle, grad_top, gain, *pieces_up, *pieces_in),
        in_specs=[SMEM] + [VMEM] * 4 + [ANY] * 20,
        out_specs=(VMEM,) * 5,
        gates=gates,
    )


def inputs_back_kernel(place, early, late, rows_in, gain, grad_middle, sum_out, *rest):
    (sums, late_sums, *ready), pieces, rest = rest[:6], rest[6:16], rest[16:]
    grad_rows, lines, whole, total, sems = rest
    copies = fetch(place, pieces, whole, sems)
    width = rows_in.shape[1]
    for tile in range(6):
        if tile % 3 == 0:
            wait_side(copies, tile // 3)
        grads = (early, late)[tile % 2]
        block = dot_nt(grads[tile // 2], whole[:, pl.ds(tile * TILE, TILE)])
        total[...] = block if tile == 0 else total[...] + block
    for part in range(4):
        at = pl.ds(part * 128, 128)
        grad = total[at, :]
        standard, scale = standardize(rows_in[at, :].astype(jnp.float32))
        back = grad_middle[at, :] + norm_pull(grad, standard, scale, gain[...])
        grad_rows[at, :] = back.astype(jnp.bfloat16)
        for index, extra in enumerate((grad * standard, grad)):
            goal = lines.at[:, pl.ds((4 + index) * width, width)]
            extra = jnp.sum(extra, axis=0, keepdims=True)
            goal[...] = extra if part == 0 else goal[...] + extra
    half = width // 2
    for row in range(3):
        for index, source in enumerate((sums, late_sums)):
            lines[:, pl.ds(row * width + index * half, half)] = source[pl.ds(row, 1), :]
    lines[:, pl.ds(3 * width, width)] = sum_out[...]
    at = 6 * width
    for source in ready:
        lines[:, pl.ds(at, source.shape[1])] = source[...]
        at += source.shape[1]


def run_inputs_back(
    place, early, late, rows_in, gain, grad_middle, sum_out, ready, pieces, gates=()
):
    length, width = rows_in.shape
    total = 6 * width + sum(line.shape[1] for line in ready[2:])
    return call(
        inputs_back_kernel,
        (shaped((length, width), jnp.bfloat16), shaped((1, total), jnp.float32)),
        [
            pltpu.VMEM((width, 3 * width), jnp.bfloat16),
            pltpu.VMEM((length, width), jnp.float32),
            pltpu.SemaphoreType.DMA((64,)),
        ],
        20,
        (place, early, late, rows_in, gain, grad_middle, sum_out, *ready, *pieces),
        in_specs=[SMEM] + [VMEM] * 12 + [ANY] * 10,
        out_specs=(VMEM,) * 2,
        flops=1 << 40,
        gates=gates,
    )


def weight_kernel(orders, skips, sizes, place, *rest):
    groups = len(skips)
    if sizes:
        mine, other_lines, rest = rest[4 * groups], rest[4 * groups + 1], rest[: 4 * groups] + rest[4 * groups + 2 :]
    inputs, outs, rest = rest[: 4 * groups], rest[4 * groups : 4 * groups + 4], rest[4 * groups + 4 :]
    wholes, (turned, sems), rest = rest[:groups], rest[groups : groups + 2], rest[groups + 2 :]
    length, rows = inputs[0].shape[0], outs[0].shape[1]
    owners = 256 // rows
    at, copies = 0, []
    for group, (skip, whole) in enumerate(zip(skips, wholes)):
        left_own, left_other, own, other = inputs[4 * group : 4 * group + 4]
        count, each = own.shape[0], own.shape[2]
        tiles, half = whole.shape[0], whole.shape[2] // 2
        for tile in range(tiles):
            low = pl.multiple_of(((place[0] // owners) ^ tile) * 256, 256)
            start = pl.multiple_of(place[1] * (256 * tiles) + low, 256)
            left = turned.at[tile % 2]
            left[:, :length] = left_own[:, pl.ds(start, 256)].T
            left[:, length:] = left_other[:, pl.ds(skip + low, 256)].T
            for index in range(count):
                for step in range(each // TILE):
                    cols = pl.ds(step * TILE, TILE)
                    block = dot_nn(left[:, :length], own[index, :, cols])
                    block += dot_nn(left[:, length:], other[index, :, cols])
                    goal = pl.ds(index * each + step * TILE, TILE)
                    whole[tile, :, goal] = block.astype(jnp.bfloat16)
            for side, order in enumerate(orders):
                for last in range(2):
                    for slot in range(8):
                        far_place = relative_place(order, slot, last)
                        if far_place // owners != tile:
                            continue
                        start = pl.multiple_of(((place[0] ^ far_place) % owners) * rows, rows)
                        copies.append(
                            pltpu.make_async_copy(
                                whole.at[tile, pl.ds(start, rows), pl.ds(side * half, half)],
                                outs[last * 2 + side].at[slot, :, pl.ds(at, half)],
                                sems.at[len(copies)],
                            )
                        )
                        copies[-1].start()
        at += half
    if sizes:
        wide_small, small, more = rest
        wide_small[...] = jnp.zeros_like(wide_small)
        start, by_size = 0, {}
        for row, size in enumerate(sizes):
            line = mine[:, start : start + size] + other_lines[:, start : start + size]
            by_size.setdefault(size, []).append((row, line))
            start += size
        for size, vectors in by_size.items():
            fold(wide_small, size // 32, vectors)
        small[...] = wide_small[...].astype(jnp.bfloat16)
        for last in range(2):
            for slot in range(8):
                chip = place[0] ^ relative_place(orders[0], slot, last)
                start = pl.multiple_of((place[1] * 16 + chip) * 32, 32)
                copies.append(
                    pltpu.make_async_copy(
                        small.at[pl.ds(start, 32), :],
                        outs[last * 2].at[slot, :, pl.ds(at, SMALL)],
                        more.at[last * 8 + slot],
                    )
                )
                copies[-1].start()
    wait_all(copies)


def run_weight(place, orders, height, groups, gates=(), sizes=(), lines=()):
    length = groups[0][0].shape[0]
    totals = [own.shape[0] * own.shape[2] for _, _, _, own, _ in groups]
    half = sum(totals) // 2
    part = shaped((8, height // 16, half), jnp.bfloat16)
    first = shaped((8, height // 16, half + (SMALL if sizes else 0)), jnp.bfloat16)
    extra = [
        pltpu.VMEM((32 * 32, SMALL), jnp.float32),
        pltpu.VMEM((32 * 32, SMALL), jnp.bfloat16),
        pltpu.SemaphoreType.DMA((16,)),
    ]
    return call(
        partial(weight_kernel, orders, tuple(group[2] for group in groups), sizes),
        (first,) * 4,
        [pltpu.VMEM((height // 256, 256, total), jnp.bfloat16) for total in totals]
        + [
            pltpu.VMEM((2, 256, 2 * length), jnp.bfloat16),
            pltpu.SemaphoreType.DMA((32 * len(groups),)),
        ]
        + (extra if sizes else []),
        22,
        (place, *(array for group in groups for array in group[:2] + group[3:]), *lines),
        in_specs=[SMEM] + [VMEM] * (4 * len(groups) + len(lines)),
        out_specs=(ANY,) * 4,
        gates=gates,
    )


def paired_body(
    inputs,
    cotangent,
    seg_lengths,
    valid_len,
    w_qkv,
    b_qkv,
    w_out,
    b_out,
    gain_one,
    shift_one,
    w_up,
    b_up,
    w_down,
    b_down,
    gain_two,
    shift_two,
):
    where = (lax.axis_index("dp") * 16 + lax.axis_index("fsdp")).astype(jnp.int32)[None]
    rows_in, grad_top = inputs[0], cotangent[0]
    vectors = (b_qkv, b_out, gain_one, shift_one, b_up, b_down, gain_two, shift_two)
    cut = w_qkv.shape[1] // 2
    edge = w_out.shape[1] // 2
    held_in = (
        jnp.concatenate([w_qkv[:, :cut], w_out[:, :edge]], axis=1)[None],
        jnp.concatenate([w_qkv[:, cut:], w_out[:, edge:]], axis=1)[None],
    )
    small = jnp.stack([jnp.pad(vector, (0, SMALL - vector.shape[0])) for vector in vectors])
    small = jnp.pad(small, ((0, w_out.shape[0] - small.shape[0]), (0, 0)))[None]
    small_far = swap_chips(small, Z_HIGH)
    place = run_place(where, seg_lengths, valid_len)
    place, small_far = tie(place, small_far)
    small = jnp.concatenate([small, small_far])
    held_up, held_down = by_side(w_up), by_side(w_down)
    top = grad_top[None]
    held_in = grown(held_in, swap_sides(held_in, LINED, 0))
    held_in = (
        jnp.concatenate([held_in[0], small], axis=2),
        jnp.concatenate([held_in[1], jnp.zeros_like(small)], axis=2),
    )
    held_in = grown(held_in, swap_sides(held_in, LINED, 1))
    held_in, held_up = tie(held_in, held_up)
    start_up = swap_sides(held_up, LINED, 0)
    plane_in = swap_sides(held_in, LINED, 2)
    start_up, plane_in = tie(start_up, plane_in)
    held_up = grown(held_up, start_up)
    held_up, held_down = tie(held_up, held_down)
    full_in = grown(held_in, plane_in)
    across_in = swap_sides(full_in, LINED, 3)
    core_in = swap_both(full_in)
    held_up = grown(held_up, swap_sides(held_up, LINED, 1))
    start_down = swap_sides(held_down, LINED, 0)
    across_in, start_down = tie(across_in, start_down)
    pieces_in = pieces_of(held_in, plane_in, across_in, core_in, swap_both(across_in))
    plane_up = swap_sides(held_up, LINED, 2)
    held_down = grown(held_down, start_down)
    plane_down = swap_sides(held_down, MIXED, 1)
    top_other = swap_cores(top)

    normed, query, key, value, *lines = run_qkv(
        place, rows_in, pieces_in, (*held_up, *held_down, top_other)
    )
    full_gain, full_bout, full_gain_two, full_shift_two, full_bdown, full_bup = lines
    plane_up, plane_down, normed = tie(plane_up, plane_down, normed)
    full_up = grown(held_up, plane_up)
    across_up = swap_sides(full_up, LINED, 3)
    core_up = swap_both(full_up)
    held_down = grown(held_down, plane_down)
    line_down = swap_sides(held_down, MIXED, 2)
    attended, exact, inverse = run_attend(place, query, key, value, (*plane_up, *held_down))
    core_up, attended = tie(core_up, attended)
    middle, normed_two, inner_half = run_out(
        place,
        rows_in,
        normed,
        attended,
        full_bout,
        full_gain_two,
        full_shift_two,
        pieces_in,
    )
    inner_other = swap_cores(inner_half)
    across_up, line_down, normed_two = tie(across_up, line_down, normed_two)
    pieces_up = pieces_of(held_up, plane_up, across_up, core_up, swap_both(across_up))
    full_down = grown(held_down, line_down)
    across_down = swap_sides(full_down, MIXED, 3)
    core_down = swap_both(full_down)
    activated, slope, outer_half = run_up(
        place, normed_two, full_bup, pieces_up, (*line_down, inner_other)
    )
    outer_other = swap_cores(outer_half)
    sum_down = run_sum(grad_top, 1 << 40, (outer_half,))
    thin = normed_two.shape[1] // 2
    parts = run_weight(
        place,
        LINED,
        activated.shape[1] // 2,
        [(activated, outer_other, thin, top, top_other)],
        (*core_down, sum_down),
    )
    across_down, parts = tie(across_down, parts)
    down_one = swap_sides(parts[2:], LINED, 3)
    pieces_down = pieces_of(held_down, line_down, across_down, core_down, swap_both(across_down))
    result, grad_hidden, sum_up = run_down(
        place, activated, slope, grad_top, middle, full_bdown, pieces_down, parts[2:]
    )
    hidden_other = swap_cores(grad_hidden[None])
    grad_middle, mixed, grad_att, sum_gain_two, sum_shift_two = run_middle_back(
        place, grad_hidden, middle, grad_top, full_gain_two, pieces_up, pieces_in
    )
    mixed = mixed[None]
    down_one, mixed = tie(down_one, mixed)
    mixed_other = swap_cores(mixed)
    down_sides = with_arrived([[parts[0]], [parts[1]]], down_one)
    down_two = reduce_step(down_sides, LINED, 2, 4)
    sum_out = run_sum(mixed[0], 1 << 35, down_one)
    hidden_other, sum_out = tie(hidden_other, sum_out)
    parts = run_weight(
        place, LINED, thin, [(normed_two, outer_other, 0, grad_hidden[None], hidden_other)]
    )
    up_one = swap_sides(parts[2:], LINED, 3)
    grads, sums = run_attend_back(
        place, 0, query, key, value, grad_att, exact, inverse, parts[2:]
    )
    down_two, mixed_other, grads = tie(down_two, mixed_other, grads)
    down_sides = with_arrived(down_sides, down_two)
    down_three = reduce_step(down_sides, LINED, 1, 2)
    grads_other = swap_cores(grads)
    late, late_sums = run_attend_back(
        place, 1, query, key, value, grad_att, exact, inverse, (grads,)
    )
    up_one, down_three, late = tie(up_one, down_three, late)
    down_sides = with_arrived(down_sides, down_three)
    down_four = reduce_step(down_sides, LINED, 0, 1)
    up_sides = with_arrived([[parts[0]], [parts[1]]], up_one)
    late_other = swap_cores(late)
    up_two = reduce_step(up_sides, LINED, 2, 4)
    grad_rows, lines = run_inputs_back(
        place,
        grads,
        late,
        rows_in,
        full_gain,
        grad_middle,
        sum_out,
        (sums, late_sums, sum_up, sum_down, sum_gain_two, sum_shift_two),
        pieces_in,
        up_one,
    )
    up_two, down_four, grads_other, late_other, lines = tie(
        up_two, down_four, grads_other, late_other, lines
    )
    down_sides = with_arrived(down_sides, down_four)
    up_sides = with_arrived(up_sides, up_two)
    up_three = reduce_step(up_sides, LINED, 1, 2)
    lines_other = swap_cores(lines)
    parts = run_weight(
        place,
        MIXED,
        thin,
        [
            (normed, inner_other, 0, grads, grads_other),
            (attended, inner_other, thin, mixed, mixed_other),
        ],
    )
    lines_other, parts = tie(lines_other, parts)
    in_sides = [[parts[0]], [parts[1]]]
    in_one = swap_sides(parts[2:], MIXED, 3)
    narrow, wide = mixed.shape[2], sum_up.shape[1]
    sizes = (2 * narrow, narrow, narrow, narrow, narrow, wide, narrow, narrow, narrow)
    parts = run_weight(
        place,
        LINED,
        thin,
        [(normed, inner_other, 0, late, late_other)],
        parts[:1],
        sizes,
        (lines, lines_other),
    )
    up_three, parts = tie(up_three, parts)
    up_sides = with_arrived(up_sides, up_three)
    up_four = reduce_step(up_sides, LINED, 0, 1)
    late_sides = [[parts[0]], [parts[1]]]
    late_one = swap_sides(parts[2:], LINED, 3)
    in_sides = with_arrived(in_sides, in_one)
    late_one, down_sides = tie(late_one, down_sides)
    late_sides = with_arrived(late_sides, late_one)
    in_sides = with_arrived(in_sides, reduce_step(in_sides, MIXED, 2, 4))
    late_sides = with_arrived(late_sides, reduce_step(late_sides, LINED, 2, 4))
    up_sides = with_arrived(up_sides, up_four)
    in_sides = with_arrived(in_sides, reduce_step(in_sides, MIXED, 1, 2))
    late_sides = with_arrived(late_sides, reduce_step(late_sides, LINED, 1, 2))
    shard_down = side_by_side([added(parts, 0, 1)[0] for parts in down_sides], 0, edge)
    shard_up = side_by_side([added(parts, 0, 1)[0] for parts in up_sides], 0, w_up.shape[1] // 2)
    shards = reduce_end(in_sides, MIXED)
    cut = cut // 2
    first = side_by_side(shards, 0, cut)
    shard_out = side_by_side(shards, cut, cut + edge)
    shards = reduce_end(late_sides, LINED)
    second = side_by_side(shards, 0, cut)
    third = edge
    shard_qkv = jnp.concatenate(
        [
            half[:, part * third : (part + 1) * third]
            for part in range(3)
            for half in (first, second)
        ],
        axis=1,
    )
    smalls = [shards[0][row, cut : cut + size // 32] for row, size in enumerate(sizes)]
    grad_bqk, grad_bv, grad_bout, grad_gain, grad_shift, grad_bup, grad_bdown, grad_gain_two, grad_shift_two = smalls
    return (
        result[None],
        grad_rows[None],
        shard_qkv,
        grad_bqk,
        grad_bv,
        shard_out,
        grad_bout,
        grad_gain,
        grad_shift,
        shard_up,
        grad_bup,
        shard_down,
        grad_bdown,
        grad_gain_two,
        grad_shift_two,
    )


def solution(mesh):
    placed = (
        P(("dp", "fsdp"), None, None),
        P(("dp", "fsdp"), None, None),
        P(("dp", "fsdp"), None),
        P(("dp", "fsdp")),
        P(("dp", "fsdp"), None),
        P(("dp", "fsdp")),
        P(("dp", "fsdp"), None),
        P(("dp", "fsdp")),
        P(("dp", "fsdp")),
        P(("dp", "fsdp")),
        P(("dp", "fsdp"), None),
        P(("dp", "fsdp")),
        P(("dp", "fsdp"), None),
        P(("dp", "fsdp")),
        P(("dp", "fsdp")),
        P(("dp", "fsdp")),
    )
    paired = dict(mesh.shape) == {"dp": 2, "fsdp": 16}
    return jax.shard_map(
        paired_body if paired else plain_body,
        mesh=mesh,
        in_specs=placed,
        out_specs=(
            P(("dp", "fsdp"), None, None),
            P(("dp", "fsdp"), None, None),
            P(("dp", "fsdp"), None),
            P(("dp", "fsdp")),
            P(("dp", "fsdp")),
            P(("dp", "fsdp"), None),
            P(("dp", "fsdp")),
            P(("dp", "fsdp")),
            P(("dp", "fsdp")),
            P(("dp", "fsdp"), None),
            P(("dp", "fsdp")),
            P(("dp", "fsdp"), None),
            P(("dp", "fsdp")),
            P(("dp", "fsdp")),
            P(("dp", "fsdp")),
        ),
        check_vma=False,
    )
```

```python
from functools import partial

import jax
import jax.numpy as jnp
from jax import lax
from jax.experimental import pallas as pl
from jax.experimental.pallas import tpu as pltpu
from jax.sharding import PartitionSpec as P

HEADS = 16


norm_eps = 1e-05
denom_eps = 1e-06
gelu_coef = 0.7978845608028654


def layer_norm(values, scale_gain, offset):
    centred = values - jnp.mean(values, axis=-1, keepdims=True)
    spread = jnp.mean(centred * centred, axis=-1, keepdims=True)
    return centred * lax.rsqrt(spread + norm_eps) * scale_gain + offset


def feature_map(values):
    return jnp.where(values > 0, values + 1.0, jnp.exp(jnp.minimum(values, 0.0)))


def gelu_tanh(values):
    return (
        0.5 * values * (1.0 + jnp.tanh(gelu_coef * (values + 0.044715 * values * values * values)))
    )


def contract_rows(left_side, right_side):
    return lax.dot_general(
        left_side, right_side, (((0,), (0,)), ((), ())), preferred_element_type=jnp.float32
    )


def contract_cols(left_side, right_side):
    return lax.dot_general(
        left_side, right_side, (((1,), (1,)), ((), ())), preferred_element_type=jnp.float32
    )


def row_masks(lengths, valid_count, row_length):
    places = jnp.arange(row_length, dtype=jnp.int32)
    bounds = jnp.stack([jnp.sum(lengths[: end + 1]) for end in range(lengths.shape[0])])
    segment = jnp.sum((places[:, None] >= bounds[None, :]).astype(jnp.int32), axis=1)
    allowed = (segment[:, None] == segment[None, :]) & (places[None, :] <= places[:, None])
    keeping = (places < valid_count).astype(jnp.float32)
    return (allowed.astype(jnp.float32), keeping)


def split_heads(matrix):
    return jnp.transpose(matrix.reshape(matrix.shape[0], HEADS, -1), (1, 0, 2))


def join_heads(stacked):
    return jnp.transpose(stacked, (1, 0, 2)).reshape(stacked.shape[1], -1)


def pull_group(first, second, third, fourth, fifth, sixth):
    return (
        lax.all_gather(first, ("dp", "fsdp"), axis=0, tiled=True),
        lax.all_gather(second, ("dp", "fsdp"), axis=0, tiled=True),
        lax.all_gather(third, ("dp", "fsdp"), axis=0, tiled=True),
        lax.all_gather(fourth, ("dp", "fsdp"), axis=0, tiled=True),
        lax.all_gather(fifth, ("dp", "fsdp"), axis=0, tiled=True),
        lax.all_gather(sixth, ("dp", "fsdp"), axis=0, tiled=True),
    )


def push_group(first, second, third, stacked):
    return (
        lax.psum_scatter(first, ("dp", "fsdp"), scatter_dimension=0, tiled=True),
        lax.psum_scatter(second, ("dp", "fsdp"), scatter_dimension=0, tiled=True),
        lax.psum_scatter(third, ("dp", "fsdp"), scatter_dimension=0, tiled=True),
        lax.psum_scatter(stacked, ("dp", "fsdp"), scatter_dimension=1, tiled=True),
    )


def head_forward(allowed, head_item):
    query_head, key_head, value_head = head_item
    scores = contract_cols(query_head, key_head) * allowed
    denominator = jnp.sum(scores, axis=1) + denom_eps
    numerator = jnp.dot(scores.astype(jnp.bfloat16), value_head, preferred_element_type=jnp.float32)
    return (numerator, denominator)


def head_backward(allowed, head_item):
    query_head, key_head, value_head, grad_numer, grad_denom = head_item
    scores = contract_cols(query_head, key_head) * allowed
    grad_prob = contract_cols(grad_numer, value_head)
    grad_value = contract_rows(scores.astype(jnp.bfloat16), grad_numer)
    grad_scores = ((grad_prob + grad_denom[:, None]) * allowed).astype(jnp.bfloat16)
    grad_query = jnp.dot(grad_scores, key_head, preferred_element_type=jnp.float32)
    grad_key = contract_rows(grad_scores, query_head)
    return (grad_query, grad_key, grad_value)


def plain_body(
    inputs,
    cotangent,
    seg_lengths,
    valid_len,
    w_qkv,
    b_qkv,
    w_out,
    b_out,
    gain_one,
    shift_one,
    w_up,
    b_up,
    w_down,
    b_down,
    gain_two,
    shift_two,
):
    token_rows = inputs[0].astype(jnp.float32)
    row_length = token_rows.shape[0]
    model_width = token_rows.shape[1]
    allowed, keeping = row_masks(seg_lengths[0], valid_len[0], row_length)
    full_qkv, full_bqkv, full_out, full_bout, full_gain, full_shift = pull_group(
        w_qkv, b_qkv, w_out, b_out, gain_one, shift_one
    )
    normed, norm_back = jax.vjp(
        layer_norm, token_rows, full_gain.astype(jnp.float32), full_shift.astype(jnp.float32)
    )
    normed_low = normed.astype(jnp.bfloat16)
    projected = jnp.dot(
        normed_low, full_qkv, preferred_element_type=jnp.float32
    ) + full_bqkv.astype(jnp.float32)
    query_feat, query_back = jax.vjp(feature_map, projected[:, :model_width])
    key_feat, key_back = jax.vjp(feature_map, projected[:, model_width : 2 * model_width])
    query_heads = split_heads(query_feat.astype(jnp.bfloat16))
    key_heads = split_heads(key_feat.astype(jnp.bfloat16))
    value_heads = split_heads(projected[:, 2 * model_width :].astype(jnp.bfloat16))
    numerator, denominator = lax.map(
        partial(head_forward, allowed), (query_heads, key_heads, value_heads)
    )
    attended = keeping[None, :, None] * numerator / denominator[:, :, None]
    attended_low = join_heads(attended).astype(jnp.bfloat16)
    middle = (
        token_rows
        + jnp.dot(attended_low, full_out, preferred_element_type=jnp.float32)
        + full_bout.astype(jnp.float32)
    )
    full_up, full_bup, full_down, full_bdown, full_gain_two, full_shift_two = pull_group(
        w_up, b_up, w_down, b_down, gain_two, shift_two
    )
    normed_two, norm_two_back = jax.vjp(
        layer_norm, middle, full_gain_two.astype(jnp.float32), full_shift_two.astype(jnp.float32)
    )
    normed_two_low = normed_two.astype(jnp.bfloat16)
    hidden = jnp.dot(normed_two_low, full_up, preferred_element_type=jnp.float32) + full_bup.astype(
        jnp.float32
    )
    activated, gelu_back = jax.vjp(gelu_tanh, hidden)
    activated_low = activated.astype(jnp.bfloat16)
    result = (
        middle
        + jnp.dot(activated_low, full_down, preferred_element_type=jnp.float32)
        + full_bdown.astype(jnp.float32)
    )
    again_up, again_bup, again_down, again_bdown, again_gain_two, again_shift_two = pull_group(
        w_up, b_up, w_down, b_down, gain_two, shift_two
    )
    grad_top = cotangent[0]
    grad_top_full = grad_top.astype(jnp.float32)
    grad_down = contract_rows(activated_low, grad_top)
    grad_bdown = jnp.sum(grad_top_full, axis=0)
    grad_hidden = gelu_back(contract_cols(grad_top, again_down))[0]
    grad_hidden_low = grad_hidden.astype(jnp.bfloat16)
    grad_bup = jnp.sum(grad_hidden_low.astype(jnp.float32), axis=0)
    grad_up = contract_rows(normed_two_low, grad_hidden_low)
    grad_normed_two = contract_cols(grad_hidden_low, again_up)
    grad_middle_norm, grad_gain_two, grad_shift_two = norm_two_back(grad_normed_two)
    grad_middle = grad_top_full + grad_middle_norm
    shard_up, shard_bup, shard_down, shard_small_two = push_group(
        grad_up, grad_bup, grad_down, jnp.stack([grad_bdown, grad_gain_two, grad_shift_two])
    )
    again_qkv, again_bqkv, again_out, again_bout, again_gain, again_shift = pull_group(
        w_qkv, b_qkv, w_out, b_out, gain_one, shift_one
    )
    grad_mixed = grad_middle.astype(jnp.bfloat16)
    grad_bout = jnp.sum(grad_mixed.astype(jnp.float32), axis=0)
    grad_wout = contract_rows(attended_low, grad_mixed)
    grad_attended = split_heads(contract_cols(grad_mixed, again_out))
    grad_numer = (keeping[None, :, None] * grad_attended / denominator[:, :, None]).astype(
        jnp.bfloat16
    )
    grad_denom = -jnp.sum(grad_attended * attended, axis=2) / denominator
    grad_query_heads, grad_key_heads, grad_value_heads = lax.map(
        partial(head_backward, allowed),
        (query_heads, key_heads, value_heads, grad_numer, grad_denom),
    )
    grad_query = query_back(join_heads(grad_query_heads))[0]
    grad_key = key_back(join_heads(grad_key_heads))[0]
    grad_projected = jnp.concatenate(
        [grad_query, grad_key, join_heads(grad_value_heads)], axis=1
    ).astype(jnp.bfloat16)
    grad_bias_all = jnp.sum(grad_projected.astype(jnp.float32), axis=0)
    grad_bias_qk = grad_bias_all[: 2 * model_width]
    grad_bias_v = grad_bias_all[2 * model_width :]
    grad_qkv = contract_rows(normed_low, grad_projected)
    grad_normed = contract_cols(grad_projected, again_qkv)
    grad_rows_norm, grad_gain_one, grad_shift_one = norm_back(grad_normed)
    grad_inputs = (grad_middle + grad_rows_norm).astype(jnp.bfloat16)
    shard_qkv, shard_bias_qk, shard_wout, shard_small_one = push_group(
        grad_qkv,
        grad_bias_qk,
        grad_wout,
        jnp.stack([grad_bout, grad_bias_v, grad_gain_one, grad_shift_one]),
    )
    return (
        result.astype(jnp.bfloat16)[None],
        grad_inputs[None],
        shard_qkv,
        shard_bias_qk,
        shard_small_one[1],
        shard_wout,
        shard_small_one[0],
        shard_small_one[2],
        shard_small_one[3],
        shard_up,
        shard_bup,
        shard_down,
        shard_small_two[0],
        shard_small_two[1],
        shard_small_two[2],
    )


HALF_LANES = 64
TILE = 512
Z_HIGH, Z_LOW, Y_BIT, X_BIT = 8, 4, 2, 1
MIXED = ((Z_HIGH, X_BIT, Z_LOW, Y_BIT), (Z_HIGH, Y_BIT, Z_LOW, X_BIT))
LINED = ((Z_HIGH, Z_LOW, X_BIT, Y_BIT), (Z_HIGH, Z_LOW, Y_BIT, X_BIT))
SMALL = 128
GROUP = 16
ANY = pl.BlockSpec(memory_space=pl.ANY)
SMEM = pl.BlockSpec(memory_space=pltpu.SMEM)
VMEM = pl.BlockSpec(memory_space=pltpu.VMEM)
MIB = 1 << 20


def swap_chips(block, bit):
    return lax.ppermute(block, "fsdp", [(place, place ^ bit) for place in range(16)])


def swap_cores(block):
    return lax.ppermute(block, "dp", [(0, 1), (1, 0)])


def relative_place(order, slot, last):
    return (
        order[0] * (slot & 1)
        + order[1] * ((slot >> 1) & 1)
        + order[2] * ((slot >> 2) & 1)
        + order[3] * last
    )


def tie(*blocks):
    return lax.optimization_barrier(blocks)


def by_side(shard):
    half = shard.shape[1] // 2
    return shard[None, :, :half], shard[None, :, half:]


def swap_sides(sides, orders, step):
    first, second = orders[0][step], orders[1][step]
    if first == second:
        return (swap_chips(jnp.stack(sides), first),)
    return swap_chips(sides[0], first), swap_chips(sides[1], second)


def sides_of(arrived):
    return (arrived[0][0], arrived[0][1]) if len(arrived) == 1 else arrived


def grown(sides, arrived):
    return tuple(jnp.concatenate([held, more]) for held, more in zip(sides, sides_of(arrived)))


def swap_both(sides):
    return swap_cores(sides[0]), swap_cores(sides[1])


def pieces_of(held, plane, across, core_held, core_across):
    plane = sides_of(plane)
    return tuple(
        block
        for side in range(2)
        for block in (held[side], plane[side], across[side], core_held[side], core_across[side])
    )


def added(parts, start, stop):
    return sum(part[start:stop].astype(jnp.float32) for part in parts)


def reduce_step(sides, orders, step, amount):
    sent = [added(parts, amount, 2 * amount).astype(jnp.bfloat16) for parts in sides]
    return swap_sides(sent, orders, step)


def with_arrived(sides, arrived):
    return [parts + [more] for parts, more in zip(sides, sides_of(arrived))]


def reduce_end(sides, orders):
    sides = with_arrived(sides, reduce_step(sides, orders, 0, 1))
    return [added(parts, 0, 1)[0] for parts in sides]


def side_by_side(sides, start, stop):
    return jnp.concatenate([side[:, start:stop] for side in sides], axis=1)


def far(array):
    return pltpu.with_memory_space_constraint(array, pltpu.HBM)


def call(kernel, outs, scratch, mib, args, in_specs, out_specs, grid=None, flops=0, gates=()):
    inputs, ignored = len(in_specs), len(gates)

    def gated(*refs):
        kernel(*refs[:inputs], *refs[inputs + ignored :])

    extra = {} if grid is None else {"grid": grid}
    near = (SMEM,) if grid else (SMEM, VMEM)
    args = [arg if spec in near else far(arg) for arg, spec in zip(args, in_specs)]
    gates = [far(gate) for gate in gates]
    if isinstance(outs, tuple):
        outs = tuple(
            out if spec in near else pltpu.HBM(out.shape, out.dtype)
            for out, spec in zip(outs, out_specs)
        )
    return pl.pallas_call(
        gated,
        out_shape=outs,
        in_specs=list(in_specs) + [ANY] * ignored,
        out_specs=out_specs,
        scratch_shapes=scratch,
        compiler_params=pltpu.CompilerParams(vmem_limit_bytes=mib * MIB),
        cost_estimate=pl.CostEstimate(flops=flops, bytes_accessed=0, transcendentals=0),
        **extra,
    )(*args, *gates)


def shaped(shape, dtype):
    return jax.ShapeDtypeStruct(shape, dtype)


def dot_nn(left, right):
    return lax.dot_general(left, right, (((1,), (0,)), ((), ())), preferred_element_type=jnp.float32)


def dot_nt(left, right):
    return lax.dot_general(left, right, (((1,), (1,)), ((), ())), preferred_element_type=jnp.float32)


def piece_at(pieces, side, core, last, slot):
    mine = pieces[5 * side : 5 * side + 5]
    if core or last:
        return mine[1 + core * 2 + last], slot
    return mine[slot // 4], slot % 4


def fetch(place, pieces, whole, sems, skip=0, orders=LINED):
    rows, half = pieces[0].shape[1], whole.shape[1] // 2
    copies = []
    for side, order in enumerate(orders):
        for core in range(2):
            for last in range(2):
                for slot in range(8):
                    piece, index = piece_at(pieces, side, core, last, slot)
                    owner = (place[1] ^ core) * 16 + (place[0] ^ relative_place(order, slot, last))
                    start = pl.multiple_of(owner * rows, rows)
                    copies.append(
                        pltpu.make_async_copy(
                            piece.at[index, :, pl.ds(skip, half)],
                            whole.at[pl.ds(start, rows), pl.ds(side * half, half)],
                            sems.at[len(copies)],
                        )
                    )
    for copy in copies:
        copy.start()
    return copies


def wait_side(copies, side):
    half = len(copies) // 2
    wait_all(copies[side * half : (side + 1) * half])


def wait_all(copies):
    for copy in copies:
        copy.wait()


def standardize(block):
    centred = block - jnp.mean(block, axis=1, keepdims=True)
    scale = lax.rsqrt(jnp.mean(centred * centred, axis=1, keepdims=True) + norm_eps)
    return centred * scale, scale


def norm_pull(grad, standard, scale, gain):
    scaled = grad * gain
    return scale * (
        scaled
        - jnp.mean(scaled, axis=1, keepdims=True)
        - standard * jnp.mean(scaled * standard, axis=1, keepdims=True)
    )


def place_kernel(where, lengths, valid, place):
    place[0] = where[0] & 15
    place[1] = where[0] >> 4
    end = lengths[0, 0]
    place[2] = end
    for image in range(1, 3):
        end = end + lengths[0, image]
        place[2 + image] = end
    place[5] = valid[0]


def run_place(where, lengths, valid):
    return call(
        place_kernel,
        shaped((6,), jnp.int32),
        [],
        8,
        (where, lengths, valid),
        in_specs=[SMEM] * 3,
        out_specs=SMEM,
    )


def fetch_small(place, pieces, small, skip, sems):
    copies = []
    for core in range(2):
        for last in range(2):
            for slot in range(8):
                piece, index = piece_at(pieces, 0, core, last, slot)
                far = relative_place(LINED[0], slot, last)
                owner = (place[1] ^ core) * 16 + (place[0] ^ far)
                start = pl.multiple_of(owner * GROUP, GROUP)
                copies.append(
                    pltpu.make_async_copy(
                        piece.at[index, pl.ds(0, GROUP), pl.ds(skip, SMALL)],
                        small.at[pl.ds(start, GROUP), :],
                        sems.at[len(copies)],
                    )
                )
                copies[-1].start()
    return copies


def tables(each):
    total = 32 * each
    column = lax.broadcasted_iota(jnp.int32, (1, total), 1).astype(jnp.float32)
    turn = jnp.floor((column + 0.5) / each)
    lane = lax.broadcasted_iota(jnp.int32, (SMALL, 1), 0).astype(jnp.float32)
    spread = jnp.where(column - turn * each == lane, 1.0, 0.0).astype(jnp.bfloat16)
    owner = lax.broadcasted_iota(jnp.int32, (32, 1), 0).astype(jnp.float32)
    return owner == turn, spread


def unfold(small, each, rows):
    mine, spread = tables(each)
    lines = []
    for row in rows:
        parts = small[pl.ds(row, 32, stride=GROUP), :].astype(jnp.bfloat16)
        parts = jnp.where(mine, dot_nn(parts, spread), 0.0)
        lines.append(jnp.sum(parts, axis=0, keepdims=True))
    return lines


def fold(small, each, vectors):
    mine, spread = tables(each)
    for row, vector in vectors:
        parts = jnp.where(mine, vector, 0.0).astype(jnp.bfloat16)
        small[pl.ds(row, 32, stride=32), :] = dot_nt(parts, spread)


def qkv_kernel(place, rows_in, *rest):
    pieces, (normed, query, key, value), lines, rest = rest[:10], rest[10:14], rest[14:20], rest[20:]
    whole, small, smalls, bias, sems, more = rest
    few = fetch_small(place, pieces, small, 4 * whole.shape[1] // 6, more)
    copies = fetch(place, pieces, whole, sems)
    wait_all(few)
    smalls[...] = small[...].astype(jnp.float32)
    width = rows_in.shape[1]
    (bias[...],) = unfold(smalls, 3 * width // 32, (0,))
    (lines[5][...],) = unfold(smalls, 4 * width // 32, (4,))
    bias_out, gain, shift, bias_down, gain_two, shift_two = unfold(
        smalls, width // 32, (1, 2, 3, 5, 6, 7)
    )
    for goal, line in zip(lines, (gain, bias_out, gain_two, shift_two, bias_down)):
        goal[...] = line
    for part in range(4):
        at = pl.ds(part * 128, 128)
        standard, _ = standardize(rows_in[at, :].astype(jnp.float32))
        normed[at, :] = (standard * gain + shift).astype(jnp.bfloat16)
    for tile in range(6):
        if tile % 3 == 0:
            wait_side(copies, tile // 3)
        cols = pl.ds(tile * TILE, TILE)
        projected = dot_nn(normed[...], whole[:, cols]) + bias[:, cols]
        goal = (query, key, value)[tile // 2]
        if tile < 4:
            projected = feature_map(projected)
        goal[:, pl.ds((tile % 2) * TILE, TILE)] = projected.astype(jnp.bfloat16)


def run_qkv(place, rows_in, pieces, gates=()):
    length, width = rows_in.shape
    narrow = shaped((length, width), jnp.bfloat16)
    line = shaped((1, width), jnp.float32)
    return call(
        qkv_kernel,
        (narrow,) * 4 + (line,) * 5 + (shaped((1, 4 * width), jnp.float32),),
        [
            pltpu.VMEM((width, 3 * width), jnp.bfloat16),
            pltpu.VMEM((32 * GROUP, SMALL), jnp.bfloat16),
            pltpu.VMEM((32 * GROUP, SMALL), jnp.float32),
            pltpu.VMEM((1, 3 * width), jnp.float32),
            pltpu.SemaphoreType.DMA((64,)),
            pltpu.SemaphoreType.DMA((32,)),
        ],
        18,
        (place, rows_in, *pieces),
        in_specs=[SMEM, VMEM] + [ANY] * 10,
        out_specs=(VMEM,) * 10,
        gates=gates,
    )


def image_of(place, positions):
    image = jnp.zeros(positions.shape, jnp.int32)
    for end in range(2, 5):
        image = image + jnp.where(positions >= place[end], 1, 0)
    return image


def allowed_block(place, length, flipped):
    first = lax.broadcasted_iota(jnp.int32, (length, 1), 0)
    second = lax.broadcasted_iota(jnp.int32, (1, length), 1)
    same = image_of(place, first) == image_of(place, second)
    ordered = (first <= second) if flipped else (second <= first)
    return jnp.where(same & ordered, 1.0, 0.0).astype(jnp.float32)


def low_lanes():
    return lax.broadcasted_iota(jnp.int32, (1, 2 * HALF_LANES), 1) < HALF_LANES


def two_heads(block):
    low = jnp.where(low_lanes(), 1.0, 0.0)
    high = (1.0 - low).astype(jnp.bfloat16)
    return jnp.concatenate([block * low.astype(jnp.bfloat16), block * high], axis=0)


def one_pair(stacked):
    half = stacked.shape[0] // 2
    return jnp.where(low_lanes(), stacked[:half], stacked[half:])


def masked(stacked, allowed):
    half = stacked.shape[0] // 2
    return jnp.concatenate(
        [(stacked[:half] * allowed).astype(jnp.bfloat16), (stacked[half:] * allowed).astype(jnp.bfloat16)],
        axis=0,
    )


def keeping_rows(place, start, amount):
    position = lax.broadcasted_iota(jnp.int32, (amount, 1), 0) + start
    return jnp.where(position < place[5], 1.0, 0.0)


def attend_kernel(place, query, key, value, attended, exact, inverse, allowed, wide):
    length, width = query.shape
    step = length // 2

    @pl.when(pl.program_id(0) == 0)
    def _():
        allowed[...] = allowed_block(place, length, False)
        wide[:, width:] = jnp.ones((length, width), jnp.bfloat16)

    wide[:, :width] = value[...]
    for part in range(2):
        rows, seen = pl.ds(part * step, step), (part + 1) * step
        scores = dot_nt(two_heads(query[rows, :]), key[:seen, :])
        total = dot_nn(masked(scores, allowed[rows, :seen]), wide[:seen, :])
        over = 1.0 / (one_pair(total[:, width:]) + denom_eps)
        inverse[rows, :] = over
        mixed = keeping_rows(place, part * step, step) * one_pair(total[:, :width]) * over
        exact[rows, :] = mixed
        attended[rows, :] = mixed.astype(jnp.bfloat16)


def run_attend(place, query, key, value, gates=()):
    length, width = query.shape
    pair = pl.BlockSpec((length, 2 * HALF_LANES), lambda p: (0, p))
    return call(
        attend_kernel,
        (
            shaped((length, width), jnp.bfloat16),
            shaped((length, width), jnp.float32),
            shaped((length, width), jnp.float32),
        ),
        [
            pltpu.VMEM((length, length), jnp.float32),
            pltpu.VMEM((length, 4 * HALF_LANES), jnp.bfloat16),
        ],
        10,
        (place, query, key, value),
        grid=(width // (2 * HALF_LANES),),
        in_specs=[SMEM] + [pair] * 3,
        out_specs=(pair,) * 3,
        gates=gates,
    )


def attend_back_pair(
    place, query, key, value, grad_att, exact, inverse, stacked, sums, allowed, flipped, left, wide
):
    length, width = query.shape
    step = length // 2
    wide[:, :width] = value[...]
    over = grad_att[...] * inverse[...]
    lane = lax.broadcasted_iota(jnp.int32, (1, width), 1)
    terms, low = over * exact[...], lane < HALF_LANES
    first = jnp.sum(jnp.where(low, terms, 0.0), axis=1, keepdims=True)
    second = jnp.sum(jnp.where(low, 0.0, terms), axis=1, keepdims=True)
    spread = -jnp.where(low, first, second)
    high = spread.astype(jnp.bfloat16).astype(jnp.float32)
    within = lane & (HALF_LANES - 1)
    spread = jnp.where(within == 0, high, jnp.where(within == 1, spread - high, 0.0))
    numer = (keeping_rows(place, 0, length) * over).astype(jnp.bfloat16)
    for head in range(2):
        here = jnp.where(low, 1.0 - head, 1.0 * head)
        at = pl.ds(head * length, length)
        left[at, :width] = numer * here.astype(jnp.bfloat16)
        left[at, width:] = (spread * here).astype(jnp.bfloat16)
    for part in range(2):
        rows, seen = pl.ds(part * step, step), (part + 1) * step
        start = part * step
        later = pl.ds(start, length - start)
        both = jnp.concatenate([left[rows, :], left[pl.ds(length + start, step), :]], axis=0)
        grad_scores = masked(dot_nt(both, wide[:seen, :]), allowed[rows, :seen])
        grad_query = one_pair(dot_nn(grad_scores, key[:seen, :]))
        full = left[later, :] + left[pl.ds(length + start, length - start), :]
        scores = masked(dot_nt(two_heads(key[rows, :]), query[later, :]), flipped[rows, later])
        grad_value = one_pair(dot_nn(scores, full[:, :width]))
        ones = jnp.concatenate([two_heads(value[rows, :]), two_heads(wide[rows, width:])], axis=1)
        grad_scores = masked(dot_nt(ones, full), flipped[rows, later])
        grad_key = one_pair(dot_nn(grad_scores, query[later, :]))
        grads = (
            grad_query * jnp.minimum(query[rows, :].astype(jnp.float32), 1.0),
            grad_key * jnp.minimum(key[rows, :].astype(jnp.float32), 1.0),
            grad_value,
        )
        for index, grad in enumerate(grads):
            low_grad, line = grad.astype(jnp.bfloat16), pl.ds(index, 1)
            stacked[index, rows, :] = low_grad
            extra = jnp.sum(low_grad.astype(jnp.float32), axis=0, keepdims=True)
            sums[line, :] = extra if part == 0 else sums[line, :] + extra


def attend_back_kernel(
    place, query, key, value, grad_att, exact, inverse, stacked, sums, allowed, flipped, left, wide
):
    length, width = query.shape[0], 2 * HALF_LANES
    pairs = query.shape[1] // width

    @pl.when(pl.program_id(0) == 0)
    def _():
        allowed[...] = allowed_block(place, length, False)
        flipped[...] = allowed_block(place, length, True)
        for pair in range(pairs):
            wide[pair, :, width:] = jnp.ones((length, width), jnp.bfloat16)

    for pair in range(pairs):
        cols = pl.ds(pair * width, width)
        attend_back_pair(
            place,
            *(ref.at[:, cols] for ref in (query, key, value, grad_att, exact, inverse)),
            stacked.at[:, :, cols],
            sums.at[:, cols],
            allowed,
            flipped,
            left.at[pair],
            wide.at[pair],
        )


def run_attend_back(place, first, query, key, value, grad_att, exact, inverse, gates=()):
    length, width = query.shape
    half = width // 2
    start = first * half // (4 * HALF_LANES)
    pair = pl.BlockSpec((length, 4 * HALF_LANES), lambda p: (0, p + start))
    stack = pl.BlockSpec((3, length, 4 * HALF_LANES), lambda p: (0, 0, p))
    lines = pl.BlockSpec((3, 4 * HALF_LANES), lambda p: (0, p))
    return call(
        attend_back_kernel,
        (shaped((3, length, half), jnp.bfloat16), shaped((3, half), jnp.float32)),
        [
            pltpu.VMEM((length, length), jnp.float32),
            pltpu.VMEM((length, length), jnp.float32),
            pltpu.VMEM((2, 2 * length, 4 * HALF_LANES), jnp.bfloat16),
            pltpu.VMEM((2, length, 4 * HALF_LANES), jnp.bfloat16),
        ],
        20,
        (place, query, key, value, grad_att, exact, inverse),
        grid=(half // (4 * HALF_LANES),),
        in_specs=[SMEM] + [pair] * 6,
        out_specs=(stack, lines),
        gates=gates,
    )


def hand_over(place, sources, goal, sems):
    copies, at = [], 0
    for source in sources:
        half = source.shape[1] // 2
        start = pl.multiple_of((1 - place[1]) * half, half)
        copies.append(
            pltpu.make_async_copy(
                source.at[:, pl.ds(start, half)], goal.at[:, pl.ds(at, half)], sems.at[len(copies)]
            )
        )
        copies[-1].start()
        at += half
    return copies


def out_kernel(place, rows_in, early, attended, bias, gain, shift, *rest):
    pieces, (middle, normed, handed, whole, sems, more) = rest[:10], rest[10:]
    copies = fetch(place, pieces, whole, sems, 3 * whole.shape[1] // 2)
    handing = hand_over(place, (early, attended), handed, more)
    for side in range(2):
        wait_side(copies, side)
        cols = pl.ds(side * TILE, TILE)
        middle[:, cols] = (
            rows_in[:, cols].astype(jnp.float32) + dot_nn(attended[...], whole[:, cols]) + bias[:, cols]
        )
    for part in range(4):
        at = pl.ds(part * 128, 128)
        standard, _ = standardize(middle[at, :])
        normed[at, :] = (standard * gain[...] + shift[...]).astype(jnp.bfloat16)
    wait_all(handing)


def run_out(place, rows_in, early, attended, bias, gain, shift, pieces, gates=()):
    length, width = rows_in.shape
    narrow = shaped((length, width), jnp.bfloat16)
    return call(
        out_kernel,
        (shaped((length, width), jnp.float32), narrow, narrow),
        [
            pltpu.VMEM((width, width), jnp.bfloat16),
            pltpu.SemaphoreType.DMA((64,)),
            pltpu.SemaphoreType.DMA((2,)),
        ],
        16,
        (place, rows_in, early, attended, bias, gain, shift, *pieces),
        in_specs=[SMEM] + [VMEM] * 6 + [ANY] * 10,
        out_specs=(VMEM, VMEM, ANY),
        gates=gates,
    )


def bend_tile(hidden, activated, slope):
    square = hidden * hidden
    rate = gelu_coef + (gelu_coef * 0.044715) * square
    bend = jnp.tanh(hidden * rate)
    share = 0.5 + 0.5 * bend
    activated[...] = (hidden * share).astype(jnp.bfloat16)
    rate = gelu_coef + (3.0 * gelu_coef * 0.044715) * square
    slope[...] = (share + (0.5 * hidden) * (1.0 - bend * bend) * rate).astype(jnp.bfloat16)


def up_kernel(place, normed, bias, *rest):
    pieces, (activated, slope, handed, whole, hidden, sems, more) = rest[:10], rest[10:]
    copies = fetch(place, pieces, whole, sems)
    tiles = whole.shape[1] // TILE

    def columns(tile):
        return pl.ds(tile * TILE, TILE)

    for tile in range(tiles + 1):
        if tile % (tiles // 2) == 0 and tile < tiles:
            wait_side(copies, tile // (tiles // 2))
        if tile < tiles:
            cols = columns(tile)
            hidden[tile % 2] = dot_nn(normed[...], whole[:, cols]) + bias[:, cols]
        if tile > 0:
            cols = columns(tile - 1)
            bend_tile(hidden[(tile - 1) % 2], activated.at[:, cols], slope.at[:, cols])

    wait_all(hand_over(place, (normed, activated), handed, more))


def run_up(place, normed, bias, pieces, gates=()):
    length, width = normed.shape
    wide = bias.shape[1]
    return call(
        up_kernel,
        (shaped((length, wide), jnp.bfloat16),) * 2
        + (shaped((length, (width + wide) // 2), jnp.bfloat16),),
        [
            pltpu.VMEM((width, wide), jnp.bfloat16),
            pltpu.VMEM((2, length, TILE), jnp.float32),
            pltpu.SemaphoreType.DMA((64,)),
            pltpu.SemaphoreType.DMA((2,)),
        ],
        26,
        (place, normed, bias, *pieces),
        in_specs=[SMEM] + [VMEM] * 2 + [ANY] * 10,
        out_specs=(VMEM, VMEM, ANY),
        gates=gates,
    )


def sum_kernel(block, total):
    total[...] = jnp.sum(block[...].astype(jnp.float32), axis=0, keepdims=True)


def run_sum(block, cover, gates=()):
    return call(
        sum_kernel,
        shaped((1, block.shape[1]), jnp.float32),
        [],
        8,
        (block,),
        in_specs=[VMEM],
        out_specs=VMEM,
        flops=cover,
        gates=gates,
    )


def down_kernel(place, activated, slope, grad_top, middle, bias, *rest):
    pieces, (result, grad_hidden, sum_up, whole, sems) = rest[:10], rest[10:]
    copies = fetch(place, pieces, whole, sems, orders=MIXED)
    wait_all(copies)
    for tile in range(4):
        cols = pl.ds(tile * 256, 256)
        result[:, cols] = (
            middle[:, cols] + bias[:, cols] + dot_nn(activated[...], whole[:, cols])
        ).astype(jnp.bfloat16)
        for half in range(2):
            cols = pl.ds((2 * tile + half) * TILE, TILE)
            grad = dot_nt(grad_top[...], whole[cols, :]) * slope[:, cols].astype(jnp.float32)
            low = grad.astype(jnp.bfloat16)
            grad_hidden[:, cols] = low
            sum_up[:, cols] = jnp.sum(low.astype(jnp.float32), axis=0, keepdims=True)


def run_down(place, activated, slope, grad_top, middle, bias, pieces, gates=()):
    length, width = middle.shape
    wide = activated.shape[1]
    return call(
        down_kernel,
        (
            shaped((length, width), jnp.bfloat16),
            shaped((length, wide), jnp.bfloat16),
            shaped((1, wide), jnp.float32),
        ),
        [
            pltpu.VMEM((wide, width), jnp.bfloat16),
            pltpu.SemaphoreType.DMA((64,)),
        ],
        30,
        (place, activated, slope, grad_top, middle, bias, *pieces),
        in_specs=[SMEM] + [VMEM] * 5 + [ANY] * 10,
        out_specs=(VMEM,) * 3,
        flops=64 * length * width * wide,
        gates=gates,
    )


def middle_back_kernel(place, grad_hidden, middle, grad_top, gain, *rest):
    pieces_up, pieces_in, rest = rest[:10], rest[10:20], rest[20:]
    grad_middle, mixed, grad_att, sum_gain, sum_shift, whole, outer, total, sems, more = rest
    copies = fetch(place, pieces_up, whole, sems)
    second = fetch(place, pieces_in, outer, more, 3 * outer.shape[1] // 2)
    step = 2 * TILE
    for tile in range(whole.shape[1] // step):
        if tile % 2 == 0:
            wait_side(copies, tile // 2)
        cols = pl.ds(tile * step, step)
        block = dot_nt(grad_hidden[:, cols], whole[:, cols])
        total[...] = block if tile == 0 else total[...] + block

    for part in range(4):
        at = pl.ds(part * 128, 128)
        grad = total[at, :]
        standard, scale = standardize(middle[at, :])
        back = grad_top[at, :].astype(jnp.float32) + norm_pull(grad, standard, scale, gain[...])
        grad_middle[at, :] = back
        low = back.astype(jnp.bfloat16)
        mixed[at, :] = low
        for goal, added in ((sum_gain, grad * standard), (sum_shift, grad)):
            added = jnp.sum(added, axis=0, keepdims=True)
            goal[...] = added if part == 0 else goal[...] + added
    wait_all(second)
    for part in range(2):
        cols = pl.ds(part * TILE, TILE)
        grad_att[:, cols] = dot_nt(mixed[...], outer[cols, :])


def run_middle_back(place, grad_hidden, middle, grad_top, gain, pieces_up, pieces_in, gates=()):
    length, width = middle.shape
    wide = grad_hidden.shape[1]
    full, line = shaped((length, width), jnp.float32), shaped((1, width), jnp.float32)
    return call(
        middle_back_kernel,
        (full, shaped((length, width), jnp.bfloat16), full, line, line),
        [
            pltpu.VMEM((width, wide), jnp.bfloat16),
            pltpu.VMEM((width, width), jnp.bfloat16),
            pltpu.VMEM((length, width), jnp.float32),
            pltpu.SemaphoreType.DMA((64,)),
            pltpu.SemaphoreType.DMA((64,)),
        ],
        30,
        (place, grad_hidden, middle, grad_top, gain, *pieces_up, *pieces_in),
        in_specs=[SMEM] + [VMEM] * 4 + [ANY] * 20,
        out_specs=(VMEM,) * 5,
        gates=gates,
    )


def inputs_back_kernel(place, early, late, rows_in, gain, grad_middle, sum_out, *rest):
    (sums, late_sums, *ready), pieces, rest = rest[:6], rest[6:16], rest[16:]
    grad_rows, lines, whole, total, sems = rest
    copies = fetch(place, pieces, whole, sems)
    width = rows_in.shape[1]
    for tile in range(6):
        if tile % 3 == 0:
            wait_side(copies, tile // 3)
        grads = (early, late)[tile % 2]
        block = dot_nt(grads[tile // 2], whole[:, pl.ds(tile * TILE, TILE)])
        total[...] = block if tile == 0 else total[...] + block
    for part in range(4):
        at = pl.ds(part * 128, 128)
        grad = total[at, :]
        standard, scale = standardize(rows_in[at, :].astype(jnp.float32))
        back = grad_middle[at, :] + norm_pull(grad, standard, scale, gain[...])
        grad_rows[at, :] = back.astype(jnp.bfloat16)
        for index, extra in enumerate((grad * standard, grad)):
            goal = lines.at[:, pl.ds((4 + index) * width, width)]
            extra = jnp.sum(extra, axis=0, keepdims=True)
            goal[...] = extra if part == 0 else goal[...] + extra
    half = width // 2
    for row in range(3):
        for index, source in enumerate((sums, late_sums)):
            lines[:, pl.ds(row * width + index * half, half)] = source[pl.ds(row, 1), :]
    lines[:, pl.ds(3 * width, width)] = sum_out[...]
    at = 6 * width
    for source in ready:
        lines[:, pl.ds(at, source.shape[1])] = source[...]
        at += source.shape[1]


def run_inputs_back(
    place, early, late, rows_in, gain, grad_middle, sum_out, ready, pieces, gates=()
):
    length, width = rows_in.shape
    total = 6 * width + sum(line.shape[1] for line in ready[2:])
    return call(
        inputs_back_kernel,
        (shaped((length, width), jnp.bfloat16), shaped((1, total), jnp.float32)),
        [
            pltpu.VMEM((width, 3 * width), jnp.bfloat16),
            pltpu.VMEM((length, width), jnp.float32),
            pltpu.SemaphoreType.DMA((64,)),
        ],
        20,
        (place, early, late, rows_in, gain, grad_middle, sum_out, *ready, *pieces),
        in_specs=[SMEM] + [VMEM] * 12 + [ANY] * 10,
        out_specs=(VMEM,) * 2,
        flops=1 << 40,
        gates=gates,
    )


def weight_kernel(orders, skips, sizes, place, *rest):
    groups = len(skips)
    if sizes:
        mine, other_lines, rest = rest[4 * groups], rest[4 * groups + 1], rest[: 4 * groups] + rest[4 * groups + 2 :]
    inputs, outs, rest = rest[: 4 * groups], rest[4 * groups : 4 * groups + 4], rest[4 * groups + 4 :]
    wholes, (turned, sems), rest = rest[:groups], rest[groups : groups + 2], rest[groups + 2 :]
    length, rows = inputs[0].shape[0], outs[0].shape[1]
    owners = 256 // rows
    at, copies = 0, []
    for group, (skip, whole) in enumerate(zip(skips, wholes)):
        left_own, left_other, own, other = inputs[4 * group : 4 * group + 4]
        count, each = own.shape[0], own.shape[2]
        tiles, half = whole.shape[0], whole.shape[2] // 2
        for tile in range(tiles):
            low = pl.multiple_of(((place[0] // owners) ^ tile) * 256, 256)
            start = pl.multiple_of(place[1] * (256 * tiles) + low, 256)
            left = turned.at[tile % 2]
            left[:, :length] = left_own[:, pl.ds(start, 256)].T
            left[:, length:] = left_other[:, pl.ds(skip + low, 256)].T
            for index in range(count):
                for step in range(each // TILE):
                    cols = pl.ds(step * TILE, TILE)
                    block = dot_nn(left[:, :length], own[index, :, cols])
                    block += dot_nn(left[:, length:], other[index, :, cols])
                    goal = pl.ds(index * each + step * TILE, TILE)
                    whole[tile, :, goal] = block.astype(jnp.bfloat16)
            for side, order in enumerate(orders):
                for last in range(2):
                    for slot in range(8):
                        far_place = relative_place(order, slot, last)
                        if far_place // owners != tile:
                            continue
                        start = pl.multiple_of(((place[0] ^ far_place) % owners) * rows, rows)
                        copies.append(
                            pltpu.make_async_copy(
                                whole.at[tile, pl.ds(start, rows), pl.ds(side * half, half)],
                                outs[last * 2 + side].at[slot, :, pl.ds(at, half)],
                                sems.at[len(copies)],
                            )
                        )
                        copies[-1].start()
        at += half
    if sizes:
        wide_small, small, more = rest
        wide_small[...] = jnp.zeros_like(wide_small)
        start, by_size = 0, {}
        for row, size in enumerate(sizes):
            line = mine[:, start : start + size] + other_lines[:, start : start + size]
            by_size.setdefault(size, []).append((row, line))
            start += size
        for size, vectors in by_size.items():
            fold(wide_small, size // 32, vectors)
        small[...] = wide_small[...].astype(jnp.bfloat16)
        for last in range(2):
            for slot in range(8):
                chip = place[0] ^ relative_place(orders[0], slot, last)
                start = pl.multiple_of((place[1] * 16 + chip) * 32, 32)
                copies.append(
                    pltpu.make_async_copy(
                        small.at[pl.ds(start, 32), :],
                        outs[last * 2].at[slot, :, pl.ds(at, SMALL)],
                        more.at[last * 8 + slot],
                    )
                )
                copies[-1].start()
    wait_all(copies)


def run_weight(place, orders, height, groups, gates=(), sizes=(), lines=()):
    length = groups[0][0].shape[0]
    totals = [own.shape[0] * own.shape[2] for _, _, _, own, _ in groups]
    half = sum(totals) // 2
    part = shaped((8, height // 16, half), jnp.bfloat16)
    first = shaped((8, height // 16, half + (SMALL if sizes else 0)), jnp.bfloat16)
    extra = [
        pltpu.VMEM((32 * 32, SMALL), jnp.float32),
        pltpu.VMEM((32 * 32, SMALL), jnp.bfloat16),
        pltpu.SemaphoreType.DMA((16,)),
    ]
    return call(
        partial(weight_kernel, orders, tuple(group[2] for group in groups), sizes),
        (first,) * 4,
        [pltpu.VMEM((height // 256, 256, total), jnp.bfloat16) for total in totals]
        + [
            pltpu.VMEM((2, 256, 2 * length), jnp.bfloat16),
            pltpu.SemaphoreType.DMA((32 * len(groups),)),
        ]
        + (extra if sizes else []),
        22,
        (place, *(array for group in groups for array in group[:2] + group[3:]), *lines),
        in_specs=[SMEM] + [VMEM] * (4 * len(groups) + len(lines)),
        out_specs=(ANY,) * 4,
        gates=gates,
    )


def paired_body(
    inputs,
    cotangent,
    seg_lengths,
    valid_len,
    w_qkv,
    b_qkv,
    w_out,
    b_out,
    gain_one,
    shift_one,
    w_up,
    b_up,
    w_down,
    b_down,
    gain_two,
    shift_two,
):
    where = (lax.axis_index("dp") * 16 + lax.axis_index("fsdp")).astype(jnp.int32)[None]
    rows_in, grad_top = inputs[0], cotangent[0]
    vectors = (b_qkv, b_out, gain_one, shift_one, b_up, b_down, gain_two, shift_two)
    cut = w_qkv.shape[1] // 2
    edge = w_out.shape[1] // 2
    held_in = (
        jnp.concatenate([w_qkv[:, :cut], w_out[:, :edge]], axis=1)[None],
        jnp.concatenate([w_qkv[:, cut:], w_out[:, edge:]], axis=1)[None],
    )
    small = jnp.stack([jnp.pad(vector, (0, SMALL - vector.shape[0])) for vector in vectors])
    small = jnp.pad(small, ((0, w_out.shape[0] - small.shape[0]), (0, 0)))[None]
    small_far = swap_chips(small, Z_HIGH)
    place = run_place(where, seg_lengths, valid_len)
    place, small_far = tie(place, small_far)
    small = jnp.concatenate([small, small_far])
    held_up, held_down = by_side(w_up), by_side(w_down)
    top = grad_top[None]
    held_in = grown(held_in, swap_sides(held_in, LINED, 0))
    held_in = (
        jnp.concatenate([held_in[0], small], axis=2),
        jnp.concatenate([held_in[1], jnp.zeros_like(small)], axis=2),
    )
    held_in = grown(held_in, swap_sides(held_in, LINED, 1))
    held_in, held_up = tie(held_in, held_up)
    start_up = swap_sides(held_up, LINED, 0)
    plane_in = swap_sides(held_in, LINED, 2)
    start_up, plane_in = tie(start_up, plane_in)
    held_up = grown(held_up, start_up)
    held_up, held_down = tie(held_up, held_down)
    full_in = grown(held_in, plane_in)
    across_in = swap_sides(full_in, LINED, 3)
    core_in = swap_both(full_in)
    held_up = grown(held_up, swap_sides(held_up, LINED, 1))
    start_down = swap_sides(held_down, LINED, 0)
    across_in, start_down = tie(across_in, start_down)
    pieces_in = pieces_of(held_in, plane_in, across_in, core_in, swap_both(across_in))
    plane_up = swap_sides(held_up, LINED, 2)
    held_down = grown(held_down, start_down)
    plane_down = swap_sides(held_down, MIXED, 1)
    top_other = swap_cores(top)

    normed, query, key, value, *lines = run_qkv(
        place, rows_in, pieces_in, (*held_up, *held_down, top_other)
    )
    full_gain, full_bout, full_gain_two, full_shift_two, full_bdown, full_bup = lines
    plane_up, plane_down, normed = tie(plane_up, plane_down, normed)
    full_up = grown(held_up, plane_up)
    across_up = swap_sides(full_up, LINED, 3)
    core_up = swap_both(full_up)
    held_down = grown(held_down, plane_down)
    line_down = swap_sides(held_down, MIXED, 2)
    attended, exact, inverse = run_attend(place, query, key, value, (*plane_up, *held_down))
    core_up, attended = tie(core_up, attended)
    middle, normed_two, inner_half = run_out(
        place,
        rows_in,
        normed,
        attended,
        full_bout,
        full_gain_two,
        full_shift_two,
        pieces_in,
    )
    inner_other = swap_cores(inner_half)
    across_up, line_down, normed_two = tie(across_up, line_down, normed_two)
    pieces_up = pieces_of(held_up, plane_up, across_up, core_up, swap_both(across_up))
    full_down = grown(held_down, line_down)
    across_down = swap_sides(full_down, MIXED, 3)
    core_down = swap_both(full_down)
    activated, slope, outer_half = run_up(
        place, normed_two, full_bup, pieces_up, (*line_down, inner_other)
    )
    outer_other = swap_cores(outer_half)
    sum_down = run_sum(grad_top, 1 << 40, (outer_half,))
    thin = normed_two.shape[1] // 2
    parts = run_weight(
        place,
        LINED,
        activated.shape[1] // 2,
        [(activated, outer_other, thin, top, top_other)],
        (*core_down, sum_down),
    )
    across_down, parts = tie(across_down, parts)
    down_one = swap_sides(parts[2:], LINED, 3)
    pieces_down = pieces_of(held_down, line_down, across_down, core_down, swap_both(across_down))
    result, grad_hidden, sum_up = run_down(
        place, activated, slope, grad_top, middle, full_bdown, pieces_down, parts[2:]
    )
    hidden_other = swap_cores(grad_hidden[None])
    grad_middle, mixed, grad_att, sum_gain_two, sum_shift_two = run_middle_back(
        place, grad_hidden, middle, grad_top, full_gain_two, pieces_up, pieces_in
    )
    mixed = mixed[None]
    down_one, mixed = tie(down_one, mixed)
    mixed_other = swap_cores(mixed)
    down_sides = with_arrived([[parts[0]], [parts[1]]], down_one)
    down_two = reduce_step(down_sides, LINED, 2, 4)
    sum_out = run_sum(mixed[0], 1 << 35, down_one)
    hidden_other, sum_out = tie(hidden_other, sum_out)
    parts = run_weight(
        place, LINED, thin, [(normed_two, outer_other, 0, grad_hidden[None], hidden_other)]
    )
    up_one = swap_sides(parts[2:], LINED, 3)
    grads, sums = run_attend_back(
        place, 0, query, key, value, grad_att, exact, inverse, parts[2:]
    )
    down_two, mixed_other, grads = tie(down_two, mixed_other, grads)
    down_sides = with_arrived(down_sides, down_two)
    down_three = reduce_step(down_sides, LINED, 1, 2)
    grads_other = swap_cores(grads)
    late, late_sums = run_attend_back(
        place, 1, query, key, value, grad_att, exact, inverse, (grads,)
    )
    up_one, late = tie(up_one, late)
    up_sides = with_arrived([[parts[0]], [parts[1]]], up_one)
    late_other = swap_cores(late)
    up_two = reduce_step(up_sides, LINED, 2, 4)
    grad_rows, lines = run_inputs_back(
        place,
        grads,
        late,
        rows_in,
        full_gain,
        grad_middle,
        sum_out,
        (sums, late_sums, sum_up, sum_down, sum_gain_two, sum_shift_two),
        pieces_in,
        up_one,
    )
    up_two, down_three, grads_other, late_other, lines = tie(
        up_two, down_three, grads_other, late_other, lines
    )
    down_sides = with_arrived(down_sides, down_three)
    up_sides = with_arrived(up_sides, up_two)
    up_three = reduce_step(up_sides, LINED, 1, 2)
    lines_other = swap_cores(lines)
    parts = run_weight(
        place,
        MIXED,
        thin,
        [
            (normed, inner_other, 0, grads, grads_other),
            (attended, inner_other, thin, mixed, mixed_other),
        ],
    )
    lines_other, parts = tie(lines_other, parts)
    in_sides = [[parts[0]], [parts[1]]]
    in_one = swap_sides(parts[2:], MIXED, 3)
    narrow, wide = mixed.shape[2], sum_up.shape[1]
    sizes = (2 * narrow, narrow, narrow, narrow, narrow, wide, narrow, narrow, narrow)
    parts = run_weight(
        place,
        LINED,
        thin,
        [(normed, inner_other, 0, late, late_other)],
        parts[:1],
        sizes,
        (lines, lines_other),
    )
    down_four = reduce_step(down_sides, LINED, 0, 1)
    up_three, parts = tie(up_three, parts)
    up_sides = with_arrived(up_sides, up_three)
    up_four = reduce_step(up_sides, LINED, 0, 1)
    late_sides = [[parts[0]], [parts[1]]]
    late_one = swap_sides(parts[2:], LINED, 3)
    in_sides = with_arrived(in_sides, in_one)
    late_one, down_four = tie(late_one, down_four)
    down_sides = with_arrived(down_sides, down_four)
    late_sides = with_arrived(late_sides, late_one)
    in_sides = with_arrived(in_sides, reduce_step(in_sides, MIXED, 2, 4))
    late_sides = with_arrived(late_sides, reduce_step(late_sides, LINED, 2, 4))
    up_sides = with_arrived(up_sides, up_four)
    in_sides = with_arrived(in_sides, reduce_step(in_sides, MIXED, 1, 2))
    late_sides = with_arrived(late_sides, reduce_step(late_sides, LINED, 1, 2))
    shard_down = side_by_side([added(parts, 0, 1)[0] for parts in down_sides], 0, edge)
    shard_up = side_by_side([added(parts, 0, 1)[0] for parts in up_sides], 0, w_up.shape[1] // 2)
    shards = reduce_end(in_sides, MIXED)
    cut = cut // 2
    first = side_by_side(shards, 0, cut)
    shard_out = side_by_side(shards, cut, cut + edge)
    shards = reduce_end(late_sides, LINED)
    second = side_by_side(shards, 0, cut)
    third = edge
    shard_qkv = jnp.concatenate(
        [
            half[:, part * third : (part + 1) * third]
            for part in range(3)
            for half in (first, second)
        ],
        axis=1,
    )
    smalls = [shards[0][row, cut : cut + size // 32] for row, size in enumerate(sizes)]
    grad_bqk, grad_bv, grad_bout, grad_gain, grad_shift, grad_bup, grad_bdown, grad_gain_two, grad_shift_two = smalls
    return (
        result[None],
        grad_rows[None],
        shard_qkv,
        grad_bqk,
        grad_bv,
        shard_out,
        grad_bout,
        grad_gain,
        grad_shift,
        shard_up,
        grad_bup,
        shard_down,
        grad_bdown,
        grad_gain_two,
        grad_shift_two,
    )


def solution(mesh):
    placed = (
        P(("dp", "fsdp"), None, None),
        P(("dp", "fsdp"), None, None),
        P(("dp", "fsdp"), None),
        P(("dp", "fsdp")),
        P(("dp", "fsdp"), None),
        P(("dp", "fsdp")),
        P(("dp", "fsdp"), None),
        P(("dp", "fsdp")),
        P(("dp", "fsdp")),
        P(("dp", "fsdp")),
        P(("dp", "fsdp"), None),
        P(("dp", "fsdp")),
        P(("dp", "fsdp"), None),
        P(("dp", "fsdp")),
        P(("dp", "fsdp")),
        P(("dp", "fsdp")),
    )
    paired = dict(mesh.shape) == {"dp": 2, "fsdp": 16}
    return jax.shard_map(
        paired_body if paired else plain_body,
        mesh=mesh,
        in_specs=placed,
        out_specs=(
            P(("dp", "fsdp"), None, None),
            P(("dp", "fsdp"), None, None),
            P(("dp", "fsdp"), None),
            P(("dp", "fsdp")),
            P(("dp", "fsdp")),
            P(("dp", "fsdp"), None),
            P(("dp", "fsdp")),
            P(("dp", "fsdp")),
            P(("dp", "fsdp")),
            P(("dp", "fsdp"), None),
            P(("dp", "fsdp")),
            P(("dp", "fsdp"), None),
            P(("dp", "fsdp")),
            P(("dp", "fsdp")),
            P(("dp", "fsdp")),
        ),
        check_vma=False,
    )
```

```python
from functools import partial

import jax
import jax.numpy as jnp
from jax import lax
from jax.experimental import pallas as pl
from jax.experimental.pallas import tpu as pltpu
from jax.sharding import PartitionSpec as P

HEADS = 16


norm_eps = 1e-05
denom_eps = 1e-06
gelu_coef = 0.7978845608028654


def layer_norm(values, scale_gain, offset):
    centred = values - jnp.mean(values, axis=-1, keepdims=True)
    spread = jnp.mean(centred * centred, axis=-1, keepdims=True)
    return centred * lax.rsqrt(spread + norm_eps) * scale_gain + offset


def feature_map(values):
    return jnp.where(values > 0, values + 1.0, jnp.exp(jnp.minimum(values, 0.0)))


def gelu_tanh(values):
    return (
        0.5 * values * (1.0 + jnp.tanh(gelu_coef * (values + 0.044715 * values * values * values)))
    )


def contract_rows(left_side, right_side):
    return lax.dot_general(
        left_side, right_side, (((0,), (0,)), ((), ())), preferred_element_type=jnp.float32
    )


def contract_cols(left_side, right_side):
    return lax.dot_general(
        left_side, right_side, (((1,), (1,)), ((), ())), preferred_element_type=jnp.float32
    )


def row_masks(lengths, valid_count, row_length):
    places = jnp.arange(row_length, dtype=jnp.int32)
    bounds = jnp.stack([jnp.sum(lengths[: end + 1]) for end in range(lengths.shape[0])])
    segment = jnp.sum((places[:, None] >= bounds[None, :]).astype(jnp.int32), axis=1)
    allowed = (segment[:, None] == segment[None, :]) & (places[None, :] <= places[:, None])
    keeping = (places < valid_count).astype(jnp.float32)
    return (allowed.astype(jnp.float32), keeping)


def split_heads(matrix):
    return jnp.transpose(matrix.reshape(matrix.shape[0], HEADS, -1), (1, 0, 2))


def join_heads(stacked):
    return jnp.transpose(stacked, (1, 0, 2)).reshape(stacked.shape[1], -1)


def pull_group(first, second, third, fourth, fifth, sixth):
    return (
        lax.all_gather(first, ("dp", "fsdp"), axis=0, tiled=True),
        lax.all_gather(second, ("dp", "fsdp"), axis=0, tiled=True),
        lax.all_gather(third, ("dp", "fsdp"), axis=0, tiled=True),
        lax.all_gather(fourth, ("dp", "fsdp"), axis=0, tiled=True),
        lax.all_gather(fifth, ("dp", "fsdp"), axis=0, tiled=True),
        lax.all_gather(sixth, ("dp", "fsdp"), axis=0, tiled=True),
    )


def push_group(first, second, third, stacked):
    return (
        lax.psum_scatter(first, ("dp", "fsdp"), scatter_dimension=0, tiled=True),
        lax.psum_scatter(second, ("dp", "fsdp"), scatter_dimension=0, tiled=True),
        lax.psum_scatter(third, ("dp", "fsdp"), scatter_dimension=0, tiled=True),
        lax.psum_scatter(stacked, ("dp", "fsdp"), scatter_dimension=1, tiled=True),
    )


def head_forward(allowed, head_item):
    query_head, key_head, value_head = head_item
    scores = contract_cols(query_head, key_head) * allowed
    denominator = jnp.sum(scores, axis=1) + denom_eps
    numerator = jnp.dot(scores.astype(jnp.bfloat16), value_head, preferred_element_type=jnp.float32)
    return (numerator, denominator)


def head_backward(allowed, head_item):
    query_head, key_head, value_head, grad_numer, grad_denom = head_item
    scores = contract_cols(query_head, key_head) * allowed
    grad_prob = contract_cols(grad_numer, value_head)
    grad_value = contract_rows(scores.astype(jnp.bfloat16), grad_numer)
    grad_scores = ((grad_prob + grad_denom[:, None]) * allowed).astype(jnp.bfloat16)
    grad_query = jnp.dot(grad_scores, key_head, preferred_element_type=jnp.float32)
    grad_key = contract_rows(grad_scores, query_head)
    return (grad_query, grad_key, grad_value)


def plain_body(
    inputs,
    cotangent,
    seg_lengths,
    valid_len,
    w_qkv,
    b_qkv,
    w_out,
    b_out,
    gain_one,
    shift_one,
    w_up,
    b_up,
    w_down,
    b_down,
    gain_two,
    shift_two,
):
    token_rows = inputs[0].astype(jnp.float32)
    row_length = token_rows.shape[0]
    model_width = token_rows.shape[1]
    allowed, keeping = row_masks(seg_lengths[0], valid_len[0], row_length)
    full_qkv, full_bqkv, full_out, full_bout, full_gain, full_shift = pull_group(
        w_qkv, b_qkv, w_out, b_out, gain_one, shift_one
    )
    normed, norm_back = jax.vjp(
        layer_norm, token_rows, full_gain.astype(jnp.float32), full_shift.astype(jnp.float32)
    )
    normed_low = normed.astype(jnp.bfloat16)
    projected = jnp.dot(
        normed_low, full_qkv, preferred_element_type=jnp.float32
    ) + full_bqkv.astype(jnp.float32)
    query_feat, query_back = jax.vjp(feature_map, projected[:, :model_width])
    key_feat, key_back = jax.vjp(feature_map, projected[:, model_width : 2 * model_width])
    query_heads = split_heads(query_feat.astype(jnp.bfloat16))
    key_heads = split_heads(key_feat.astype(jnp.bfloat16))
    value_heads = split_heads(projected[:, 2 * model_width :].astype(jnp.bfloat16))
    numerator, denominator = lax.map(
        partial(head_forward, allowed), (query_heads, key_heads, value_heads)
    )
    attended = keeping[None, :, None] * numerator / denominator[:, :, None]
    attended_low = join_heads(attended).astype(jnp.bfloat16)
    middle = (
        token_rows
        + jnp.dot(attended_low, full_out, preferred_element_type=jnp.float32)
        + full_bout.astype(jnp.float32)
    )
    full_up, full_bup, full_down, full_bdown, full_gain_two, full_shift_two = pull_group(
        w_up, b_up, w_down, b_down, gain_two, shift_two
    )
    normed_two, norm_two_back = jax.vjp(
        layer_norm, middle, full_gain_two.astype(jnp.float32), full_shift_two.astype(jnp.float32)
    )
    normed_two_low = normed_two.astype(jnp.bfloat16)
    hidden = jnp.dot(normed_two_low, full_up, preferred_element_type=jnp.float32) + full_bup.astype(
        jnp.float32
    )
    activated, gelu_back = jax.vjp(gelu_tanh, hidden)
    activated_low = activated.astype(jnp.bfloat16)
    result = (
        middle
        + jnp.dot(activated_low, full_down, preferred_element_type=jnp.float32)
        + full_bdown.astype(jnp.float32)
    )
    again_up, again_bup, again_down, again_bdown, again_gain_two, again_shift_two = pull_group(
        w_up, b_up, w_down, b_down, gain_two, shift_two
    )
    grad_top = cotangent[0]
    grad_top_full = grad_top.astype(jnp.float32)
    grad_down = contract_rows(activated_low, grad_top)
    grad_bdown = jnp.sum(grad_top_full, axis=0)
    grad_hidden = gelu_back(contract_cols(grad_top, again_down))[0]
    grad_hidden_low = grad_hidden.astype(jnp.bfloat16)
    grad_bup = jnp.sum(grad_hidden_low.astype(jnp.float32), axis=0)
    grad_up = contract_rows(normed_two_low, grad_hidden_low)
    grad_normed_two = contract_cols(grad_hidden_low, again_up)
    grad_middle_norm, grad_gain_two, grad_shift_two = norm_two_back(grad_normed_two)
    grad_middle = grad_top_full + grad_middle_norm
    shard_up, shard_bup, shard_down, shard_small_two = push_group(
        grad_up, grad_bup, grad_down, jnp.stack([grad_bdown, grad_gain_two, grad_shift_two])
    )
    again_qkv, again_bqkv, again_out, again_bout, again_gain, again_shift = pull_group(
        w_qkv, b_qkv, w_out, b_out, gain_one, shift_one
    )
    grad_mixed = grad_middle.astype(jnp.bfloat16)
    grad_bout = jnp.sum(grad_mixed.astype(jnp.float32), axis=0)
    grad_wout = contract_rows(attended_low, grad_mixed)
    grad_attended = split_heads(contract_cols(grad_mixed, again_out))
    grad_numer = (keeping[None, :, None] * grad_attended / denominator[:, :, None]).astype(
        jnp.bfloat16
    )
    grad_denom = -jnp.sum(grad_attended * attended, axis=2) / denominator
    grad_query_heads, grad_key_heads, grad_value_heads = lax.map(
        partial(head_backward, allowed),
        (query_heads, key_heads, value_heads, grad_numer, grad_denom),
    )
    grad_query = query_back(join_heads(grad_query_heads))[0]
    grad_key = key_back(join_heads(grad_key_heads))[0]
    grad_projected = jnp.concatenate(
        [grad_query, grad_key, join_heads(grad_value_heads)], axis=1
    ).astype(jnp.bfloat16)
    grad_bias_all = jnp.sum(grad_projected.astype(jnp.float32), axis=0)
    grad_bias_qk = grad_bias_all[: 2 * model_width]
    grad_bias_v = grad_bias_all[2 * model_width :]
    grad_qkv = contract_rows(normed_low, grad_projected)
    grad_normed = contract_cols(grad_projected, again_qkv)
    grad_rows_norm, grad_gain_one, grad_shift_one = norm_back(grad_normed)
    grad_inputs = (grad_middle + grad_rows_norm).astype(jnp.bfloat16)
    shard_qkv, shard_bias_qk, shard_wout, shard_small_one = push_group(
        grad_qkv,
        grad_bias_qk,
        grad_wout,
        jnp.stack([grad_bout, grad_bias_v, grad_gain_one, grad_shift_one]),
    )
    return (
        result.astype(jnp.bfloat16)[None],
        grad_inputs[None],
        shard_qkv,
        shard_bias_qk,
        shard_small_one[1],
        shard_wout,
        shard_small_one[0],
        shard_small_one[2],
        shard_small_one[3],
        shard_up,
        shard_bup,
        shard_down,
        shard_small_two[0],
        shard_small_two[1],
        shard_small_two[2],
    )


HALF_LANES = 64
TILE = 512
Z_HIGH, Z_LOW, Y_BIT, X_BIT = 8, 4, 2, 1
MIXED = ((Z_HIGH, X_BIT, Z_LOW, Y_BIT), (Z_HIGH, Y_BIT, Z_LOW, X_BIT))
LINED = ((Z_HIGH, Z_LOW, X_BIT, Y_BIT), (Z_HIGH, Z_LOW, Y_BIT, X_BIT))
SMALL = 128
GROUP = 16
ANY = pl.BlockSpec(memory_space=pl.ANY)
SMEM = pl.BlockSpec(memory_space=pltpu.SMEM)
VMEM = pl.BlockSpec(memory_space=pltpu.VMEM)
MIB = 1 << 20


def swap_chips(block, bit):
    return lax.ppermute(block, "fsdp", [(place, place ^ bit) for place in range(16)])


def swap_cores(block):
    return lax.ppermute(block, "dp", [(0, 1), (1, 0)])


def relative_place(order, slot, last):
    return (
        order[0] * (slot & 1)
        + order[1] * ((slot >> 1) & 1)
        + order[2] * ((slot >> 2) & 1)
        + order[3] * last
    )


def tie(*blocks):
    return lax.optimization_barrier(blocks)


def by_side(shard):
    half = shard.shape[1] // 2
    return shard[None, :, :half], shard[None, :, half:]


def swap_sides(sides, orders, step):
    first, second = orders[0][step], orders[1][step]
    if first == second:
        return (swap_chips(jnp.stack(sides), first),)
    return swap_chips(sides[0], first), swap_chips(sides[1], second)


def sides_of(arrived):
    return (arrived[0][0], arrived[0][1]) if len(arrived) == 1 else arrived


def grown(sides, arrived):
    return tuple(jnp.concatenate([held, more]) for held, more in zip(sides, sides_of(arrived)))


def swap_both(sides):
    return swap_cores(sides[0]), swap_cores(sides[1])


def pieces_of(held, plane, across, core_held, core_across):
    plane = sides_of(plane)
    return tuple(
        block
        for side in range(2)
        for block in (held[side], plane[side], across[side], core_held[side], core_across[side])
    )


def added(parts, start, stop):
    return sum(part[start:stop].astype(jnp.float32) for part in parts)


def reduce_step(sides, orders, step, amount):
    sent = [added(parts, amount, 2 * amount).astype(jnp.bfloat16) for parts in sides]
    return swap_sides(sent, orders, step)


def with_arrived(sides, arrived):
    return [parts + [more] for parts, more in zip(sides, sides_of(arrived))]


def reduce_end(sides, orders):
    sides = with_arrived(sides, reduce_step(sides, orders, 0, 1))
    return [added(parts, 0, 1)[0] for parts in sides]


def side_by_side(sides, start, stop):
    return jnp.concatenate([side[:, start:stop] for side in sides], axis=1)


def far(array):
    return pltpu.with_memory_space_constraint(array, pltpu.HBM)


def call(kernel, outs, scratch, mib, args, in_specs, out_specs, grid=None, flops=0, gates=()):
    inputs, ignored = len(in_specs), len(gates)

    def gated(*refs):
        kernel(*refs[:inputs], *refs[inputs + ignored :])

    extra = {} if grid is None else {"grid": grid}
    near = (SMEM,) if grid else (SMEM, VMEM)
    args = [arg if spec in near else far(arg) for arg, spec in zip(args, in_specs)]
    gates = [far(gate) for gate in gates]
    if isinstance(outs, tuple):
        outs = tuple(
            out if spec in near else pltpu.HBM(out.shape, out.dtype)
            for out, spec in zip(outs, out_specs)
        )
    return pl.pallas_call(
        gated,
        out_shape=outs,
        in_specs=list(in_specs) + [ANY] * ignored,
        out_specs=out_specs,
        scratch_shapes=scratch,
        compiler_params=pltpu.CompilerParams(vmem_limit_bytes=mib * MIB),
        cost_estimate=pl.CostEstimate(flops=flops, bytes_accessed=0, transcendentals=0),
        **extra,
    )(*args, *gates)


def shaped(shape, dtype):
    return jax.ShapeDtypeStruct(shape, dtype)


def dot_nn(left, right):
    return lax.dot_general(left, right, (((1,), (0,)), ((), ())), preferred_element_type=jnp.float32)


def dot_nt(left, right):
    return lax.dot_general(left, right, (((1,), (1,)), ((), ())), preferred_element_type=jnp.float32)


def piece_at(pieces, side, core, last, slot):
    mine = pieces[5 * side : 5 * side + 5]
    if core or last:
        return mine[1 + core * 2 + last], slot
    return mine[slot // 4], slot % 4


def fetch(place, pieces, whole, sems, skip=0, orders=LINED):
    rows, half = pieces[0].shape[1], whole.shape[1] // 2
    copies = []
    for side, order in enumerate(orders):
        for core in range(2):
            for last in range(2):
                for slot in range(8):
                    piece, index = piece_at(pieces, side, core, last, slot)
                    owner = (place[1] ^ core) * 16 + (place[0] ^ relative_place(order, slot, last))
                    start = pl.multiple_of(owner * rows, rows)
                    copies.append(
                        pltpu.make_async_copy(
                            piece.at[index, :, pl.ds(skip, half)],
                            whole.at[pl.ds(start, rows), pl.ds(side * half, half)],
                            sems.at[len(copies)],
                        )
                    )
    for copy in copies:
        copy.start()
    return copies


def wait_side(copies, side):
    half = len(copies) // 2
    wait_all(copies[side * half : (side + 1) * half])


def wait_all(copies):
    for copy in copies:
        copy.wait()


def standardize(block):
    centred = block - jnp.mean(block, axis=1, keepdims=True)
    scale = lax.rsqrt(jnp.mean(centred * centred, axis=1, keepdims=True) + norm_eps)
    return centred * scale, scale


def norm_pull(grad, standard, scale, gain):
    scaled = grad * gain
    return scale * (
        scaled
        - jnp.mean(scaled, axis=1, keepdims=True)
        - standard * jnp.mean(scaled * standard, axis=1, keepdims=True)
    )


def place_kernel(where, lengths, valid, place):
    place[0] = where[0] & 15
    place[1] = where[0] >> 4
    end = lengths[0, 0]
    place[2] = end
    for image in range(1, 3):
        end = end + lengths[0, image]
        place[2 + image] = end
    place[5] = valid[0]


def run_place(where, lengths, valid):
    return call(
        place_kernel,
        shaped((6,), jnp.int32),
        [],
        8,
        (where, lengths, valid),
        in_specs=[SMEM] * 3,
        out_specs=SMEM,
    )


def fetch_small(place, pieces, small, skip, sems):
    copies = []
    for core in range(2):
        for last in range(2):
            for slot in range(8):
                piece, index = piece_at(pieces, 0, core, last, slot)
                far = relative_place(LINED[0], slot, last)
                owner = (place[1] ^ core) * 16 + (place[0] ^ far)
                start = pl.multiple_of(owner * GROUP, GROUP)
                copies.append(
                    pltpu.make_async_copy(
                        piece.at[index, pl.ds(0, GROUP), pl.ds(skip, SMALL)],
                        small.at[pl.ds(start, GROUP), :],
                        sems.at[len(copies)],
                    )
                )
                copies[-1].start()
    return copies


def tables(each):
    total = 32 * each
    column = lax.broadcasted_iota(jnp.int32, (1, total), 1).astype(jnp.float32)
    turn = jnp.floor((column + 0.5) / each)
    lane = lax.broadcasted_iota(jnp.int32, (SMALL, 1), 0).astype(jnp.float32)
    spread = jnp.where(column - turn * each == lane, 1.0, 0.0).astype(jnp.bfloat16)
    owner = lax.broadcasted_iota(jnp.int32, (32, 1), 0).astype(jnp.float32)
    return owner == turn, spread


def unfold(small, each, rows):
    mine, spread = tables(each)
    lines = []
    for row in rows:
        parts = small[pl.ds(row, 32, stride=GROUP), :].astype(jnp.bfloat16)
        parts = jnp.where(mine, dot_nn(parts, spread), 0.0)
        lines.append(jnp.sum(parts, axis=0, keepdims=True))
    return lines


def fold(small, each, vectors):
    mine, spread = tables(each)
    for row, vector in vectors:
        parts = jnp.where(mine, vector, 0.0).astype(jnp.bfloat16)
        small[pl.ds(row, 32, stride=32), :] = dot_nt(parts, spread)


def qkv_kernel(place, rows_in, *rest):
    pieces, (normed, query, key, value), lines, rest = rest[:10], rest[10:14], rest[14:20], rest[20:]
    whole, small, smalls, bias, sems, more = rest
    few = fetch_small(place, pieces, small, 4 * whole.shape[1] // 6, more)
    copies = fetch(place, pieces, whole, sems)
    wait_all(few)
    smalls[...] = small[...].astype(jnp.float32)
    width = rows_in.shape[1]
    (bias[...],) = unfold(smalls, 3 * width // 32, (0,))
    (lines[5][...],) = unfold(smalls, 4 * width // 32, (4,))
    bias_out, gain, shift, bias_down, gain_two, shift_two = unfold(
        smalls, width // 32, (1, 2, 3, 5, 6, 7)
    )
    for goal, line in zip(lines, (gain, bias_out, gain_two, shift_two, bias_down)):
        goal[...] = line
    for part in range(4):
        at = pl.ds(part * 128, 128)
        standard, _ = standardize(rows_in[at, :].astype(jnp.float32))
        normed[at, :] = (standard * gain + shift).astype(jnp.bfloat16)
    for tile in range(6):
        if tile % 3 == 0:
            wait_side(copies, tile // 3)
        cols = pl.ds(tile * TILE, TILE)
        projected = dot_nn(normed[...], whole[:, cols]) + bias[:, cols]
        goal = (query, key, value)[tile // 2]
        if tile < 4:
            projected = feature_map(projected)
        goal[:, pl.ds((tile % 2) * TILE, TILE)] = projected.astype(jnp.bfloat16)


def run_qkv(place, rows_in, pieces, gates=()):
    length, width = rows_in.shape
    narrow = shaped((length, width), jnp.bfloat16)
    line = shaped((1, width), jnp.float32)
    return call(
        qkv_kernel,
        (narrow,) * 4 + (line,) * 5 + (shaped((1, 4 * width), jnp.float32),),
        [
            pltpu.VMEM((width, 3 * width), jnp.bfloat16),
            pltpu.VMEM((32 * GROUP, SMALL), jnp.bfloat16),
            pltpu.VMEM((32 * GROUP, SMALL), jnp.float32),
            pltpu.VMEM((1, 3 * width), jnp.float32),
            pltpu.SemaphoreType.DMA((64,)),
            pltpu.SemaphoreType.DMA((32,)),
        ],
        18,
        (place, rows_in, *pieces),
        in_specs=[SMEM, VMEM] + [ANY] * 10,
        out_specs=(VMEM,) * 10,
        gates=gates,
    )


def image_of(place, positions):
    image = jnp.zeros(positions.shape, jnp.int32)
    for end in range(2, 5):
        image = image + jnp.where(positions >= place[end], 1, 0)
    return image


def allowed_block(place, length, flipped):
    first = lax.broadcasted_iota(jnp.int32, (length, 1), 0)
    second = lax.broadcasted_iota(jnp.int32, (1, length), 1)
    same = image_of(place, first) == image_of(place, second)
    ordered = (first <= second) if flipped else (second <= first)
    return jnp.where(same & ordered, 1.0, 0.0).astype(jnp.float32)


def low_lanes():
    return lax.broadcasted_iota(jnp.int32, (1, 2 * HALF_LANES), 1) < HALF_LANES


def two_heads(block):
    low = jnp.where(low_lanes(), 1.0, 0.0)
    high = (1.0 - low).astype(jnp.bfloat16)
    return jnp.concatenate([block * low.astype(jnp.bfloat16), block * high], axis=0)


def one_pair(stacked):
    half = stacked.shape[0] // 2
    return jnp.where(low_lanes(), stacked[:half], stacked[half:])


def masked(stacked, allowed):
    half = stacked.shape[0] // 2
    return jnp.concatenate(
        [(stacked[:half] * allowed).astype(jnp.bfloat16), (stacked[half:] * allowed).astype(jnp.bfloat16)],
        axis=0,
    )


def keeping_rows(place, start, amount):
    position = lax.broadcasted_iota(jnp.int32, (amount, 1), 0) + start
    return jnp.where(position < place[5], 1.0, 0.0)


def attend_kernel(place, query, key, value, attended, exact, inverse, allowed, wide):
    length, width = query.shape
    step = length // 2

    @pl.when(pl.program_id(0) == 0)
    def _():
        allowed[...] = allowed_block(place, length, False)
        wide[:, width:] = jnp.ones((length, width), jnp.bfloat16)

    wide[:, :width] = value[...]
    for part in range(2):
        rows, seen = pl.ds(part * step, step), (part + 1) * step
        scores = dot_nt(two_heads(query[rows, :]), key[:seen, :])
        total = dot_nn(masked(scores, allowed[rows, :seen]), wide[:seen, :])
        over = 1.0 / (one_pair(total[:, width:]) + denom_eps)
        inverse[rows, :] = over
        mixed = keeping_rows(place, part * step, step) * one_pair(total[:, :width]) * over
        exact[rows, :] = mixed
        attended[rows, :] = mixed.astype(jnp.bfloat16)


def run_attend(place, query, key, value, gates=()):
    length, width = query.shape
    pair = pl.BlockSpec((length, 2 * HALF_LANES), lambda p: (0, p))
    return call(
        attend_kernel,
        (
            shaped((length, width), jnp.bfloat16),
            shaped((length, width), jnp.float32),
            shaped((length, width), jnp.float32),
        ),
        [
            pltpu.VMEM((length, length), jnp.float32),
            pltpu.VMEM((length, 4 * HALF_LANES), jnp.bfloat16),
        ],
        10,
        (place, query, key, value),
        grid=(width // (2 * HALF_LANES),),
        in_specs=[SMEM] + [pair] * 3,
        out_specs=(pair,) * 3,
        gates=gates,
    )


def attend_back_pair(
    place, query, key, value, grad_att, exact, inverse, stacked, sums, allowed, flipped, left, wide
):
    length, width = query.shape
    step = length // 2
    wide[:, :width] = value[...]
    over = grad_att[...] * inverse[...]
    lane = lax.broadcasted_iota(jnp.int32, (1, width), 1)
    terms, low = over * exact[...], lane < HALF_LANES
    first = jnp.sum(jnp.where(low, terms, 0.0), axis=1, keepdims=True)
    second = jnp.sum(jnp.where(low, 0.0, terms), axis=1, keepdims=True)
    spread = -jnp.where(low, first, second)
    high = spread.astype(jnp.bfloat16).astype(jnp.float32)
    within = lane & (HALF_LANES - 1)
    spread = jnp.where(within == 0, high, jnp.where(within == 1, spread - high, 0.0))
    numer = (keeping_rows(place, 0, length) * over).astype(jnp.bfloat16)
    for head in range(2):
        here = jnp.where(low, 1.0 - head, 1.0 * head)
        at = pl.ds(head * length, length)
        left[at, :width] = numer * here.astype(jnp.bfloat16)
        left[at, width:] = (spread * here).astype(jnp.bfloat16)
    for part in range(2):
        rows, seen = pl.ds(part * step, step), (part + 1) * step
        start = part * step
        later = pl.ds(start, length - start)
        both = jnp.concatenate([left[rows, :], left[pl.ds(length + start, step), :]], axis=0)
        grad_scores = masked(dot_nt(both, wide[:seen, :]), allowed[rows, :seen])
        grad_query = one_pair(dot_nn(grad_scores, key[:seen, :]))
        full = left[later, :] + left[pl.ds(length + start, length - start), :]
        scores = masked(dot_nt(two_heads(key[rows, :]), query[later, :]), flipped[rows, later])
        grad_value = one_pair(dot_nn(scores, full[:, :width]))
        ones = jnp.concatenate([two_heads(value[rows, :]), two_heads(wide[rows, width:])], axis=1)
        grad_scores = masked(dot_nt(ones, full), flipped[rows, later])
        grad_key = one_pair(dot_nn(grad_scores, query[later, :]))
        grads = (
            grad_query * jnp.minimum(query[rows, :].astype(jnp.float32), 1.0),
            grad_key * jnp.minimum(key[rows, :].astype(jnp.float32), 1.0),
            grad_value,
        )
        for index, grad in enumerate(grads):
            low_grad, line = grad.astype(jnp.bfloat16), pl.ds(index, 1)
            stacked[index, rows, :] = low_grad
            extra = jnp.sum(low_grad.astype(jnp.float32), axis=0, keepdims=True)
            sums[line, :] = extra if part == 0 else sums[line, :] + extra


def attend_back_kernel(
    place, query, key, value, grad_att, exact, inverse, stacked, sums, allowed, flipped, left, wide
):
    length, width = query.shape[0], 2 * HALF_LANES
    pairs = query.shape[1] // width

    @pl.when(pl.program_id(0) == 0)
    def _():
        allowed[...] = allowed_block(place, length, False)
        flipped[...] = allowed_block(place, length, True)
        for pair in range(pairs):
            wide[pair, :, width:] = jnp.ones((length, width), jnp.bfloat16)

    for pair in range(pairs):
        cols = pl.ds(pair * width, width)
        attend_back_pair(
            place,
            *(ref.at[:, cols] for ref in (query, key, value, grad_att, exact, inverse)),
            stacked.at[:, :, cols],
            sums.at[:, cols],
            allowed,
            flipped,
            left.at[pair],
            wide.at[pair],
        )


def run_attend_back(place, first, query, key, value, grad_att, exact, inverse, gates=()):
    length, width = query.shape
    half = width // 2
    start = first * half // (4 * HALF_LANES)
    pair = pl.BlockSpec((length, 4 * HALF_LANES), lambda p: (0, p + start))
    stack = pl.BlockSpec((3, length, 4 * HALF_LANES), lambda p: (0, 0, p))
    lines = pl.BlockSpec((3, 4 * HALF_LANES), lambda p: (0, p))
    return call(
        attend_back_kernel,
        (shaped((3, length, half), jnp.bfloat16), shaped((3, half), jnp.float32)),
        [
            pltpu.VMEM((length, length), jnp.float32),
            pltpu.VMEM((length, length), jnp.float32),
            pltpu.VMEM((2, 2 * length, 4 * HALF_LANES), jnp.bfloat16),
            pltpu.VMEM((2, length, 4 * HALF_LANES), jnp.bfloat16),
        ],
        20,
        (place, query, key, value, grad_att, exact, inverse),
        grid=(half // (4 * HALF_LANES),),
        in_specs=[SMEM] + [pair] * 6,
        out_specs=(stack, lines),
        gates=gates,
    )


def hand_over(place, sources, goal, sems):
    copies, at = [], 0
    for source in sources:
        half = source.shape[1] // 2
        start = pl.multiple_of((1 - place[1]) * half, half)
        copies.append(
            pltpu.make_async_copy(
                source.at[:, pl.ds(start, half)], goal.at[:, pl.ds(at, half)], sems.at[len(copies)]
            )
        )
        copies[-1].start()
        at += half
    return copies


def out_kernel(place, rows_in, early, attended, bias, gain, shift, *rest):
    pieces, (middle, normed, handed, whole, sems, more) = rest[:10], rest[10:]
    copies = fetch(place, pieces, whole, sems, 3 * whole.shape[1] // 2)
    handing = hand_over(place, (early, attended), handed, more)
    for side in range(2):
        wait_side(copies, side)
        cols = pl.ds(side * TILE, TILE)
        middle[:, cols] = (
            rows_in[:, cols].astype(jnp.float32) + dot_nn(attended[...], whole[:, cols]) + bias[:, cols]
        )
    for part in range(4):
        at = pl.ds(part * 128, 128)
        standard, _ = standardize(middle[at, :])
        normed[at, :] = (standard * gain[...] + shift[...]).astype(jnp.bfloat16)
    wait_all(handing)


def run_out(place, rows_in, early, attended, bias, gain, shift, pieces, gates=()):
    length, width = rows_in.shape
    narrow = shaped((length, width), jnp.bfloat16)
    return call(
        out_kernel,
        (shaped((length, width), jnp.float32), narrow, narrow),
        [
            pltpu.VMEM((width, width), jnp.bfloat16),
            pltpu.SemaphoreType.DMA((64,)),
            pltpu.SemaphoreType.DMA((2,)),
        ],
        16,
        (place, rows_in, early, attended, bias, gain, shift, *pieces),
        in_specs=[SMEM] + [VMEM] * 6 + [ANY] * 10,
        out_specs=(VMEM, VMEM, ANY),
        gates=gates,
    )


def bend_tile(hidden, activated, slope):
    square = hidden * hidden
    rate = gelu_coef + (gelu_coef * 0.044715) * square
    bend = jnp.tanh(hidden * rate)
    share = 0.5 + 0.5 * bend
    activated[...] = (hidden * share).astype(jnp.bfloat16)
    rate = gelu_coef + (3.0 * gelu_coef * 0.044715) * square
    slope[...] = (share + (0.5 * hidden) * (1.0 - bend * bend) * rate).astype(jnp.bfloat16)


def up_kernel(place, normed, bias, *rest):
    pieces, (activated, slope, handed, whole, hidden, sems, more) = rest[:10], rest[10:]
    copies = fetch(place, pieces, whole, sems)
    tiles = whole.shape[1] // TILE

    def columns(tile):
        return pl.ds(tile * TILE, TILE)

    for tile in range(tiles + 1):
        if tile % (tiles // 2) == 0 and tile < tiles:
            wait_side(copies, tile // (tiles // 2))
        if tile < tiles:
            cols = columns(tile)
            hidden[tile % 2] = dot_nn(normed[...], whole[:, cols]) + bias[:, cols]
        if tile > 0:
            cols = columns(tile - 1)
            bend_tile(hidden[(tile - 1) % 2], activated.at[:, cols], slope.at[:, cols])

    wait_all(hand_over(place, (normed, activated), handed, more))


def run_up(place, normed, bias, pieces, gates=()):
    length, width = normed.shape
    wide = bias.shape[1]
    return call(
        up_kernel,
        (shaped((length, wide), jnp.bfloat16),) * 2
        + (shaped((length, (width + wide) // 2), jnp.bfloat16),),
        [
            pltpu.VMEM((width, wide), jnp.bfloat16),
            pltpu.VMEM((2, length, TILE), jnp.float32),
            pltpu.SemaphoreType.DMA((64,)),
            pltpu.SemaphoreType.DMA((2,)),
        ],
        26,
        (place, normed, bias, *pieces),
        in_specs=[SMEM] + [VMEM] * 2 + [ANY] * 10,
        out_specs=(VMEM, VMEM, ANY),
        gates=gates,
    )


def sum_kernel(block, total):
    total[...] = jnp.sum(block[...].astype(jnp.float32), axis=0, keepdims=True)


def run_sum(block, cover, gates=()):
    return call(
        sum_kernel,
        shaped((1, block.shape[1]), jnp.float32),
        [],
        8,
        (block,),
        in_specs=[VMEM],
        out_specs=VMEM,
        flops=cover,
        gates=gates,
    )


def down_kernel(place, activated, slope, grad_top, middle, bias, *rest):
    pieces, (result, grad_hidden, sum_up, whole, sems) = rest[:10], rest[10:]
    copies = fetch(place, pieces, whole, sems, orders=MIXED)
    wait_all(copies)
    for tile in range(4):
        cols = pl.ds(tile * 256, 256)
        result[:, cols] = (
            middle[:, cols] + bias[:, cols] + dot_nn(activated[...], whole[:, cols])
        ).astype(jnp.bfloat16)
        for half in range(2):
            cols = pl.ds((2 * tile + half) * TILE, TILE)
            grad = dot_nt(grad_top[...], whole[cols, :]) * slope[:, cols].astype(jnp.float32)
            low = grad.astype(jnp.bfloat16)
            grad_hidden[:, cols] = low
            sum_up[:, cols] = jnp.sum(low.astype(jnp.float32), axis=0, keepdims=True)


def run_down(place, activated, slope, grad_top, middle, bias, pieces, gates=()):
    length, width = middle.shape
    wide = activated.shape[1]
    return call(
        down_kernel,
        (
            shaped((length, width), jnp.bfloat16),
            shaped((length, wide), jnp.bfloat16),
            shaped((1, wide), jnp.float32),
        ),
        [
            pltpu.VMEM((wide, width), jnp.bfloat16),
            pltpu.SemaphoreType.DMA((64,)),
        ],
        30,
        (place, activated, slope, grad_top, middle, bias, *pieces),
        in_specs=[SMEM] + [VMEM] * 5 + [ANY] * 10,
        out_specs=(VMEM,) * 3,
        flops=64 * length * width * wide,
        gates=gates,
    )


def middle_back_kernel(place, grad_hidden, middle, grad_top, gain, *rest):
    pieces_up, pieces_in, rest = rest[:10], rest[10:20], rest[20:]
    grad_middle, mixed, grad_att, sum_gain, sum_shift, whole, outer, total, sems, more = rest
    copies = fetch(place, pieces_up, whole, sems)
    second = fetch(place, pieces_in, outer, more, 3 * outer.shape[1] // 2)
    step = 2 * TILE
    for tile in range(whole.shape[1] // step):
        if tile % 2 == 0:
            wait_side(copies, tile // 2)
        cols = pl.ds(tile * step, step)
        block = dot_nt(grad_hidden[:, cols], whole[:, cols])
        total[...] = block if tile == 0 else total[...] + block

    for part in range(4):
        at = pl.ds(part * 128, 128)
        grad = total[at, :]
        standard, scale = standardize(middle[at, :])
        back = grad_top[at, :].astype(jnp.float32) + norm_pull(grad, standard, scale, gain[...])
        grad_middle[at, :] = back
        low = back.astype(jnp.bfloat16)
        mixed[at, :] = low
        for goal, added in ((sum_gain, grad * standard), (sum_shift, grad)):
            added = jnp.sum(added, axis=0, keepdims=True)
            goal[...] = added if part == 0 else goal[...] + added
    wait_all(second)
    for part in range(2):
        cols = pl.ds(part * TILE, TILE)
        grad_att[:, cols] = dot_nt(mixed[...], outer[cols, :])


def run_middle_back(place, grad_hidden, middle, grad_top, gain, pieces_up, pieces_in, gates=()):
    length, width = middle.shape
    wide = grad_hidden.shape[1]
    full, line = shaped((length, width), jnp.float32), shaped((1, width), jnp.float32)
    return call(
        middle_back_kernel,
        (full, shaped((length, width), jnp.bfloat16), full, line, line),
        [
            pltpu.VMEM((width, wide), jnp.bfloat16),
            pltpu.VMEM((width, width), jnp.bfloat16),
            pltpu.VMEM((length, width), jnp.float32),
            pltpu.SemaphoreType.DMA((64,)),
            pltpu.SemaphoreType.DMA((64,)),
        ],
        30,
        (place, grad_hidden, middle, grad_top, gain, *pieces_up, *pieces_in),
        in_specs=[SMEM] + [VMEM] * 4 + [ANY] * 20,
        out_specs=(VMEM,) * 5,
        gates=gates,
    )


def inputs_back_kernel(place, early, late, rows_in, gain, grad_middle, sum_out, *rest):
    (sums, late_sums, *ready), pieces, rest = rest[:6], rest[6:16], rest[16:]
    grad_rows, lines, whole, total, sems = rest
    copies = fetch(place, pieces, whole, sems)
    width = rows_in.shape[1]
    for tile in range(6):
        if tile % 3 == 0:
            wait_side(copies, tile // 3)
        grads = (early, late)[tile % 2]
        block = dot_nt(grads[tile // 2], whole[:, pl.ds(tile * TILE, TILE)])
        total[...] = block if tile == 0 else total[...] + block
    for part in range(4):
        at = pl.ds(part * 128, 128)
        grad = total[at, :]
        standard, scale = standardize(rows_in[at, :].astype(jnp.float32))
        back = grad_middle[at, :] + norm_pull(grad, standard, scale, gain[...])
        grad_rows[at, :] = back.astype(jnp.bfloat16)
        for index, extra in enumerate((grad * standard, grad)):
            goal = lines.at[:, pl.ds((4 + index) * width, width)]
            extra = jnp.sum(extra, axis=0, keepdims=True)
            goal[...] = extra if part == 0 else goal[...] + extra
    half = width // 2
    for row in range(3):
        for index, source in enumerate((sums, late_sums)):
            lines[:, pl.ds(row * width + index * half, half)] = source[pl.ds(row, 1), :]
    lines[:, pl.ds(3 * width, width)] = sum_out[...]
    at = 6 * width
    for source in ready:
        lines[:, pl.ds(at, source.shape[1])] = source[...]
        at += source.shape[1]


def run_inputs_back(
    place, early, late, rows_in, gain, grad_middle, sum_out, ready, pieces, gates=()
):
    length, width = rows_in.shape
    total = 6 * width + sum(line.shape[1] for line in ready[2:])
    return call(
        inputs_back_kernel,
        (shaped((length, width), jnp.bfloat16), shaped((1, total), jnp.float32)),
        [
            pltpu.VMEM((width, 3 * width), jnp.bfloat16),
            pltpu.VMEM((length, width), jnp.float32),
            pltpu.SemaphoreType.DMA((64,)),
        ],
        20,
        (place, early, late, rows_in, gain, grad_middle, sum_out, *ready, *pieces),
        in_specs=[SMEM] + [VMEM] * 12 + [ANY] * 10,
        out_specs=(VMEM,) * 2,
        flops=1 << 34,
        gates=gates,
    )


def weight_kernel(orders, skips, sizes, place, *rest):
    groups = len(skips)
    if sizes:
        mine, other_lines, rest = rest[4 * groups], rest[4 * groups + 1], rest[: 4 * groups] + rest[4 * groups + 2 :]
    inputs, outs, rest = rest[: 4 * groups], rest[4 * groups : 4 * groups + 4], rest[4 * groups + 4 :]
    wholes, (turned, sems), rest = rest[:groups], rest[groups : groups + 2], rest[groups + 2 :]
    length, rows = inputs[0].shape[0], outs[0].shape[1]
    owners = 256 // rows
    at, copies = 0, []
    for group, (skip, whole) in enumerate(zip(skips, wholes)):
        left_own, left_other, own, other = inputs[4 * group : 4 * group + 4]
        count, each = own.shape[0], own.shape[2]
        tiles, half = whole.shape[0], whole.shape[2] // 2
        for tile in range(tiles):
            low = pl.multiple_of(((place[0] // owners) ^ tile) * 256, 256)
            start = pl.multiple_of(place[1] * (256 * tiles) + low, 256)
            left = turned.at[tile % 2]
            left[:, :length] = left_own[:, pl.ds(start, 256)].T
            left[:, length:] = left_other[:, pl.ds(skip + low, 256)].T
            for index in range(count):
                for step in range(each // TILE):
                    cols = pl.ds(step * TILE, TILE)
                    block = dot_nn(left[:, :length], own[index, :, cols])
                    block += dot_nn(left[:, length:], other[index, :, cols])
                    goal = pl.ds(index * each + step * TILE, TILE)
                    whole[tile, :, goal] = block.astype(jnp.bfloat16)
            for side, order in enumerate(orders):
                for last in range(2):
                    for slot in range(8):
                        far_place = relative_place(order, slot, last)
                        if far_place // owners != tile:
                            continue
                        start = pl.multiple_of(((place[0] ^ far_place) % owners) * rows, rows)
                        copies.append(
                            pltpu.make_async_copy(
                                whole.at[tile, pl.ds(start, rows), pl.ds(side * half, half)],
                                outs[last * 2 + side].at[slot, :, pl.ds(at, half)],
                                sems.at[len(copies)],
                            )
                        )
                        copies[-1].start()
        at += half
    if sizes:
        wide_small, small, more = rest
        wide_small[...] = jnp.zeros_like(wide_small)
        start, by_size = 0, {}
        for row, size in enumerate(sizes):
            line = mine[:, start : start + size] + other_lines[:, start : start + size]
            by_size.setdefault(size, []).append((row, line))
            start += size
        for size, vectors in by_size.items():
            fold(wide_small, size // 32, vectors)
        small[...] = wide_small[...].astype(jnp.bfloat16)
        for last in range(2):
            for slot in range(8):
                chip = place[0] ^ relative_place(orders[0], slot, last)
                start = pl.multiple_of((place[1] * 16 + chip) * 32, 32)
                copies.append(
                    pltpu.make_async_copy(
                        small.at[pl.ds(start, 32), :],
                        outs[last * 2].at[slot, :, pl.ds(at, SMALL)],
                        more.at[last * 8 + slot],
                    )
                )
                copies[-1].start()
    wait_all(copies)


def run_weight(place, orders, height, groups, gates=(), sizes=(), lines=()):
    length = groups[0][0].shape[0]
    totals = [own.shape[0] * own.shape[2] for _, _, _, own, _ in groups]
    half = sum(totals) // 2
    part = shaped((8, height // 16, half), jnp.bfloat16)
    first = shaped((8, height // 16, half + (SMALL if sizes else 0)), jnp.bfloat16)
    extra = [
        pltpu.VMEM((32 * 32, SMALL), jnp.float32),
        pltpu.VMEM((32 * 32, SMALL), jnp.bfloat16),
        pltpu.SemaphoreType.DMA((16,)),
    ]
    return call(
        partial(weight_kernel, orders, tuple(group[2] for group in groups), sizes),
        (first,) * 4,
        [pltpu.VMEM((height // 256, 256, total), jnp.bfloat16) for total in totals]
        + [
            pltpu.VMEM((2, 256, 2 * length), jnp.bfloat16),
            pltpu.SemaphoreType.DMA((32 * len(groups),)),
        ]
        + (extra if sizes else []),
        22,
        (place, *(array for group in groups for array in group[:2] + group[3:]), *lines),
        in_specs=[SMEM] + [VMEM] * (4 * len(groups) + len(lines)),
        out_specs=(ANY,) * 4,
        gates=gates,
    )


def paired_body(
    inputs,
    cotangent,
    seg_lengths,
    valid_len,
    w_qkv,
    b_qkv,
    w_out,
    b_out,
    gain_one,
    shift_one,
    w_up,
    b_up,
    w_down,
    b_down,
    gain_two,
    shift_two,
):
    where = (lax.axis_index("dp") * 16 + lax.axis_index("fsdp")).astype(jnp.int32)[None]
    rows_in, grad_top = inputs[0], cotangent[0]
    vectors = (b_qkv, b_out, gain_one, shift_one, b_up, b_down, gain_two, shift_two)
    cut = w_qkv.shape[1] // 2
    edge = w_out.shape[1] // 2
    held_in = (
        jnp.concatenate([w_qkv[:, :cut], w_out[:, :edge]], axis=1)[None],
        jnp.concatenate([w_qkv[:, cut:], w_out[:, edge:]], axis=1)[None],
    )
    small = jnp.stack([jnp.pad(vector, (0, SMALL - vector.shape[0])) for vector in vectors])
    small = jnp.pad(small, ((0, w_out.shape[0] - small.shape[0]), (0, 0)))[None]
    small_far = swap_chips(small, Z_HIGH)
    place = run_place(where, seg_lengths, valid_len)
    place, small_far = tie(place, small_far)
    small = jnp.concatenate([small, small_far])
    held_up, held_down = by_side(w_up), by_side(w_down)
    top = grad_top[None]
    held_in = grown(held_in, swap_sides(held_in, LINED, 0))
    held_in = (
        jnp.concatenate([held_in[0], small], axis=2),
        jnp.concatenate([held_in[1], jnp.zeros_like(small)], axis=2),
    )
    held_in = grown(held_in, swap_sides(held_in, LINED, 1))
    held_in, held_up = tie(held_in, held_up)
    start_up = swap_sides(held_up, LINED, 0)
    plane_in = swap_sides(held_in, LINED, 2)
    start_up, plane_in = tie(start_up, plane_in)
    held_up = grown(held_up, start_up)
    held_up, held_down = tie(held_up, held_down)
    full_in = grown(held_in, plane_in)
    across_in = swap_sides(full_in, LINED, 3)
    core_in = swap_both(full_in)
    held_up = grown(held_up, swap_sides(held_up, LINED, 1))
    start_down = swap_sides(held_down, LINED, 0)
    across_in, start_down = tie(across_in, start_down)
    pieces_in = pieces_of(held_in, plane_in, across_in, core_in, swap_both(across_in))
    plane_up = swap_sides(held_up, LINED, 2)
    held_down = grown(held_down, start_down)
    plane_down = swap_sides(held_down, MIXED, 1)
    top_other = swap_cores(top)

    normed, query, key, value, *lines = run_qkv(
        place, rows_in, pieces_in, (*held_up, *held_down, top_other)
    )
    full_gain, full_bout, full_gain_two, full_shift_two, full_bdown, full_bup = lines
    plane_up, plane_down, normed = tie(plane_up, plane_down, normed)
    full_up = grown(held_up, plane_up)
    across_up = swap_sides(full_up, LINED, 3)
    core_up = swap_both(full_up)
    held_down = grown(held_down, plane_down)
    line_down = swap_sides(held_down, MIXED, 2)
    attended, exact, inverse = run_attend(place, query, key, value, (*plane_up, *held_down))
    core_up, attended = tie(core_up, attended)
    middle, normed_two, inner_half = run_out(
        place,
        rows_in,
        normed,
        attended,
        full_bout,
        full_gain_two,
        full_shift_two,
        pieces_in,
    )
    inner_other = swap_cores(inner_half)
    across_up, line_down, normed_two = tie(across_up, line_down, normed_two)
    pieces_up = pieces_of(held_up, plane_up, across_up, core_up, swap_both(across_up))
    full_down = grown(held_down, line_down)
    across_down = swap_sides(full_down, MIXED, 3)
    core_down = swap_both(full_down)
    activated, slope, outer_half = run_up(
        place, normed_two, full_bup, pieces_up, (*line_down, inner_other)
    )
    outer_other = swap_cores(outer_half)
    sum_down = run_sum(grad_top, 1 << 35, (outer_half,))
    thin = normed_two.shape[1] // 2
    parts = run_weight(
        place,
        LINED,
        activated.shape[1] // 2,
        [(activated, outer_other, thin, top, top_other)],
        (*core_down, sum_down),
    )
    across_down, parts = tie(across_down, parts)
    down_one = swap_sides(parts[2:], LINED, 3)
    pieces_down = pieces_of(held_down, line_down, across_down, core_down, swap_both(across_down))
    result, grad_hidden, sum_up = run_down(
        place, activated, slope, grad_top, middle, full_bdown, pieces_down, parts[2:]
    )
    hidden_other = swap_cores(grad_hidden[None])
    grad_middle, mixed, grad_att, sum_gain_two, sum_shift_two = run_middle_back(
        place, grad_hidden, middle, grad_top, full_gain_two, pieces_up, pieces_in
    )
    mixed = mixed[None]
    down_one, mixed = tie(down_one, mixed)
    mixed_other = swap_cores(mixed)
    down_sides = with_arrived([[parts[0]], [parts[1]]], down_one)
    down_two = reduce_step(down_sides, LINED, 2, 4)
    sum_out = run_sum(mixed[0], 1 << 35, down_one)
    hidden_other, sum_out = tie(hidden_other, sum_out)
    parts = run_weight(
        place, LINED, thin, [(normed_two, outer_other, 0, grad_hidden[None], hidden_other)]
    )
    up_one = swap_sides(parts[2:], LINED, 3)
    grads, sums = run_attend_back(
        place, 0, query, key, value, grad_att, exact, inverse, parts[2:]
    )
    down_two, mixed_other, grads = tie(down_two, mixed_other, grads)
    down_sides = with_arrived(down_sides, down_two)
    down_three = reduce_step(down_sides, LINED, 1, 2)
    grads_other = swap_cores(grads)
    late, late_sums = run_attend_back(
        place, 1, query, key, value, grad_att, exact, inverse, (grads,)
    )
    up_one, late = tie(up_one, late)
    up_sides = with_arrived([[parts[0]], [parts[1]]], up_one)
    late_other = swap_cores(late)
    up_two = reduce_step(up_sides, LINED, 2, 4)
    grad_rows, lines = run_inputs_back(
        place,
        grads,
        late,
        rows_in,
        full_gain,
        grad_middle,
        sum_out,
        (sums, late_sums, sum_up, sum_down, sum_gain_two, sum_shift_two),
        pieces_in,
        up_one,
    )
    up_two, down_three, grads_other, late_other, lines = tie(
        up_two, down_three, grads_other, late_other, lines
    )
    down_sides = with_arrived(down_sides, down_three)
    up_sides = with_arrived(up_sides, up_two)
    up_three = reduce_step(up_sides, LINED, 1, 2)
    lines_other = swap_cores(lines)
    parts = run_weight(
        place,
        MIXED,
        thin,
        [
            (normed, inner_other, 0, grads, grads_other),
            (attended, inner_other, thin, mixed, mixed_other),
        ],
    )
    lines_other, parts = tie(lines_other, parts)
    in_sides = [[parts[0]], [parts[1]]]
    in_one = swap_sides(parts[2:], MIXED, 3)
    narrow, wide = mixed.shape[2], sum_up.shape[1]
    sizes = (2 * narrow, narrow, narrow, narrow, narrow, wide, narrow, narrow, narrow)
    parts = run_weight(
        place,
        LINED,
        thin,
        [(normed, inner_other, 0, late, late_other)],
        parts[:1],
        sizes,
        (lines, lines_other),
    )
    down_four = reduce_step(down_sides, LINED, 0, 1)
    up_three, parts = tie(up_three, parts)
    up_sides = with_arrived(up_sides, up_three)
    up_four = reduce_step(up_sides, LINED, 0, 1)
    late_sides = [[parts[0]], [parts[1]]]
    late_one = swap_sides(parts[2:], LINED, 3)
    in_sides = with_arrived(in_sides, in_one)
    late_one, down_four = tie(late_one, down_four)
    down_sides = with_arrived(down_sides, down_four)
    late_sides = with_arrived(late_sides, late_one)
    in_sides = with_arrived(in_sides, reduce_step(in_sides, MIXED, 2, 4))
    late_sides = with_arrived(late_sides, reduce_step(late_sides, LINED, 2, 4))
    up_sides = with_arrived(up_sides, up_four)
    in_sides = with_arrived(in_sides, reduce_step(in_sides, MIXED, 1, 2))
    late_sides = with_arrived(late_sides, reduce_step(late_sides, LINED, 1, 2))
    shard_down = side_by_side([added(parts, 0, 1)[0] for parts in down_sides], 0, edge)
    shard_up = side_by_side([added(parts, 0, 1)[0] for parts in up_sides], 0, w_up.shape[1] // 2)
    shards = reduce_end(in_sides, MIXED)
    cut = cut // 2
    first = side_by_side(shards, 0, cut)
    shard_out = side_by_side(shards, cut, cut + edge)
    shards = reduce_end(late_sides, LINED)
    second = side_by_side(shards, 0, cut)
    third = edge
    shard_qkv = jnp.concatenate(
        [
            half[:, part * third : (part + 1) * third]
            for part in range(3)
            for half in (first, second)
        ],
        axis=1,
    )
    smalls = [shards[0][row, cut : cut + size // 32] for row, size in enumerate(sizes)]
    grad_bqk, grad_bv, grad_bout, grad_gain, grad_shift, grad_bup, grad_bdown, grad_gain_two, grad_shift_two = smalls
    return (
        result[None],
        grad_rows[None],
        shard_qkv,
        grad_bqk,
        grad_bv,
        shard_out,
        grad_bout,
        grad_gain,
        grad_shift,
        shard_up,
        grad_bup,
        shard_down,
        grad_bdown,
        grad_gain_two,
        grad_shift_two,
    )


def solution(mesh):
    placed = (
        P(("dp", "fsdp"), None, None),
        P(("dp", "fsdp"), None, None),
        P(("dp", "fsdp"), None),
        P(("dp", "fsdp")),
        P(("dp", "fsdp"), None),
        P(("dp", "fsdp")),
        P(("dp", "fsdp"), None),
        P(("dp", "fsdp")),
        P(("dp", "fsdp")),
        P(("dp", "fsdp")),
        P(("dp", "fsdp"), None),
        P(("dp", "fsdp")),
        P(("dp", "fsdp"), None),
        P(("dp", "fsdp")),
        P(("dp", "fsdp")),
        P(("dp", "fsdp")),
    )
    paired = dict(mesh.shape) == {"dp": 2, "fsdp": 16}
    return jax.shard_map(
        paired_body if paired else plain_body,
        mesh=mesh,
        in_specs=placed,
        out_specs=(
            P(("dp", "fsdp"), None, None),
            P(("dp", "fsdp"), None, None),
            P(("dp", "fsdp"), None),
            P(("dp", "fsdp")),
            P(("dp", "fsdp")),
            P(("dp", "fsdp"), None),
            P(("dp", "fsdp")),
            P(("dp", "fsdp")),
            P(("dp", "fsdp")),
            P(("dp", "fsdp"), None),
            P(("dp", "fsdp")),
            P(("dp", "fsdp"), None),
            P(("dp", "fsdp")),
            P(("dp", "fsdp")),
            P(("dp", "fsdp")),
        ),
        check_vma=False,
    )
```

```python
from functools import partial

import jax
import jax.numpy as jnp
from jax import lax
from jax.experimental import pallas as pl
from jax.experimental.pallas import tpu as pltpu
from jax.sharding import PartitionSpec as P

HEADS = 16


norm_eps = 1e-05
denom_eps = 1e-06
gelu_coef = 0.7978845608028654


def layer_norm(values, scale_gain, offset):
    centred = values - jnp.mean(values, axis=-1, keepdims=True)
    spread = jnp.mean(centred * centred, axis=-1, keepdims=True)
    return centred * lax.rsqrt(spread + norm_eps) * scale_gain + offset


def feature_map(values):
    return jnp.where(values > 0, values + 1.0, jnp.exp(jnp.minimum(values, 0.0)))


def gelu_tanh(values):
    return (
        0.5 * values * (1.0 + jnp.tanh(gelu_coef * (values + 0.044715 * values * values * values)))
    )


def contract_rows(left_side, right_side):
    return lax.dot_general(
        left_side, right_side, (((0,), (0,)), ((), ())), preferred_element_type=jnp.float32
    )


def contract_cols(left_side, right_side):
    return lax.dot_general(
        left_side, right_side, (((1,), (1,)), ((), ())), preferred_element_type=jnp.float32
    )


def row_masks(lengths, valid_count, row_length):
    places = jnp.arange(row_length, dtype=jnp.int32)
    bounds = jnp.stack([jnp.sum(lengths[: end + 1]) for end in range(lengths.shape[0])])
    segment = jnp.sum((places[:, None] >= bounds[None, :]).astype(jnp.int32), axis=1)
    allowed = (segment[:, None] == segment[None, :]) & (places[None, :] <= places[:, None])
    keeping = (places < valid_count).astype(jnp.float32)
    return (allowed.astype(jnp.float32), keeping)


def split_heads(matrix):
    return jnp.transpose(matrix.reshape(matrix.shape[0], HEADS, -1), (1, 0, 2))


def join_heads(stacked):
    return jnp.transpose(stacked, (1, 0, 2)).reshape(stacked.shape[1], -1)


def pull_group(first, second, third, fourth, fifth, sixth):
    return (
        lax.all_gather(first, ("dp", "fsdp"), axis=0, tiled=True),
        lax.all_gather(second, ("dp", "fsdp"), axis=0, tiled=True),
        lax.all_gather(third, ("dp", "fsdp"), axis=0, tiled=True),
        lax.all_gather(fourth, ("dp", "fsdp"), axis=0, tiled=True),
        lax.all_gather(fifth, ("dp", "fsdp"), axis=0, tiled=True),
        lax.all_gather(sixth, ("dp", "fsdp"), axis=0, tiled=True),
    )


def push_group(first, second, third, stacked):
    return (
        lax.psum_scatter(first, ("dp", "fsdp"), scatter_dimension=0, tiled=True),
        lax.psum_scatter(second, ("dp", "fsdp"), scatter_dimension=0, tiled=True),
        lax.psum_scatter(third, ("dp", "fsdp"), scatter_dimension=0, tiled=True),
        lax.psum_scatter(stacked, ("dp", "fsdp"), scatter_dimension=1, tiled=True),
    )


def head_forward(allowed, head_item):
    query_head, key_head, value_head = head_item
    scores = contract_cols(query_head, key_head) * allowed
    denominator = jnp.sum(scores, axis=1) + denom_eps
    numerator = jnp.dot(scores.astype(jnp.bfloat16), value_head, preferred_element_type=jnp.float32)
    return (numerator, denominator)


def head_backward(allowed, head_item):
    query_head, key_head, value_head, grad_numer, grad_denom = head_item
    scores = contract_cols(query_head, key_head) * allowed
    grad_prob = contract_cols(grad_numer, value_head)
    grad_value = contract_rows(scores.astype(jnp.bfloat16), grad_numer)
    grad_scores = ((grad_prob + grad_denom[:, None]) * allowed).astype(jnp.bfloat16)
    grad_query = jnp.dot(grad_scores, key_head, preferred_element_type=jnp.float32)
    grad_key = contract_rows(grad_scores, query_head)
    return (grad_query, grad_key, grad_value)


def plain_body(
    inputs,
    cotangent,
    seg_lengths,
    valid_len,
    w_qkv,
    b_qkv,
    w_out,
    b_out,
    gain_one,
    shift_one,
    w_up,
    b_up,
    w_down,
    b_down,
    gain_two,
    shift_two,
):
    token_rows = inputs[0].astype(jnp.float32)
    row_length = token_rows.shape[0]
    model_width = token_rows.shape[1]
    allowed, keeping = row_masks(seg_lengths[0], valid_len[0], row_length)
    full_qkv, full_bqkv, full_out, full_bout, full_gain, full_shift = pull_group(
        w_qkv, b_qkv, w_out, b_out, gain_one, shift_one
    )
    normed, norm_back = jax.vjp(
        layer_norm, token_rows, full_gain.astype(jnp.float32), full_shift.astype(jnp.float32)
    )
    normed_low = normed.astype(jnp.bfloat16)
    projected = jnp.dot(
        normed_low, full_qkv, preferred_element_type=jnp.float32
    ) + full_bqkv.astype(jnp.float32)
    query_feat, query_back = jax.vjp(feature_map, projected[:, :model_width])
    key_feat, key_back = jax.vjp(feature_map, projected[:, model_width : 2 * model_width])
    query_heads = split_heads(query_feat.astype(jnp.bfloat16))
    key_heads = split_heads(key_feat.astype(jnp.bfloat16))
    value_heads = split_heads(projected[:, 2 * model_width :].astype(jnp.bfloat16))
    numerator, denominator = lax.map(
        partial(head_forward, allowed), (query_heads, key_heads, value_heads)
    )
    attended = keeping[None, :, None] * numerator / denominator[:, :, None]
    attended_low = join_heads(attended).astype(jnp.bfloat16)
    middle = (
        token_rows
        + jnp.dot(attended_low, full_out, preferred_element_type=jnp.float32)
        + full_bout.astype(jnp.float32)
    )
    full_up, full_bup, full_down, full_bdown, full_gain_two, full_shift_two = pull_group(
        w_up, b_up, w_down, b_down, gain_two, shift_two
    )
    normed_two, norm_two_back = jax.vjp(
        layer_norm, middle, full_gain_two.astype(jnp.float32), full_shift_two.astype(jnp.float32)
    )
    normed_two_low = normed_two.astype(jnp.bfloat16)
    hidden = jnp.dot(normed_two_low, full_up, preferred_element_type=jnp.float32) + full_bup.astype(
        jnp.float32
    )
    activated, gelu_back = jax.vjp(gelu_tanh, hidden)
    activated_low = activated.astype(jnp.bfloat16)
    result = (
        middle
        + jnp.dot(activated_low, full_down, preferred_element_type=jnp.float32)
        + full_bdown.astype(jnp.float32)
    )
    again_up, again_bup, again_down, again_bdown, again_gain_two, again_shift_two = pull_group(
        w_up, b_up, w_down, b_down, gain_two, shift_two
    )
    grad_top = cotangent[0]
    grad_top_full = grad_top.astype(jnp.float32)
    grad_down = contract_rows(activated_low, grad_top)
    grad_bdown = jnp.sum(grad_top_full, axis=0)
    grad_hidden = gelu_back(contract_cols(grad_top, again_down))[0]
    grad_hidden_low = grad_hidden.astype(jnp.bfloat16)
    grad_bup = jnp.sum(grad_hidden_low.astype(jnp.float32), axis=0)
    grad_up = contract_rows(normed_two_low, grad_hidden_low)
    grad_normed_two = contract_cols(grad_hidden_low, again_up)
    grad_middle_norm, grad_gain_two, grad_shift_two = norm_two_back(grad_normed_two)
    grad_middle = grad_top_full + grad_middle_norm
    shard_up, shard_bup, shard_down, shard_small_two = push_group(
        grad_up, grad_bup, grad_down, jnp.stack([grad_bdown, grad_gain_two, grad_shift_two])
    )
    again_qkv, again_bqkv, again_out, again_bout, again_gain, again_shift = pull_group(
        w_qkv, b_qkv, w_out, b_out, gain_one, shift_one
    )
    grad_mixed = grad_middle.astype(jnp.bfloat16)
    grad_bout = jnp.sum(grad_mixed.astype(jnp.float32), axis=0)
    grad_wout = contract_rows(attended_low, grad_mixed)
    grad_attended = split_heads(contract_cols(grad_mixed, again_out))
    grad_numer = (keeping[None, :, None] * grad_attended / denominator[:, :, None]).astype(
        jnp.bfloat16
    )
    grad_denom = -jnp.sum(grad_attended * attended, axis=2) / denominator
    grad_query_heads, grad_key_heads, grad_value_heads = lax.map(
        partial(head_backward, allowed),
        (query_heads, key_heads, value_heads, grad_numer, grad_denom),
    )
    grad_query = query_back(join_heads(grad_query_heads))[0]
    grad_key = key_back(join_heads(grad_key_heads))[0]
    grad_projected = jnp.concatenate(
        [grad_query, grad_key, join_heads(grad_value_heads)], axis=1
    ).astype(jnp.bfloat16)
    grad_bias_all = jnp.sum(grad_projected.astype(jnp.float32), axis=0)
    grad_bias_qk = grad_bias_all[: 2 * model_width]
    grad_bias_v = grad_bias_all[2 * model_width :]
    grad_qkv = contract_rows(normed_low, grad_projected)
    grad_normed = contract_cols(grad_projected, again_qkv)
    grad_rows_norm, grad_gain_one, grad_shift_one = norm_back(grad_normed)
    grad_inputs = (grad_middle + grad_rows_norm).astype(jnp.bfloat16)
    shard_qkv, shard_bias_qk, shard_wout, shard_small_one = push_group(
        grad_qkv,
        grad_bias_qk,
        grad_wout,
        jnp.stack([grad_bout, grad_bias_v, grad_gain_one, grad_shift_one]),
    )
    return (
        result.astype(jnp.bfloat16)[None],
        grad_inputs[None],
        shard_qkv,
        shard_bias_qk,
        shard_small_one[1],
        shard_wout,
        shard_small_one[0],
        shard_small_one[2],
        shard_small_one[3],
        shard_up,
        shard_bup,
        shard_down,
        shard_small_two[0],
        shard_small_two[1],
        shard_small_two[2],
    )


HALF_LANES = 64
TILE = 512
Z_HIGH, Z_LOW, Y_BIT, X_BIT = 8, 4, 2, 1
MIXED = ((Z_HIGH, X_BIT, Z_LOW, Y_BIT), (Z_HIGH, Y_BIT, Z_LOW, X_BIT))
LINED = ((Z_HIGH, Z_LOW, X_BIT, Y_BIT), (Z_HIGH, Z_LOW, Y_BIT, X_BIT))
SMALL = 128
GROUP = 16
ANY = pl.BlockSpec(memory_space=pl.ANY)
SMEM = pl.BlockSpec(memory_space=pltpu.SMEM)
VMEM = pl.BlockSpec(memory_space=pltpu.VMEM)
MIB = 1 << 20


def swap_chips(block, bit):
    return lax.ppermute(block, "fsdp", [(place, place ^ bit) for place in range(16)])


def swap_cores(block):
    return lax.ppermute(block, "dp", [(0, 1), (1, 0)])


def relative_place(order, slot, last):
    return (
        order[0] * (slot & 1)
        + order[1] * ((slot >> 1) & 1)
        + order[2] * ((slot >> 2) & 1)
        + order[3] * last
    )


def tie(*blocks):
    return lax.optimization_barrier(blocks)


def by_side(shard):
    half = shard.shape[1] // 2
    return shard[None, :, :half], shard[None, :, half:]


def swap_sides(sides, orders, step):
    first, second = orders[0][step], orders[1][step]
    if first == second:
        return (swap_chips(jnp.stack(sides), first),)
    return swap_chips(sides[0], first), swap_chips(sides[1], second)


def sides_of(arrived):
    return (arrived[0][0], arrived[0][1]) if len(arrived) == 1 else arrived


def grown(sides, arrived):
    return tuple(jnp.concatenate([held, more]) for held, more in zip(sides, sides_of(arrived)))


def swap_both(sides):
    return swap_cores(sides[0]), swap_cores(sides[1])


def pieces_of(held, plane, across, core_held, core_across):
    plane = sides_of(plane)
    return tuple(
        block
        for side in range(2)
        for block in (held[side], plane[side], across[side], core_held[side], core_across[side])
    )


def added(parts, start, stop):
    return sum(part[start:stop].astype(jnp.float32) for part in parts)


def reduce_step(sides, orders, step, amount):
    sent = [added(parts, amount, 2 * amount).astype(jnp.bfloat16) for parts in sides]
    return swap_sides(sent, orders, step)


def with_arrived(sides, arrived):
    return [parts + [more] for parts, more in zip(sides, sides_of(arrived))]


def reduce_end(sides, orders):
    sides = with_arrived(sides, reduce_step(sides, orders, 0, 1))
    return [added(parts, 0, 1)[0] for parts in sides]


def side_by_side(sides, start, stop):
    return jnp.concatenate([side[:, start:stop] for side in sides], axis=1)


def far(array):
    return pltpu.with_memory_space_constraint(array, pltpu.HBM)


def call(kernel, outs, scratch, mib, args, in_specs, out_specs, grid=None, flops=0, gates=()):
    inputs, ignored = len(in_specs), len(gates)

    def gated(*refs):
        kernel(*refs[:inputs], *refs[inputs + ignored :])

    extra = {} if grid is None else {"grid": grid}
    near = (SMEM,) if grid else (SMEM, VMEM)
    args = [arg if spec in near else far(arg) for arg, spec in zip(args, in_specs)]
    gates = [far(gate) for gate in gates]
    if isinstance(outs, tuple):
        outs = tuple(
            out if spec in near else pltpu.HBM(out.shape, out.dtype)
            for out, spec in zip(outs, out_specs)
        )
    return pl.pallas_call(
        gated,
        out_shape=outs,
        in_specs=list(in_specs) + [ANY] * ignored,
        out_specs=out_specs,
        scratch_shapes=scratch,
        compiler_params=pltpu.CompilerParams(vmem_limit_bytes=mib * MIB),
        cost_estimate=pl.CostEstimate(flops=flops, bytes_accessed=0, transcendentals=0),
        **extra,
    )(*args, *gates)


def shaped(shape, dtype):
    return jax.ShapeDtypeStruct(shape, dtype)


def dot_nn(left, right):
    return lax.dot_general(left, right, (((1,), (0,)), ((), ())), preferred_element_type=jnp.float32)


def dot_nt(left, right):
    return lax.dot_general(left, right, (((1,), (1,)), ((), ())), preferred_element_type=jnp.float32)


def piece_at(pieces, side, core, last, slot):
    mine = pieces[5 * side : 5 * side + 5]
    if core or last:
        return mine[1 + core * 2 + last], slot
    return mine[slot // 4], slot % 4


def fetch(place, pieces, whole, sems, skip=0, orders=LINED):
    rows, half = pieces[0].shape[1], whole.shape[1] // 2
    copies = []
    for side, order in enumerate(orders):
        for core in range(2):
            for last in range(2):
                for slot in range(8):
                    piece, index = piece_at(pieces, side, core, last, slot)
                    owner = (place[1] ^ core) * 16 + (place[0] ^ relative_place(order, slot, last))
                    start = pl.multiple_of(owner * rows, rows)
                    copies.append(
                        pltpu.make_async_copy(
                            piece.at[index, :, pl.ds(skip, half)],
                            whole.at[pl.ds(start, rows), pl.ds(side * half, half)],
                            sems.at[len(copies)],
                        )
                    )
    for copy in copies:
        copy.start()
    return copies


def wait_side(copies, side):
    half = len(copies) // 2
    wait_all(copies[side * half : (side + 1) * half])


def wait_all(copies):
    for copy in copies:
        copy.wait()


def standardize(block):
    centred = block - jnp.mean(block, axis=1, keepdims=True)
    scale = lax.rsqrt(jnp.mean(centred * centred, axis=1, keepdims=True) + norm_eps)
    return centred * scale, scale


def norm_pull(grad, standard, scale, gain):
    scaled = grad * gain
    return scale * (
        scaled
        - jnp.mean(scaled, axis=1, keepdims=True)
        - standard * jnp.mean(scaled * standard, axis=1, keepdims=True)
    )


def place_kernel(where, lengths, valid, place):
    place[0] = where[0] & 15
    place[1] = where[0] >> 4
    end = lengths[0, 0]
    place[2] = end
    for image in range(1, 3):
        end = end + lengths[0, image]
        place[2 + image] = end
    place[5] = valid[0]


def run_place(where, lengths, valid):
    return call(
        place_kernel,
        shaped((6,), jnp.int32),
        [],
        8,
        (where, lengths, valid),
        in_specs=[SMEM] * 3,
        out_specs=SMEM,
    )


def fetch_small(place, pieces, small, skip, sems):
    copies = []
    for core in range(2):
        for last in range(2):
            for slot in range(8):
                piece, index = piece_at(pieces, 0, core, last, slot)
                far = relative_place(LINED[0], slot, last)
                owner = (place[1] ^ core) * 16 + (place[0] ^ far)
                start = pl.multiple_of(owner * GROUP, GROUP)
                copies.append(
                    pltpu.make_async_copy(
                        piece.at[index, pl.ds(0, GROUP), pl.ds(skip, SMALL)],
                        small.at[pl.ds(start, GROUP), :],
                        sems.at[len(copies)],
                    )
                )
                copies[-1].start()
    return copies


def tables(each):
    total = 32 * each
    column = lax.broadcasted_iota(jnp.int32, (1, total), 1).astype(jnp.float32)
    turn = jnp.floor((column + 0.5) / each)
    lane = lax.broadcasted_iota(jnp.int32, (SMALL, 1), 0).astype(jnp.float32)
    spread = jnp.where(column - turn * each == lane, 1.0, 0.0).astype(jnp.bfloat16)
    owner = lax.broadcasted_iota(jnp.int32, (32, 1), 0).astype(jnp.float32)
    return owner == turn, spread


def unfold(small, each, rows):
    mine, spread = tables(each)
    lines = []
    for row in rows:
        parts = small[pl.ds(row, 32, stride=GROUP), :].astype(jnp.bfloat16)
        parts = jnp.where(mine, dot_nn(parts, spread), 0.0)
        lines.append(jnp.sum(parts, axis=0, keepdims=True))
    return lines


def fold(small, each, vectors):
    mine, spread = tables(each)
    for row, vector in vectors:
        parts = jnp.where(mine, vector, 0.0).astype(jnp.bfloat16)
        small[pl.ds(row, 32, stride=32), :] = dot_nt(parts, spread)


def qkv_kernel(place, rows_in, *rest):
    pieces, (normed, query, key, value), lines, rest = rest[:10], rest[10:14], rest[14:20], rest[20:]
    whole, small, smalls, bias, sems, more = rest
    few = fetch_small(place, pieces, small, 4 * whole.shape[1] // 6, more)
    copies = fetch(place, pieces, whole, sems)
    wait_all(few)
    smalls[...] = small[...].astype(jnp.float32)
    width = rows_in.shape[1]
    (bias[...],) = unfold(smalls, 3 * width // 32, (0,))
    (lines[5][...],) = unfold(smalls, 4 * width // 32, (4,))
    bias_out, gain, shift, bias_down, gain_two, shift_two = unfold(
        smalls, width // 32, (1, 2, 3, 5, 6, 7)
    )
    for goal, line in zip(lines, (gain, bias_out, gain_two, shift_two, bias_down)):
        goal[...] = line
    for part in range(4):
        at = pl.ds(part * 128, 128)
        standard, _ = standardize(rows_in[at, :].astype(jnp.float32))
        normed[at, :] = (standard * gain + shift).astype(jnp.bfloat16)
    for tile in range(6):
        if tile % 3 == 0:
            wait_side(copies, tile // 3)
        cols = pl.ds(tile * TILE, TILE)
        projected = dot_nn(normed[...], whole[:, cols]) + bias[:, cols]
        goal = (query, key, value)[tile // 2]
        if tile < 4:
            projected = feature_map(projected)
        goal[:, pl.ds((tile % 2) * TILE, TILE)] = projected.astype(jnp.bfloat16)


def run_qkv(place, rows_in, pieces, gates=()):
    length, width = rows_in.shape
    narrow = shaped((length, width), jnp.bfloat16)
    line = shaped((1, width), jnp.float32)
    return call(
        qkv_kernel,
        (narrow,) * 4 + (line,) * 5 + (shaped((1, 4 * width), jnp.float32),),
        [
            pltpu.VMEM((width, 3 * width), jnp.bfloat16),
            pltpu.VMEM((32 * GROUP, SMALL), jnp.bfloat16),
            pltpu.VMEM((32 * GROUP, SMALL), jnp.float32),
            pltpu.VMEM((1, 3 * width), jnp.float32),
            pltpu.SemaphoreType.DMA((64,)),
            pltpu.SemaphoreType.DMA((32,)),
        ],
        18,
        (place, rows_in, *pieces),
        in_specs=[SMEM, VMEM] + [ANY] * 10,
        out_specs=(VMEM,) * 10,
        gates=gates,
    )


def image_of(place, positions):
    image = jnp.zeros(positions.shape, jnp.int32)
    for end in range(2, 5):
        image = image + jnp.where(positions >= place[end], 1, 0)
    return image


def allowed_block(place, length, flipped):
    first = lax.broadcasted_iota(jnp.int32, (length, 1), 0)
    second = lax.broadcasted_iota(jnp.int32, (1, length), 1)
    same = image_of(place, first) == image_of(place, second)
    ordered = (first <= second) if flipped else (second <= first)
    return jnp.where(same & ordered, 1.0, 0.0).astype(jnp.float32)


def low_lanes():
    return lax.broadcasted_iota(jnp.int32, (1, 2 * HALF_LANES), 1) < HALF_LANES


def two_heads(block):
    low = jnp.where(low_lanes(), 1.0, 0.0)
    high = (1.0 - low).astype(jnp.bfloat16)
    return jnp.concatenate([block * low.astype(jnp.bfloat16), block * high], axis=0)


def one_pair(stacked):
    half = stacked.shape[0] // 2
    return jnp.where(low_lanes(), stacked[:half], stacked[half:])


def masked(stacked, allowed):
    half = stacked.shape[0] // 2
    return jnp.concatenate(
        [(stacked[:half] * allowed).astype(jnp.bfloat16), (stacked[half:] * allowed).astype(jnp.bfloat16)],
        axis=0,
    )


def keeping_rows(place, start, amount):
    position = lax.broadcasted_iota(jnp.int32, (amount, 1), 0) + start
    return jnp.where(position < place[5], 1.0, 0.0)


def attend_kernel(place, query, key, value, attended, exact, inverse, allowed, wide):
    length, width = query.shape
    step = length // 2

    @pl.when(pl.program_id(0) == 0)
    def _():
        allowed[...] = allowed_block(place, length, False)
        wide[:, width:] = jnp.ones((length, width), jnp.bfloat16)

    wide[:, :width] = value[...]
    for part in range(2):
        rows, seen = pl.ds(part * step, step), (part + 1) * step
        scores = dot_nt(two_heads(query[rows, :]), key[:seen, :])
        total = dot_nn(masked(scores, allowed[rows, :seen]), wide[:seen, :])
        over = 1.0 / (one_pair(total[:, width:]) + denom_eps)
        inverse[rows, :] = over
        mixed = keeping_rows(place, part * step, step) * one_pair(total[:, :width]) * over
        exact[rows, :] = mixed
        attended[rows, :] = mixed.astype(jnp.bfloat16)


def run_attend(place, query, key, value, gates=()):
    length, width = query.shape
    pair = pl.BlockSpec((length, 2 * HALF_LANES), lambda p: (0, p))
    return call(
        attend_kernel,
        (
            shaped((length, width), jnp.bfloat16),
            shaped((length, width), jnp.float32),
            shaped((length, width), jnp.float32),
        ),
        [
            pltpu.VMEM((length, length), jnp.float32),
            pltpu.VMEM((length, 4 * HALF_LANES), jnp.bfloat16),
        ],
        10,
        (place, query, key, value),
        grid=(width // (2 * HALF_LANES),),
        in_specs=[SMEM] + [pair] * 3,
        out_specs=(pair,) * 3,
        gates=gates,
    )


def attend_back_pair(
    place, query, key, value, grad_att, exact, inverse, stacked, sums, allowed, flipped, left, wide
):
    length, width = query.shape
    step = length // 2
    wide[:, :width] = value[...]
    over = grad_att[...] * inverse[...]
    lane = lax.broadcasted_iota(jnp.int32, (1, width), 1)
    terms, low = over * exact[...], lane < HALF_LANES
    first = jnp.sum(jnp.where(low, terms, 0.0), axis=1, keepdims=True)
    second = jnp.sum(jnp.where(low, 0.0, terms), axis=1, keepdims=True)
    spread = -jnp.where(low, first, second)
    high = spread.astype(jnp.bfloat16).astype(jnp.float32)
    within = lane & (HALF_LANES - 1)
    spread = jnp.where(within == 0, high, jnp.where(within == 1, spread - high, 0.0))
    numer = (keeping_rows(place, 0, length) * over).astype(jnp.bfloat16)
    for head in range(2):
        here = jnp.where(low, 1.0 - head, 1.0 * head)
        at = pl.ds(head * length, length)
        left[at, :width] = numer * here.astype(jnp.bfloat16)
        left[at, width:] = (spread * here).astype(jnp.bfloat16)
    for part in range(2):
        rows, seen = pl.ds(part * step, step), (part + 1) * step
        start = part * step
        later = pl.ds(start, length - start)
        both = jnp.concatenate([left[rows, :], left[pl.ds(length + start, step), :]], axis=0)
        grad_scores = masked(dot_nt(both, wide[:seen, :]), allowed[rows, :seen])
        grad_query = one_pair(dot_nn(grad_scores, key[:seen, :]))
        full = left[later, :] + left[pl.ds(length + start, length - start), :]
        scores = masked(dot_nt(two_heads(key[rows, :]), query[later, :]), flipped[rows, later])
        grad_value = one_pair(dot_nn(scores, full[:, :width]))
        ones = jnp.concatenate([two_heads(value[rows, :]), two_heads(wide[rows, width:])], axis=1)
        grad_scores = masked(dot_nt(ones, full), flipped[rows, later])
        grad_key = one_pair(dot_nn(grad_scores, query[later, :]))
        grads = (
            grad_query * jnp.minimum(query[rows, :].astype(jnp.float32), 1.0),
            grad_key * jnp.minimum(key[rows, :].astype(jnp.float32), 1.0),
            grad_value,
        )
        for index, grad in enumerate(grads):
            low_grad, line = grad.astype(jnp.bfloat16), pl.ds(index, 1)
            stacked[index, rows, :] = low_grad
            extra = jnp.sum(low_grad.astype(jnp.float32), axis=0, keepdims=True)
            sums[line, :] = extra if part == 0 else sums[line, :] + extra


def attend_back_kernel(
    place, query, key, value, grad_att, exact, inverse, stacked, sums, allowed, flipped, left, wide
):
    length, width = query.shape[0], 2 * HALF_LANES
    pairs = query.shape[1] // width

    @pl.when(pl.program_id(0) == 0)
    def _():
        allowed[...] = allowed_block(place, length, False)
        flipped[...] = allowed_block(place, length, True)
        for pair in range(pairs):
            wide[pair, :, width:] = jnp.ones((length, width), jnp.bfloat16)

    for pair in range(pairs):
        cols = pl.ds(pair * width, width)
        attend_back_pair(
            place,
            *(ref.at[:, cols] for ref in (query, key, value, grad_att, exact, inverse)),
            stacked.at[:, :, cols],
            sums.at[:, cols],
            allowed,
            flipped,
            left.at[pair],
            wide.at[pair],
        )


def run_attend_back(place, first, query, key, value, grad_att, exact, inverse, gates=()):
    length, width = query.shape
    half = width // 2
    start = first * half // (4 * HALF_LANES)
    pair = pl.BlockSpec((length, 4 * HALF_LANES), lambda p: (0, p + start))
    stack = pl.BlockSpec((3, length, 4 * HALF_LANES), lambda p: (0, 0, p))
    lines = pl.BlockSpec((3, 4 * HALF_LANES), lambda p: (0, p))
    return call(
        attend_back_kernel,
        (shaped((3, length, half), jnp.bfloat16), shaped((3, half), jnp.float32)),
        [
            pltpu.VMEM((length, length), jnp.float32),
            pltpu.VMEM((length, length), jnp.float32),
            pltpu.VMEM((2, 2 * length, 4 * HALF_LANES), jnp.bfloat16),
            pltpu.VMEM((2, length, 4 * HALF_LANES), jnp.bfloat16),
        ],
        20,
        (place, query, key, value, grad_att, exact, inverse),
        grid=(half // (4 * HALF_LANES),),
        in_specs=[SMEM] + [pair] * 6,
        out_specs=(stack, lines),
        gates=gates,
    )


def hand_over(place, sources, goal, sems):
    copies, at = [], 0
    for source in sources:
        half = source.shape[1] // 2
        start = pl.multiple_of((1 - place[1]) * half, half)
        copies.append(
            pltpu.make_async_copy(
                source.at[:, pl.ds(start, half)], goal.at[:, pl.ds(at, half)], sems.at[len(copies)]
            )
        )
        copies[-1].start()
        at += half
    return copies


def out_kernel(place, rows_in, early, attended, bias, gain, shift, *rest):
    pieces, (middle, normed, handed, whole, sems, more) = rest[:10], rest[10:]
    copies = fetch(place, pieces, whole, sems, 3 * whole.shape[1] // 2)
    handing = hand_over(place, (early, attended), handed, more)
    for side in range(2):
        wait_side(copies, side)
        cols = pl.ds(side * TILE, TILE)
        middle[:, cols] = (
            rows_in[:, cols].astype(jnp.float32) + dot_nn(attended[...], whole[:, cols]) + bias[:, cols]
        )
    for part in range(4):
        at = pl.ds(part * 128, 128)
        standard, _ = standardize(middle[at, :])
        normed[at, :] = (standard * gain[...] + shift[...]).astype(jnp.bfloat16)
    wait_all(handing)


def run_out(place, rows_in, early, attended, bias, gain, shift, pieces, gates=()):
    length, width = rows_in.shape
    narrow = shaped((length, width), jnp.bfloat16)
    return call(
        out_kernel,
        (shaped((length, width), jnp.float32), narrow, narrow),
        [
            pltpu.VMEM((width, width), jnp.bfloat16),
            pltpu.SemaphoreType.DMA((64,)),
            pltpu.SemaphoreType.DMA((2,)),
        ],
        16,
        (place, rows_in, early, attended, bias, gain, shift, *pieces),
        in_specs=[SMEM] + [VMEM] * 6 + [ANY] * 10,
        out_specs=(VMEM, VMEM, ANY),
        gates=gates,
    )


def bend_tile(hidden, activated, slope):
    square = hidden * hidden
    rate = gelu_coef + (gelu_coef * 0.044715) * square
    bend = jnp.tanh(hidden * rate)
    share = 0.5 + 0.5 * bend
    activated[...] = (hidden * share).astype(jnp.bfloat16)
    rate = gelu_coef + (3.0 * gelu_coef * 0.044715) * square
    slope[...] = (share + (0.5 * hidden) * (1.0 - bend * bend) * rate).astype(jnp.bfloat16)


def up_kernel(place, normed, bias, *rest):
    pieces, (activated, slope, handed, whole, hidden, sems, more) = rest[:10], rest[10:]
    copies = fetch(place, pieces, whole, sems)
    tiles = whole.shape[1] // TILE

    def columns(tile):
        return pl.ds(tile * TILE, TILE)

    for tile in range(tiles + 1):
        if tile % (tiles // 2) == 0 and tile < tiles:
            wait_side(copies, tile // (tiles // 2))
        if tile < tiles:
            cols = columns(tile)
            hidden[tile % 2] = dot_nn(normed[...], whole[:, cols]) + bias[:, cols]
        if tile > 0:
            cols = columns(tile - 1)
            bend_tile(hidden[(tile - 1) % 2], activated.at[:, cols], slope.at[:, cols])

    wait_all(hand_over(place, (normed, activated), handed, more))


def run_up(place, normed, bias, pieces, gates=()):
    length, width = normed.shape
    wide = bias.shape[1]
    return call(
        up_kernel,
        (shaped((length, wide), jnp.bfloat16),) * 2
        + (shaped((length, (width + wide) // 2), jnp.bfloat16),),
        [
            pltpu.VMEM((width, wide), jnp.bfloat16),
            pltpu.VMEM((2, length, TILE), jnp.float32),
            pltpu.SemaphoreType.DMA((64,)),
            pltpu.SemaphoreType.DMA((2,)),
        ],
        26,
        (place, normed, bias, *pieces),
        in_specs=[SMEM] + [VMEM] * 2 + [ANY] * 10,
        out_specs=(VMEM, VMEM, ANY),
        gates=gates,
    )


def sum_kernel(block, total):
    total[...] = jnp.sum(block[...].astype(jnp.float32), axis=0, keepdims=True)


def run_sum(block, cover, gates=()):
    return call(
        sum_kernel,
        shaped((1, block.shape[1]), jnp.float32),
        [],
        8,
        (block,),
        in_specs=[VMEM],
        out_specs=VMEM,
        flops=cover,
        gates=gates,
    )


def down_kernel(place, activated, slope, grad_top, middle, bias, *rest):
    pieces, (result, grad_hidden, sum_up, whole, sems) = rest[:10], rest[10:]
    copies = fetch(place, pieces, whole, sems, orders=MIXED)
    wait_all(copies)
    for tile in range(4):
        cols = pl.ds(tile * 256, 256)
        result[:, cols] = (
            middle[:, cols] + bias[:, cols] + dot_nn(activated[...], whole[:, cols])
        ).astype(jnp.bfloat16)
        for half in range(2):
            cols = pl.ds((2 * tile + half) * TILE, TILE)
            grad = dot_nt(grad_top[...], whole[cols, :]) * slope[:, cols].astype(jnp.float32)
            low = grad.astype(jnp.bfloat16)
            grad_hidden[:, cols] = low
            sum_up[:, cols] = jnp.sum(low.astype(jnp.float32), axis=0, keepdims=True)


def run_down(place, activated, slope, grad_top, middle, bias, pieces, gates=()):
    length, width = middle.shape
    wide = activated.shape[1]
    return call(
        down_kernel,
        (
            shaped((length, width), jnp.bfloat16),
            shaped((length, wide), jnp.bfloat16),
            shaped((1, wide), jnp.float32),
        ),
        [
            pltpu.VMEM((wide, width), jnp.bfloat16),
            pltpu.SemaphoreType.DMA((64,)),
        ],
        30,
        (place, activated, slope, grad_top, middle, bias, *pieces),
        in_specs=[SMEM] + [VMEM] * 5 + [ANY] * 10,
        out_specs=(VMEM,) * 3,
        flops=64 * length * width * wide,
        gates=gates,
    )


def middle_back_kernel(place, grad_hidden, middle, grad_top, gain, *rest):
    pieces_up, pieces_in, rest = rest[:10], rest[10:20], rest[20:]
    grad_middle, mixed, grad_att, sum_gain, sum_shift, whole, outer, total, sems, more = rest
    copies = fetch(place, pieces_up, whole, sems)
    second = fetch(place, pieces_in, outer, more, 3 * outer.shape[1] // 2)
    step = 2 * TILE
    for tile in range(whole.shape[1] // step):
        if tile % 2 == 0:
            wait_side(copies, tile // 2)
        cols = pl.ds(tile * step, step)
        block = dot_nt(grad_hidden[:, cols], whole[:, cols])
        total[...] = block if tile == 0 else total[...] + block

    for part in range(4):
        at = pl.ds(part * 128, 128)
        grad = total[at, :]
        standard, scale = standardize(middle[at, :])
        back = grad_top[at, :].astype(jnp.float32) + norm_pull(grad, standard, scale, gain[...])
        grad_middle[at, :] = back
        low = back.astype(jnp.bfloat16)
        mixed[at, :] = low
        for goal, added in ((sum_gain, grad * standard), (sum_shift, grad)):
            added = jnp.sum(added, axis=0, keepdims=True)
            goal[...] = added if part == 0 else goal[...] + added
    wait_all(second)
    for part in range(2):
        cols = pl.ds(part * TILE, TILE)
        grad_att[:, cols] = dot_nt(mixed[...], outer[cols, :])


def run_middle_back(place, grad_hidden, middle, grad_top, gain, pieces_up, pieces_in, gates=()):
    length, width = middle.shape
    wide = grad_hidden.shape[1]
    full, line = shaped((length, width), jnp.float32), shaped((1, width), jnp.float32)
    return call(
        middle_back_kernel,
        (full, shaped((length, width), jnp.bfloat16), full, line, line),
        [
            pltpu.VMEM((width, wide), jnp.bfloat16),
            pltpu.VMEM((width, width), jnp.bfloat16),
            pltpu.VMEM((length, width), jnp.float32),
            pltpu.SemaphoreType.DMA((64,)),
            pltpu.SemaphoreType.DMA((64,)),
        ],
        30,
        (place, grad_hidden, middle, grad_top, gain, *pieces_up, *pieces_in),
        in_specs=[SMEM] + [VMEM] * 4 + [ANY] * 20,
        out_specs=(VMEM,) * 5,
        gates=gates,
    )


def inputs_back_kernel(place, early, late, rows_in, gain, grad_middle, sum_out, *rest):
    (sums, late_sums, *ready), pieces, rest = rest[:6], rest[6:16], rest[16:]
    grad_rows, lines, whole, total, sems = rest
    copies = fetch(place, pieces, whole, sems)
    width = rows_in.shape[1]
    for tile in range(6):
        if tile % 3 == 0:
            wait_side(copies, tile // 3)
        grads = (early, late)[tile % 2]
        block = dot_nt(grads[tile // 2], whole[:, pl.ds(tile * TILE, TILE)])
        total[...] = block if tile == 0 else total[...] + block
    for part in range(4):
        at = pl.ds(part * 128, 128)
        grad = total[at, :]
        standard, scale = standardize(rows_in[at, :].astype(jnp.float32))
        back = grad_middle[at, :] + norm_pull(grad, standard, scale, gain[...])
        grad_rows[at, :] = back.astype(jnp.bfloat16)
        for index, extra in enumerate((grad * standard, grad)):
            goal = lines.at[:, pl.ds((4 + index) * width, width)]
            extra = jnp.sum(extra, axis=0, keepdims=True)
            goal[...] = extra if part == 0 else goal[...] + extra
    half = width // 2
    for row in range(3):
        for index, source in enumerate((sums, late_sums)):
            lines[:, pl.ds(row * width + index * half, half)] = source[pl.ds(row, 1), :]
    lines[:, pl.ds(3 * width, width)] = sum_out[...]
    at = 6 * width
    for source in ready:
        lines[:, pl.ds(at, source.shape[1])] = source[...]
        at += source.shape[1]


def run_inputs_back(
    place, early, late, rows_in, gain, grad_middle, sum_out, ready, pieces, gates=()
):
    length, width = rows_in.shape
    total = 6 * width + sum(line.shape[1] for line in ready[2:])
    return call(
        inputs_back_kernel,
        (shaped((length, width), jnp.bfloat16), shaped((1, total), jnp.float32)),
        [
            pltpu.VMEM((width, 3 * width), jnp.bfloat16),
            pltpu.VMEM((length, width), jnp.float32),
            pltpu.SemaphoreType.DMA((64,)),
        ],
        20,
        (place, early, late, rows_in, gain, grad_middle, sum_out, *ready, *pieces),
        in_specs=[SMEM] + [VMEM] * 12 + [ANY] * 10,
        out_specs=(VMEM,) * 2,
        flops=1 << 34,
        gates=gates,
    )


def weight_kernel(orders, skips, sizes, place, *rest):
    groups = len(skips)
    if sizes:
        mine, other_lines, rest = rest[4 * groups], rest[4 * groups + 1], rest[: 4 * groups] + rest[4 * groups + 2 :]
    inputs, outs, rest = rest[: 4 * groups], rest[4 * groups : 4 * groups + 4], rest[4 * groups + 4 :]
    wholes, (turned, sems), rest = rest[:groups], rest[groups : groups + 2], rest[groups + 2 :]
    length, rows = inputs[0].shape[0], outs[0].shape[1]
    owners = 256 // rows
    at, copies = 0, []
    if sizes:
        wide_small, small, more = rest
        at = sum(whole.shape[2] // 2 for whole in wholes)
        wide_small[...] = jnp.zeros_like(wide_small)
        start, by_size = 0, {}
        for row, size in enumerate(sizes):
            line = mine[:, start : start + size] + other_lines[:, start : start + size]
            by_size.setdefault(size, []).append((row, line))
            start += size
        for size, vectors in by_size.items():
            fold(wide_small, size // 32, vectors)
        small[...] = wide_small[...].astype(jnp.bfloat16)
        for last in range(2):
            for slot in range(8):
                chip = place[0] ^ relative_place(orders[0], slot, last)
                start = pl.multiple_of((place[1] * 16 + chip) * 32, 32)
                copies.append(
                    pltpu.make_async_copy(
                        small.at[pl.ds(start, 32), :],
                        outs[last * 2].at[slot, :, pl.ds(at, SMALL)],
                        more.at[last * 8 + slot],
                    )
                )
                copies[-1].start()
    at, few = 0, len(copies)
    for group, (skip, whole) in enumerate(zip(skips, wholes)):
        left_own, left_other, own, other = inputs[4 * group : 4 * group + 4]
        count, each = own.shape[0], own.shape[2]
        tiles, half = whole.shape[0], whole.shape[2] // 2
        for tile in range(tiles):
            low = pl.multiple_of(((place[0] // owners) ^ tile) * 256, 256)
            start = pl.multiple_of(place[1] * (256 * tiles) + low, 256)
            left = turned.at[tile % 2]
            left[:, :length] = left_own[:, pl.ds(start, 256)].T
            left[:, length:] = left_other[:, pl.ds(skip + low, 256)].T
            for index in range(count):
                for step in range(each // TILE):
                    cols = pl.ds(step * TILE, TILE)
                    block = dot_nn(left[:, :length], own[index, :, cols])
                    block += dot_nn(left[:, length:], other[index, :, cols])
                    goal = pl.ds(index * each + step * TILE, TILE)
                    whole[tile, :, goal] = block.astype(jnp.bfloat16)
            for side, order in enumerate(orders):
                for last in range(2):
                    for slot in range(8):
                        far_place = relative_place(order, slot, last)
                        if far_place // owners != tile:
                            continue
                        start = pl.multiple_of(((place[0] ^ far_place) % owners) * rows, rows)
                        copies.append(
                            pltpu.make_async_copy(
                                whole.at[tile, pl.ds(start, rows), pl.ds(side * half, half)],
                                outs[last * 2 + side].at[slot, :, pl.ds(at, half)],
                                sems.at[len(copies) - few],
                            )
                        )
                        copies[-1].start()
        at += half
    wait_all(copies)


def run_weight(place, orders, height, groups, gates=(), sizes=(), lines=()):
    length = groups[0][0].shape[0]
    totals = [own.shape[0] * own.shape[2] for _, _, _, own, _ in groups]
    half = sum(totals) // 2
    part = shaped((8, height // 16, half), jnp.bfloat16)
    first = shaped((8, height // 16, half + (SMALL if sizes else 0)), jnp.bfloat16)
    extra = [
        pltpu.VMEM((32 * 32, SMALL), jnp.float32),
        pltpu.VMEM((32 * 32, SMALL), jnp.bfloat16),
        pltpu.SemaphoreType.DMA((16,)),
    ]
    return call(
        partial(weight_kernel, orders, tuple(group[2] for group in groups), sizes),
        (first,) * 4,
        [pltpu.VMEM((height // 256, 256, total), jnp.bfloat16) for total in totals]
        + [
            pltpu.VMEM((2, 256, 2 * length), jnp.bfloat16),
            pltpu.SemaphoreType.DMA((32 * len(groups),)),
        ]
        + (extra if sizes else []),
        22,
        (place, *(array for group in groups for array in group[:2] + group[3:]), *lines),
        in_specs=[SMEM] + [VMEM] * (4 * len(groups) + len(lines)),
        out_specs=(ANY,) * 4,
        gates=gates,
    )


def paired_body(
    inputs,
    cotangent,
    seg_lengths,
    valid_len,
    w_qkv,
    b_qkv,
    w_out,
    b_out,
    gain_one,
    shift_one,
    w_up,
    b_up,
    w_down,
    b_down,
    gain_two,
    shift_two,
):
    where = (lax.axis_index("dp") * 16 + lax.axis_index("fsdp")).astype(jnp.int32)[None]
    rows_in, grad_top = inputs[0], cotangent[0]
    vectors = (b_qkv, b_out, gain_one, shift_one, b_up, b_down, gain_two, shift_two)
    cut = w_qkv.shape[1] // 2
    edge = w_out.shape[1] // 2
    held_in = (
        jnp.concatenate([w_qkv[:, :cut], w_out[:, :edge]], axis=1)[None],
        jnp.concatenate([w_qkv[:, cut:], w_out[:, edge:]], axis=1)[None],
    )
    small = jnp.stack([jnp.pad(vector, (0, SMALL - vector.shape[0])) for vector in vectors])
    small = jnp.pad(small, ((0, w_out.shape[0] - small.shape[0]), (0, 0)))[None]
    small_far = swap_chips(small, Z_HIGH)
    place = run_place(where, seg_lengths, valid_len)
    place, small_far = tie(place, small_far)
    small = jnp.concatenate([small, small_far])
    held_up, held_down = by_side(w_up), by_side(w_down)
    top = grad_top[None]
    held_in = grown(held_in, swap_sides(held_in, LINED, 0))
    held_in = (
        jnp.concatenate([held_in[0], small], axis=2),
        jnp.concatenate([held_in[1], jnp.zeros_like(small)], axis=2),
    )
    held_in = grown(held_in, swap_sides(held_in, LINED, 1))
    held_in, held_up = tie(held_in, held_up)
    start_up = swap_sides(held_up, LINED, 0)
    plane_in = swap_sides(held_in, LINED, 2)
    start_up, plane_in = tie(start_up, plane_in)
    held_up = grown(held_up, start_up)
    held_up, held_down = tie(held_up, held_down)
    full_in = grown(held_in, plane_in)
    across_in = swap_sides(full_in, LINED, 3)
    core_in = swap_both(full_in)
    held_up = grown(held_up, swap_sides(held_up, LINED, 1))
    start_down = swap_sides(held_down, LINED, 0)
    across_in, start_down = tie(across_in, start_down)
    pieces_in = pieces_of(held_in, plane_in, across_in, core_in, swap_both(across_in))
    plane_up = swap_sides(held_up, LINED, 2)
    held_down = grown(held_down, start_down)
    plane_down = swap_sides(held_down, MIXED, 1)
    top_other = swap_cores(top)

    normed, query, key, value, *lines = run_qkv(
        place, rows_in, pieces_in, (*held_up, *held_down, top_other)
    )
    full_gain, full_bout, full_gain_two, full_shift_two, full_bdown, full_bup = lines
    plane_up, plane_down, normed = tie(plane_up, plane_down, normed)
    full_up = grown(held_up, plane_up)
    across_up = swap_sides(full_up, LINED, 3)
    core_up = swap_both(full_up)
    held_down = grown(held_down, plane_down)
    line_down = swap_sides(held_down, MIXED, 2)
    attended, exact, inverse = run_attend(place, query, key, value, (*plane_up, *held_down))
    core_up, attended = tie(core_up, attended)
    middle, normed_two, inner_half = run_out(
        place,
        rows_in,
        normed,
        attended,
        full_bout,
        full_gain_two,
        full_shift_two,
        pieces_in,
    )
    inner_other = swap_cores(inner_half)
    across_up, line_down, normed_two = tie(across_up, line_down, normed_two)
    pieces_up = pieces_of(held_up, plane_up, across_up, core_up, swap_both(across_up))
    full_down = grown(held_down, line_down)
    across_down = swap_sides(full_down, MIXED, 3)
    core_down = swap_both(full_down)
    activated, slope, outer_half = run_up(
        place, normed_two, full_bup, pieces_up, (*line_down, inner_other)
    )
    outer_other = swap_cores(outer_half)
    sum_down = run_sum(grad_top, 1 << 35, (outer_half,))
    thin = normed_two.shape[1] // 2
    parts = run_weight(
        place,
        LINED,
        activated.shape[1] // 2,
        [(activated, outer_other, thin, top, top_other)],
        (*core_down, sum_down),
    )
    across_down, parts = tie(across_down, parts)
    down_one = swap_sides(parts[2:], LINED, 3)
    pieces_down = pieces_of(held_down, line_down, across_down, core_down, swap_both(across_down))
    result, grad_hidden, sum_up = run_down(
        place, activated, slope, grad_top, middle, full_bdown, pieces_down, parts[2:]
    )
    hidden_other = swap_cores(grad_hidden[None])
    grad_middle, mixed, grad_att, sum_gain_two, sum_shift_two = run_middle_back(
        place, grad_hidden, middle, grad_top, full_gain_two, pieces_up, pieces_in
    )
    mixed = mixed[None]
    down_one, mixed = tie(down_one, mixed)
    mixed_other = swap_cores(mixed)
    down_sides = with_arrived([[parts[0]], [parts[1]]], down_one)
    down_two = reduce_step(down_sides, LINED, 2, 4)
    sum_out = run_sum(mixed[0], 1 << 35, down_one)
    hidden_other, sum_out = tie(hidden_other, sum_out)
    parts = run_weight(
        place, LINED, thin, [(normed_two, outer_other, 0, grad_hidden[None], hidden_other)]
    )
    up_one = swap_sides(parts[2:], LINED, 3)
    grads, sums = run_attend_back(
        place, 0, query, key, value, grad_att, exact, inverse, parts[2:]
    )
    down_two, mixed_other, grads = tie(down_two, mixed_other, grads)
    down_sides = with_arrived(down_sides, down_two)
    down_three = reduce_step(down_sides, LINED, 1, 2)
    grads_other = swap_cores(grads)
    late, late_sums = run_attend_back(
        place, 1, query, key, value, grad_att, exact, inverse, (grads,)
    )
    up_one, late = tie(up_one, late)
    up_sides = with_arrived([[parts[0]], [parts[1]]], up_one)
    late_other = swap_cores(late)
    up_two = reduce_step(up_sides, LINED, 2, 4)
    grad_rows, lines = run_inputs_back(
        place,
        grads,
        late,
        rows_in,
        full_gain,
        grad_middle,
        sum_out,
        (sums, late_sums, sum_up, sum_down, sum_gain_two, sum_shift_two),
        pieces_in,
        up_one,
    )
    up_two, down_three, grads_other, late_other, lines = tie(
        up_two, down_three, grads_other, late_other, lines
    )
    down_sides = with_arrived(down_sides, down_three)
    up_sides = with_arrived(up_sides, up_two)
    up_three = reduce_step(up_sides, LINED, 1, 2)
    lines_other = swap_cores(lines)
    parts = run_weight(
        place,
        MIXED,
        thin,
        [
            (normed, inner_other, 0, grads, grads_other),
            (attended, inner_other, thin, mixed, mixed_other),
        ],
    )
    lines_other, parts = tie(lines_other, parts)
    in_sides = [[parts[0]], [parts[1]]]
    in_one = swap_sides(parts[2:], MIXED, 3)
    narrow, wide = mixed.shape[2], sum_up.shape[1]
    sizes = (2 * narrow, narrow, narrow, narrow, narrow, wide, narrow, narrow, narrow)
    parts = run_weight(
        place,
        LINED,
        thin,
        [(normed, inner_other, 0, late, late_other)],
        parts[:1],
        sizes,
        (lines, lines_other),
    )
    down_four = reduce_step(down_sides, LINED, 0, 1)
    up_three, parts = tie(up_three, parts)
    up_sides = with_arrived(up_sides, up_three)
    up_four = reduce_step(up_sides, LINED, 0, 1)
    late_sides = [[parts[0]], [parts[1]]]
    late_one = swap_sides(parts[2:], LINED, 3)
    in_sides = with_arrived(in_sides, in_one)
    late_one, down_four = tie(late_one, down_four)
    down_sides = with_arrived(down_sides, down_four)
    late_sides = with_arrived(late_sides, late_one)
    in_sides = with_arrived(in_sides, reduce_step(in_sides, MIXED, 2, 4))
    late_sides = with_arrived(late_sides, reduce_step(late_sides, LINED, 2, 4))
    up_sides = with_arrived(up_sides, up_four)
    in_sides = with_arrived(in_sides, reduce_step(in_sides, MIXED, 1, 2))
    late_sides = with_arrived(late_sides, reduce_step(late_sides, LINED, 1, 2))
    shard_down = side_by_side([added(parts, 0, 1)[0] for parts in down_sides], 0, edge)
    shard_up = side_by_side([added(parts, 0, 1)[0] for parts in up_sides], 0, w_up.shape[1] // 2)
    shards = reduce_end(in_sides, MIXED)
    cut = cut // 2
    first = side_by_side(shards, 0, cut)
    shard_out = side_by_side(shards, cut, cut + edge)
    shards = reduce_end(late_sides, LINED)
    second = side_by_side(shards, 0, cut)
    third = edge
    shard_qkv = jnp.concatenate(
        [
            half[:, part * third : (part + 1) * third]
            for part in range(3)
            for half in (first, second)
        ],
        axis=1,
    )
    smalls = [shards[0][row, cut : cut + size // 32] for row, size in enumerate(sizes)]
    grad_bqk, grad_bv, grad_bout, grad_gain, grad_shift, grad_bup, grad_bdown, grad_gain_two, grad_shift_two = smalls
    return (
        result[None],
        grad_rows[None],
        shard_qkv,
        grad_bqk,
        grad_bv,
        shard_out,
        grad_bout,
        grad_gain,
        grad_shift,
        shard_up,
        grad_bup,
        shard_down,
        grad_bdown,
        grad_gain_two,
        grad_shift_two,
    )


def solution(mesh):
    placed = (
        P(("dp", "fsdp"), None, None),
        P(("dp", "fsdp"), None, None),
        P(("dp", "fsdp"), None),
        P(("dp", "fsdp")),
        P(("dp", "fsdp"), None),
        P(("dp", "fsdp")),
        P(("dp", "fsdp"), None),
        P(("dp", "fsdp")),
        P(("dp", "fsdp")),
        P(("dp", "fsdp")),
        P(("dp", "fsdp"), None),
        P(("dp", "fsdp")),
        P(("dp", "fsdp"), None),
        P(("dp", "fsdp")),
        P(("dp", "fsdp")),
        P(("dp", "fsdp")),
    )
    paired = dict(mesh.shape) == {"dp": 2, "fsdp": 16}
    return jax.shard_map(
        paired_body if paired else plain_body,
        mesh=mesh,
        in_specs=placed,
        out_specs=(
            P(("dp", "fsdp"), None, None),
            P(("dp", "fsdp"), None, None),
            P(("dp", "fsdp"), None),
            P(("dp", "fsdp")),
            P(("dp", "fsdp")),
            P(("dp", "fsdp"), None),
            P(("dp", "fsdp")),
            P(("dp", "fsdp")),
            P(("dp", "fsdp")),
            P(("dp", "fsdp"), None),
            P(("dp", "fsdp")),
            P(("dp", "fsdp"), None),
            P(("dp", "fsdp")),
            P(("dp", "fsdp")),
            P(("dp", "fsdp")),
        ),
        check_vma=False,
    )
```
